32 devices in a mesh: dp: 16 (over z, x, core), tensor: 2 (over y).
Axes of the slice: x: 2, y: 2, z: 4, core: 2. Of those that a mesh axis runs over, the one named last changes fastest.
Arguments:
- tokens: bfloat16 [8192, 2048], P(('dp', 'tensor')), may hold values from -6 to 6
- layer_input: bfloat16 [8192, 256], P(('dp', 'tensor')), may hold values from -6 to 6
- block_ids: int32 [1, 8192], replicated, may hold values from 0 to 63, never falling along the last dimension, each value on 1 to 256 neighbouring positions
- block_table: int32 [1, 64, 64], replicated, may hold values from 0 to 1, as said below
- w_query: bfloat16 [2048, 2048], P('dp', 'tensor'), may hold values from -0.125 to 0.125
- w_key: bfloat16 [2048, 512], P('dp', 'tensor'), may hold values from -0.125 to 0.125
- w_value: bfloat16 [2048, 512], P('dp', 'tensor'), may hold values from -0.125 to 0.125
- w_output: bfloat16 [2048, 2048], P('tensor', 'dp'), may hold values from -0.125 to 0.125
- w_left: bfloat16 [2048, 64], P('dp'), may hold values from -0.125 to 0.125
- w_right: bfloat16 [64, 2048], P(None, 'dp'), may hold values from -0.75 to 0.75
- w_gate: bfloat16 [2048, 8192], P('dp', 'tensor'), may hold values from -0.125 to 0.125
- w_up: bfloat16 [2048, 8192], P('dp', 'tensor'), may hold values from -0.125 to 0.125
- w_down: bfloat16 [8192, 2048], P('tensor', 'dp'), may hold values from -0.0625 to 0.0625
- w_layer_gate: bfloat16 [2048, 256], P('dp'), may hold values from -0.125 to 0.125
- w_layer_proj: bfloat16 [256, 2048], P(None, 'dp'), may hold values from -0.375 to 0.375
- query_gain: bfloat16 [256], P('dp'), may hold values from 0.19921875 to 0.5
- key_gain: bfloat16 [256], P('dp'), may hold values from 0.19921875 to 0.5
- gain_input: bfloat16 [2048], P('dp'), may hold values from 0.5 to 1.5
- gain_attn_out: bfloat16 [2048], P('dp'), may hold values from 0.5 to 1.5
- gain_laurel: bfloat16 [2048], P('dp'), may hold values from 0.5 to 1.5
- gain_ffw_in: bfloat16 [2048], P('dp'), may hold values from 0.5 to 1.5
- gain_ffw_out: bfloat16 [2048], P('dp'), may hold values from 0.5 to 1.5
- gain_layer_out: bfloat16 [2048], P('dp'), may hold values from 0.5 to 1.5
- out_grad: bfloat16 [8192, 2048], P(('dp', 'tensor')), may hold values from -6 to 6
Outputs:
- output: bfloat16 [8192, 2048], P(('dp', 'tensor'))
- grad_tokens: float32 [8192, 2048], P(('dp', 'tensor'))
- grad_layer_input: float32 [8192, 256], P(('dp', 'tensor'))
- grad_w_query: float32 [2048, 2048], P('dp', 'tensor')
- grad_w_key: float32 [2048, 512], P('dp', 'tensor')
- grad_w_value: float32 [2048, 512], P('dp', 'tensor')
- grad_w_output: float32 [2048, 2048], P('tensor', 'dp')
- grad_w_left: float32 [2048, 64], P('dp')
- grad_w_right: float32 [64, 2048], P(None, 'dp')
- grad_w_gate: float32 [2048, 8192], P('dp', 'tensor')
- grad_w_up: float32 [2048, 8192], P('dp', 'tensor')
- grad_w_down: float32 [8192, 2048], P('tensor', 'dp')
- grad_w_layer_gate: float32 [2048, 256], P('dp')
- grad_w_layer_proj: float32 [256, 2048], P(None, 'dp')
- grad_query_gain: float32 [256], P('dp')
- grad_key_gain: float32 [256], P('dp')
- grad_gain_input: float32 [2048], P('dp')
- grad_gain_attn_out: float32 [2048], P('dp')
- grad_gain_laurel: float32 [2048], P('dp')
- grad_gain_ffw_in: float32 [2048], P('dp')
- grad_gain_ffw_out: float32 [2048], P('dp')
- grad_gain_layer_out: float32 [2048], P('dp')
The draws below stay inside these ranges and needn't reach their ends.
Inputs may be any that keep to these rules, and one draw needn't show every extreme that they name: `block_ids`: in each sequence the block numbers never fall, every number below 64 occurs, a block holds 1 to 256 tokens and one holds exactly 256. `block_table`: entry (r, i, j) is 1 where j == i, and 0 where j > i or j <= i - 2; the others are 0 or 1.
All inputs are finite; a program needn't handle non-finite values.
Results may differ from the reference program's by a relative error of at most 0.02.
Values may be sent and summed in bfloat16 or wider, within the bound.
A program may use at most 256 MiB of HBM per device.

```python
import math
import jax
import jax.numpy as jnp
import numpy as np
from jax import lax

D = 2048
H = 8
KV = 2
HD = 256
FF = 8192
R = 64
P_SIZE = 256
WINDOW = 512
BLKTOK = 256
SEQ = 8192
ROWS = 1
TOKENS = 8192
NBLK = 64


def draw_block_table(key, part):
    breaks = jax.random.randint(key, (ROWS, NBLK), 0, 3)
    starts = jnp.where(breaks == 0, 1, 0).astype(jnp.int32)
    starts = jnp.where(jnp.arange(NBLK)[None, :] == 0, 1, starts).astype(jnp.int32)
    documents = jnp.cumsum(starts, axis=1)
    query_side = jnp.arange(NBLK, dtype=jnp.int32)[:, None]
    key_side = jnp.arange(NBLK, dtype=jnp.int32)[None, :]
    nearby = (key_side <= query_side) & (key_side > query_side - WINDOW // BLKTOK)
    same_doc = documents[:, :, None] == documents[:, None, :]
    return (nearby[None] & same_doc).astype(jnp.int32)


def level_of(own_key, dims, shards, smallest, largest):
    def one(dim, blocks):
        draws = jax.random.uniform(jax.random.fold_in(jax.random.fold_in(own_key, 6), dim), (blocks,), jnp.float32, smallest / len(shards), largest / len(shards))
        return jnp.repeat(jnp.exp(draws), dims[dim] // blocks).reshape((-1,) + (1,) * (len(dims) - dim - 1))

    level = one(*shards[0])
    for cut in shards[1:]:
        level = level * one(*cut)
    return level


def length_profile(number_of, total, reach, lean):
    portions = [(1 << 20) // math.isqrt(rank ** lean) + 1 for rank in range(2, number_of + 1)]
    surplus, holding = total - reach - (number_of - 1), [1] * (number_of - 1)
    while surplus > 0:
        free = [i for i in range(number_of - 1) if holding[i] < reach]
        mass, left = sum([portions[i] for i in free]), surplus
        for i in free:
            extra = min(reach - holding[i], max(1, left * portions[i] // mass), surplus)
            holding[i] = holding[i] + extra
            surplus = surplus - extra
    return np.array([reach] + holding)


def uneven(own_key, number_of, total, limit, skew):
    if number_of == 2:
        one = jax.random.randint(own_key, (), max(1, total - limit), min(limit, total - 1) + 1)
        return jnp.stack([one, total - one])
    lengths = jnp.asarray(length_profile(number_of, total, limit, skew), jnp.int32)
    couples = (number_of - 1) // 2
    source_of, taker = lengths[1:1 + 2 * couples:2], lengths[2:2 + 2 * couples:2]
    margin = jnp.minimum(source_of - 1, limit - taker)
    moved = jax.random.randint(jax.random.fold_in(own_key, 1), (couples,), 0, 1 << 20) % (margin + 1)
    lengths = lengths.at[1:1 + 2 * couples:2].set(source_of - moved).at[2:2 + 2 * couples:2].set(taker + moved)
    return lengths[jax.random.permutation(jax.random.fold_in(own_key, 2), number_of)]


def noise(stream_key, dims, spread, most, cuts=(), held_as=jnp.bfloat16):
    entries = jax.random.normal(stream_key, dims, jnp.float32) * spread
    if len(cuts) > 0:
        entries = level_of(stream_key, dims, cuts, -0.22, 0.18) * entries
    return jnp.clip(entries, min=-most, max=most).astype(held_as)


def setup_inputs(seed: int = 0) -> dict:
    streams_of = jax.random.split(jax.random.key(seed), 25)
    return {
        "tokens": noise(streams_of[0], (TOKENS, D), 1.0, 6.0, ((0, 32),)),
        "layer_input": noise(streams_of[1], (TOKENS, P_SIZE), 1.0, 6.0, ((0, 32),)),
        "block_ids": jax.vmap(lambda own: jnp.searchsorted(jnp.cumsum(uneven(own, NBLK, SEQ, BLKTOK, 0)), jnp.arange(SEQ), side="right"))(jax.random.split(streams_of[2], ROWS)).reshape((ROWS, SEQ)).astype(jnp.int32),
        "block_table": draw_block_table(jax.random.fold_in(streams_of[24], 71), 0),
        "w_query": noise(streams_of[4], (D, H * HD), D ** -0.5, 0.125, ((0, 16), (1, 2))),
        "w_key": noise(streams_of[5], (D, KV * HD), D ** -0.5, 0.125, ((0, 16), (1, 2))),
        "w_value": noise(streams_of[6], (D, KV * HD), D ** -0.5, 0.125, ((0, 16), (1, 2))),
        "w_output": noise(streams_of[7], (H * HD, D), (H * HD) ** -0.5, 0.125, ((0, 2), (1, 16))),
        "w_left": noise(streams_of[8], (D, R), D ** -0.5, 0.125, ((0, 16),)),
        "w_right": noise(streams_of[9], (R, D), R ** -0.5, 0.75, ((1, 16),)),
        "w_gate": noise(streams_of[10], (D, FF), D ** -0.5, 0.125, ((0, 16), (1, 2))),
        "w_up": noise(streams_of[11], (D, FF), D ** -0.5, 0.125, ((0, 16), (1, 2))),
        "w_down": noise(streams_of[12], (FF, D), FF ** -0.5, 0.0625, ((0, 2), (1, 16))),
        "w_layer_gate": noise(streams_of[13], (D, P_SIZE), D ** -0.5, 0.125, ((0, 16),)),
        "w_layer_proj": noise(streams_of[14], (P_SIZE, D), P_SIZE ** -0.5, 0.375, ((1, 16),)),
        "query_gain": jnp.clip(0.19921875 + 0.30078125 * jax.random.uniform(streams_of[15], (HD,), jnp.float32) ** level_of(streams_of[15], (HD,), ((0, 16),), -0.2, 0.2), 0.19921875, 0.5).astype(jnp.bfloat16),
        "key_gain": jnp.clip(0.19921875 + 0.30078125 * jax.random.uniform(streams_of[16], (HD,), jnp.float32) ** level_of(streams_of[16], (HD,), ((0, 16),), -0.2, 0.2), 0.19921875, 0.5).astype(jnp.bfloat16),
        "gain_input": jnp.clip(1.0 + 0.1 * jax.random.normal(streams_of[17], (D,), jnp.float32), 0.5, 1.5).astype(jnp.bfloat16),
        "gain_attn_out": jnp.clip(1.0 + 0.1 * jax.random.normal(streams_of[18], (D,), jnp.float32), 0.5, 1.5).astype(jnp.bfloat16),
        "gain_laurel": jnp.clip(1.0 + 0.1 * jax.random.normal(streams_of[19], (D,), jnp.float32), 0.5, 1.5).astype(jnp.bfloat16),
        "gain_ffw_in": jnp.clip(1.0 + 0.1 * jax.random.normal(streams_of[20], (D,), jnp.float32), 0.5, 1.5).astype(jnp.bfloat16),
        "gain_ffw_out": jnp.clip(1.0 + 0.1 * jax.random.normal(streams_of[21], (D,), jnp.float32), 0.5, 1.5).astype(jnp.bfloat16),
        "gain_layer_out": jnp.clip(1.0 + 0.1 * jax.random.normal(streams_of[22], (D,), jnp.float32), 0.5, 1.5).astype(jnp.bfloat16),
        "out_grad": noise(streams_of[23], (TOKENS, D), 1.0, 6.0, ((0, 32),)),
    }


@jax.custom_vjp
def low(v):
    return lax.optimization_barrier(v.astype(jnp.bfloat16)).astype(jnp.float32)

@jax.custom_vjp
def low_back(v):
    return v

def low_keep(v):
    return (low(v), None)

def low_pass(kept, grad):
    return (grad,)

def back_keep(v):
    return (v, None)

def back_low(kept, grad):
    return (low(grad),)
low.defvjp(low_keep, low_pass)
low_back.defvjp(back_keep, back_low)
EPS = 1e-06
ROOT_HALF = 0.7071067811865476
NEGATIVE = -1e+30

def norm_gain(values, gains):
    return values * lax.rsqrt(lax.optimization_barrier(jnp.mean(values * values, axis=-1, keepdims=True)) + EPS) * gains

def norm_plain(values):
    return values * lax.rsqrt(lax.optimization_barrier(jnp.mean(values * values, axis=-1, keepdims=True)) + EPS)

def gelu_tanh(values):
    return jax.nn.gelu(values, approximate=True)

def rope_tables(row_count, head_width):
    positions = jnp.arange(row_count, dtype=jnp.float32)[:, None]
    frequency = 10000.0 ** (-2.0 * jnp.arange(head_width // 2, dtype=jnp.float32) / head_width)
    angles = positions * frequency[None, :]
    return (jnp.cos(angles), jnp.sin(angles))

def rotate(values, cosines, sines):
    half_width = values.shape[-1] // 2
    front_half = values[..., :half_width]
    back_half = values[..., half_width:]
    cos_wide = cosines[:, None, :]
    sin_wide = sines[:, None, :]
    return jnp.concatenate([front_half * cos_wide - back_half * sin_wide, back_half * cos_wide + front_half * sin_wide], axis=-1)

def matmul(left_in, right_in):
    return jnp.dot(left_in, right_in, precision=lax.Precision.HIGHEST)

def attention(query_low, key_low, value_low, ids_row, table_row):
    seq_len = query_low.shape[0]
    query_block = min(512, seq_len)
    span = query_block + WINDOW + BLKTOK
    key_pad = jnp.pad(key_low, ((WINDOW, BLKTOK), (0, 0), (0, 0)))
    value_pad = jnp.pad(value_low, ((WINDOW, BLKTOK), (0, 0), (0, 0)))
    ids_pad = jnp.pad(ids_row, (WINDOW, BLKTOK), constant_values=-1).astype(jnp.int32)
    starts = (jnp.arange(seq_len // query_block, dtype=jnp.int32) * query_block).astype(jnp.int32)

    def one_block(start):
        query_part = lax.dynamic_slice_in_dim(query_low, start, query_block, 0)
        key_part = lax.dynamic_slice_in_dim(key_pad, start, span, 0)
        value_part = lax.dynamic_slice_in_dim(value_pad, start, span, 0)
        query_ids = lax.dynamic_slice_in_dim(ids_row, start, query_block, 0)
        key_ids = lax.dynamic_slice_in_dim(ids_pad, start, span, 0)
        safe_ids = jnp.maximum(key_ids, 0).astype(jnp.int32)
        allowed = (table_row[query_ids[:, None], safe_ids[None, :]] == 1) & (key_ids[None, :] >= 0)
        scores = low_back(jnp.einsum('qkgd,ckd->kgqc', query_part, key_part, precision=lax.Precision.HIGHEST))
        scores = jnp.where(allowed[None, None], scores, NEGATIVE)
        probs = low(jax.nn.softmax(scores, axis=-1))
        return jnp.einsum('kgqc,ckd->qkgd', probs, value_part, precision=lax.Precision.HIGHEST)
    blocks = lax.map(jax.checkpoint(one_block), starts)
    return blocks.reshape(seq_len, H * HD)

def layer_row(params, row_items):
    w_query, w_key, w_value, w_output, w_left, w_right, w_gate, w_up, w_down, w_layer_gate, w_layer_proj, query_gain, key_gain, gain_input, gain_attn_out, gain_laurel, gain_ffw_in, gain_ffw_out, gain_layer_out = params
    tokens_row, layer_row_in, ids_row, table_row = row_items
    seq_len = tokens_row.shape[0]
    normed = norm_gain(tokens_row, gain_input)
    normed_low = low(normed)
    query_raw = low_back(matmul(normed_low, w_query)).reshape(seq_len, H, HD)
    key_raw = low_back(matmul(normed_low, w_key)).reshape(seq_len, KV, HD)
    value_raw = low_back(matmul(normed_low, w_value)).reshape(seq_len, KV, HD)
    cosines, sines = rope_tables(seq_len, HD)
    query_low = low(rotate(norm_gain(query_raw, query_gain), cosines, sines)).reshape(seq_len, KV, H // KV, HD)
    key_low = low(rotate(norm_gain(key_raw, key_gain), cosines, sines))
    value_low = low(norm_plain(value_raw))
    heads = attention(query_low, key_low, value_low, ids_row, table_row)
    heads_low = low(low_back(heads))
    attn_out = low_back(matmul(heads_low, w_output))
    attn_normed = norm_gain(attn_out, gain_attn_out)
    left_low = low(low_back(matmul(normed_low, w_left)))
    right_out = low_back(matmul(left_low, w_right))
    mixed = (tokens_row + attn_normed + (normed + norm_gain(right_out, gain_laurel))) * ROOT_HALF
    ffw_low = low(norm_gain(mixed, gain_ffw_in))
    gate_raw = low_back(matmul(ffw_low, w_gate))
    up_raw = low_back(matmul(ffw_low, w_up))
    hidden_low = low(gelu_tanh(gate_raw) * up_raw)
    ffw_out = low_back(matmul(hidden_low, w_down))
    block_mid = mixed + norm_gain(ffw_out, gain_ffw_out)
    layer_pre = low_back(matmul(low(block_mid), w_layer_gate))
    gated_low = low(gelu_tanh(layer_pre) * layer_row_in)
    layer_proj = low_back(matmul(gated_low, w_layer_proj))
    return block_mid + norm_gain(layer_proj, gain_layer_out)

def reference(tokens, layer_input, block_ids, block_table, w_query, w_key, w_value, w_output, w_left, w_right, w_gate, w_up, w_down, w_layer_gate, w_layer_proj, query_gain, key_gain, gain_input, gain_attn_out, gain_laurel, gain_ffw_in, gain_ffw_out, gain_layer_out, out_grad):
    params = jax.tree.map(lambda matrix: matrix.astype(jnp.float32), (w_query, w_key, w_value, w_output, w_left, w_right, w_gate, w_up, w_down, w_layer_gate, w_layer_proj, query_gain, key_gain, gain_input, gain_attn_out, gain_laurel, gain_ffw_in, gain_ffw_out, gain_layer_out))

    def forward(inputs, per_layer, weights):

        def one_row(row_items):
            return layer_row(weights, row_items)
        row_items = (inputs.reshape(ROWS, SEQ, D), per_layer.reshape(ROWS, SEQ, P_SIZE), block_ids, block_table)
        return lax.map(jax.checkpoint(one_row), row_items).reshape(ROWS * SEQ, D)
    result, pullback = jax.vjp(forward, tokens.astype(jnp.float32), layer_input.astype(jnp.float32), params)
    grad_tokens, grad_layer, grads = pullback(out_grad.astype(jnp.float32))
    g_query, g_key, g_value, g_output, g_left, g_right, g_gate, g_up, g_down, g_lgate, g_lproj, g_qgain, g_kgain, g_input, g_attn, g_laurel, g_ffw_in, g_ffw_out, g_layer = grads
    return (result.astype(jnp.bfloat16), grad_tokens, grad_layer, g_query, g_key, g_value, g_output, g_left, g_right, g_gate, g_up, g_down, g_lgate, g_lproj, g_qgain, g_kgain, g_input, g_attn, g_laurel, g_ffw_in, g_ffw_out, g_layer)
```

```python
import jax
import jax.numpy as jnp
from jax import lax
from jax.sharding import PartitionSpec as P

HD = 256
EPS = 1e-06
ROOT_HALF = 0.7071067811865476
NEGATIVE = -1e30
F32 = jnp.float32
BF16 = jnp.bfloat16


def norm_gain(values, gains):
    return values * lax.rsqrt(jnp.mean(values * values, axis=-1, keepdims=True) + EPS) * gains


def norm_plain(values):
    return values * lax.rsqrt(jnp.mean(values * values, axis=-1, keepdims=True) + EPS)


def gelu_tanh(values):
    return jax.nn.gelu(values, approximate=True)


def rope_tables(positions, head_width):
    positions = positions.astype(F32)[:, None]
    frequency = 10000.0 ** (-2.0 * jnp.arange(head_width // 2, dtype=F32) / head_width)
    angles = positions * frequency[None, :]
    return (jnp.cos(angles), jnp.sin(angles))


def rotate(values, cosines, sines):
    half_width = values.shape[-1] // 2
    front_half = values[..., :half_width]
    back_half = values[..., half_width:]
    cos_wide = cosines[:, None, :]
    sin_wide = sines[:, None, :]
    return jnp.concatenate(
        [
            front_half * cos_wide - back_half * sin_wide,
            back_half * cos_wide + front_half * sin_wide,
        ],
        axis=-1,
    )


def to_float(values):
    return values.astype(F32)


def low(values):
    return values.astype(BF16)


def product(left_in, right_in):
    return jnp.dot(left_in, right_in, preferred_element_type=F32)


def product_t(left_in, right_in):
    return lax.dot_general(left_in, right_in, (((1,), (1,)), ((), ())), preferred_element_type=F32)


def product_l(left_in, right_in):
    return lax.dot_general(left_in, right_in, (((0,), (0,)), ((), ())), preferred_element_type=F32)


def tie(*values):
    return lax.optimization_barrier(values)


class Ring:
    def __init__(self):
        self.devices = lax.axis_size("dp")
        self.chips = self.devices // 2
        order = list(range(0, self.chips, 2)) + list(range(self.chips - 1, 0, -2))
        self.cw = [
            (2 * order[p] + c, 2 * order[(p + 1) % self.chips] + c)
            for p in range(self.chips)
            for c in range(2)
        ]
        self.ccw = [(b, a) for a, b in self.cw]
        self.core_pairs = [(d, d ^ 1) for d in range(self.devices)]
        me = lax.axis_index("dp")
        self.core = lax.rem(me, 2)
        self.chip = me // 2
        self.place = jnp.where(
            lax.rem(self.chip, 2) == 0, self.chip // 2, self.chips - 1 - self.chip // 2
        )

    def chip_at(self, offset):
        place = lax.rem(self.place + offset + self.chips, self.chips)
        return jnp.where(place < self.chips // 2, 2 * place, 2 * (self.chips - 1 - place) + 1)

    def up(self, values):
        return lax.ppermute(values, "dp", self.cw)

    def down(self, values):
        return lax.ppermute(values, "dp", self.ccw)

    def swap(self, values):
        return lax.ppermute(values, "dp", self.core_pairs)


def across(values):
    return lax.ppermute(values, "tensor", [(0, 1), (1, 0)])


class Gather:
    def __init__(self, ring, block):
        self.ring = ring
        self.rows = block.shape[0]
        self.going_up = block
        self.going_down = block
        self.parts = [(0, 0, block)]
        self.step_count = 0

    def step(self):
        ring, half = self.ring, self.ring.chips // 2
        self.step_count += 1
        k = self.step_count
        if k < half:
            self.going_up = ring.up(self.going_up)
            self.going_down = ring.down(self.going_down)
            self.parts += [(-k, 0, self.going_up), (k, 0, self.going_down)]
        else:
            cut = self.rows // 2
            self.going_up = ring.up(self.going_up[:cut])
            self.going_down = ring.down(self.going_down[cut:])
            self.parts += [(half, 0, self.going_up), (half, cut, self.going_down)]

    def after(self, other):
        self.going_up, self.going_down, _ = tie(
            self.going_up, self.going_down, (other.going_up, other.going_down)
        )

    def assemble(self):
        whole = jnp.zeros((self.ring.chips * self.rows,) + self.parts[0][2].shape[1:], BF16)
        for offset, row, part in self.parts:
            start = self.ring.chip_at(offset) * self.rows + row
            whole = lax.dynamic_update_slice_in_dim(whole, part, start, 0)
        return whole


class Reduce:
    def __init__(self, ring, part):
        self.ring = ring
        self.part = part
        self.step_count = 0

    def step(self):
        ring, half = self.ring, self.ring.chips // 2
        self.step_count += 1
        k = self.step_count
        if k == 1:
            term = low(self.part(half))
            self.cut = term.shape[0] // 2
            up, down = term[: self.cut], term[self.cut :]
        else:
            d = half + 1 - k
            up_term, down_term = self.part(d), self.part(-d)
            if k == 2:
                rest = jnp.zeros(self.got_up.shape, F32)
                up = low(up_term + jnp.concatenate([to_float(self.got_up), rest], axis=0))
                down = low(down_term + jnp.concatenate([rest, to_float(self.got_down)], axis=0))
            else:
                up = low(up_term + to_float(self.got_up))
                down = low(down_term + to_float(self.got_down))
        self.got_up = ring.up(up)
        self.got_down = ring.down(down)

    def result(self):
        return self.part(0) + to_float(self.got_up) + to_float(self.got_down)

    def after(self, other):
        pass


def local(
    tokens,
    layer_input,
    block_ids,
    block_table,
    w_query,
    w_key,
    w_value,
    w_output,
    w_left,
    w_right,
    w_gate,
    w_up,
    w_down,
    w_layer_gate,
    w_layer_proj,
    query_gain,
    key_gain,
    gain_input,
    gain_attn_out,
    gain_laurel,
    gain_ffw_in,
    gain_ffw_out,
    gain_layer_out,
    out_grad,
):
    ring = Ring()
    side = lax.axis_index("tensor")
    core = ring.core
    rows = w_query.shape[0]
    own = tokens.shape[0]
    width = tokens.shape[1]
    q_cols = w_query.shape[1]
    kv_cols = w_key.shape[1]
    rank = w_left.shape[1]
    small = w_layer_gate.shape[1]
    ff_cols = w_gate.shape[1] // 2
    chips = ring.chips

    def gain_block(query_part, key_part, parts):
        count = query_part.shape[0]
        columns = parts + [
            jnp.pad(query_part, (0, rows - count)),
            jnp.pad(key_part, (0, rows - count)),
        ]
        block = jnp.stack(columns, axis=1)
        return jnp.pad(block, ((0, 0), (0, 128 - block.shape[1])))

    gains = gain_block(
        query_gain,
        key_gain,
        [gain_input, gain_attn_out, gain_laurel, gain_ffw_in, gain_ffw_out, gain_layer_out],
    )
    other_tokens = across(tokens)

    def core_split(matrix):
        mine = lax.dynamic_slice_in_dim(matrix, core * ff_cols, ff_cols, 1)
        theirs = lax.dynamic_slice_in_dim(matrix, (1 - core) * ff_cols, ff_cols, 1)
        got = ring.swap(theirs)
        return jnp.where(
            core == 0,
            jnp.concatenate([mine, got], axis=0),
            jnp.concatenate([got, mine], axis=0),
        )

    first_pack = jnp.concatenate([w_query, w_key, w_value, gains], axis=1)
    second_pack = jnp.concatenate(
        [w_output.T, w_left, w_right.T, w_layer_gate, w_layer_proj.T], axis=1
    )
    gate_block = core_split(w_gate)
    up_block = core_split(w_up)
    down_block = core_split(w_down.T)

    half = chips // 2
    ga = Gather(ring, first_pack)
    gb = Gather(ring, second_pack)
    for _ in range(half):
        ga.step()
        gb.step()
    gg = Gather(ring, gate_block)
    gu = Gather(ring, up_block)
    gg.after(ga)
    gu.after(gb)
    for _ in range(half):
        gg.step()
        gu.step()
    gd0 = Gather(ring, down_block[:rows])
    gd1 = Gather(ring, down_block[rows:])
    gd0.after(gg)
    gd1.after(gu)
    for _ in range(half):
        gd0.step()
        gd1.step()

    def by_core(gather):
        mine = gather.assemble()
        theirs = ring.swap(mine)
        mine = mine.reshape(chips, 1, rows, -1)
        theirs = theirs.reshape(chips, 1, rows, -1)
        both = jnp.where(
            core == 0,
            jnp.concatenate([mine, theirs], axis=1),
            jnp.concatenate([theirs, mine], axis=1),
        )
        return both.reshape(width, -1)

    first_all = by_core(ga)
    second_all = by_core(gb)
    query_full = first_all[:, :q_cols]
    key_full = first_all[:, q_cols : q_cols + kv_cols]
    value_full = first_all[:, q_cols + kv_cols : q_cols + 2 * kv_cols]
    gains_full = first_all[:, q_cols + 2 * kv_cols :]
    output_t = second_all[:, :q_cols]
    left_full = second_all[:, q_cols : q_cols + rank]
    right_t = second_all[:, q_cols + rank : q_cols + 2 * rank]
    lgate_full = second_all[:, q_cols + 2 * rank : q_cols + 2 * rank + small]
    lproj_t = second_all[:, q_cols + 2 * rank + small :]
    gate_full = gg.assemble()
    up_full = gu.assemble()

    def down_whole():
        top = gd0.assemble().reshape(chips, 1, rows, ff_cols)
        bottom = gd1.assemble().reshape(chips, 1, rows, ff_cols)
        return jnp.concatenate([top, bottom], axis=1).reshape(width, ff_cols)

    down_t = down_whole()

    gain_columns = to_float(gains_full[:, :8])
    (
        input_scale,
        attn_scale,
        laurel_scale,
        ffw_in_scale,
        ffw_out_scale,
        layer_scale,
    ) = (gain_columns[:, i] for i in range(6))
    head_part = query_gain.shape[0]

    def head_gain(column):
        return column.reshape(ring.devices, rows)[:, :head_part].reshape(HD)

    query_scale = head_gain(gain_columns[:, 6])
    key_scale = head_gain(gain_columns[:, 7])

    inputs = to_float(tokens)
    normed, input_norm_back = jax.vjp(norm_gain, inputs, input_scale)
    normed_low = low(normed)
    seq_rows = jnp.concatenate(
        [normed_low, low(norm_gain(to_float(other_tokens), input_scale))], axis=0
    )
    piece_len = 2 * own
    seq_total = block_ids.shape[1]
    per_seq = seq_total // piece_len
    dp_index = lax.axis_index("dp")
    row_index = dp_index // per_seq
    slot = lax.rem(dp_index, per_seq)
    first = slot * piece_len
    has_before = slot > 0
    has_after = slot < per_seq - 1
    query_raw = product(seq_rows, query_full)
    key_raw = product(seq_rows, key_full)
    value_raw = product(seq_rows, value_full)
    natural = jnp.arange(piece_len, dtype=jnp.int32)
    here = first + lax.rem(natural + side * own, piece_len)
    cosines, sines = rope_tables(here, HD)

    def prepare(query_in, key_in, value_in, query_gains, key_gains):
        query_out = rotate(
            norm_gain(query_in.reshape(piece_len, -1, HD), query_gains), cosines, sines
        )
        key_out = rotate(norm_gain(key_in.reshape(piece_len, -1, HD), key_gains), cosines, sines)
        return (query_out, key_out, norm_plain(value_in.reshape(piece_len, -1, HD)))

    prepared, prepare_back = jax.vjp(
        prepare, query_raw, key_raw, value_raw, query_scale, key_scale
    )
    query_rot, key_rot, value_nrm = prepared
    heads_local = query_rot.shape[1]
    kv_local = key_rot.shape[1]
    group = heads_local // kv_local
    query_low = low(query_rot).reshape(piece_len, kv_local, group, HD)

    def in_order(values):
        return jnp.where(
            side == 0, values, jnp.concatenate([values[own:], values[:own]], axis=0)
        )

    kv_own = in_order(jnp.concatenate([low(key_rot), low(value_nrm)], axis=1))
    reach_after = min(256, piece_len)
    forward_pairs = [(i, i + 1) for i in range(ring.devices - 1)]
    backward_pairs = [(i + 1, i) for i in range(ring.devices - 1)]
    kv_before = lax.ppermute(kv_own, "dp", forward_pairs)
    kv_after = lax.ppermute(kv_own[:reach_after], "dp", backward_pairs)
    kv_all = jnp.concatenate([kv_before, kv_own, kv_after], axis=0)
    keys_all = kv_all[:, :kv_local]
    values_all = kv_all[:, kv_local:]

    ids_row = lax.dynamic_index_in_dim(block_ids, row_index, 0, keepdims=False)
    table_row = lax.dynamic_index_in_dim(block_table, row_index, 0, keepdims=False)
    own_ids = lax.dynamic_slice_in_dim(ids_row, first, piece_len, 0)
    before_ids = lax.dynamic_slice_in_dim(ids_row, jnp.maximum(first - piece_len, 0), piece_len, 0)
    before_ids = jnp.where(has_before, before_ids, -2)
    after_ids = lax.dynamic_slice_in_dim(
        ids_row, jnp.minimum(first + piece_len, seq_total - reach_after), reach_after, 0
    )
    after_ids = jnp.where(has_after, after_ids, -2)
    key_ids = jnp.concatenate([before_ids, own_ids, after_ids], axis=0)
    query_ids = in_order(own_ids)
    block_count = block_table.shape[-1]
    number_rows = jnp.arange(block_count, dtype=jnp.int32)
    sees_last = jnp.sum(
        jnp.where(number_rows[None, :] == number_rows[:, None] - 1, table_row, 0), axis=1
    )
    query_sees = jnp.sum(
        jnp.where(query_ids[:, None] == number_rows[None, :], sees_last[None, :], 0), axis=1
    )
    previous_ids = jnp.where(query_sees == 1, query_ids - 1, query_ids)

    def scores_for():
        allowed = (query_ids[:, None] == key_ids[None, :]) | (
            previous_ids[:, None] == key_ids[None, :]
        )
        scores = jnp.einsum("qkgd,ckd->kgqc", query_low, keys_all, preferred_element_type=F32)
        return jnp.where(allowed[None, None], scores, NEGATIVE)

    scores = scores_for()
    highest = jnp.max(scores, axis=-1, keepdims=True)
    weights_exp = jnp.exp(scores - highest)
    totals = jnp.sum(weights_exp, axis=-1, keepdims=True)
    probs_low = low(weights_exp / totals)
    attended = jnp.einsum("kgqc,ckd->qkgd", probs_low, values_all, preferred_element_type=F32)
    log_totals = highest + jnp.log(totals)
    heads_low = low(attended.reshape(piece_len, heads_local * HD))

    def sum_sides(partial):
        return partial[:own] + to_float(across(low(partial[own:])))

    def both_sides(values):
        return jnp.concatenate([values, across(values)], axis=0)

    def four_ways(values):
        pair = both_sides(values)
        return jnp.concatenate([pair, ring.swap(pair)], axis=0)

    def sum_four(partial):
        pair = partial[: 2 * own] + to_float(ring.swap(low(partial[2 * own :])))
        return sum_sides(pair)

    attn_out = sum_sides(product_t(heads_low, output_t))
    attn_normed, attn_norm_back = jax.vjp(norm_gain, attn_out, attn_scale)
    left_low = low(product(normed_low, left_full))
    right_out = product_t(left_low, right_t)
    laurel_normed, laurel_back = jax.vjp(norm_gain, right_out, laurel_scale)
    mixed = (inputs + attn_normed + (normed + laurel_normed)) * ROOT_HALF
    ffw_normed, ffw_norm_back = jax.vjp(norm_gain, mixed, ffw_in_scale)
    ffw_rows = four_ways(low(ffw_normed))

    gate_raw = product(ffw_rows, gate_full)
    up_raw = product(ffw_rows, up_full)

    def activate(gate_in, up_in):
        return gelu_tanh(gate_in) * up_in

    hidden, activate_back = jax.vjp(activate, gate_raw, up_raw)
    hidden_low = low(hidden)
    ffw_out = sum_four(product_t(hidden_low, down_t))
    ffw_out_normed, ffw_out_back = jax.vjp(norm_gain, ffw_out, ffw_out_scale)
    block_mid = mixed + ffw_out_normed
    mid_low = low(block_mid)
    layer_pre = product(mid_low, lgate_full)

    def layer_gate_fn(pre_values, per_layer):
        return gelu_tanh(pre_values) * per_layer

    gated, gated_back = jax.vjp(layer_gate_fn, layer_pre, to_float(layer_input))
    gated_low = low(gated)
    layer_proj = product_t(gated_low, lproj_t)
    proj_normed, proj_back = jax.vjp(norm_gain, layer_proj, layer_scale)
    result = block_mid + proj_normed

    grad_out = to_float(out_grad)
    d_proj, d_layer_scale = proj_back(grad_out)
    d_proj_low = low(d_proj)
    d_gated = product(d_proj_low, lproj_t)
    grad_lproj_t = product_l(d_proj_low, gated_low)
    d_pre, grad_layer_input = gated_back(d_gated)
    d_pre_low = low(d_pre)
    d_mid = grad_out + product_t(d_pre_low, lgate_full)
    grad_lgate = product_l(mid_low, d_pre_low)
    d_ffw_out, d_ffw_out_scale = ffw_out_back(d_mid)
    d_ffw_rows = four_ways(low(d_ffw_out))
    d_hidden = product(d_ffw_rows, down_t)
    d_gate, d_up = activate_back(d_hidden)
    d_gate_low = low(d_gate)
    d_up_low = low(d_up)

    def columns_at(values, offset, start, count):
        return lax.dynamic_slice_in_dim(
            values, ring.chip_at(offset) * (2 * rows) + start, count, 1
        )

    rd0 = Reduce(
        ring, lambda o: product_l(columns_at(d_ffw_rows, o, 0, rows), hidden_low)
    )
    rd1 = Reduce(
        ring, lambda o: product_l(columns_at(d_ffw_rows, o, rows, rows), hidden_low)
    )
    rg = Reduce(ring, lambda o: product_l(columns_at(ffw_rows, o, 0, 2 * rows), d_gate_low))
    ru = Reduce(ring, lambda o: product_l(columns_at(ffw_rows, o, 0, 2 * rows), d_up_low))
    for _ in range(half):
        rd0.step()
        rd1.step()
    d_gate_ring, d_up_ring, _ = tie(
        d_gate_low, d_up_low, (rd0.got_up, rd0.got_down, rd1.got_up, rd1.got_down)
    )
    rg.part = lambda o: product_l(columns_at(ffw_rows, o, 0, 2 * rows), d_gate_ring)
    ru.part = lambda o: product_l(columns_at(ffw_rows, o, 0, 2 * rows), d_up_ring)
    for _ in range(half):
        rg.step()
        ru.step()

    d_ffw_normed = sum_four(product_t(d_gate_low, gate_full) + product_t(d_up_low, up_full))
    d_mixed_extra, d_ffw_in_scale = ffw_norm_back(d_ffw_normed)
    d_branch = (d_mid + d_mixed_extra) * ROOT_HALF
    d_attn, d_attn_scale = attn_norm_back(d_branch)
    d_attn_rows = both_sides(low(d_attn))
    d_right, d_laurel_scale = laurel_back(d_branch)
    d_right_low = low(d_right)
    grad_right_t = product_l(d_right_low, left_low)
    d_left_low = low(product(d_right_low, right_t))
    grad_left = product_l(normed_low, d_left_low)
    d_normed = d_branch + product_t(d_left_low, left_full)
    d_heads = low(product(d_attn_rows, output_t)).reshape(piece_len, kv_local, group, HD)

    probs = jnp.exp(scores_for() - log_totals)
    probs_low = low(probs)
    d_values_all = jnp.einsum("kgqc,qkgd->ckd", probs_low, d_heads, preferred_element_type=F32)
    d_probs = jnp.einsum("qkgd,ckd->kgqc", d_heads, values_all, preferred_element_type=F32)
    deltas = jnp.sum(probs * d_probs, axis=-1, keepdims=True)
    d_scores = low(probs * (d_probs - deltas))
    d_keys_all = jnp.einsum("kgqc,qkgd->ckd", d_scores, query_low, preferred_element_type=F32)
    d_query_rot = jnp.einsum("kgqc,ckd->qkgd", d_scores, keys_all, preferred_element_type=F32)
    d_kv_all = jnp.concatenate([d_keys_all, d_values_all], axis=1)
    to_before = low(d_kv_all[:piece_len])
    to_after = low(d_kv_all[2 * piece_len :])
    from_after = to_float(lax.ppermute(to_before, "dp", backward_pairs))
    from_before = to_float(lax.ppermute(to_after, "dp", forward_pairs))
    d_kv = d_kv_all[piece_len : 2 * piece_len] + from_after
    d_kv = d_kv + jnp.pad(from_before, ((0, piece_len - reach_after), (0, 0), (0, 0)))
    d_kv = in_order(d_kv)
    d_query, d_key, d_value, query_scale_grad, key_scale_grad = prepare_back(
        (d_query_rot.reshape(piece_len, heads_local, HD), d_kv[:, :kv_local], d_kv[:, kv_local:])
    )
    d_query_low = low(d_query)
    d_key_low = low(d_key)
    d_value_low = low(d_value)
    d_normed = d_normed + sum_sides(
        product_t(d_query_low, query_full)
        + product_t(d_key_low, key_full)
        + product_t(d_value_low, value_full)
    )
    d_inputs_extra, d_input_scale = input_norm_back(d_normed)
    grad_tokens = d_branch + d_inputs_extra

    def over_cores(grad):
        blocks = grad.reshape(chips, 2, rows, -1)
        mine = lax.dynamic_index_in_dim(blocks, core, 1, keepdims=False)
        theirs = lax.dynamic_index_in_dim(blocks, 1 - core, 1, keepdims=False)
        return mine + to_float(ring.swap(low(theirs)))

    def ring_of(blocks):
        return Reduce(
            ring, lambda o: lax.dynamic_index_in_dim(blocks, ring.chip_at(o), 0, keepdims=False)
        )

    d_qkv = jnp.concatenate([d_query_low, d_key_low, d_value_low], axis=1)
    grad_output_t = product_l(d_attn_rows, heads_low)
    grad_qkv = product_l(seq_rows, d_qkv)

    def head_gain_back(grads):
        padded = jnp.pad(grads.reshape(ring.devices, head_part), ((0, 0), (0, rows - head_part)))
        return padded.reshape(width)

    gain_grads = jnp.stack(
        [
            d_input_scale,
            d_attn_scale,
            d_laurel_scale,
            d_ffw_in_scale,
            d_ffw_out_scale,
            d_layer_scale,
            head_gain_back(query_scale_grad),
            head_gain_back(key_scale_grad),
        ],
        axis=1,
    )
    gain_grads = jnp.pad(gain_grads, ((0, 0), (0, 128 - gain_grads.shape[1])))
    small_grads = jnp.concatenate(
        [grad_left, grad_right_t, grad_lgate, grad_lproj_t, gain_grads], axis=1
    )
    small_blocks = over_cores(small_grads)
    part_rows = rows // 2
    small_halves = small_blocks.reshape(chips, 2, part_rows, -1)
    small_mine = lax.dynamic_index_in_dim(small_halves, side, 1, keepdims=False)
    small_theirs = lax.dynamic_index_in_dim(small_halves, 1 - side, 1, keepdims=False)
    small_mine = small_mine + to_float(across(low(small_theirs)))

    ro = ring_of(over_cores(grad_output_t))
    rq = ring_of(over_cores(grad_qkv))
    rs = ring_of(small_mine)
    for _ in range(half):
        ro.step()
        rq.step()
        rs.step()

    def back_to_rows(block):
        mine = lax.dynamic_slice_in_dim(block, core * rows, rows, 0)
        theirs = lax.dynamic_slice_in_dim(block, (1 - core) * rows, rows, 0)
        got = ring.swap(theirs)
        return jnp.where(
            core == 0,
            jnp.concatenate([mine, got], axis=1),
            jnp.concatenate([got, mine], axis=1),
        )

    out_down_t = back_to_rows(jnp.concatenate([rd0.result(), rd1.result()], axis=0))
    out_gate = back_to_rows(rg.result())
    out_up = back_to_rows(ru.result())
    out_output = ro.result().T
    out_qkv = rq.result()
    small_half = rs.result()
    small_other = across(small_half)
    out_small = jnp.where(
        side == 0,
        jnp.concatenate([small_half, small_other], axis=0),
        jnp.concatenate([small_other, small_half], axis=0),
    )
    out_gains = out_small[:, 2 * rank + 2 * small :]
    return (
        low(result),
        grad_tokens,
        grad_layer_input,
        out_qkv[:, :q_cols],
        out_qkv[:, q_cols : q_cols + kv_cols],
        out_qkv[:, q_cols + kv_cols :],
        out_output,
        out_small[:, :rank],
        out_small[:, rank : 2 * rank].T,
        out_gate,
        out_up,
        out_down_t.T,
        out_small[:, 2 * rank : 2 * rank + small],
        out_small[:, 2 * rank + small : 2 * rank + 2 * small].T,
        out_gains[:head_part, 6],
        out_gains[:head_part, 7],
        out_gains[:, 0],
        out_gains[:, 1],
        out_gains[:, 2],
        out_gains[:, 3],
        out_gains[:, 4],
        out_gains[:, 5],
    )


def solution(mesh):
    both = P(("dp", "tensor"), None)
    rows_split = P("dp", "tensor")
    cols_split = P("tensor", "dp")
    by_row = P("dp", None)
    by_col = P(None, "dp")
    flat = P("dp")
    return jax.shard_map(
        local,
        mesh=mesh,
        in_specs=(
            (both, both, P(), P(), rows_split, rows_split, rows_split, cols_split)
            + (by_row, by_col, rows_split, rows_split, cols_split, by_row, by_col)
            + (flat,) * 8
            + (both,)
        ),
        out_specs=(
            (both, both, both, rows_split, rows_split, rows_split, cols_split)
            + (by_row, by_col, rows_split, rows_split, cols_split, by_row, by_col)
            + (flat,) * 8
        ),
        check_vma=False,
    )
```

```python
import functools

import jax
import jax.numpy as jnp
from jax import lax
from jax.experimental import pallas as pl
from jax.experimental.pallas import tpu as pltpu
from jax.sharding import PartitionSpec as P

HD = 256
EPS = 1e-06
ROOT_HALF = 0.7071067811865476
NEGATIVE = -1e30
F32 = jnp.float32
BF16 = jnp.bfloat16


def norm_gain(values, gains):
    return values * lax.rsqrt(jnp.mean(values * values, axis=-1, keepdims=True) + EPS) * gains


def norm_plain(values):
    return values * lax.rsqrt(jnp.mean(values * values, axis=-1, keepdims=True) + EPS)


def gelu_tanh(values):
    return jax.nn.gelu(values, approximate=True)


def rope_tables(positions, head_width):
    positions = positions.astype(F32)[:, None]
    frequency = 10000.0 ** (-2.0 * jnp.arange(head_width // 2, dtype=F32) / head_width)
    angles = positions * frequency[None, :]
    return (jnp.cos(angles), jnp.sin(angles))


def rotate(values, cosines, sines):
    half_width = values.shape[-1] // 2
    front_half = values[..., :half_width]
    back_half = values[..., half_width:]
    cos_wide = cosines[:, None, :]
    sin_wide = sines[:, None, :]
    return jnp.concatenate(
        [
            front_half * cos_wide - back_half * sin_wide,
            back_half * cos_wide + front_half * sin_wide,
        ],
        axis=-1,
    )


def to_float(values):
    return values.astype(F32)


def low(values):
    return values.astype(BF16)


def product(left_in, right_in):
    return jnp.dot(left_in, right_in, preferred_element_type=F32)


def product_t(left_in, right_in):
    return lax.dot_general(left_in, right_in, (((1,), (1,)), ((), ())), preferred_element_type=F32)


def product_l(left_in, right_in):
    return lax.dot_general(left_in, right_in, (((0,), (0,)), ((), ())), preferred_element_type=F32)


def tie(*values):
    return lax.optimization_barrier(values)


class Ring:
    def __init__(self):
        self.devices = lax.axis_size("dp")
        self.chips = self.devices // 2
        order = list(range(0, self.chips, 2)) + list(range(self.chips - 1, 0, -2))
        self.cw = [
            (2 * order[p] + c, 2 * order[(p + 1) % self.chips] + c)
            for p in range(self.chips)
            for c in range(2)
        ]
        self.ccw = [(b, a) for a, b in self.cw]
        self.core_pairs = [(d, d ^ 1) for d in range(self.devices)]
        me = lax.axis_index("dp")
        self.core = lax.rem(me, 2)
        self.chip = me // 2
        self.place = jnp.where(
            lax.rem(self.chip, 2) == 0, self.chip // 2, self.chips - 1 - self.chip // 2
        )

    def chip_at(self, offset):
        place = lax.rem(self.place + offset + self.chips, self.chips)
        return jnp.where(place < self.chips // 2, 2 * place, 2 * (self.chips - 1 - place) + 1)

    def up(self, values):
        return lax.ppermute(values, "dp", self.cw)

    def down(self, values):
        return lax.ppermute(values, "dp", self.ccw)

    def swap(self, values):
        return lax.ppermute(values, "dp", self.core_pairs)


def across(values):
    return lax.ppermute(values, "tensor", [(0, 1), (1, 0)])


def remote(source, target, sends, receives, index, device):
    return pltpu.make_async_remote_copy(
        src_ref=source,
        dst_ref=target,
        send_sem=sends.at[index],
        recv_sem=receives.at[index],
        device_id=device,
        device_id_type=pl.DeviceIdType.MESH,
    )


def greet(devices):
    barrier = pltpu.get_barrier_semaphore()
    for device in devices:
        pl.semaphore_signal(
            barrier, inc=1, device_id=device, device_id_type=pl.DeviceIdType.MESH
        )
    pl.semaphore_wait(barrier, len(devices))


def block_rows(ref, start, count):
    return ref.at[pl.ds(pl.multiple_of(start, 16), count)]


class Hops:
    def __init__(self):
        me = lax.axis_index("dp")
        self.chips = lax.axis_size("dp") // 2
        self.core = lax.rem(me, 2)
        self.chip = me // 2
        self.place = jnp.where(
            lax.rem(self.chip, 2) == 0, self.chip // 2, self.chips - 1 - self.chip // 2
        )
        self.partner = {"dp": self.chip * 2 + 1 - self.core}
        self.above = {"dp": self.chip_at(1) * 2 + self.core}
        self.below = {"dp": self.chip_at(-1) * 2 + self.core}
        self.across = {"tensor": 1 - lax.axis_index("tensor")}

    def chip_at(self, offset):
        place = lax.rem(self.place + offset + self.chips, self.chips)
        return jnp.where(place < self.chips // 2, 2 * place, 2 * (self.chips - 1 - place) + 1)


def first_kernel(count, ff_cols, *refs):
    blocks, refs = refs[:count], refs[count:]
    (gate, up, down, tokens), refs = refs[:4], refs[4:]
    wholes, refs = refs[:count], refs[count:]
    (gate_up_own, down_own, other_tokens), refs = refs[:3], refs[3:]
    stages, refs = refs[: 3 + count], refs[3 + count :]
    in_sems, out_sems, ring_send, ring_recv, pair_send, pair_recv, ff_send, ff_recv = refs
    hops = Hops()
    half = hops.chips // 2
    rows = blocks[0].shape[0]
    greet([hops.above, hops.below, hops.partner, hops.across])
    started = []

    def place(ref, offset, top, size):
        return block_rows(ref, (2 * hops.chip_at(offset) + hops.core) * rows + top, size)

    def to_partner(number, which, offset, top, size, source=None):
        spot = place(wholes[which], offset, top, size)
        copy = remote(
            spot if source is None else source,
            spot,
            pair_send,
            pair_recv,
            (number, which),
            hops.partner,
        )
        copy.start()
        started.append(copy)
        pairs.append(copy)

    def onward(direction, k, which, offset, top, size, source=None):
        spot = place(wholes[which], offset, top, size)
        copy = remote(
            spot if source is None else source,
            spot,
            ring_send,
            ring_recv,
            (direction, k, which),
            hops.above if direction == 0 else hops.below,
        )
        copy.start()
        started.append(copy)
        arrivals[(direction, k, which)] = copy

    pairs, arrivals, locals_ = [], {}, []
    for which in range(count):
        for direction in range(2):
            onward(direction, 0, which, 0, 0, rows, blocks[which])
    own_rows = pl.ds(pl.multiple_of(hops.core * rows, 16), rows)
    mine = pl.ds(pl.multiple_of(hops.core * ff_cols, 128), ff_cols)
    theirs = pl.ds(pl.multiple_of((1 - hops.core) * ff_cols, 128), ff_cols)
    targets = [
        gate_up_own.at[own_rows, pl.ds(0, ff_cols)],
        gate_up_own.at[own_rows, pl.ds(ff_cols, ff_cols)],
        down_own.at[own_rows],
    ]
    ff_copies = [remote(tokens, other_tokens, ff_send, ff_recv, (3,), hops.across)]
    ff_copies[0].start()
    for number, (weight, target) in enumerate(zip((gate, up, down), targets)):
        copy = remote(
            weight.at[:, theirs], target, ff_send, ff_recv, (number,), hops.partner
        )
        copy.start()
        ff_copies.append(copy)
        locals_.append((weight.at[:, mine], target, number))
    for which in range(count):
        to_partner(0, which, 0, 0, rows, blocks[which])
        locals_.append((blocks[which], place(wholes[which], 0, 0, rows), 3 + which))
    loads = [
        pltpu.make_async_copy(source, stages[number], in_sems.at[number])
        for source, _, number in locals_
    ]
    for copy in loads:
        copy.start()
    stores = [
        pltpu.make_async_copy(stages[number], target, out_sems.at[number])
        for _, target, number in locals_
    ]
    for load, store in zip(loads, stores):
        load.wait()
        store.start()
    cut = rows // 2
    for k in range(1, half + 1):
        for which in range(count):
            for direction in range(2):
                arrivals[(direction, k - 1, which)].wait_recv()
                offset = -k if direction == 0 else k
                if k < half - 1:
                    onward(direction, k, which, offset, 0, rows)
                elif k == half - 1:
                    onward(direction, k, which, offset, direction * cut, cut)
                if k < half:
                    to_partner(2 * k - 1 + direction, which, offset, 0, rows)
                else:
                    to_partner(2 * k - 1 + direction, which, half, direction * cut, cut)
    for copy in ff_copies + pairs:
        copy.wait_recv()
    for copy in ff_copies + started:
        copy.wait_send()
    for copy in stores:
        copy.wait()


ANY = pl.BlockSpec(memory_space=pl.ANY)


def comm_call(kernel, number, operands, shapes, stages, semaphores, name):
    moved = sum(v.size * 2 for v in shapes)
    return pl.pallas_call(
        kernel,
        out_shape=shapes,
        in_specs=[ANY] * len(operands),
        out_specs=[ANY] * len(shapes),
        scratch_shapes=stages + [pltpu.SemaphoreType.DMA(shape) for shape in semaphores],
        compiler_params=pltpu.CompilerParams(
            collective_id=number, has_side_effects=True, vmem_limit_bytes=16 * 2**20
        ),
        cost_estimate=pl.CostEstimate(flops=0, bytes_accessed=8 * moved, transcendentals=0),
        name=name,
    )(*operands)


def first_gather(blocks, gate, up, down, tokens):
    chips = lax.axis_size("dp") // 2
    half = chips // 2
    rows = blocks[0].shape[0]
    ff_cols = gate.shape[1] // 2
    count = len(blocks)
    shapes = [
        jax.ShapeDtypeStruct((2 * chips * rows, block.shape[1]), block.dtype) for block in blocks
    ] + [
        jax.ShapeDtypeStruct((2 * rows, 2 * ff_cols), gate.dtype),
        jax.ShapeDtypeStruct((2 * rows, ff_cols), gate.dtype),
        jax.ShapeDtypeStruct(tokens.shape, tokens.dtype),
    ]
    stages = [pltpu.VMEM((rows, ff_cols), gate.dtype)] * 3 + [
        pltpu.VMEM(block.shape, block.dtype) for block in blocks
    ]
    semaphores = [
        (3 + count,),
        (3 + count,),
        (2, half, count),
        (2, half, count),
        (2 * half + 1, count),
        (2 * half + 1, count),
        (4,),
        (4,),
    ]
    out = comm_call(
        functools.partial(first_kernel, count, ff_cols),
        0,
        (*blocks, gate, up, down, tokens),
        shapes,
        stages,
        semaphores,
        "first_gather",
    )
    return out[:count], out[count:]


GELU_SCALE = 0.7978845608028654
GELU_CUBE = 0.044715
ROW_TILE = 1024


def fill(spots, whole, parts):
    for number, part in enumerate(parts):
        size = part.shape[0]
        whole[pl.ds(pl.multiple_of(spots[number], size), size), :] = part[...]


def gate_up_kernel(count, spots, x, *refs):
    gate_parts, up_parts = refs[:count], refs[count : 2 * count]
    raw, hidden, weights = refs[2 * count :]
    gate_w, up_w = weights.at[0], weights.at[1]
    fill(spots, gate_w, gate_parts)
    fill(spots, up_w, up_parts)

    @pl.loop(0, x.shape[0] // min(ROW_TILE, x.shape[0]))
    def _(i):
        at = pl.ds(pl.multiple_of(i * ROW_TILE, ROW_TILE), ROW_TILE)
        rows = x[at, :]
        gate = product(rows, gate_w[...])
        up = product(rows, up_w[...])
        raw[0, at, :] = low(gate)
        raw[1, at, :] = low(up)
        bend = jnp.tanh(GELU_SCALE * (gate + GELU_CUBE * gate * gate * gate))
        hidden[at, :] = low(0.5 * gate * (1.0 + bend) * up)


def hidden_back_kernel(count, spots, x, raw, *refs):
    parts, (out, whole) = refs[:count], refs[count:]
    fill(spots, whole, parts)

    @pl.loop(0, x.shape[0] // min(ROW_TILE, x.shape[0]))
    def _(i):
        at = pl.ds(pl.multiple_of(i * ROW_TILE, ROW_TILE), ROW_TILE)
        d_hidden = product(x[at, :], whole[...])
        gate = to_float(raw[0, at, :])
        up = to_float(raw[1, at, :])
        square = gate * gate
        bend = jnp.tanh(GELU_SCALE * gate * (1.0 + GELU_CUBE * square))
        plus = 0.5 * (1.0 + bend)
        slope = plus + 0.5 * gate * (1.0 - bend * bend) * GELU_SCALE * (
            1.0 + 3.0 * GELU_CUBE * square
        )
        out[0, at, :] = low(d_hidden * up * slope)
        out[1, at, :] = low(d_hidden * gate * plus)


def columns_kernel(count, spots, h, *refs):
    parts, (out, whole) = refs[:count], refs[count:]
    fill(spots, whole, parts)
    step = pl.program_id(0)
    width = out.shape[1]
    cols = min(512, width)


    @pl.loop(0, width // cols)
    def _(j):
        across_ = pl.ds(pl.multiple_of(j * cols, cols), cols)
        term = product_t(h[0], whole[across_, :])

        @pl.when(step == 0)
        def _():
            out[:, across_] = term

        @pl.when(step > 0)
        def _():
            out[:, across_] = out[:, across_] + term


def block_kernel(where, spots, x, d, *refs):
    got, (out, turned) = refs[:-2], refs[-2:]

    @pl.when(pl.program_id(0) == 0)
    def _():
        turned[...] = x[...].T

    term = product(turned[...], d[0])
    if where == "none":
        out[...] = term.astype(out.dtype)
    elif where == "all":
        out[...] = low(term + to_float(got[0][...]))
    else:
        cut = got[0].shape[0]
        top, bottom = term[:cut], term[cut:]
        if where == "top":
            top = top + to_float(got[0][...])
        else:
            bottom = bottom + to_float(got[0][...])
        out[:cut, :] = low(top)
        out[cut:, :] = low(bottom)


def grid_call(kernel, spots, grid, operands, in_specs, shapes, out_specs, scratch, flops, name):
    moved = sum(v.size * v.dtype.itemsize for v in (*operands, *jax.tree.leaves(shapes)))
    return pl.pallas_call(
        kernel,
        grid_spec=pltpu.PrefetchScalarGridSpec(
            num_scalar_prefetch=1,
            grid=grid,
            in_specs=in_specs,
            out_specs=out_specs,
            scratch_shapes=scratch,
        ),
        out_shape=shapes,
        compiler_params=pltpu.CompilerParams(
            dimension_semantics=("arbitrary",) * len(grid), vmem_limit_bytes=56 * 2**20
        ),
        cost_estimate=pl.CostEstimate(flops=flops, bytes_accessed=moved, transcendentals=0),
        name=name,
    )(spots, *operands)


def once(shape):
    return pl.BlockSpec(
        shape, lambda *index: (0,) * len(shape), pipeline_mode=pl.Buffered(buffer_count=1)
    )


def gate_up(x, spots, parts, tile=512):
    count, (m, width), ff = len(parts), x.shape, parts[0].shape[1] // 2
    tiles = ff // tile
    part_specs = [pl.BlockSpec((p.shape[0], tile), lambda n, s: (0, n)) for p in parts] + [
        pl.BlockSpec((p.shape[0], tile), lambda n, s: (0, n + tiles)) for p in parts
    ]
    return grid_call(
        functools.partial(gate_up_kernel, count),
        spots,
        (tiles,),
        (x, *parts, *parts),
        [once((m, width))] + part_specs,
        [
            jax.ShapeDtypeStruct((2, m, ff), BF16),
            jax.ShapeDtypeStruct((m, ff), BF16),
            jax.ShapeDtypeStruct((2, width, ff), BF16),
        ],
        [
            pl.BlockSpec((2, m, tile), lambda n, s: (0, 0, n)),
            pl.BlockSpec((m, tile), lambda n, s: (0, n)),
            pl.BlockSpec((2, width, tile), lambda n, s: (0, 0, n)),
        ],
        [],
        4 * m * width * ff,
        "gate_up",
    )


def hidden_back(x, raw, spots, parts, tile=256):
    count, (m, width), ff = len(parts), x.shape, parts[0].shape[1]
    part_specs = [pl.BlockSpec((p.shape[0], tile), lambda n, s: (0, n)) for p in parts]
    return grid_call(
        functools.partial(hidden_back_kernel, count),
        spots,
        (ff // tile,),
        (x, raw, *parts),
        [once((m, width)), pl.BlockSpec((2, m, tile), lambda n, s: (0, 0, n))] + part_specs,
        jax.ShapeDtypeStruct((2, m, ff), BF16),
        pl.BlockSpec((2, m, tile), lambda n, s: (0, 0, n)),
        [pltpu.VMEM((width, tile), BF16)],
        2 * m * width * ff,
        "hidden_back",
    )


def columns_out(h, spots, parts, width, tile=1024):
    count, (groups, m, ff) = len(parts), h.shape
    tile = min(tile, ff)
    tiles = ff // tile
    part_specs = [pl.BlockSpec((p.shape[0], tile), lambda f, s: (0, f)) for p in parts]
    return grid_call(
        functools.partial(columns_kernel, count),
        spots,
        (groups * tiles,),
        (h, *parts),
        [pl.BlockSpec((1, m, tile), lambda f, s: (f // tiles, 0, f % tiles))] + part_specs,
        jax.ShapeDtypeStruct((m, width), F32),
        once((m, width)),
        [pltpu.VMEM((width, tile), BF16)],
        2 * groups * m * width * ff,
        "columns_out",
    )


def block_grad(x, d, chip, size, got=None, where="none", dtype=BF16, tile=2048):
    (m, _), (groups, _, ff) = x.shape, d.shape
    tile = min(tile, ff)
    tiles = ff // tile
    more = [] if got is None else [got]
    if size % 128:
        x = lax.dynamic_slice_in_dim(x, chip * size, size, 1)
        chip = jnp.zeros((), jnp.int32)
    return grid_call(
        functools.partial(block_kernel, where),
        chip.reshape(1).astype(jnp.int32),
        (groups * tiles,),
        (x, d, *more),
        [
            pl.BlockSpec((m, size), lambda f, s: (0, s[0])),
            pl.BlockSpec((1, m, tile), lambda f, s: (f // tiles, 0, f % tiles)),
        ]
        + [pl.BlockSpec((v.shape[0], tile), lambda f, s: (0, f)) for v in more],
        jax.ShapeDtypeStruct((size, groups * ff), dtype),
        pl.BlockSpec((size, tile), lambda f, s: (0, f)),
        [pltpu.VMEM((size, m), BF16)],
        2 * groups * m * size * ff,
        "block_grad",
    )


def row_kernel(pairs, spots, *refs):
    xs, ds = refs[:pairs], refs[pairs : 2 * pairs]
    more, out = refs[2 * pairs : -1], refs[-1]
    start = 0
    for x, d in zip(xs, ds):
        cols = d.shape[1]
        out[:, start : start + cols] = product_l(x[...], d[...]).astype(out.dtype)
        start += cols
    out[:, start:] = more[0][...].astype(out.dtype)
    if len(more) > 1:
        out[...] = out[...] + more[1][...].astype(out.dtype)


def row_grads(pairs, last, which, chips, rows, got, dtype):
    xs, ds = [x for x, _ in pairs], [d for _, d in pairs]
    cols = sum(d.shape[1] for d in ds) + last.shape[1]
    more = [] if got is None else [got]
    return grid_call(
        functools.partial(row_kernel, len(pairs)),
        (2 * jnp.arange(chips) + which).astype(jnp.int32),
        (chips,),
        (*xs, *ds, last, *more),
        [pl.BlockSpec((x.shape[0], rows), lambda j, s: (0, s[j])) for x in xs]
        + [once(d.shape) for d in ds]
        + [pl.BlockSpec((rows, last.shape[1]), lambda j, s: (s[j], 0))]
        + [pl.BlockSpec((rows, cols), lambda j, s: (j, 0)) for _ in more],
        jax.ShapeDtypeStruct((chips * rows, cols), dtype),
        pl.BlockSpec((rows, cols), lambda j, s: (j, 0)),
        [],
        sum(2 * d.size * chips * rows for d in ds),
        "row_grads",
    )


def last_kernel(count, *refs):
    terms, refs = refs[:count], refs[count:]
    outs, refs = refs[:count], refs[count:]
    sent, refs = refs[:count], refs[count:]
    got, refs = refs[:count], refs[count:]
    ring_send, ring_recv = refs
    hops = Hops()
    half = hops.chips // 2
    rows = outs[0].shape[0]
    cut = rows // 2
    greet([hops.above, hops.below])
    copies = {}

    def term(which, offset, top, size):
        at = pl.multiple_of(hops.chip_at(offset) * rows + top, 16)
        return terms[which][pl.ds(at, size), :]

    def send(which, direction, k, size):
        copy = remote(
            sent[which].at[direction, k, pl.ds(0, size)],
            got[which].at[direction, k, pl.ds(0, size)],
            ring_send,
            ring_recv,
            (direction, k, which),
            hops.above if direction == 0 else hops.below,
        )
        copy.start()
        copies[(which, direction, k)] = copy

    for which in range(count):
        for direction in range(2):
            sent[which][direction, 0, :cut, :] = low(term(which, half, direction * cut, cut))
            send(which, direction, 0, cut)
    for k in range(1, half):
        offset = half - k
        for which in range(count):
            for direction in range(2):
                there = offset if direction == 0 else -offset
                copies[(which, direction, k - 1)].wait_recv()
                came = got[which].at[direction, k - 1]
                if k == 1:
                    near, far = direction * cut, (1 - direction) * cut
                    sent[which][direction, k, near : near + cut, :] = low(
                        term(which, there, near, cut) + to_float(came[:cut, :])
                    )
                    sent[which][direction, k, far : far + cut, :] = low(
                        term(which, there, far, cut)
                    )
                else:
                    sent[which][direction, k] = low(
                        term(which, there, 0, rows) + to_float(came[...])
                    )
                send(which, direction, k, rows)
    for which in range(count):
        for direction in range(2):
            copies[(which, direction, half - 1)].wait_recv()
        outs[which][...] = (
            term(which, 0, 0, rows)
            + to_float(got[which][0, half - 1])
            + to_float(got[which][1, half - 1])
        )
    for copy in copies.values():
        copy.wait_send()


def last_reduce(terms):
    chips = lax.axis_size("dp") // 2
    half = chips // 2
    rows = terms[0].shape[0] // chips
    count = len(terms)
    moved = sum(v.size * 2 for v in terms)
    vmem = pl.BlockSpec(memory_space=pltpu.VMEM)
    buffers = [pltpu.VMEM((2, half, rows, v.shape[1]), BF16) for v in terms]
    return pl.pallas_call(
        functools.partial(last_kernel, count),
        out_shape=[jax.ShapeDtypeStruct((rows, v.shape[1]), F32) for v in terms],
        in_specs=[vmem] * count,
        out_specs=[vmem] * count,
        scratch_shapes=buffers
        + buffers
        + [pltpu.SemaphoreType.DMA((2, half, count)), pltpu.SemaphoreType.DMA((2, half, count))],
        compiler_params=pltpu.CompilerParams(
            collective_id=2, has_side_effects=True, vmem_limit_bytes=48 * 2**20
        ),
        cost_estimate=pl.CostEstimate(flops=0, bytes_accessed=8 * moved, transcendentals=0),
        name="last_reduce",
    )(*terms)


class Gather:
    def __init__(self, ring, block):
        self.ring = ring
        self.rows = block.shape[0]
        self.held = [block, block]
        self.parts = [(0, 0, block)]
        self.step_count = 0

    def step(self):
        ring, half = self.ring, self.ring.chips // 2
        self.step_count += 1
        k = self.step_count
        going_up, going_down = self.held
        if k < half:
            self.held = [ring.up(going_up), ring.down(going_down)]
            self.parts += [(-k, 0, self.held[0]), (k, 0, self.held[1])]
        else:
            cut = self.rows // 2
            self.held = [ring.up(going_up[:cut]), ring.down(going_down[cut:])]
            self.parts += [(half, 0, self.held[0]), (half, cut, self.held[1])]

    def pieces(self):
        spots = [self.ring.chip_at(o) * self.rows + row for o, row, _ in self.parts]
        return jnp.stack(spots).astype(jnp.int32), [part for _, _, part in self.parts]


class BlockReduce:
    def __init__(self, ring, x, d, size):
        self.ring, self.x, self.d, self.size = ring, x, d, size
        self.step_count = 0
        self.held = []

    def term(self, offset, got=None, where="none"):
        return block_grad(self.x, self.d, self.ring.chip_at(offset), self.size, got, where)

    def step(self):
        ring, half = self.ring, self.ring.chips // 2
        self.step_count += 1
        k = self.step_count
        if k == 1:
            term = self.term(half)
            cut = term.shape[0] // 2
            up, down = term[:cut], term[cut:]
        else:
            d = half + 1 - k
            up = self.term(d, self.held[0], "top" if k == 2 else "all")
            down = self.term(-d, self.held[1], "bottom" if k == 2 else "all")
        self.held = [ring.up(up), ring.down(down)]

    def result(self):
        term = block_grad(self.x, self.d, self.ring.chip_at(0), self.size, dtype=F32)
        return term + to_float(self.held[0]) + to_float(self.held[1])


def region(body):
    shapes = jax.eval_shape(body)
    yes = lax.optimization_barrier(jnp.array(True))
    return lax.cond(
        yes,
        body,
        lambda: jax.tree.map(lambda v: jnp.zeros(v.shape, v.dtype), shapes),
    )


def meet(rings, *values):
    held, values = tie([r.held for r in rings], values)
    for r, h in zip(rings, held):
        r.held = h
    return values if len(values) != 1 else values[0]


def local(
    tokens,
    layer_input,
    block_ids,
    block_table,
    w_query,
    w_key,
    w_value,
    w_output,
    w_left,
    w_right,
    w_gate,
    w_up,
    w_down,
    w_layer_gate,
    w_layer_proj,
    query_gain,
    key_gain,
    gain_input,
    gain_attn_out,
    gain_laurel,
    gain_ffw_in,
    gain_ffw_out,
    gain_layer_out,
    out_grad,
):
    ring = Ring()
    side = lax.axis_index("tensor")
    core = ring.core
    rows = w_query.shape[0]
    own = tokens.shape[0]
    width = tokens.shape[1]
    q_cols = w_query.shape[1]
    kv_cols = w_key.shape[1]
    rank = w_left.shape[1]
    small = w_layer_gate.shape[1]
    ff_cols = w_gate.shape[1] // 2
    chips = ring.chips

    def gain_block(query_part, key_part, parts):
        count = query_part.shape[0]
        columns = parts + [
            jnp.pad(query_part, (0, rows - count)),
            jnp.pad(key_part, (0, rows - count)),
        ]
        block = jnp.stack(columns, axis=1)
        return jnp.pad(block, ((0, 0), (0, 128 - block.shape[1])))

    gains = gain_block(
        query_gain,
        key_gain,
        [gain_input, gain_attn_out, gain_laurel, gain_ffw_in, gain_ffw_out, gain_layer_out],
    )
    half = chips // 2
    (qkv_full, output_t, small_full), (*ff_own, other_tokens) = first_gather(
        [
            jnp.concatenate([w_query, w_key, w_value], axis=1),
            w_output.T,
            jnp.concatenate([w_left, w_right.T, w_layer_gate, w_layer_proj.T, gains], axis=1),
        ],
        w_gate,
        w_up,
        w_down.T,
        tokens,
    )
    left_full = small_full[:, :rank]
    right_t = small_full[:, rank : 2 * rank]
    lgate_full = small_full[:, 2 * rank : 2 * rank + small]
    lproj_t = small_full[:, 2 * rank + small : 2 * rank + 2 * small]
    gains_full = small_full[:, 2 * rank + 2 * small :]

    gain_columns = to_float(gains_full[:, :8])
    (
        input_scale,
        attn_scale,
        laurel_scale,
        ffw_in_scale,
        ffw_out_scale,
        layer_scale,
    ) = (gain_columns[:, i] for i in range(6))
    head_part = query_gain.shape[0]

    def head_gain(column):
        return column.reshape(ring.devices, rows)[:, :head_part].reshape(HD)

    query_scale = head_gain(gain_columns[:, 6])
    key_scale = head_gain(gain_columns[:, 7])

    piece_len = 2 * own
    seq_total = block_ids.shape[1]
    per_seq = seq_total // piece_len
    dp_index = lax.axis_index("dp")
    row_index = dp_index // per_seq
    slot = lax.rem(dp_index, per_seq)
    first = slot * piece_len
    has_before = slot > 0
    has_after = slot < per_seq - 1
    natural = jnp.arange(piece_len, dtype=jnp.int32)
    here = first + lax.rem(natural + side * own, piece_len)
    cosines, sines = rope_tables(here, HD)
    reach_after = min(256, piece_len)
    forward_pairs = [(i, i + 1) for i in range(ring.devices - 1)]
    backward_pairs = [(i + 1, i) for i in range(ring.devices - 1)]

    def in_order(values):
        return jnp.where(
            side == 0, values, jnp.concatenate([values[own:], values[:own]], axis=0)
        )

    ids_row = lax.dynamic_index_in_dim(block_ids, row_index, 0, keepdims=False)
    table_row = lax.dynamic_index_in_dim(block_table, row_index, 0, keepdims=False)
    own_ids = lax.dynamic_slice_in_dim(ids_row, first, piece_len, 0)
    before_ids = lax.dynamic_slice_in_dim(ids_row, jnp.maximum(first - piece_len, 0), piece_len, 0)
    before_ids = jnp.where(has_before, before_ids, -2)
    after_ids = lax.dynamic_slice_in_dim(
        ids_row, jnp.minimum(first + piece_len, seq_total - reach_after), reach_after, 0
    )
    after_ids = jnp.where(has_after, after_ids, -2)
    key_ids = jnp.concatenate([before_ids, own_ids, after_ids], axis=0)
    query_ids = in_order(own_ids)
    block_count = block_table.shape[-1]
    number_rows = jnp.arange(block_count, dtype=jnp.int32)
    sees_last = jnp.sum(
        jnp.where(number_rows[None, :] == number_rows[:, None] - 1, table_row, 0), axis=1
    )
    query_sees = jnp.sum(
        jnp.where(query_ids[:, None] == number_rows[None, :], sees_last[None, :], 0), axis=1
    )
    previous_ids = jnp.where(query_sees == 1, query_ids - 1, query_ids)

    def prepare(qkv_in, query_gains, key_gains):
        query_in = qkv_in[:, :q_cols]
        key_in = qkv_in[:, q_cols : q_cols + kv_cols]
        value_in = qkv_in[:, q_cols + kv_cols :]
        query_out = rotate(
            norm_gain(query_in.reshape(piece_len, -1, HD), query_gains), cosines, sines
        )
        key_out = rotate(norm_gain(key_in.reshape(piece_len, -1, HD), key_gains), cosines, sines)
        return (query_out, key_out, norm_plain(value_in.reshape(piece_len, -1, HD)))

    heads_local = q_cols // HD
    kv_local = kv_cols // HD
    group = heads_local // kv_local

    def scores_for(query_low, keys_all):
        allowed = (query_ids[:, None] == key_ids[None, :]) | (
            previous_ids[:, None] == key_ids[None, :]
        )
        scores = jnp.einsum("qkgd,ckd->kgqc", query_low, keys_all, preferred_element_type=F32)
        return jnp.where(allowed[None, None], scores, NEGATIVE)

    def sum_sides(partial):
        return partial[:own] + to_float(across(low(partial[own:])))

    def both_sides(values):
        return jnp.concatenate([values, across(values)], axis=0)

    def four_ways(values):
        pair = both_sides(values)
        return jnp.concatenate([pair, ring.swap(pair)], axis=0)

    def sum_four(partial):
        pair = partial[: 2 * own] + to_float(ring.swap(low(partial[2 * own :])))
        return sum_sides(pair)

    def attend():
        normed_low = low(norm_gain(to_float(tokens), input_scale))
        seq_rows = jnp.concatenate(
            [normed_low, low(norm_gain(to_float(other_tokens), input_scale))], axis=0
        )
        qkv_raw = product(seq_rows, qkv_full)
        query_rot, key_rot, value_nrm = prepare(qkv_raw, query_scale, key_scale)
        query_low = low(query_rot).reshape(piece_len, kv_local, group, HD)
        kv_own = in_order(jnp.concatenate([low(key_rot), low(value_nrm)], axis=1))
        kv_before = lax.ppermute(kv_own, "dp", forward_pairs)
        kv_after = lax.ppermute(kv_own[:reach_after], "dp", backward_pairs)
        kv_all = jnp.concatenate([kv_before, kv_own, kv_after], axis=0)
        scores = scores_for(query_low, kv_all[:, :kv_local])
        highest = jnp.max(scores, axis=-1, keepdims=True)
        weights_exp = jnp.exp(scores - highest)
        totals = jnp.sum(weights_exp, axis=-1, keepdims=True)
        probs_low = low(weights_exp / totals)
        attended = jnp.einsum(
            "kgqc,ckd->qkgd", probs_low, kv_all[:, kv_local:], preferred_element_type=F32
        )
        log_totals = highest + jnp.log(totals)
        heads_low = low(attended.reshape(piece_len, heads_local * HD))
        return seq_rows, qkv_raw, query_low, kv_all, log_totals, heads_low

    gu = Gather(ring, ff_own[0])
    dn = Gather(ring, ff_own[1])
    gu.step()
    seq_rows, qkv_raw, query_low, kv_all, log_totals, heads_low = region(attend)
    heads_low = meet([gu], heads_low)
    gu.step()

    def join(heads_low):
        attn_out = sum_sides(product_t(heads_low, output_t))
        normed = norm_gain(to_float(tokens), input_scale)
        left_low = low(product(low(normed), left_full))
        right_out = product_t(left_low, right_t)
        laurel_normed = norm_gain(right_out, laurel_scale)
        attn_normed = norm_gain(attn_out, attn_scale)
        mixed = (to_float(tokens) + attn_normed + (normed + laurel_normed)) * ROOT_HALF
        return attn_out, left_low, right_out, mixed, low(norm_gain(mixed, ffw_in_scale))

    attn_out, left_low, right_out, mixed, ffw_low = region(lambda: join(heads_low))
    ffw_low = meet([gu], ffw_low)
    gu.step()
    ffw_rows = region(lambda: four_ways(ffw_low))
    ffw_rows = meet([gu], ffw_rows)
    for _ in range(half - 4):
        gu.step()
        ffw_rows = meet([gu], ffw_rows)
    gu.step()
    ffw_rows = meet([gu], ffw_rows)

    gu_spots, gu_parts = gu.pieces()
    dn.step()
    raw, hidden_low, gu_weights = region(lambda: gate_up(ffw_rows, gu_spots, gu_parts))
    raw, hidden_low = meet([dn], raw, hidden_low)
    for _ in range(half - 1):
        dn.step()
        raw, hidden_low = meet([dn], raw, hidden_low)
    dn_spots, dn_parts = dn.pieces()
    ffw_out = sum_four(columns_out(hidden_low[None], dn_spots, dn_parts, width))
    ffw_out_normed, ffw_out_back = jax.vjp(norm_gain, ffw_out, ffw_out_scale)
    block_mid = mixed + ffw_out_normed
    mid_low = low(block_mid)
    layer_pre = product(mid_low, lgate_full)

    def layer_gate_fn(pre_values, per_layer):
        return gelu_tanh(pre_values) * per_layer

    gated, gated_back = jax.vjp(layer_gate_fn, layer_pre, to_float(layer_input))
    gated_low = low(gated)
    layer_proj = product_t(gated_low, lproj_t)
    proj_normed, proj_back = jax.vjp(norm_gain, layer_proj, layer_scale)
    result = block_mid + proj_normed

    grad_out = to_float(out_grad)
    d_proj, d_layer_scale = proj_back(grad_out)
    d_proj_low = low(d_proj)
    d_gated = product(d_proj_low, lproj_t)
    d_pre, grad_layer_input = gated_back(d_gated)
    d_pre_low = low(d_pre)
    d_mid = grad_out + product_t(d_pre_low, lgate_full)
    d_ffw_out, d_ffw_out_scale = ffw_out_back(d_mid)
    d_ffw_rows = four_ways(low(d_ffw_out))
    d_ffw_rows, d_mid = tie(d_ffw_rows, d_mid)

    rd = BlockReduce(ring, d_ffw_rows, hidden_low[None], 2 * rows)
    rd.step()
    d_gate_up = region(lambda: hidden_back(d_ffw_rows, raw, dn_spots, dn_parts))
    d_gate_up = meet([rd], d_gate_up)
    rg = BlockReduce(ring, ffw_rows, d_gate_up, 2 * rows)
    rd.step()
    for _ in range(half - 4):
        d_gate_up = meet([rd], d_gate_up)
        rd.step()
    partial = region(
        lambda: product_t(d_gate_up[0], gu_weights[0]) + product_t(d_gate_up[1], gu_weights[1])
    )
    partial = meet([rd], partial)
    rd.step()
    rg.step()

    def back_3():
        d_ffw_normed = sum_four(partial)
        _, back = jax.vjp(norm_gain, mixed, ffw_in_scale)
        d_mixed_extra, d_ffw_in_scale = back(d_ffw_normed)
        d_branch = (d_mid + d_mixed_extra) * ROOT_HALF
        _, back = jax.vjp(norm_gain, attn_out, attn_scale)
        d_attn, d_attn_scale = back(d_branch)
        return d_ffw_in_scale, d_attn_scale, d_branch, low(d_attn)

    d_ffw_in_scale, d_attn_scale, d_branch, d_attn_low = meet([rd, rg], *region(back_3))
    rd.step()
    rg.step()

    def back_4():
        d_attn_rows = both_sides(d_attn_low)
        d_heads = low(product(d_attn_rows, output_t)).reshape(piece_len, kv_local, group, HD)
        keys_all, values_all = kv_all[:, :kv_local], kv_all[:, kv_local:]
        probs = jnp.exp(scores_for(query_low, keys_all) - log_totals)
        probs_low = low(probs)
        d_values_all = jnp.einsum(
            "kgqc,qkgd->ckd", probs_low, d_heads, preferred_element_type=F32
        )
        d_probs = jnp.einsum("qkgd,ckd->kgqc", d_heads, values_all, preferred_element_type=F32)
        deltas = jnp.sum(probs * d_probs, axis=-1, keepdims=True)
        d_scores = low(probs * (d_probs - deltas))
        d_keys_all = jnp.einsum("kgqc,qkgd->ckd", d_scores, query_low, preferred_element_type=F32)
        d_query_rot = jnp.einsum("kgqc,ckd->qkgd", d_scores, keys_all, preferred_element_type=F32)
        d_kv_all = jnp.concatenate([d_keys_all, d_values_all], axis=1)
        return d_attn_rows, d_kv_all, d_query_rot

    d_attn_rows, d_kv_all, d_query_rot = meet([rd, rg], *region(back_4))
    rg.step()
    for _ in range(half - 4):
        d_kv_all = meet([rg], d_kv_all)
        rg.step()

    def back_5():
        to_before = low(d_kv_all[:piece_len])
        to_after = low(d_kv_all[2 * piece_len :])
        from_after = to_float(lax.ppermute(to_before, "dp", backward_pairs))
        from_before = to_float(lax.ppermute(to_after, "dp", forward_pairs))
        d_kv = d_kv_all[piece_len : 2 * piece_len] + from_after
        d_kv = d_kv + jnp.pad(from_before, ((0, piece_len - reach_after), (0, 0), (0, 0)))
        d_kv = in_order(d_kv)
        _, back = jax.vjp(prepare, qkv_raw, query_scale, key_scale)
        d_qkv, query_scale_grad, key_scale_grad = back(
            (
                d_query_rot.reshape(piece_len, heads_local, HD),
                d_kv[:, :kv_local],
                d_kv[:, kv_local:],
            )
        )
        return low(d_qkv), query_scale_grad, key_scale_grad

    d_qkv_low, query_scale_grad, key_scale_grad = meet([rg], *region(back_5))
    rg.step()

    def own_columns(values, which):
        blocks = values.reshape(values.shape[0], chips, 2, rows)
        return lax.dynamic_index_in_dim(blocks, which, 2, keepdims=False).reshape(
            values.shape[0], chips * rows
        )

    def both_cores(pairs, last):
        if rows % 128 == 0:
            theirs = row_grads(pairs, last, 1 - core, chips, rows, None, BF16)
            return row_grads(pairs, last, core, chips, rows, ring.swap(theirs), F32)

        def terms(which):
            return jnp.concatenate(
                [product_l(own_columns(x, which), d) for x, d in pairs]
                + [own_columns(last.T, which).T],
                axis=1,
            )

        return terms(core) + to_float(ring.swap(low(terms(1 - core))))

    def head_gain_back(grads):
        padded = jnp.pad(grads.reshape(ring.devices, head_part), ((0, 0), (0, rows - head_part)))
        return padded.reshape(width)

    def back_6():
        normed, input_norm_back = jax.vjp(norm_gain, to_float(tokens), input_scale)
        _, laurel_back = jax.vjp(norm_gain, right_out, laurel_scale)
        d_right, d_laurel_scale = laurel_back(d_branch)
        d_right_low = low(d_right)
        d_left_low = low(product(d_right_low, right_t))
        d_normed = d_branch + product_t(d_left_low, left_full)
        d_normed = d_normed + sum_sides(product_t(d_qkv_low, qkv_full))
        d_inputs_extra, d_input_scale = input_norm_back(d_normed)
        grad_tokens = d_branch + d_inputs_extra
        gain_grads = jnp.stack(
            [
                d_input_scale,
                d_attn_scale,
                d_laurel_scale,
                d_ffw_in_scale,
                d_ffw_out_scale,
                d_layer_scale,
                head_gain_back(query_scale_grad),
                head_gain_back(key_scale_grad),
            ],
            axis=0,
        )
        gain_grads = jnp.pad(gain_grads, ((0, 120), (0, 0))).T
        summed = both_cores(
            [
                (d_attn_rows, heads_low),
                (seq_rows, d_qkv_low),
                (mid_low, d_pre_low),
                (d_proj_low, gated_low),
                (low(normed), d_left_low),
                (d_right_low, left_low),
            ],
            gain_grads,
        )
        large = 2 * q_cols + 2 * kv_cols
        part = (summed.shape[1] - large) // 2
        small_mine = lax.dynamic_slice_in_dim(summed, large + side * part, part, 1)
        small_theirs = lax.dynamic_slice_in_dim(summed, large + (1 - side) * part, part, 1)
        small_mine = small_mine + to_float(across(low(small_theirs)))
        return grad_tokens, summed[:, : large // 2], summed[:, large // 2 : large], small_mine

    grad_tokens, *blocks = meet([rg], *region(back_6))

    def finish_feed_forward():
        down_sum = rd.result()
        gate_up_sum = rg.result()
        return (
            back_to_rows(down_sum),
            back_to_rows(gate_up_sum[:, :ff_cols]),
            back_to_rows(gate_up_sum[:, ff_cols:]),
        )

    def back_to_rows(block):
        mine = lax.dynamic_slice_in_dim(block, core * rows, rows, 0)
        theirs = lax.dynamic_slice_in_dim(block, (1 - core) * rows, rows, 0)
        got = ring.swap(theirs)
        return jnp.where(
            core == 0,
            jnp.concatenate([mine, got], axis=1),
            jnp.concatenate([got, mine], axis=1),
        )

    out_down_t, out_gate, out_up = region(finish_feed_forward)
    one, two, small_half = last_reduce(blocks)
    total = jnp.concatenate([one, two], axis=1)
    out_output = total[:, :q_cols].T
    out_qkv = total[:, q_cols:]
    small_other = across(small_half)
    out_small = jnp.where(
        side == 0,
        jnp.concatenate([small_half, small_other], axis=1),
        jnp.concatenate([small_other, small_half], axis=1),
    )
    out_gains = out_small[:, 2 * rank + 2 * small :]
    return (
        low(result),
        grad_tokens,
        grad_layer_input,
        out_qkv[:, :q_cols],
        out_qkv[:, q_cols : q_cols + kv_cols],
        out_qkv[:, q_cols + kv_cols :],
        out_output,
        out_small[:, 2 * small : 2 * small + rank],
        out_small[:, 2 * small + rank : 2 * small + 2 * rank].T,
        out_gate,
        out_up,
        out_down_t.T,
        out_small[:, :small],
        out_small[:, small : 2 * small].T,
        out_gains[:head_part, 6],
        out_gains[:head_part, 7],
        out_gains[:, 0],
        out_gains[:, 1],
        out_gains[:, 2],
        out_gains[:, 3],
        out_gains[:, 4],
        out_gains[:, 5],
    )


def solution(mesh):
    both = P(("dp", "tensor"), None)
    rows_split = P("dp", "tensor")
    cols_split = P("tensor", "dp")
    by_row = P("dp", None)
    by_col = P(None, "dp")
    flat = P("dp")
    return jax.shard_map(
        local,
        mesh=mesh,
        in_specs=(
            (both, both, P(), P(), rows_split, rows_split, rows_split, cols_split)
            + (by_row, by_col, rows_split, rows_split, cols_split, by_row, by_col)
            + (flat,) * 8
            + (both,)
        ),
        out_specs=(
            (both, both, both, rows_split, rows_split, rows_split, cols_split)
            + (by_row, by_col, rows_split, rows_split, cols_split, by_row, by_col)
            + (flat,) * 8
        ),
        check_vma=False,
    )
```

```python
import functools

import jax
import jax.numpy as jnp
from jax import lax
from jax.experimental import pallas as pl
from jax.experimental.pallas import tpu as pltpu
from jax.sharding import PartitionSpec as P

HD = 256
EPS = 1e-06
ROOT_HALF = 0.7071067811865476
NEGATIVE = -1e30
F32 = jnp.float32
BF16 = jnp.bfloat16


def norm_gain(values, gains):
    return values * lax.rsqrt(jnp.mean(values * values, axis=-1, keepdims=True) + EPS) * gains


def norm_plain(values):
    return values * lax.rsqrt(jnp.mean(values * values, axis=-1, keepdims=True) + EPS)


def gelu_tanh(values):
    return jax.nn.gelu(values, approximate=True)


def rope_tables(positions, head_width):
    positions = positions.astype(F32)[:, None]
    frequency = 10000.0 ** (-2.0 * jnp.arange(head_width // 2, dtype=F32) / head_width)
    angles = positions * frequency[None, :]
    return (jnp.cos(angles), jnp.sin(angles))


def rotate(values, cosines, sines):
    half_width = values.shape[-1] // 2
    front_half = values[..., :half_width]
    back_half = values[..., half_width:]
    cos_wide = cosines[:, None, :]
    sin_wide = sines[:, None, :]
    return jnp.concatenate(
        [
            front_half * cos_wide - back_half * sin_wide,
            back_half * cos_wide + front_half * sin_wide,
        ],
        axis=-1,
    )


def to_float(values):
    return values.astype(F32)


def low(values):
    return values.astype(BF16)


def product(left_in, right_in):
    return jnp.dot(left_in, right_in, preferred_element_type=F32)


def product_t(left_in, right_in):
    return lax.dot_general(left_in, right_in, (((1,), (1,)), ((), ())), preferred_element_type=F32)


def product_l(left_in, right_in):
    return lax.dot_general(left_in, right_in, (((0,), (0,)), ((), ())), preferred_element_type=F32)


def tie(*values):
    return lax.optimization_barrier(values)


class Ring:
    def __init__(self):
        self.devices = lax.axis_size("dp")
        self.chips = self.devices // 2
        order = list(range(0, self.chips, 2)) + list(range(self.chips - 1, 0, -2))
        self.cw = [
            (2 * order[p] + c, 2 * order[(p + 1) % self.chips] + c)
            for p in range(self.chips)
            for c in range(2)
        ]
        self.ccw = [(b, a) for a, b in self.cw]
        self.core_pairs = [(d, d ^ 1) for d in range(self.devices)]
        me = lax.axis_index("dp")
        self.core = lax.rem(me, 2)
        self.chip = me // 2
        self.place = jnp.where(
            lax.rem(self.chip, 2) == 0, self.chip // 2, self.chips - 1 - self.chip // 2
        )

    def chip_at(self, offset):
        place = lax.rem(self.place + offset + self.chips, self.chips)
        return jnp.where(place < self.chips // 2, 2 * place, 2 * (self.chips - 1 - place) + 1)

    def up(self, values):
        return lax.ppermute(values, "dp", self.cw)

    def down(self, values):
        return lax.ppermute(values, "dp", self.ccw)

    def swap(self, values):
        return lax.ppermute(values, "dp", self.core_pairs)


def across(values):
    return lax.ppermute(values, "tensor", [(0, 1), (1, 0)])


def remote(source, target, sends, receives, index, device):
    return pltpu.make_async_remote_copy(
        src_ref=source,
        dst_ref=target,
        send_sem=sends.at[index],
        recv_sem=receives.at[index],
        device_id=device,
        device_id_type=pl.DeviceIdType.MESH,
    )


def greet(devices):
    barrier = pltpu.get_barrier_semaphore()
    for device in devices:
        pl.semaphore_signal(
            barrier, inc=1, device_id=device, device_id_type=pl.DeviceIdType.MESH
        )
    pl.semaphore_wait(barrier, len(devices))


def block_rows(ref, start, count):
    return ref.at[pl.ds(pl.multiple_of(start, 16), count)]


class Hops:
    def __init__(self):
        me = lax.axis_index("dp")
        self.chips = lax.axis_size("dp") // 2
        self.core = lax.rem(me, 2)
        self.chip = me // 2
        self.place = jnp.where(
            lax.rem(self.chip, 2) == 0, self.chip // 2, self.chips - 1 - self.chip // 2
        )
        self.partner = {"dp": self.chip * 2 + 1 - self.core}
        self.above = {"dp": self.chip_at(1) * 2 + self.core}
        self.below = {"dp": self.chip_at(-1) * 2 + self.core}
        self.across = {"tensor": 1 - lax.axis_index("tensor")}

    def chip_at(self, offset):
        place = lax.rem(self.place + offset + self.chips, self.chips)
        return jnp.where(place < self.chips // 2, 2 * place, 2 * (self.chips - 1 - place) + 1)


def first_kernel(count, ff_cols, *refs):
    blocks, refs = refs[:count], refs[count:]
    (gate, up, down, tokens), refs = refs[:4], refs[4:]
    wholes, refs = refs[:count], refs[count:]
    (gate_up_own, down_own, other_tokens), refs = refs[:3], refs[3:]
    stages, refs = refs[: 3 + count], refs[3 + count :]
    in_sems, out_sems, ring_send, ring_recv, pair_send, pair_recv, ff_send, ff_recv = refs
    hops = Hops()
    half = hops.chips // 2
    rows = blocks[0].shape[0]
    greet([hops.above, hops.below, hops.partner, hops.across])
    started = []

    def place(ref, offset, top, size):
        return block_rows(ref, (2 * hops.chip_at(offset) + hops.core) * rows + top, size)

    def to_partner(number, which, offset, top, size, source=None):
        spot = place(wholes[which], offset, top, size)
        copy = remote(
            spot if source is None else source,
            spot,
            pair_send,
            pair_recv,
            (number, which),
            hops.partner,
        )
        copy.start()
        started.append(copy)
        pairs.append(copy)

    def onward(direction, k, which, offset, top, size, source=None):
        spot = place(wholes[which], offset, top, size)
        copy = remote(
            spot if source is None else source,
            spot,
            ring_send,
            ring_recv,
            (direction, k, which),
            hops.above if direction == 0 else hops.below,
        )
        copy.start()
        started.append(copy)
        arrivals[(direction, k, which)] = copy

    pairs, arrivals, locals_ = [], {}, []
    for which in range(count):
        for direction in range(2):
            onward(direction, 0, which, 0, 0, rows, blocks[which])
    own_rows = pl.ds(pl.multiple_of(hops.core * rows, 16), rows)
    mine = pl.ds(pl.multiple_of(hops.core * ff_cols, 128), ff_cols)
    theirs = pl.ds(pl.multiple_of((1 - hops.core) * ff_cols, 128), ff_cols)
    targets = [
        gate_up_own.at[own_rows, pl.ds(0, ff_cols)],
        gate_up_own.at[own_rows, pl.ds(ff_cols, ff_cols)],
        down_own.at[own_rows],
    ]
    ff_copies = [remote(tokens, other_tokens, ff_send, ff_recv, (3,), hops.across)]
    ff_copies[0].start()
    for number, (weight, target) in enumerate(zip((gate, up, down), targets)):
        copy = remote(
            weight.at[:, theirs], target, ff_send, ff_recv, (number,), hops.partner
        )
        copy.start()
        ff_copies.append(copy)
        locals_.append((weight.at[:, mine], target, number))
    for which in range(count):
        to_partner(0, which, 0, 0, rows, blocks[which])
        locals_.append((blocks[which], place(wholes[which], 0, 0, rows), 3 + which))
    loads = [
        pltpu.make_async_copy(source, stages[number], in_sems.at[number])
        for source, _, number in locals_
    ]
    for copy in loads:
        copy.start()
    stores = [
        pltpu.make_async_copy(stages[number], target, out_sems.at[number])
        for _, target, number in locals_
    ]
    for load, store in zip(loads, stores):
        load.wait()
        store.start()
    cut = rows // 2
    for k in range(1, half + 1):
        for which in range(count):
            for direction in range(2):
                arrivals[(direction, k - 1, which)].wait_recv()
                offset = -k if direction == 0 else k
                if k < half - 1:
                    onward(direction, k, which, offset, 0, rows)
                elif k == half - 1:
                    onward(direction, k, which, offset, direction * cut, cut)
                if k < half:
                    to_partner(2 * k - 1 + direction, which, offset, 0, rows)
                else:
                    to_partner(2 * k - 1 + direction, which, half, direction * cut, cut)
    for copy in ff_copies + pairs:
        copy.wait_recv()
    for copy in ff_copies + started:
        copy.wait_send()
    for copy in stores:
        copy.wait()


ANY = pl.BlockSpec(memory_space=pl.ANY)


def comm_call(kernel, number, operands, shapes, stages, semaphores, name):
    moved = sum(v.size * 2 for v in shapes)
    return pl.pallas_call(
        kernel,
        out_shape=shapes,
        in_specs=[ANY] * len(operands),
        out_specs=[ANY] * len(shapes),
        scratch_shapes=stages + [pltpu.SemaphoreType.DMA(shape) for shape in semaphores],
        compiler_params=pltpu.CompilerParams(
            collective_id=number, has_side_effects=True, vmem_limit_bytes=16 * 2**20
        ),
        cost_estimate=pl.CostEstimate(flops=0, bytes_accessed=8 * moved, transcendentals=0),
        name=name,
    )(*operands)


def first_gather(blocks, gate, up, down, tokens):
    chips = lax.axis_size("dp") // 2
    half = chips // 2
    rows = blocks[0].shape[0]
    ff_cols = gate.shape[1] // 2
    count = len(blocks)
    shapes = [
        jax.ShapeDtypeStruct((2 * chips * rows, block.shape[1]), block.dtype) for block in blocks
    ] + [
        jax.ShapeDtypeStruct((2 * rows, 2 * ff_cols), gate.dtype),
        jax.ShapeDtypeStruct((2 * rows, ff_cols), gate.dtype),
        jax.ShapeDtypeStruct(tokens.shape, tokens.dtype),
    ]
    stages = [pltpu.VMEM((rows, ff_cols), gate.dtype)] * 3 + [
        pltpu.VMEM(block.shape, block.dtype) for block in blocks
    ]
    semaphores = [
        (3 + count,),
        (3 + count,),
        (2, half, count),
        (2, half, count),
        (2 * half + 1, count),
        (2 * half + 1, count),
        (4,),
        (4,),
    ]
    out = comm_call(
        functools.partial(first_kernel, count, ff_cols),
        0,
        (*blocks, gate, up, down, tokens),
        shapes,
        stages,
        semaphores,
        "first_gather",
    )
    return out[:count], out[count:]


GELU_SCALE = 0.7978845608028654
GELU_CUBE = 0.044715
ROW_TILE = 1024


def fill(spots, whole, parts):
    for number, part in enumerate(parts):
        size = part.shape[0]
        whole[pl.ds(pl.multiple_of(spots[number], size), size), :] = part[...]


def gate_up_kernel(count, spots, x, *refs):
    gate_parts, up_parts = refs[:count], refs[count : 2 * count]
    raw, hidden, weights = refs[2 * count :]
    gate_w, up_w = weights.at[0], weights.at[1]
    fill(spots, gate_w, gate_parts)
    fill(spots, up_w, up_parts)

    @pl.loop(0, x.shape[0] // min(ROW_TILE, x.shape[0]))
    def _(i):
        at = pl.ds(pl.multiple_of(i * ROW_TILE, ROW_TILE), ROW_TILE)
        rows = x[at, :]
        gate = product(rows, gate_w[...])
        up = product(rows, up_w[...])
        raw[0, at, :] = low(gate)
        raw[1, at, :] = low(up)
        bend = jnp.tanh(GELU_SCALE * (gate + GELU_CUBE * gate * gate * gate))
        hidden[at, :] = low(0.5 * gate * (1.0 + bend) * up)


def hidden_back_kernel(count, spots, x, raw, *refs):
    parts, (out, whole) = refs[:count], refs[count:]
    fill(spots, whole, parts)

    @pl.loop(0, x.shape[0] // min(ROW_TILE, x.shape[0]))
    def _(i):
        at = pl.ds(pl.multiple_of(i * ROW_TILE, ROW_TILE), ROW_TILE)
        d_hidden = product(x[at, :], whole[...])
        gate = to_float(raw[0, at, :])
        up = to_float(raw[1, at, :])
        square = gate * gate
        bend = jnp.tanh(GELU_SCALE * gate * (1.0 + GELU_CUBE * square))
        plus = 0.5 * (1.0 + bend)
        slope = plus + 0.5 * gate * (1.0 - bend * bend) * GELU_SCALE * (
            1.0 + 3.0 * GELU_CUBE * square
        )
        out[0, at, :] = low(d_hidden * up * slope)
        out[1, at, :] = low(d_hidden * gate * plus)


def columns_kernel(count, spots, h, *refs):
    parts, (out, whole) = refs[:count], refs[count:]
    fill(spots, whole, parts)
    step = pl.program_id(0)
    width = out.shape[1]
    cols = min(512, width)


    @pl.loop(0, width // cols)
    def _(j):
        across_ = pl.ds(pl.multiple_of(j * cols, cols), cols)
        term = product_t(h[0], whole[across_, :])

        @pl.when(step == 0)
        def _():
            out[:, across_] = term

        @pl.when(step > 0)
        def _():
            out[:, across_] = out[:, across_] + term


def block_kernel(count, spots, *refs):
    xs, d = refs[:count], refs[count]
    outs, turned = refs[count + 1 : 2 * count + 1], refs[2 * count + 1 :]

    @pl.when(pl.program_id(0) == 0)
    def _():
        for x, t in zip(xs, turned):
            t[...] = x[...].T

    for t, out in zip(turned, outs):
        out[...] = low(product(t[...], d[0]))


def grid_call(kernel, spots, grid, operands, in_specs, shapes, out_specs, scratch, flops, name):
    moved = sum(v.size * v.dtype.itemsize for v in (*operands, *jax.tree.leaves(shapes)))
    if flops == 0:
        moved = 0
    return pl.pallas_call(
        kernel,
        grid_spec=pltpu.PrefetchScalarGridSpec(
            num_scalar_prefetch=1,
            grid=grid,
            in_specs=in_specs,
            out_specs=out_specs,
            scratch_shapes=scratch,
        ),
        out_shape=shapes,
        compiler_params=pltpu.CompilerParams(
            dimension_semantics=("arbitrary",) * len(grid), vmem_limit_bytes=56 * 2**20
        ),
        cost_estimate=pl.CostEstimate(flops=flops, bytes_accessed=moved, transcendentals=0),
        name=name,
    )(spots, *operands)


def once(shape):
    return pl.BlockSpec(
        shape, lambda *index: (0,) * len(shape), pipeline_mode=pl.Buffered(buffer_count=1)
    )


def gate_up(x, spots, parts, tile=512):
    count, (m, width), ff = len(parts), x.shape, parts[0].shape[1] // 2
    tiles = ff // tile
    part_specs = [pl.BlockSpec((p.shape[0], tile), lambda n, s: (0, n)) for p in parts] + [
        pl.BlockSpec((p.shape[0], tile), lambda n, s: (0, n + tiles)) for p in parts
    ]
    return grid_call(
        functools.partial(gate_up_kernel, count),
        spots,
        (tiles,),
        (x, *parts, *parts),
        [once((m, width))] + part_specs,
        [
            jax.ShapeDtypeStruct((2, m, ff), BF16),
            jax.ShapeDtypeStruct((m, ff), BF16),
            jax.ShapeDtypeStruct((2, width, ff), BF16),
        ],
        [
            pl.BlockSpec((2, m, tile), lambda n, s: (0, 0, n)),
            pl.BlockSpec((m, tile), lambda n, s: (0, n)),
            pl.BlockSpec((2, width, tile), lambda n, s: (0, 0, n)),
        ],
        [],
        4 * m * width * ff,
        "gate_up",
    )


def hidden_back(x, raw, spots, parts, tile=256):
    count, (m, width), ff = len(parts), x.shape, parts[0].shape[1]
    part_specs = [pl.BlockSpec((p.shape[0], tile), lambda n, s: (0, n)) for p in parts]
    return grid_call(
        functools.partial(hidden_back_kernel, count),
        spots,
        (ff // tile,),
        (x, raw, *parts),
        [once((m, width)), pl.BlockSpec((2, m, tile), lambda n, s: (0, 0, n))] + part_specs,
        jax.ShapeDtypeStruct((2, m, ff), BF16),
        pl.BlockSpec((2, m, tile), lambda n, s: (0, 0, n)),
        [pltpu.VMEM((width, tile), BF16)],
        2 * m * width * ff,
        "hidden_back",
    )


def columns_out(h, spots, parts, width, tile=1024):
    count, (groups, m, ff) = len(parts), h.shape
    tile = min(tile, ff)
    tiles = ff // tile
    part_specs = [pl.BlockSpec((p.shape[0], tile), lambda f, s: (0, f)) for p in parts]
    return grid_call(
        functools.partial(columns_kernel, count),
        spots,
        (groups * tiles,),
        (h, *parts),
        [pl.BlockSpec((1, m, tile), lambda f, s: (f // tiles, 0, f % tiles))] + part_specs,
        jax.ShapeDtypeStruct((m, width), F32),
        once((m, width)),
        [pltpu.VMEM((width, tile), BF16)],
        2 * groups * m * width * ff,
        "columns_out",
    )


def block_grads(x, d, chips, size, tile=1024):
    (m, _), (groups, _, ff) = x.shape, d.shape
    count = len(chips)
    tile = min(tile, ff)
    tiles = ff // tile
    spots = jnp.stack(chips).astype(jnp.int32)
    if size % 128:
        xs = [lax.dynamic_slice_in_dim(x, chip * size, size, 1) for chip in chips]
        x_specs = [once((m, size))] * count
    else:
        xs = [x] * count
        x_specs = [
            pl.BlockSpec((m, size), functools.partial(lambda i, f, s: (0, s[i]), i))
            for i in range(count)
        ]
    return grid_call(
        functools.partial(block_kernel, count),
        spots,
        (groups * tiles,),
        (*xs, d),
        x_specs + [pl.BlockSpec((1, m, tile), lambda f, s: (f // tiles, 0, f % tiles))],
        [jax.ShapeDtypeStruct((size, groups * ff), BF16)] * count,
        [pl.BlockSpec((size, tile), lambda f, s: (0, f))] * count,
        [pltpu.VMEM((size, m), BF16)] * count,
        0,
        "block_grads",
    )


def row_kernel(pairs, spots, *refs):
    xs, ds = refs[:pairs], refs[pairs : 2 * pairs]
    last, mine, theirs, both = refs[2 * pairs :]
    rows = mine.shape[0]
    core = spots[0]
    start = 0
    for x, d in zip(xs, ds):
        cols = d.shape[1]
        both[:, start : start + cols] = product_l(x[...], d[...])
        start += cols
    both[:, start:] = last[...]
    mine[...] = both[pl.ds(pl.multiple_of(core * rows, 128), rows), :]
    theirs[...] = low(both[pl.ds(pl.multiple_of((1 - core) * rows, 128), rows), :])


def row_grads(pairs, last, core, chips, rows):
    xs, ds = [x for x, _ in pairs], [d for _, d in pairs]
    cols = sum(d.shape[1] for d in ds) + last.shape[1]
    if rows % 128:

        def own_columns(values, which):
            blocks = values.reshape(values.shape[0], chips, 2, rows)
            return lax.dynamic_index_in_dim(blocks, which, 2, keepdims=False).reshape(
                values.shape[0], chips * rows
            )

        def terms(which):
            return jnp.concatenate(
                [product_l(own_columns(x, which), d) for x, d in pairs]
                + [own_columns(last.T, which).T],
                axis=1,
            )

        return terms(core), low(terms(1 - core))
    block = pl.BlockSpec((rows, cols), lambda j, s: (j, 0))
    return grid_call(
        functools.partial(row_kernel, len(pairs)),
        core.reshape(1).astype(jnp.int32),
        (chips,),
        (*xs, *ds, last),
        [pl.BlockSpec((x.shape[0], 2 * rows), lambda j, s: (0, j)) for x in xs]
        + [once(d.shape) for d in ds]
        + [pl.BlockSpec((2 * rows, last.shape[1]), lambda j, s: (j, 0))],
        [
            jax.ShapeDtypeStruct((chips * rows, cols), F32),
            jax.ShapeDtypeStruct((chips * rows, cols), BF16),
        ],
        [block, block],
        [pltpu.VMEM((2 * rows, cols), F32)],
        sum(4 * d.size * chips * rows for d in ds),
        "row_grads",
    )


def last_kernel(large, *refs):
    mine, theirs, refs = refs[0], refs[1], refs[2:]
    ff_terms, refs = refs[:6], refs[6:]
    (main, little, *ff_outs), refs = refs[:5], refs[5:]
    own, core_got, side_sent, side_got, first, got, refs = *refs[:6], refs[6:]
    ff_held, (ff_sent,), refs = refs[:6], refs[6:7], refs[7:]
    loads, core_send, core_recv, side_send, side_recv, ring_send, ring_recv, ff_send, ff_recv = refs
    hops = Hops()
    side = lax.axis_index("tensor")
    half = hops.chips // 2
    rows = main.shape[0]
    part = little.shape[1]
    ff_cols = ff_sent.shape[2]
    cut = rows // 2
    greet([hops.above, hops.below, hops.partner, hops.across])
    order = [half]
    for k in range(1, half):
        order += [half - k, k - half]
    order.append(0)

    def rows_at(offset, top=0, size=rows):
        return pl.ds(pl.multiple_of(hops.chip_at(offset) * rows + top, 16), size)

    started, arriving = [], []
    for i, offset in enumerate(order):
        at = rows_at(offset)
        copy = remote(
            theirs.at[at], core_got.at[at], core_send, core_recv, (i,), hops.partner
        )
        copy.start()
        load = pltpu.make_async_copy(mine.at[at], own.at[at], loads.at[i])
        load.start()
        started.append(copy)
        arriving.append((copy, load))
    ff_loads = [
        pltpu.make_async_copy(source, target, loads.at[len(order) + i])
        for i, (source, target) in enumerate(zip(ff_terms, ff_held))
    ]
    for load in ff_loads:
        load.start()

    sides = {}
    my_part = pl.ds(pl.multiple_of(large + side * part, 128), part)
    their_part = pl.ds(pl.multiple_of(large + (1 - side) * part, 128), part)

    def ready(i):
        at = rows_at(order[i])
        copy, load = arriving[i]
        load.wait()
        copy.wait_recv()
        own[at, :] = own[at, :] + to_float(core_got[at, :])
        side_sent[at, :] = low(own[at, their_part])
        copy = remote(
            side_sent.at[at], side_got.at[at], side_send, side_recv, (i,), hops.across
        )
        copy.start()
        started.append(copy)
        sides[order[i]] = copy

    pieces = [(0, large // 2), (large // 2, large // 2), (large, part)]
    copies = {}

    def term(which, offset, top, size):
        at = rows_at(offset, top, size)
        start, cols = pieces[which]
        if which < 2:
            return own[at, start : start + cols]
        return own[at, my_part] + to_float(side_got[at, :])

    def send(which, direction, k, source, top, size):
        start, cols = pieces[which]
        copy = remote(
            source,
            got.at[direction, k, pl.ds(top, size), pl.ds(start, cols)],
            ring_send,
            ring_recv,
            (direction, k, which),
            hops.above if direction == 0 else hops.below,
        )
        copy.start()
        started.append(copy)
        copies[(which, direction, k)] = copy

    def step(which, k):
        start, cols = pieces[which]
        for direction in range(2):
            near, far = direction * cut, (1 - direction) * cut
            if k == 0:
                first[direction, :, start : start + cols] = low(term(which, half, near, cut))
                source = first.at[direction, :, pl.ds(start, cols)]
                send(which, direction, 0, source, near, cut)
                continue
            offset = (half - k) * (1 if direction == 0 else -1)
            copies[(which, direction, k - 1)].wait_recv()
            if k == 1:
                held = got[direction, 0, near : near + cut, start : start + cols]
                got[direction, 0, near : near + cut, start : start + cols] = low(
                    term(which, offset, near, cut) + to_float(held)
                )
                got[direction, 0, far : far + cut, start : start + cols] = low(
                    term(which, offset, far, cut)
                )
            else:
                held = got[direction, k - 1, :, start : start + cols]
                got[direction, k - 1, :, start : start + cols] = low(
                    term(which, offset, 0, rows) + to_float(held)
                )
            source = got.at[direction, k - 1, :, pl.ds(start, cols)]
            send(which, direction, k, source, 0, rows)

    def end_feed_forward():
        for load in ff_loads:
            load.wait()
        wide, wide_up, wide_down, narrow, narrow_up, narrow_down = ff_held
        my_rows = pl.ds(pl.multiple_of(hops.core * rows, 16), rows)
        their_rows = pl.ds(pl.multiple_of((1 - hops.core) * rows, 16), rows)
        my_cols = pl.ds(pl.multiple_of(hops.core * ff_cols, 128), ff_cols)
        groups = [
            (wide, wide_up, wide_down, 0),
            (wide, wide_up, wide_down, ff_cols),
            (narrow, narrow_up, narrow_down, 0),
        ]
        for i, (base, up, down, start) in enumerate(groups):
            cols = slice(start, start + ff_cols)

            def total(at):
                return to_float(base[at, cols]) + to_float(up[at, cols]) + to_float(down[at, cols])

            ff_sent[i] = total(their_rows)
            copy = remote(
                ff_sent.at[i], ff_outs[i].at[:, my_cols], ff_send, ff_recv, (i,), hops.partner
            )
            copy.start()
            ff_copies.append(copy)
            ff_outs[i][:, my_cols] = total(my_rows)

    ff_copies = []
    ready(0)
    step(0, 0)
    step(1, 0)
    ready(1)
    ready(2)
    sides[half].wait_recv()
    step(2, 0)
    for k in range(1, half):
        step(0, k)
        step(1, k)
        if k == 1:
            end_feed_forward()
        for i in range(2 * k + 1, min(2 * k + 3, len(order))):
            ready(i)
        sides[half - k].wait_recv()
        sides[k - half].wait_recv()
        step(2, k)
    sides[0].wait_recv()
    for which, (start, cols) in enumerate(pieces):
        for direction in range(2):
            copies[(which, direction, half - 1)].wait_recv()
        total = (
            term(which, 0, 0, rows)
            + to_float(got[0, half - 1, :, start : start + cols])
            + to_float(got[1, half - 1, :, start : start + cols])
        )
        if which < 2:
            main[:, start : start + cols] = total
        else:
            little[...] = total
    for copy in ff_copies:
        copy.wait_recv()
    for copy in ff_copies + started:
        copy.wait_send()


def last_reduce(mine, theirs, large, ff_terms):
    chips = lax.axis_size("dp") // 2
    half = chips // 2
    tall, cols = mine.shape
    rows = tall // chips
    part = (cols - large) // 2
    ff = ff_terms[3].shape[1]
    vmem = pl.BlockSpec(memory_space=pltpu.VMEM)
    dma = pltpu.SemaphoreType.DMA
    return pl.pallas_call(
        functools.partial(last_kernel, large),
        out_shape=[
            jax.ShapeDtypeStruct((rows, large), F32),
            jax.ShapeDtypeStruct((rows, part), F32),
        ]
        + [jax.ShapeDtypeStruct((rows, 2 * ff), F32)] * 3,
        in_specs=[ANY] * 8,
        out_specs=[vmem] * 5,
        scratch_shapes=[
            pltpu.VMEM((tall, cols), F32),
            pltpu.VMEM((tall, cols), BF16),
            pltpu.VMEM((tall, part), BF16),
            pltpu.VMEM((tall, part), BF16),
            pltpu.VMEM((2, rows // 2, large + part), BF16),
            pltpu.VMEM((2, half, rows, large + part), BF16),
        ]
        + [pltpu.VMEM(v.shape, v.dtype) for v in ff_terms]
        + [
            pltpu.VMEM((3, rows, ff), F32),
            dma((2 * half + 6,)),
            dma((2 * half,)),
            dma((2 * half,)),
            dma((2 * half,)),
            dma((2 * half,)),
            dma((2, half, 3)),
            dma((2, half, 3)),
            dma((3,)),
            dma((3,)),
        ],
        compiler_params=pltpu.CompilerParams(
            collective_id=2, has_side_effects=True, vmem_limit_bytes=56 * 2**20
        ),
        cost_estimate=pl.CostEstimate(
            flops=0, bytes_accessed=20 * mine.size * 4, transcendentals=0
        ),
        name="last_reduce",
    )(mine, theirs, *ff_terms)


def forward_kernel(hops_done, tile, x_own, *refs):
    count = 2 * hops_done + 1
    gu_parts, (dn_own,), refs = refs[:count], refs[count : count + 1], refs[count + 1 :]
    (x_out, gu_full, gu_land, dn_full, raw, hidden, result), refs = refs[:7], refs[7:]
    x, dn, hidden_v, pairs, core_sent, core_got, side_sent, side_got, refs = *refs[:8], refs[8:]
    x_send, x_recv, gu_send, gu_recv, dn_send, dn_recv, core_sems, side_sems, loads, stores = refs
    hops = Hops()
    half, chips = hops.chips // 2, hops.chips
    own = x_own.shape[0]
    size, ff = dn_own.shape
    cut = size // 2
    greet([hops.above, hops.below, hops.partner, hops.across])
    started, saved = [], []

    def begin(copy, where=started):
        copy.start()
        where.append(copy)
        return copy

    def spot(ref, offset, top=0, tall=size):
        return block_rows(ref, hops.chip_at(offset) * size + top, tall)

    def span(k):
        return (0, size) if k < half else (None, cut)

    def gu_hop(k):
        copies = []
        for direction, ahead in ((0, hops.above), (1, hops.below)):
            offset = (1 - k) * (1 if direction == 0 else -1)
            top, tall = (0, size) if k < half else (direction * cut, cut)
            target = spot(gu_land, offset, top, tall)
            if k == hops_done + 1:
                held = gu_parts[2 * k - 3 + direction] if k > 1 else gu_parts[0]
                source = block_rows(held, top, tall)
            else:
                source = target
            index = (direction, k - hops_done - 1)
            copies.append(begin(remote(source, target, gu_send, gu_recv, index, ahead)))
        return copies

    def dn_hop(k):
        copies = []
        for direction, ahead in ((0, hops.above), (1, hops.below)):
            offset = (1 - k) * (1 if direction == 0 else -1)
            top, tall = (0, size) if k < half else (direction * cut, cut)
            block = spot(dn, offset, top, tall)
            copies.append(begin(remote(block, block, dn_send, dn_recv, (direction, k - 1), ahead)))
        return copies

    def arrive(copies):
        for copy in copies:
            copy.wait_recv()

    moving = gu_hop(hops_done + 1)
    mine, far = pl.ds(0, own), pl.ds(own, own)
    near, opposite = pl.ds(2 * own, own), pl.ds(3 * own, own)
    load_x = begin(pltpu.make_async_copy(x_own, x.at[mine], loads.at[0]), saved)
    load_dn = begin(pltpu.make_async_copy(dn_own, spot(dn, 0), loads.at[1]), saved)
    from_far = begin(remote(x_own, x.at[far], x_send, x_recv, (0,), hops.across))
    from_near = begin(remote(x_own, x.at[near], x_send, x_recv, (1,), hops.partner))
    from_far.wait_recv()
    passed = begin(remote(x.at[far], x.at[opposite], x_send, x_recv, (2,), hops.partner))
    from_near.wait_recv()
    passed.wait_recv()
    load_x.wait()
    begin(pltpu.make_async_copy(x, x_out, stores.at[0]), saved)
    load_dn.wait()
    arrive(moving)
    for k in range(hops_done + 2, half + 1):
        moving = gu_hop(k)
        arrive(moving)
    moving = dn_hop(1)

    offsets = list(range(hops_done + 1, half)) + list(range(-half + 1, -hops_done)) + [half]
    order = [0]
    for k in range(1, hops_done + 1):
        order += [-k, k]
    tiles = ff // tile

    def body(*tiles_of):
        ins, (raw_tile, hidden_tile, weights) = tiles_of[:-3], tiles_of[-3:]
        step = pl.program_id(0)
        every = order + offsets
        for group in range(2):
            for number, offset in enumerate(every):
                at = pl.ds(pl.multiple_of(hops.chip_at(offset) * size, size), size)
                weights[group, at, :] = ins[group * len(every) + number][...]
        gate = product(x[...], weights[0])
        up = product(x[...], weights[1])
        raw_tile[0] = low(gate)
        raw_tile[1] = low(up)
        bend = jnp.tanh(GELU_SCALE * (gate + GELU_CUBE * gate * gate * gate))
        value = low(0.5 * gate * (1.0 + bend) * up)
        hidden_tile[...] = value
        hidden_v[:, pl.ds(pl.multiple_of(step * tile, tile), tile)] = value

    def part_spec(row, group):
        return pl.BlockSpec((size, tile), lambda n: (row, n + group * tiles))

    in_specs, operands = [], []
    for group in range(2):
        for ref in gu_parts:
            in_specs.append(part_spec(0, group))
            operands.append(ref)
        for offset in offsets:
            in_specs.append(part_spec(hops.chip_at(offset), group))
            operands.append(gu_land)
    m, width = x.shape
    pltpu.emit_pipeline(
        body,
        grid=(tiles,),
        in_specs=in_specs,
        out_specs=[
            pl.BlockSpec((2, m, tile), lambda n: (0, 0, n)),
            pl.BlockSpec((m, tile), lambda n: (0, n)),
            pl.BlockSpec((2, width, tile), lambda n: (0, 0, n)),
        ],
    )(*operands, raw, hidden, gu_full)

    order, core_copies, side_copies = [], [], []

    def block_out(offset):
        i = len(order)
        order.append(offset)
        at = pl.ds(pl.multiple_of(hops.chip_at(offset) * size, size), size)
        out = product_t(hidden_v[...], dn[at, :])
        pairs[i] = out[: 2 * own]
        core_sent[i] = low(out[2 * own :])
        copy = remote(
            core_sent.at[i], core_got.at[i], core_sems.at[0], core_sems.at[1], (i,), hops.partner
        )
        core_copies.append(begin(copy))

    def core_sum():
        i = len(side_copies)
        core_copies[i].wait_recv()
        both = pairs[i] + to_float(core_got[i])
        side_sent[i] = low(both[own:])
        copy = remote(
            side_sent.at[i], side_got.at[i], side_sems.at[0], side_sems.at[1], (i,), hops.across
        )
        side_copies.append(begin(copy))
        at = pl.ds(pl.multiple_of(hops.chip_at(order[i]) * size, size), size)
        result[:, at] = both[:own]

    for k in range(1, half + 1):
        arrive(moving)
        if k < half:
            moving = dn_hop(k + 1)
        if k == 1:
            block_out(0)
        if k < half:
            block_out(-k)
            core_sum()
            block_out(k)
            core_sum()
        else:
            block_out(half)
            core_sum()
    begin(pltpu.make_async_copy(dn, dn_full, stores.at[1]), saved)
    core_sum()
    for i, copy in enumerate(side_copies):
        copy.wait_recv()
        at = pl.ds(pl.multiple_of(hops.chip_at(order[i]) * size, size), size)
        result[:, at] = result[:, at] + to_float(side_got[i])
    for copy in started:
        copy.wait_send()
    for copy in saved[2:]:
        copy.wait()


def forward(x_own, gu_parts, dn_own, hops_done, tile=512):
    chips = lax.axis_size("dp") // 2
    half = chips // 2
    own, width = x_own.shape
    size, ff = dn_own.shape
    tile = min(tile, ff)
    m = 4 * own
    dma = pltpu.SemaphoreType.DMA
    vmem = pl.BlockSpec(memory_space=pltpu.VMEM)
    return pl.pallas_call(
        functools.partial(forward_kernel, hops_done, tile),
        out_shape=[
            jax.ShapeDtypeStruct((m, width), BF16),
            jax.ShapeDtypeStruct((2, width, ff), BF16),
            jax.ShapeDtypeStruct((width, 2 * ff), BF16),
            jax.ShapeDtypeStruct((width, ff), BF16),
            jax.ShapeDtypeStruct((2, m, ff), BF16),
            jax.ShapeDtypeStruct((m, ff), BF16),
            jax.ShapeDtypeStruct((own, width), F32),
        ],
        in_specs=[ANY] * (len(gu_parts) + 2),
        out_specs=[ANY] * 6 + [vmem],
        scratch_shapes=[
            pltpu.VMEM((m, width), BF16),
            pltpu.VMEM((width, ff), BF16),
            pltpu.VMEM((m, ff), BF16),
            pltpu.VMEM((chips, 2 * own, size), F32),
            pltpu.VMEM((chips, 2 * own, size), BF16),
            pltpu.VMEM((chips, 2 * own, size), BF16),
            pltpu.VMEM((chips, own, size), BF16),
            pltpu.VMEM((chips, own, size), BF16),
            dma((3,)),
            dma((3,)),
            dma((2, half - hops_done)),
            dma((2, half - hops_done)),
            dma((2, half)),
            dma((2, half)),
            dma((2, chips)),
            dma((2, chips)),
            dma((2,)),
            dma((2,)),
        ],
        compiler_params=pltpu.CompilerParams(
            collective_id=3, has_side_effects=True, vmem_limit_bytes=60 * 2**20
        ),
        cost_estimate=pl.CostEstimate(
            flops=6 * m * width * ff, bytes_accessed=0, transcendentals=0
        ),
        name="forward",
    )(x_own, *gu_parts, dn_own)


class Gather:
    def __init__(self, ring, block):
        self.ring = ring
        self.rows = block.shape[0]
        self.held = [block, block]
        self.parts = [(0, 0, block)]
        self.step_count = 0

    def step(self):
        ring, half = self.ring, self.ring.chips // 2
        self.step_count += 1
        k = self.step_count
        going_up, going_down = self.held
        if k < half:
            self.held = [ring.up(going_up), ring.down(going_down)]
            self.parts += [(-k, 0, self.held[0]), (k, 0, self.held[1])]
        else:
            cut = self.rows // 2
            self.held = [ring.up(going_up[:cut]), ring.down(going_down[cut:])]
            self.parts += [(half, 0, self.held[0]), (half, cut, self.held[1])]

    def pieces(self):
        spots = [self.ring.chip_at(o) * self.rows + row for o, row, _ in self.parts]
        return jnp.stack(spots).astype(jnp.int32), [part for _, _, part in self.parts]


class BlockReduce:
    def __init__(self, ring, x, d, size):
        self.ring, self.x, self.d, self.size = ring, x, d, size
        self.step_count = 0
        self.held = []

    def terms(self, ahead=0):
        half = self.ring.chips // 2
        k = self.step_count + 1 + ahead
        if k == 1:
            offsets = (half,)
        elif k > half:
            offsets = (0,)
        else:
            offsets = (half + 1 - k, k - 1 - half)
        return block_grads(self.x, self.d, [self.ring.chip_at(o) for o in offsets], self.size)

    def step(self, terms):
        ring, half = self.ring, self.ring.chips // 2
        self.step_count += 1
        k = self.step_count
        cut = self.size // 2
        if k == 1:
            up, down = terms[0][:cut], terms[0][cut:]
        else:
            up, down = terms
            if k == 2:
                up = up.at[:cut].set(low(to_float(up[:cut]) + to_float(self.held[0])))
                down = down.at[cut:].set(low(to_float(down[cut:]) + to_float(self.held[1])))
            else:
                up = low(to_float(up) + to_float(self.held[0]))
                down = low(to_float(down) + to_float(self.held[1]))
        self.held = [ring.up(up), ring.down(down)]


def region(body):
    shapes = jax.eval_shape(body)
    yes = lax.optimization_barrier(jnp.array(True))
    return lax.cond(
        yes,
        body,
        lambda: jax.tree.map(lambda v: jnp.zeros(v.shape, v.dtype), shapes),
    )


def meet(rings, *values):
    held, values = tie([r.held for r in rings], values)
    for r, h in zip(rings, held):
        r.held = h
    return values if len(values) != 1 else values[0]


def local(
    tokens,
    layer_input,
    block_ids,
    block_table,
    w_query,
    w_key,
    w_value,
    w_output,
    w_left,
    w_right,
    w_gate,
    w_up,
    w_down,
    w_layer_gate,
    w_layer_proj,
    query_gain,
    key_gain,
    gain_input,
    gain_attn_out,
    gain_laurel,
    gain_ffw_in,
    gain_ffw_out,
    gain_layer_out,
    out_grad,
):
    ring = Ring()
    side = lax.axis_index("tensor")
    core = ring.core
    rows = w_query.shape[0]
    own = tokens.shape[0]
    width = tokens.shape[1]
    q_cols = w_query.shape[1]
    kv_cols = w_key.shape[1]
    rank = w_left.shape[1]
    small = w_layer_gate.shape[1]
    ff_cols = w_gate.shape[1] // 2
    chips = ring.chips

    def gain_block(query_part, key_part, parts):
        count = query_part.shape[0]
        columns = parts + [
            jnp.pad(query_part, (0, rows - count)),
            jnp.pad(key_part, (0, rows - count)),
        ]
        block = jnp.stack(columns, axis=1)
        return jnp.pad(block, ((0, 0), (0, 128 - block.shape[1])))

    gains = gain_block(
        query_gain,
        key_gain,
        [gain_input, gain_attn_out, gain_laurel, gain_ffw_in, gain_ffw_out, gain_layer_out],
    )
    half = chips // 2
    (qkv_full, output_t, small_full), (*ff_own, other_tokens) = first_gather(
        [
            jnp.concatenate([w_query, w_key, w_value], axis=1),
            w_output.T,
            jnp.concatenate([w_left, w_right.T, w_layer_gate, w_layer_proj.T, gains], axis=1),
        ],
        w_gate,
        w_up,
        w_down.T,
        tokens,
    )
    left_full = small_full[:, :rank]
    right_t = small_full[:, rank : 2 * rank]
    lgate_full = small_full[:, 2 * rank : 2 * rank + small]
    lproj_t = small_full[:, 2 * rank + small : 2 * rank + 2 * small]
    gains_full = small_full[:, 2 * rank + 2 * small :]

    gain_columns = to_float(gains_full[:, :8])
    (
        input_scale,
        attn_scale,
        laurel_scale,
        ffw_in_scale,
        ffw_out_scale,
        layer_scale,
    ) = (gain_columns[:, i] for i in range(6))
    head_part = query_gain.shape[0]

    def head_gain(column):
        return column.reshape(ring.devices, rows)[:, :head_part].reshape(HD)

    query_scale = head_gain(gain_columns[:, 6])
    key_scale = head_gain(gain_columns[:, 7])

    piece_len = 2 * own
    seq_total = block_ids.shape[1]
    per_seq = seq_total // piece_len
    dp_index = lax.axis_index("dp")
    row_index = dp_index // per_seq
    slot = lax.rem(dp_index, per_seq)
    first = slot * piece_len
    has_before = slot > 0
    has_after = slot < per_seq - 1
    natural = jnp.arange(piece_len, dtype=jnp.int32)
    here = first + lax.rem(natural + side * own, piece_len)
    cosines, sines = rope_tables(here, HD)
    reach_after = min(256, piece_len)
    forward_pairs = [(i, i + 1) for i in range(ring.devices - 1)]
    backward_pairs = [(i + 1, i) for i in range(ring.devices - 1)]

    def in_order(values):
        return jnp.where(
            side == 0, values, jnp.concatenate([values[own:], values[:own]], axis=0)
        )

    ids_row = lax.dynamic_index_in_dim(block_ids, row_index, 0, keepdims=False)
    table_row = lax.dynamic_index_in_dim(block_table, row_index, 0, keepdims=False)
    own_ids = lax.dynamic_slice_in_dim(ids_row, first, piece_len, 0)
    before_ids = lax.dynamic_slice_in_dim(ids_row, jnp.maximum(first - piece_len, 0), piece_len, 0)
    before_ids = jnp.where(has_before, before_ids, -2)
    after_ids = lax.dynamic_slice_in_dim(
        ids_row, jnp.minimum(first + piece_len, seq_total - reach_after), reach_after, 0
    )
    after_ids = jnp.where(has_after, after_ids, -2)
    key_ids = jnp.concatenate([before_ids, own_ids, after_ids], axis=0)
    query_ids = in_order(own_ids)
    block_count = block_table.shape[-1]
    number_rows = jnp.arange(block_count, dtype=jnp.int32)
    sees_last = jnp.sum(
        jnp.where(number_rows[None, :] == number_rows[:, None] - 1, table_row, 0), axis=1
    )
    query_sees = jnp.sum(
        jnp.where(query_ids[:, None] == number_rows[None, :], sees_last[None, :], 0), axis=1
    )
    previous_ids = jnp.where(query_sees == 1, query_ids - 1, query_ids)

    def prepare(qkv_in, query_gains, key_gains):
        query_in = qkv_in[:, :q_cols]
        key_in = qkv_in[:, q_cols : q_cols + kv_cols]
        value_in = qkv_in[:, q_cols + kv_cols :]
        query_out = rotate(
            norm_gain(query_in.reshape(piece_len, -1, HD), query_gains), cosines, sines
        )
        key_out = rotate(norm_gain(key_in.reshape(piece_len, -1, HD), key_gains), cosines, sines)
        return (query_out, key_out, norm_plain(value_in.reshape(piece_len, -1, HD)))

    heads_local = q_cols // HD
    kv_local = kv_cols // HD
    group = heads_local // kv_local

    def scores_for(query_low, keys_all):
        allowed = (query_ids[:, None] == key_ids[None, :]) | (
            previous_ids[:, None] == key_ids[None, :]
        )
        scores = jnp.einsum("qkgd,ckd->kgqc", query_low, keys_all, preferred_element_type=F32)
        return jnp.where(allowed[None, None], scores, NEGATIVE)

    def sum_sides(partial, beside=None):
        got = across(low(partial[own:]))
        if beside is None:
            return partial[:own] + to_float(got)
        got, beside = tie(got, beside())
        return partial[:own] + to_float(got), beside

    def both_sides(values, beside=None):
        got = across(values)
        if beside is None:
            return jnp.concatenate([values, got], axis=0)
        got, beside = tie(got, beside())
        return jnp.concatenate([values, got], axis=0), beside

    def four_ways(values):
        pair = both_sides(values)
        return jnp.concatenate([pair, ring.swap(pair)], axis=0)

    def sum_four(partial, beside=None):
        pair = partial[: 2 * own] + to_float(ring.swap(low(partial[2 * own :])))
        return sum_sides(pair, beside)

    def attend():
        normed_low = low(norm_gain(to_float(tokens), input_scale))
        seq_rows = jnp.concatenate(
            [normed_low, low(norm_gain(to_float(other_tokens), input_scale))], axis=0
        )
        qkv_raw = product(seq_rows, qkv_full)
        query_rot, key_rot, value_nrm = prepare(qkv_raw, query_scale, key_scale)
        query_low = low(query_rot).reshape(piece_len, kv_local, group, HD)
        kv_own = in_order(jnp.concatenate([low(key_rot), low(value_nrm)], axis=1))
        kv_before = lax.ppermute(kv_own, "dp", forward_pairs)
        kv_after = lax.ppermute(kv_own[:reach_after], "dp", backward_pairs)
        kv_all = jnp.concatenate([kv_before, kv_own, kv_after], axis=0)
        scores = scores_for(query_low, kv_all[:, :kv_local])
        highest = jnp.max(scores, axis=-1, keepdims=True)
        weights_exp = jnp.exp(scores - highest)
        totals = jnp.sum(weights_exp, axis=-1, keepdims=True)
        probs_low = low(weights_exp / totals)
        attended = jnp.einsum(
            "kgqc,ckd->qkgd", probs_low, kv_all[:, kv_local:], preferred_element_type=F32
        )
        log_totals = highest + jnp.log(totals)
        heads_low = low(attended.reshape(piece_len, heads_local * HD))
        return seq_rows, qkv_raw, query_low, kv_all, log_totals, heads_low

    gu = Gather(ring, ff_own[0])
    dn = Gather(ring, ff_own[1])
    gu.step()
    seq_rows, qkv_raw, query_low, kv_all, log_totals, heads_low = region(attend)
    heads_low = meet([gu], heads_low)
    gu.step()

    def join(heads_low):
        attn_out = sum_sides(product_t(heads_low, output_t))
        normed = norm_gain(to_float(tokens), input_scale)
        left_low = low(product(low(normed), left_full))
        right_out = product_t(left_low, right_t)
        laurel_normed = norm_gain(right_out, laurel_scale)
        attn_normed = norm_gain(attn_out, attn_scale)
        mixed = (to_float(tokens) + attn_normed + (normed + laurel_normed)) * ROOT_HALF
        return attn_out, left_low, right_out, mixed, low(norm_gain(mixed, ffw_in_scale))

    attn_out, left_low, right_out, mixed, ffw_low = region(lambda: join(heads_low))
    ffw_low = meet([gu], ffw_low)
    if (2 * rows) % 256 == 0:
        parts = [part for _, _, part in gu.parts]
        ffw_rows, gu_weights, _, dn_whole, raw, hidden_low, ffw_out = forward(
            ffw_low, parts, ff_own[1], 2
        )
        dn_spots, dn_parts = jnp.zeros((1,), jnp.int32), [dn_whole]
    else:
        gu.step()
        ffw_rows = region(lambda: four_ways(ffw_low))
        ffw_rows = meet([gu], ffw_rows)
        for _ in range(half - 4):
            gu.step()
            ffw_rows = meet([gu], ffw_rows)
        gu.step()
        ffw_rows = meet([gu], ffw_rows)

        gu_spots, gu_parts = gu.pieces()
        dn.step()
        raw, hidden_low, gu_weights = region(lambda: gate_up(ffw_rows, gu_spots, gu_parts))
        raw, hidden_low = meet([dn], raw, hidden_low)
        for _ in range(half - 1):
            dn.step()
            raw, hidden_low = meet([dn], raw, hidden_low)
        dn_spots, dn_parts = dn.pieces()
        ffw_out = sum_four(columns_out(hidden_low[None], dn_spots, dn_parts, width))
    ffw_out_normed, ffw_out_back = jax.vjp(norm_gain, ffw_out, ffw_out_scale)
    block_mid = mixed + ffw_out_normed
    mid_low = low(block_mid)
    layer_pre = product(mid_low, lgate_full)

    def layer_gate_fn(pre_values, per_layer):
        return gelu_tanh(pre_values) * per_layer

    gated, gated_back = jax.vjp(layer_gate_fn, layer_pre, to_float(layer_input))
    gated_low = low(gated)
    layer_proj = product_t(gated_low, lproj_t)
    proj_normed, proj_back = jax.vjp(norm_gain, layer_proj, layer_scale)
    result = block_mid + proj_normed

    grad_out = to_float(out_grad)
    d_proj, d_layer_scale = proj_back(grad_out)
    d_proj_low = low(d_proj)
    d_gated = product(d_proj_low, lproj_t)
    d_pre, grad_layer_input = gated_back(d_gated)
    d_pre_low = low(d_pre)
    d_mid = grad_out + product_t(d_pre_low, lgate_full)
    d_ffw_out, d_ffw_out_scale = ffw_out_back(d_mid)
    d_ffw_rows = four_ways(low(d_ffw_out))
    d_ffw_rows, d_mid = tie(d_ffw_rows, d_mid)

    rd = BlockReduce(ring, d_ffw_rows, hidden_low[None], 2 * rows)
    rd.step(rd.terms())
    d_gate_up, down_terms = region(
        lambda: (hidden_back(d_ffw_rows, raw, dn_spots, dn_parts), rd.terms())
    )
    d_gate_up, down_terms = meet([rd], d_gate_up, down_terms)
    rd.step(down_terms)
    rg = BlockReduce(ring, ffw_rows, d_gate_up, 2 * rows)
    for _ in range(half - 4):
        rd.step(meet([rd], region(rd.terms)))

    def back_2():
        partial = product_t(d_gate_up[0], gu_weights[0]) + product_t(d_gate_up[1], gu_weights[1])
        return partial, rd.terms(), rg.terms()

    partial, down_terms, terms = meet([rd], *region(back_2))
    rd.step(down_terms)
    rg.step(terms)

    def back_3():
        d_ffw_normed, terms = sum_four(partial, lambda: (rd.terms(), rg.terms()))
        _, back = jax.vjp(norm_gain, mixed, ffw_in_scale)
        d_mixed_extra, d_ffw_in_scale = back(d_ffw_normed)
        d_branch = (d_mid + d_mixed_extra) * ROOT_HALF
        _, back = jax.vjp(norm_gain, attn_out, attn_scale)
        d_attn, d_attn_scale = back(d_branch)
        return terms, d_ffw_in_scale, d_attn_scale, d_branch, low(d_attn)

    terms, d_ffw_in_scale, d_attn_scale, d_branch, d_attn_low = meet([rd, rg], *region(back_3))
    rd.step(terms[0])
    rg.step(terms[1])

    def back_4():
        d_attn_rows, terms = both_sides(d_attn_low, rg.terms)
        d_heads = low(product(d_attn_rows, output_t)).reshape(piece_len, kv_local, group, HD)
        keys_all, values_all = kv_all[:, :kv_local], kv_all[:, kv_local:]
        probs = jnp.exp(scores_for(query_low, keys_all) - log_totals)
        probs_low = low(probs)
        d_values_all = jnp.einsum(
            "kgqc,qkgd->ckd", probs_low, d_heads, preferred_element_type=F32
        )
        d_probs = jnp.einsum("qkgd,ckd->kgqc", d_heads, values_all, preferred_element_type=F32)
        deltas = jnp.sum(probs * d_probs, axis=-1, keepdims=True)
        d_scores = low(probs * (d_probs - deltas))
        d_keys_all = jnp.einsum("kgqc,qkgd->ckd", d_scores, query_low, preferred_element_type=F32)
        d_query_rot = jnp.einsum("kgqc,ckd->qkgd", d_scores, keys_all, preferred_element_type=F32)
        d_kv_all = jnp.concatenate([d_keys_all, d_values_all], axis=1)
        return terms, d_attn_rows, d_kv_all, d_query_rot

    terms, d_attn_rows, d_kv_all, d_query_rot = meet([rd, rg], *region(back_4))
    rg.step(terms)
    for _ in range(half - 4):
        rg.step(meet([rg], region(rg.terms)))

    def back_5():
        to_before = low(d_kv_all[:piece_len])
        to_after = low(d_kv_all[2 * piece_len :])
        from_after = to_float(lax.ppermute(to_before, "dp", backward_pairs))
        from_before = to_float(lax.ppermute(to_after, "dp", forward_pairs))
        from_after, from_before, terms = tie(from_after, from_before, rg.terms())
        d_kv = d_kv_all[piece_len : 2 * piece_len] + from_after
        d_kv = d_kv + jnp.pad(from_before, ((0, piece_len - reach_after), (0, 0), (0, 0)))
        d_kv = in_order(d_kv)
        _, back = jax.vjp(prepare, qkv_raw, query_scale, key_scale)
        d_qkv, query_scale_grad, key_scale_grad = back(
            (
                d_query_rot.reshape(piece_len, heads_local, HD),
                d_kv[:, :kv_local],
                d_kv[:, kv_local:],
            )
        )
        return terms, low(d_qkv), query_scale_grad, key_scale_grad

    terms, d_qkv_low, query_scale_grad, key_scale_grad = meet([rg], *region(back_5))
    rg.step(terms)

    def head_gain_back(grads):
        padded = jnp.pad(grads.reshape(ring.devices, head_part), ((0, 0), (0, rows - head_part)))
        return padded.reshape(width)

    def back_6():
        normed, input_norm_back = jax.vjp(norm_gain, to_float(tokens), input_scale)
        _, laurel_back = jax.vjp(norm_gain, right_out, laurel_scale)
        d_right, d_laurel_scale = laurel_back(d_branch)
        d_right_low = low(d_right)
        d_left_low = low(product(d_right_low, right_t))
        d_normed = d_branch + product_t(d_left_low, left_full)
        d_more, ends = sum_sides(
            product_t(d_qkv_low, qkv_full), lambda: (rd.terms(), rg.terms())
        )
        d_normed = d_normed + d_more
        d_inputs_extra, d_input_scale = input_norm_back(d_normed)
        grad_tokens = d_branch + d_inputs_extra
        gain_grads = jnp.stack(
            [
                d_input_scale,
                d_attn_scale,
                d_laurel_scale,
                d_ffw_in_scale,
                d_ffw_out_scale,
                d_layer_scale,
                head_gain_back(query_scale_grad),
                head_gain_back(key_scale_grad),
            ],
            axis=0,
        )
        gain_grads = jnp.pad(gain_grads, ((0, 120), (0, 0))).T
        pairs = [
            (d_attn_rows, heads_low),
            (seq_rows, d_qkv_low),
            (mid_low, d_pre_low),
            (d_proj_low, gated_low),
            (low(normed), d_left_low),
            (d_right_low, left_low),
        ]
        return grad_tokens, ends, row_grads(pairs, gain_grads, core, chips, rows)

    grad_tokens, (down_end, gate_up_end), (mine, theirs) = meet([rg], *region(back_6))
    total, small_half, out_gate, out_up, out_down_t = last_reduce(
        mine,
        theirs,
        2 * q_cols + 2 * kv_cols,
        [gate_up_end[0], *rg.held, down_end[0], *rd.held],
    )
    out_output = total[:, :q_cols].T
    out_qkv = total[:, q_cols:]
    small_other = across(small_half)
    out_small = jnp.where(
        side == 0,
        jnp.concatenate([small_half, small_other], axis=1),
        jnp.concatenate([small_other, small_half], axis=1),
    )
    out_gains = out_small[:, 2 * rank + 2 * small :]
    return (
        low(result),
        grad_tokens,
        grad_layer_input,
        out_qkv[:, :q_cols],
        out_qkv[:, q_cols : q_cols + kv_cols],
        out_qkv[:, q_cols + kv_cols :],
        out_output,
        out_small[:, 2 * small : 2 * small + rank],
        out_small[:, 2 * small + rank : 2 * small + 2 * rank].T,
        out_gate,
        out_up,
        out_down_t.T,
        out_small[:, :small],
        out_small[:, small : 2 * small].T,
        out_gains[:head_part, 6],
        out_gains[:head_part, 7],
        out_gains[:, 0],
        out_gains[:, 1],
        out_gains[:, 2],
        out_gains[:, 3],
        out_gains[:, 4],
        out_gains[:, 5],
    )


def solution(mesh):
    both = P(("dp", "tensor"), None)
    rows_split = P("dp", "tensor")
    cols_split = P("tensor", "dp")
    by_row = P("dp", None)
    by_col = P(None, "dp")
    flat = P("dp")
    return jax.shard_map(
        local,
        mesh=mesh,
        in_specs=(
            (both, both, P(), P(), rows_split, rows_split, rows_split, cols_split)
            + (by_row, by_col, rows_split, rows_split, cols_split, by_row, by_col)
            + (flat,) * 8
            + (both,)
        ),
        out_specs=(
            (both, both, both, rows_split, rows_split, rows_split, cols_split)
            + (by_row, by_col, rows_split, rows_split, cols_split, by_row, by_col)
            + (flat,) * 8
        ),
        check_vma=False,
    )
```

```python
import functools

import jax
import jax.numpy as jnp
from jax import lax
from jax.experimental import pallas as pl
from jax.experimental.pallas import tpu as pltpu
from jax.sharding import PartitionSpec as P

HD = 256
EPS = 1e-06
ROOT_HALF = 0.7071067811865476
NEGATIVE = -1e30
F32 = jnp.float32
BF16 = jnp.bfloat16


def norm_gain(values, gains):
    return values * lax.rsqrt(jnp.mean(values * values, axis=-1, keepdims=True) + EPS) * gains


def norm_plain(values):
    return values * lax.rsqrt(jnp.mean(values * values, axis=-1, keepdims=True) + EPS)


def gelu_tanh(values):
    return jax.nn.gelu(values, approximate=True)


def rope_tables(positions, head_width):
    positions = positions.astype(F32)[:, None]
    frequency = 10000.0 ** (-2.0 * jnp.arange(head_width // 2, dtype=F32) / head_width)
    angles = positions * frequency[None, :]
    return (jnp.cos(angles), jnp.sin(angles))


def rotate(values, cosines, sines):
    half_width = values.shape[-1] // 2
    front_half = values[..., :half_width]
    back_half = values[..., half_width:]
    cos_wide = cosines[:, None, :]
    sin_wide = sines[:, None, :]
    return jnp.concatenate(
        [
            front_half * cos_wide - back_half * sin_wide,
            back_half * cos_wide + front_half * sin_wide,
        ],
        axis=-1,
    )


def to_float(values):
    return values.astype(F32)


def low(values):
    return values.astype(BF16)


def product(left_in, right_in):
    return jnp.dot(left_in, right_in, preferred_element_type=F32)


def product_t(left_in, right_in):
    return lax.dot_general(left_in, right_in, (((1,), (1,)), ((), ())), preferred_element_type=F32)


def product_l(left_in, right_in):
    return lax.dot_general(left_in, right_in, (((0,), (0,)), ((), ())), preferred_element_type=F32)


def tie(*values):
    return lax.optimization_barrier(values)


class Ring:
    def __init__(self):
        self.devices = lax.axis_size("dp")
        self.chips = self.devices // 2
        order = list(range(0, self.chips, 2)) + list(range(self.chips - 1, 0, -2))
        self.cw = [
            (2 * order[p] + c, 2 * order[(p + 1) % self.chips] + c)
            for p in range(self.chips)
            for c in range(2)
        ]
        self.ccw = [(b, a) for a, b in self.cw]
        self.core_pairs = [(d, d ^ 1) for d in range(self.devices)]
        me = lax.axis_index("dp")
        self.core = lax.rem(me, 2)
        self.chip = me // 2
        self.place = jnp.where(
            lax.rem(self.chip, 2) == 0, self.chip // 2, self.chips - 1 - self.chip // 2
        )

    def chip_at(self, offset):
        place = lax.rem(self.place + offset + self.chips, self.chips)
        return jnp.where(place < self.chips // 2, 2 * place, 2 * (self.chips - 1 - place) + 1)

    def up(self, values):
        return lax.ppermute(values, "dp", self.cw)

    def down(self, values):
        return lax.ppermute(values, "dp", self.ccw)

    def swap(self, values):
        return lax.ppermute(values, "dp", self.core_pairs)


def across(values):
    return lax.ppermute(values, "tensor", [(0, 1), (1, 0)])


def remote(source, target, sends, receives, index, device):
    return pltpu.make_async_remote_copy(
        src_ref=source,
        dst_ref=target,
        send_sem=sends.at[index],
        recv_sem=receives.at[index],
        device_id=device,
        device_id_type=pl.DeviceIdType.MESH,
    )


def greet(devices):
    barrier = pltpu.get_barrier_semaphore()
    for device in devices:
        pl.semaphore_signal(
            barrier, inc=1, device_id=device, device_id_type=pl.DeviceIdType.MESH
        )
    pl.semaphore_wait(barrier, len(devices))


def block_rows(ref, start, count):
    return ref.at[pl.ds(pl.multiple_of(start, 16), count)]


class Hops:
    def __init__(self):
        me = lax.axis_index("dp")
        self.chips = lax.axis_size("dp") // 2
        self.core = lax.rem(me, 2)
        self.chip = me // 2
        self.place = jnp.where(
            lax.rem(self.chip, 2) == 0, self.chip // 2, self.chips - 1 - self.chip // 2
        )
        self.partner = {"dp": self.chip * 2 + 1 - self.core}
        self.above = {"dp": self.chip_at(1) * 2 + self.core}
        self.below = {"dp": self.chip_at(-1) * 2 + self.core}
        self.across = {"tensor": 1 - lax.axis_index("tensor")}

    def chip_at(self, offset):
        place = lax.rem(self.place + offset + self.chips, self.chips)
        return jnp.where(place < self.chips // 2, 2 * place, 2 * (self.chips - 1 - place) + 1)


def first_kernel(count, ff_cols, *refs):
    blocks, refs = refs[:count], refs[count:]
    (gate, up, down, tokens), refs = refs[:4], refs[4:]
    wholes, refs = refs[:count], refs[count:]
    (gate_up_own, down_own, other_tokens), refs = refs[:3], refs[3:]
    stages, refs = refs[: 3 + count], refs[3 + count :]
    in_sems, out_sems, ring_send, ring_recv, pair_send, pair_recv, ff_send, ff_recv = refs
    hops = Hops()
    half = hops.chips // 2
    rows = blocks[0].shape[0]
    greet([hops.above, hops.below, hops.partner, hops.across])
    started = []

    def place(ref, offset, top, size):
        return block_rows(ref, (2 * hops.chip_at(offset) + hops.core) * rows + top, size)

    def to_partner(number, which, offset, top, size, source=None):
        spot = place(wholes[which], offset, top, size)
        copy = remote(
            spot if source is None else source,
            spot,
            pair_send,
            pair_recv,
            (number, which),
            hops.partner,
        )
        copy.start()
        started.append(copy)
        pairs.append(copy)

    def onward(direction, k, which, offset, top, size, source=None):
        spot = place(wholes[which], offset, top, size)
        copy = remote(
            spot if source is None else source,
            spot,
            ring_send,
            ring_recv,
            (direction, k, which),
            hops.above if direction == 0 else hops.below,
        )
        copy.start()
        started.append(copy)
        arrivals[(direction, k, which)] = copy

    pairs, arrivals, locals_ = [], {}, []
    for which in range(count):
        for direction in range(2):
            onward(direction, 0, which, 0, 0, rows, blocks[which])
    own_rows = pl.ds(pl.multiple_of(hops.core * rows, 16), rows)
    mine = pl.ds(pl.multiple_of(hops.core * ff_cols, 128), ff_cols)
    theirs = pl.ds(pl.multiple_of((1 - hops.core) * ff_cols, 128), ff_cols)
    targets = [
        gate_up_own.at[own_rows, pl.ds(0, ff_cols)],
        gate_up_own.at[own_rows, pl.ds(ff_cols, ff_cols)],
        down_own.at[own_rows],
    ]
    ff_copies = [remote(tokens, other_tokens, ff_send, ff_recv, (3,), hops.across)]
    ff_copies[0].start()
    for number, (weight, target) in enumerate(zip((gate, up, down), targets)):
        copy = remote(
            weight.at[:, theirs], target, ff_send, ff_recv, (number,), hops.partner
        )
        copy.start()
        ff_copies.append(copy)
        locals_.append((weight.at[:, mine], target, number))
    for which in range(count):
        to_partner(0, which, 0, 0, rows, blocks[which])
        locals_.append((blocks[which], place(wholes[which], 0, 0, rows), 3 + which))
    loads = [
        pltpu.make_async_copy(source, stages[number], in_sems.at[number])
        for source, _, number in locals_
    ]
    for copy in loads:
        copy.start()
    stores = [
        pltpu.make_async_copy(stages[number], target, out_sems.at[number])
        for _, target, number in locals_
    ]
    for load, store in zip(loads, stores):
        load.wait()
        store.start()
    cut = rows // 2
    for k in range(1, half + 1):
        for which in range(count):
            for direction in range(2):
                arrivals[(direction, k - 1, which)].wait_recv()
                offset = -k if direction == 0 else k
                if k < half - 1:
                    onward(direction, k, which, offset, 0, rows)
                elif k == half - 1:
                    onward(direction, k, which, offset, direction * cut, cut)
                if k < half:
                    to_partner(2 * k - 1 + direction, which, offset, 0, rows)
                else:
                    to_partner(2 * k - 1 + direction, which, half, direction * cut, cut)
    for copy in ff_copies + pairs:
        copy.wait_recv()
    for copy in ff_copies + started:
        copy.wait_send()
    for copy in stores:
        copy.wait()


ANY = pl.BlockSpec(memory_space=pl.ANY)


def comm_call(kernel, number, operands, shapes, stages, semaphores, name):
    moved = sum(v.size * 2 for v in shapes)
    return pl.pallas_call(
        kernel,
        out_shape=shapes,
        in_specs=[ANY] * len(operands),
        out_specs=[ANY] * len(shapes),
        scratch_shapes=stages + [pltpu.SemaphoreType.DMA(shape) for shape in semaphores],
        compiler_params=pltpu.CompilerParams(
            collective_id=number, has_side_effects=True, vmem_limit_bytes=16 * 2**20
        ),
        cost_estimate=pl.CostEstimate(flops=0, bytes_accessed=8 * moved, transcendentals=0),
        name=name,
    )(*operands)


def first_gather(blocks, gate, up, down, tokens):
    chips = lax.axis_size("dp") // 2
    half = chips // 2
    rows = blocks[0].shape[0]
    ff_cols = gate.shape[1] // 2
    count = len(blocks)
    shapes = [
        jax.ShapeDtypeStruct((2 * chips * rows, block.shape[1]), block.dtype) for block in blocks
    ] + [
        jax.ShapeDtypeStruct((2 * rows, 2 * ff_cols), gate.dtype),
        jax.ShapeDtypeStruct((2 * rows, ff_cols), gate.dtype),
        jax.ShapeDtypeStruct(tokens.shape, tokens.dtype),
    ]
    stages = [pltpu.VMEM((rows, ff_cols), gate.dtype)] * 3 + [
        pltpu.VMEM(block.shape, block.dtype) for block in blocks
    ]
    semaphores = [
        (3 + count,),
        (3 + count,),
        (2, half, count),
        (2, half, count),
        (2 * half + 1, count),
        (2 * half + 1, count),
        (4,),
        (4,),
    ]
    out = comm_call(
        functools.partial(first_kernel, count, ff_cols),
        0,
        (*blocks, gate, up, down, tokens),
        shapes,
        stages,
        semaphores,
        "first_gather",
    )
    return out[:count], out[count:]


GELU_SCALE = 0.7978845608028654
GELU_CUBE = 0.044715
ROW_TILE = 1024


def fill(spots, whole, parts):
    for number, part in enumerate(parts):
        size = part.shape[0]
        whole[pl.ds(pl.multiple_of(spots[number], size), size), :] = part[...]


def gate_up_kernel(count, spots, x, *refs):
    gate_parts, up_parts = refs[:count], refs[count : 2 * count]
    raw, hidden, weights = refs[2 * count :]
    gate_w, up_w = weights.at[0], weights.at[1]
    fill(spots, gate_w, gate_parts)
    fill(spots, up_w, up_parts)

    @pl.loop(0, x.shape[0] // min(ROW_TILE, x.shape[0]))
    def _(i):
        at = pl.ds(pl.multiple_of(i * ROW_TILE, ROW_TILE), ROW_TILE)
        rows = x[at, :]
        gate = product(rows, gate_w[...])
        up = product(rows, up_w[...])
        raw[0, at, :] = low(gate)
        raw[1, at, :] = low(up)
        bend = jnp.tanh(GELU_SCALE * (gate + GELU_CUBE * gate * gate * gate))
        hidden[at, :] = low(0.5 * gate * (1.0 + bend) * up)


def hidden_back_kernel(count, spots, x, raw, *refs):
    parts, (out, whole) = refs[:count], refs[count:]
    fill(spots, whole, parts)

    @pl.loop(0, x.shape[0] // min(ROW_TILE, x.shape[0]))
    def _(i):
        at = pl.ds(pl.multiple_of(i * ROW_TILE, ROW_TILE), ROW_TILE)
        d_hidden = product(x[at, :], whole[...])
        gate = to_float(raw[0, at, :])
        up = to_float(raw[1, at, :])
        square = gate * gate
        bend = jnp.tanh(GELU_SCALE * gate * (1.0 + GELU_CUBE * square))
        plus = 0.5 * (1.0 + bend)
        slope = plus + 0.5 * gate * (1.0 - bend * bend) * GELU_SCALE * (
            1.0 + 3.0 * GELU_CUBE * square
        )
        out[0, at, :] = low(d_hidden * up * slope)
        out[1, at, :] = low(d_hidden * gate * plus)


def columns_kernel(count, spots, h, *refs):
    parts, (out, whole) = refs[:count], refs[count:]
    fill(spots, whole, parts)
    step = pl.program_id(0)
    width = out.shape[1]
    cols = min(512, width)


    @pl.loop(0, width // cols)
    def _(j):
        across_ = pl.ds(pl.multiple_of(j * cols, cols), cols)
        term = product_t(h[0], whole[across_, :])

        @pl.when(step == 0)
        def _():
            out[:, across_] = term

        @pl.when(step > 0)
        def _():
            out[:, across_] = out[:, across_] + term


def block_kernel(count, came, spots, *refs):
    xs, d, refs = refs[:count], refs[count], refs[count + 1 :]
    gots, refs = refs[:came], refs[came:]
    outs, turned = refs[:count], refs[count:]

    @pl.when(pl.program_id(0) == 0)
    def _():
        for x, t in zip(xs, turned):
            t[...] = x[...].T

    for i, (t, out) in enumerate(zip(turned, outs)):
        term = product(t[...], d[0])
        if came == 0:
            out[...] = low(term)
        elif gots[i].shape == out.shape:
            out[...] = low(term + to_float(gots[i][...]))
        else:
            cut = gots[i].shape[0]
            near, far = slice(i * cut, (i + 1) * cut), slice((1 - i) * cut, (2 - i) * cut)
            out[near, :] = low(term[near] + to_float(gots[i][...]))
            out[far, :] = low(term[far])


def grid_call(kernel, spots, grid, operands, in_specs, shapes, out_specs, scratch, flops, name):
    moved = sum(v.size * v.dtype.itemsize for v in (*operands, *jax.tree.leaves(shapes)))
    if flops == 0:
        moved = 0
    return pl.pallas_call(
        kernel,
        grid_spec=pltpu.PrefetchScalarGridSpec(
            num_scalar_prefetch=1,
            grid=grid,
            in_specs=in_specs,
            out_specs=out_specs,
            scratch_shapes=scratch,
        ),
        out_shape=shapes,
        compiler_params=pltpu.CompilerParams(
            dimension_semantics=("arbitrary",) * len(grid), vmem_limit_bytes=56 * 2**20
        ),
        cost_estimate=pl.CostEstimate(flops=flops, bytes_accessed=moved, transcendentals=0),
        name=name,
    )(spots, *operands)


def once(shape):
    return pl.BlockSpec(
        shape, lambda *index: (0,) * len(shape), pipeline_mode=pl.Buffered(buffer_count=1)
    )


def gate_up(x, spots, parts, tile=512):
    count, (m, width), ff = len(parts), x.shape, parts[0].shape[1] // 2
    tiles = ff // tile
    part_specs = [pl.BlockSpec((p.shape[0], tile), lambda n, s: (0, n)) for p in parts] + [
        pl.BlockSpec((p.shape[0], tile), lambda n, s: (0, n + tiles)) for p in parts
    ]
    return grid_call(
        functools.partial(gate_up_kernel, count),
        spots,
        (tiles,),
        (x, *parts, *parts),
        [once((m, width))] + part_specs,
        [
            jax.ShapeDtypeStruct((2, m, ff), BF16),
            jax.ShapeDtypeStruct((m, ff), BF16),
            jax.ShapeDtypeStruct((2, width, ff), BF16),
        ],
        [
            pl.BlockSpec((2, m, tile), lambda n, s: (0, 0, n)),
            pl.BlockSpec((m, tile), lambda n, s: (0, n)),
            pl.BlockSpec((2, width, tile), lambda n, s: (0, 0, n)),
        ],
        [],
        4 * m * width * ff,
        "gate_up",
    )


def hidden_back(x, raw, spots, parts, tile=256):
    count, (m, width), ff = len(parts), x.shape, parts[0].shape[1]
    part_specs = [pl.BlockSpec((p.shape[0], tile), lambda n, s: (0, n)) for p in parts]
    return grid_call(
        functools.partial(hidden_back_kernel, count),
        spots,
        (ff // tile,),
        (x, raw, *parts),
        [once((m, width)), pl.BlockSpec((2, m, tile), lambda n, s: (0, 0, n))] + part_specs,
        jax.ShapeDtypeStruct((2, m, ff), BF16),
        pl.BlockSpec((2, m, tile), lambda n, s: (0, 0, n)),
        [pltpu.VMEM((width, tile), BF16)],
        2 * m * width * ff,
        "hidden_back",
    )


def columns_out(h, spots, parts, width, tile=1024):
    count, (groups, m, ff) = len(parts), h.shape
    tile = min(tile, ff)
    tiles = ff // tile
    part_specs = [pl.BlockSpec((p.shape[0], tile), lambda f, s: (0, f)) for p in parts]
    return grid_call(
        functools.partial(columns_kernel, count),
        spots,
        (groups * tiles,),
        (h, *parts),
        [pl.BlockSpec((1, m, tile), lambda f, s: (f // tiles, 0, f % tiles))] + part_specs,
        jax.ShapeDtypeStruct((m, width), F32),
        once((m, width)),
        [pltpu.VMEM((width, tile), BF16)],
        2 * groups * m * width * ff,
        "columns_out",
    )


def block_grads(x, d, chips, size, gots=(), tile=1024):
    (m, _), (groups, _, ff) = x.shape, d.shape
    count = len(chips)
    tile = min(tile, ff)
    tiles = ff // tile
    spots = jnp.stack(chips).astype(jnp.int32)
    if size % 128:
        xs = [lax.dynamic_slice_in_dim(x, chip * size, size, 1) for chip in chips]
        x_specs = [once((m, size))] * count
    else:
        xs = [x] * count
        x_specs = [
            pl.BlockSpec((m, size), functools.partial(lambda i, f, s: (0, s[i]), i))
            for i in range(count)
        ]
    return grid_call(
        functools.partial(block_kernel, count, len(gots)),
        spots,
        (groups * tiles,),
        (*xs, d, *gots),
        x_specs
        + [pl.BlockSpec((1, m, tile), lambda f, s: (f // tiles, 0, f % tiles))]
        + [pl.BlockSpec((v.shape[0], tile), lambda f, s: (0, f)) for v in gots],
        [jax.ShapeDtypeStruct((size, groups * ff), BF16)] * count,
        [pl.BlockSpec((size, tile), lambda f, s: (0, f))] * count,
        [pltpu.VMEM((size, m), BF16)] * count,
        0,
        "block_grads",
    )


def row_kernel(pairs, spots, *refs):
    xs, ds = refs[:pairs], refs[pairs : 2 * pairs]
    last, mine, theirs, both = refs[2 * pairs :]
    rows = mine.shape[0]
    core = spots[0]
    start = 0
    for x, d in zip(xs, ds):
        cols = d.shape[1]
        both[:, start : start + cols] = product_l(x[...], d[...])
        start += cols
    both[:, start:] = last[...]
    mine[...] = both[pl.ds(pl.multiple_of(core * rows, 128), rows), :]
    theirs[...] = low(both[pl.ds(pl.multiple_of((1 - core) * rows, 128), rows), :])


def row_grads(pairs, last, core, chips, rows):
    xs, ds = [x for x, _ in pairs], [d for _, d in pairs]
    cols = sum(d.shape[1] for d in ds) + last.shape[1]
    if rows % 128:

        def own_columns(values, which):
            blocks = values.reshape(values.shape[0], chips, 2, rows)
            return lax.dynamic_index_in_dim(blocks, which, 2, keepdims=False).reshape(
                values.shape[0], chips * rows
            )

        def terms(which):
            return jnp.concatenate(
                [product_l(own_columns(x, which), d) for x, d in pairs]
                + [own_columns(last.T, which).T],
                axis=1,
            )

        return terms(core), low(terms(1 - core))
    block = pl.BlockSpec((rows, cols), lambda j, s: (j, 0))
    return grid_call(
        functools.partial(row_kernel, len(pairs)),
        core.reshape(1).astype(jnp.int32),
        (chips,),
        (*xs, *ds, last),
        [pl.BlockSpec((x.shape[0], 2 * rows), lambda j, s: (0, j)) for x in xs]
        + [once(d.shape) for d in ds]
        + [pl.BlockSpec((2 * rows, last.shape[1]), lambda j, s: (j, 0))],
        [
            jax.ShapeDtypeStruct((chips * rows, cols), F32),
            jax.ShapeDtypeStruct((chips * rows, cols), BF16),
        ],
        [block, block],
        [pltpu.VMEM((2 * rows, cols), F32)],
        sum(4 * d.size * chips * rows for d in ds),
        "row_grads",
    )


def last_kernel(large, *refs):
    mine, theirs, refs = refs[0], refs[1], refs[2:]
    ff_terms, refs = refs[:6], refs[6:]
    (main, little, *ff_outs), refs = refs[:5], refs[5:]
    own, core_got, side_sent, side_got, first, got, refs = *refs[:6], refs[6:]
    ff_held, (ff_sent,), refs = refs[:6], refs[6:7], refs[7:]
    loads, core_send, core_recv, side_send, side_recv, ring_send, ring_recv, ff_send, ff_recv = refs
    hops = Hops()
    side = lax.axis_index("tensor")
    half = hops.chips // 2
    rows = main.shape[0]
    part = little.shape[1]
    ff_cols = ff_sent.shape[2]
    cut = rows // 2
    greet([hops.above, hops.below, hops.partner, hops.across])
    order = [half]
    for k in range(1, half):
        order += [half - k, k - half]
    order.append(0)

    def rows_at(offset, top=0, size=rows):
        return pl.ds(pl.multiple_of(hops.chip_at(offset) * rows + top, 16), size)

    started, arriving = [], []
    for i, offset in enumerate(order):
        at = rows_at(offset)
        copy = remote(
            theirs.at[at], core_got.at[at], core_send, core_recv, (i,), hops.partner
        )
        copy.start()
        load = pltpu.make_async_copy(mine.at[at], own.at[at], loads.at[i])
        load.start()
        started.append(copy)
        arriving.append((copy, load))
    ff_loads = [
        pltpu.make_async_copy(source, target, loads.at[len(order) + i])
        for i, (source, target) in enumerate(zip(ff_terms, ff_held))
    ]
    for load in ff_loads:
        load.start()

    sides = {}
    my_part = pl.ds(pl.multiple_of(large + side * part, 128), part)
    their_part = pl.ds(pl.multiple_of(large + (1 - side) * part, 128), part)

    def ready(i):
        at = rows_at(order[i])
        copy, load = arriving[i]
        load.wait()
        copy.wait_recv()
        own[at, :] = own[at, :] + to_float(core_got[at, :])
        side_sent[at, :] = low(own[at, their_part])
        copy = remote(
            side_sent.at[at], side_got.at[at], side_send, side_recv, (i,), hops.across
        )
        copy.start()
        started.append(copy)
        sides[order[i]] = copy

    pieces = [(0, large // 2), (large // 2, large // 2), (large, part)]
    copies = {}

    def term(which, offset, top, size):
        at = rows_at(offset, top, size)
        start, cols = pieces[which]
        if which < 2:
            return own[at, start : start + cols]
        return own[at, my_part] + to_float(side_got[at, :])

    def send(which, direction, k, source, top, size):
        start, cols = pieces[which]
        copy = remote(
            source,
            got.at[direction, k, pl.ds(top, size), pl.ds(start, cols)],
            ring_send,
            ring_recv,
            (direction, k, which),
            hops.above if direction == 0 else hops.below,
        )
        copy.start()
        started.append(copy)
        copies[(which, direction, k)] = copy

    def step(which, k):
        start, cols = pieces[which]
        for direction in range(2):
            near, far = direction * cut, (1 - direction) * cut
            if k == 0:
                first[direction, :, start : start + cols] = low(term(which, half, near, cut))
                source = first.at[direction, :, pl.ds(start, cols)]
                send(which, direction, 0, source, near, cut)
                continue
            offset = (half - k) * (1 if direction == 0 else -1)
            copies[(which, direction, k - 1)].wait_recv()
            if k == 1:
                held = got[direction, 0, near : near + cut, start : start + cols]
                got[direction, 0, near : near + cut, start : start + cols] = low(
                    term(which, offset, near, cut) + to_float(held)
                )
                got[direction, 0, far : far + cut, start : start + cols] = low(
                    term(which, offset, far, cut)
                )
            else:
                held = got[direction, k - 1, :, start : start + cols]
                got[direction, k - 1, :, start : start + cols] = low(
                    term(which, offset, 0, rows) + to_float(held)
                )
            source = got.at[direction, k - 1, :, pl.ds(start, cols)]
            send(which, direction, k, source, 0, rows)

    def end_feed_forward():
        for load in ff_loads:
            load.wait()
        wide, wide_up, wide_down, narrow, narrow_up, narrow_down = ff_held
        my_rows = pl.ds(pl.multiple_of(hops.core * rows, 16), rows)
        their_rows = pl.ds(pl.multiple_of((1 - hops.core) * rows, 16), rows)
        my_cols = pl.ds(pl.multiple_of(hops.core * ff_cols, 128), ff_cols)
        groups = [
            (wide, wide_up, wide_down, 0),
            (wide, wide_up, wide_down, ff_cols),
            (narrow, narrow_up, narrow_down, 0),
        ]
        for i, (base, up, down, start) in enumerate(groups):
            cols = slice(start, start + ff_cols)

            def total(at):
                return to_float(base[at, cols]) + to_float(up[at, cols]) + to_float(down[at, cols])

            ff_sent[i] = total(their_rows)
            copy = remote(
                ff_sent.at[i], ff_outs[i].at[:, my_cols], ff_send, ff_recv, (i,), hops.partner
            )
            copy.start()
            ff_copies.append(copy)
            ff_outs[i][:, my_cols] = total(my_rows)

    ff_copies = []
    ready(0)
    step(0, 0)
    step(1, 0)
    ready(1)
    ready(2)
    sides[half].wait_recv()
    step(2, 0)
    for k in range(1, half):
        step(0, k)
        step(1, k)
        if k == 1:
            end_feed_forward()
        for i in range(2 * k + 1, min(2 * k + 3, len(order))):
            ready(i)
        sides[half - k].wait_recv()
        sides[k - half].wait_recv()
        step(2, k)
    sides[0].wait_recv()
    for which, (start, cols) in enumerate(pieces):
        for direction in range(2):
            copies[(which, direction, half - 1)].wait_recv()
        total = (
            term(which, 0, 0, rows)
            + to_float(got[0, half - 1, :, start : start + cols])
            + to_float(got[1, half - 1, :, start : start + cols])
        )
        if which < 2:
            main[:, start : start + cols] = total
        else:
            little[...] = total
    for copy in ff_copies:
        copy.wait_recv()
    for copy in ff_copies + started:
        copy.wait_send()


def last_reduce(mine, theirs, large, ff_terms):
    chips = lax.axis_size("dp") // 2
    half = chips // 2
    tall, cols = mine.shape
    rows = tall // chips
    part = (cols - large) // 2
    ff = ff_terms[3].shape[1]
    vmem = pl.BlockSpec(memory_space=pltpu.VMEM)
    dma = pltpu.SemaphoreType.DMA
    return pl.pallas_call(
        functools.partial(last_kernel, large),
        out_shape=[
            jax.ShapeDtypeStruct((rows, large), F32),
            jax.ShapeDtypeStruct((rows, part), F32),
        ]
        + [jax.ShapeDtypeStruct((rows, 2 * ff), F32)] * 3,
        in_specs=[ANY] * 8,
        out_specs=[vmem] * 5,
        scratch_shapes=[
            pltpu.VMEM((tall, cols), F32),
            pltpu.VMEM((tall, cols), BF16),
            pltpu.VMEM((tall, part), BF16),
            pltpu.VMEM((tall, part), BF16),
            pltpu.VMEM((2, rows // 2, large + part), BF16),
            pltpu.VMEM((2, half, rows, large + part), BF16),
        ]
        + [pltpu.VMEM(v.shape, v.dtype) for v in ff_terms]
        + [
            pltpu.VMEM((3, rows, ff), F32),
            dma((2 * half + 6,)),
            dma((2 * half,)),
            dma((2 * half,)),
            dma((2 * half,)),
            dma((2 * half,)),
            dma((2, half, 3)),
            dma((2, half, 3)),
            dma((3,)),
            dma((3,)),
        ],
        compiler_params=pltpu.CompilerParams(
            collective_id=2, has_side_effects=True, vmem_limit_bytes=56 * 2**20
        ),
        cost_estimate=pl.CostEstimate(
            flops=0, bytes_accessed=20 * mine.size * 4, transcendentals=0
        ),
        name="last_reduce",
    )(mine, theirs, *ff_terms)


def forward_kernel(hops_done, tile, x_own, *refs):
    count = 2 * hops_done + 1
    gu_parts, (dn_own,), refs = refs[:count], refs[count : count + 1], refs[count + 1 :]
    (x_out, gu_full, gu_land, dn_full, raw, hidden, result), refs = refs[:7], refs[7:]
    x, dn, hidden_v, pairs, core_sent, core_got, side_sent, side_got, refs = *refs[:8], refs[8:]
    x_send, x_recv, gu_send, gu_recv, dn_send, dn_recv, core_sems, side_sems, loads, stores = refs
    hops = Hops()
    half, chips = hops.chips // 2, hops.chips
    own = x_own.shape[0]
    size, ff = dn_own.shape
    cut = size // 2
    greet([hops.above, hops.below, hops.partner, hops.across])
    started, saved = [], []

    def begin(copy, where=started):
        copy.start()
        where.append(copy)
        return copy

    def spot(ref, offset, top=0, tall=size):
        return block_rows(ref, hops.chip_at(offset) * size + top, tall)

    def span(k):
        return (0, size) if k < half else (None, cut)

    def gu_hop(k):
        copies = []
        for direction, ahead in ((0, hops.above), (1, hops.below)):
            offset = (1 - k) * (1 if direction == 0 else -1)
            top, tall = (0, size) if k < half else (direction * cut, cut)
            target = spot(gu_land, offset, top, tall)
            if k == hops_done + 1:
                held = gu_parts[2 * k - 3 + direction] if k > 1 else gu_parts[0]
                source = block_rows(held, top, tall)
            else:
                source = target
            index = (direction, k - hops_done - 1)
            copies.append(begin(remote(source, target, gu_send, gu_recv, index, ahead)))
        return copies

    def dn_hop(k):
        copies = []
        for direction, ahead in ((0, hops.above), (1, hops.below)):
            offset = (1 - k) * (1 if direction == 0 else -1)
            top, tall = (0, size) if k < half else (direction * cut, cut)
            block = spot(dn, offset, top, tall)
            copies.append(begin(remote(block, block, dn_send, dn_recv, (direction, k - 1), ahead)))
        return copies

    def arrive(copies):
        for copy in copies:
            copy.wait_recv()

    moving = gu_hop(hops_done + 1)
    mine, far = pl.ds(0, own), pl.ds(own, own)
    near, opposite = pl.ds(2 * own, own), pl.ds(3 * own, own)
    load_x = begin(pltpu.make_async_copy(x_own, x.at[mine], loads.at[0]), saved)
    load_dn = begin(pltpu.make_async_copy(dn_own, spot(dn, 0), loads.at[1]), saved)
    from_far = begin(remote(x_own, x.at[far], x_send, x_recv, (0,), hops.across))
    from_near = begin(remote(x_own, x.at[near], x_send, x_recv, (1,), hops.partner))
    from_far.wait_recv()
    passed = begin(remote(x.at[far], x.at[opposite], x_send, x_recv, (2,), hops.partner))
    from_near.wait_recv()
    passed.wait_recv()
    load_x.wait()
    begin(pltpu.make_async_copy(x, x_out, stores.at[0]), saved)
    load_dn.wait()
    arrive(moving)
    for k in range(hops_done + 2, half + 1):
        moving = gu_hop(k)
        arrive(moving)
    moving = dn_hop(1)

    offsets = list(range(hops_done + 1, half)) + list(range(-half + 1, -hops_done)) + [half]
    order = [0]
    for k in range(1, hops_done + 1):
        order += [-k, k]
    tiles = ff // tile

    def body(*tiles_of):
        ins, (raw_tile, hidden_tile, weights) = tiles_of[:-3], tiles_of[-3:]
        step = pl.program_id(0)
        every = order + offsets
        for group in range(2):
            for number, offset in enumerate(every):
                at = pl.ds(pl.multiple_of(hops.chip_at(offset) * size, size), size)
                weights[group, at, :] = ins[group * len(every) + number][...]
        gate = product(x[...], weights[0])
        up = product(x[...], weights[1])
        raw_tile[0] = low(gate)
        raw_tile[1] = low(up)
        bend = jnp.tanh(GELU_SCALE * (gate + GELU_CUBE * gate * gate * gate))
        value = low(0.5 * gate * (1.0 + bend) * up)
        hidden_tile[...] = value
        hidden_v[:, pl.ds(pl.multiple_of(step * tile, tile), tile)] = value

    def part_spec(row, group):
        return pl.BlockSpec((size, tile), lambda n: (row, n + group * tiles))

    in_specs, operands = [], []
    for group in range(2):
        for ref in gu_parts:
            in_specs.append(part_spec(0, group))
            operands.append(ref)
        for offset in offsets:
            in_specs.append(part_spec(hops.chip_at(offset), group))
            operands.append(gu_land)
    m, width = x.shape
    pltpu.emit_pipeline(
        body,
        grid=(tiles,),
        in_specs=in_specs,
        out_specs=[
            pl.BlockSpec((2, m, tile), lambda n: (0, 0, n)),
            pl.BlockSpec((m, tile), lambda n: (0, n)),
            pl.BlockSpec((2, width, tile), lambda n: (0, 0, n)),
        ],
    )(*operands, raw, hidden, gu_full)

    order, core_copies, side_copies = [], [], []

    def block_out(offset):
        i = len(order)
        order.append(offset)
        at = pl.ds(pl.multiple_of(hops.chip_at(offset) * size, size), size)
        out = product_t(hidden_v[...], dn[at, :])
        pairs[i] = out[: 2 * own]
        core_sent[i] = low(out[2 * own :])
        copy = remote(
            core_sent.at[i], core_got.at[i], core_sems.at[0], core_sems.at[1], (i,), hops.partner
        )
        core_copies.append(begin(copy))

    def core_sum():
        i = len(side_copies)
        core_copies[i].wait_recv()
        both = pairs[i] + to_float(core_got[i])
        side_sent[i] = low(both[own:])
        copy = remote(
            side_sent.at[i], side_got.at[i], side_sems.at[0], side_sems.at[1], (i,), hops.across
        )
        side_copies.append(begin(copy))
        at = pl.ds(pl.multiple_of(hops.chip_at(order[i]) * size, size), size)
        result[:, at] = both[:own]

    for k in range(1, half + 1):
        arrive(moving)
        if k < half:
            moving = dn_hop(k + 1)
        if k == 1:
            block_out(0)
        if k < half:
            block_out(-k)
            core_sum()
            block_out(k)
            core_sum()
        else:
            block_out(half)
            core_sum()
    begin(pltpu.make_async_copy(dn, dn_full, stores.at[1]), saved)
    core_sum()
    for i, copy in enumerate(side_copies):
        copy.wait_recv()
        at = pl.ds(pl.multiple_of(hops.chip_at(order[i]) * size, size), size)
        result[:, at] = result[:, at] + to_float(side_got[i])
    for copy in started:
        copy.wait_send()
    for copy in saved[2:]:
        copy.wait()


def forward(x_own, gu_parts, dn_own, hops_done, tile=512):
    chips = lax.axis_size("dp") // 2
    half = chips // 2
    own, width = x_own.shape
    size, ff = dn_own.shape
    tile = min(tile, ff)
    m = 4 * own
    dma = pltpu.SemaphoreType.DMA
    vmem = pl.BlockSpec(memory_space=pltpu.VMEM)
    return pl.pallas_call(
        functools.partial(forward_kernel, hops_done, tile),
        out_shape=[
            jax.ShapeDtypeStruct((m, width), BF16),
            jax.ShapeDtypeStruct((2, width, ff), BF16),
            jax.ShapeDtypeStruct((width, 2 * ff), BF16),
            jax.ShapeDtypeStruct((width, ff), BF16),
            jax.ShapeDtypeStruct((2, m, ff), BF16),
            jax.ShapeDtypeStruct((m, ff), BF16),
            jax.ShapeDtypeStruct((own, width), F32),
        ],
        in_specs=[ANY] * (len(gu_parts) + 2),
        out_specs=[ANY] * 6 + [vmem],
        scratch_shapes=[
            pltpu.VMEM((m, width), BF16),
            pltpu.VMEM((width, ff), BF16),
            pltpu.VMEM((m, ff), BF16),
            pltpu.VMEM((chips, 2 * own, size), F32),
            pltpu.VMEM((chips, 2 * own, size), BF16),
            pltpu.VMEM((chips, 2 * own, size), BF16),
            pltpu.VMEM((chips, own, size), BF16),
            pltpu.VMEM((chips, own, size), BF16),
            dma((3,)),
            dma((3,)),
            dma((2, half - hops_done)),
            dma((2, half - hops_done)),
            dma((2, half)),
            dma((2, half)),
            dma((2, chips)),
            dma((2, chips)),
            dma((2,)),
            dma((2,)),
        ],
        compiler_params=pltpu.CompilerParams(
            collective_id=3, has_side_effects=True, vmem_limit_bytes=60 * 2**20
        ),
        cost_estimate=pl.CostEstimate(
            flops=6 * m * width * ff, bytes_accessed=0, transcendentals=0
        ),
        name="forward",
    )(x_own, *gu_parts, dn_own)


def backward_kernel(d_own, hidden, raw, dn_full, gu_full, rows_in, *refs):
    (x_out, d_gu_out, held_up, held_down, wide_up, wide_down, result), refs = refs[:7], refs[7:]
    x, dn, hid, d_gu, raw_v, gu_v, first, got, refs = *refs[:8], refs[8:]
    pairs, core_sent, core_got, side_sent, side_got, refs = *refs[:5], refs[5:]
    rows_v, wide_first, refs = *refs[:2], refs[2:]
    x_send, x_recv, ring_send, ring_recv, core_sems, side_sems, wide_sems, loads, stores = refs
    hops = Hops()
    half, chips = hops.chips // 2, hops.chips
    own = d_own.shape[0]
    size, ff = held_up.shape
    cut = size // 2
    m = x.shape[0]
    cols = min(512, ff)
    greet([hops.above, hops.below, hops.partner, hops.across])
    started, saved = [], []

    def begin(copy, where=started):
        copy.start()
        where.append(copy)
        return copy

    def load(source, target, number):
        copy = pltpu.make_async_copy(source, target, loads.at[number])
        copy.start()
        return copy

    def part(r):
        return pl.ds(r * own, own)

    from_far = begin(remote(d_own, x.at[part(1)], x_send, x_recv, (0,), hops.across))
    from_near = begin(remote(d_own, x.at[part(2)], x_send, x_recv, (1,), hops.partner))
    load_x = load(d_own, x.at[part(0)], 0)
    load_dn = load(dn_full, dn, 1)
    rows_order = (0, 2, 1, 3)
    raw_loads = {}

    def load_raw(i):
        r = rows_order[i]
        raw_loads[r] = load(raw.at[:, part(r)], raw_v.at[i % 2], 3 + i)

    def load_gu(j):
        return load(gu_full.at[:, pl.ds(j * size, size)], gu_v.at[j % 2], 7 + j)

    load_raw(0)
    load_raw(1)
    load_hid = load(hidden, hid, 2)
    far_block = pl.ds(pl.multiple_of(hops.chip_at(half) * size, size), size)
    load_rows = load(rows_in.at[:, far_block], rows_v, 7 + chips)

    def hidden_part(i):
        r = rows_order[i]
        at = part(r)
        raw_loads[r].wait()

        @pl.loop(0, ff // cols)
        def _(c):
            across_ = pl.ds(pl.multiple_of(c * cols, cols), cols)
            d_hidden = product(x[at, :], dn[:, across_])
            gate = to_float(raw_v[i % 2, 0, :, across_])
            up = to_float(raw_v[i % 2, 1, :, across_])
            square = gate * gate
            bend = jnp.tanh(GELU_SCALE * gate * (1.0 + GELU_CUBE * square))
            plus = 0.5 * (1.0 + bend)
            slope = plus + 0.5 * gate * (1.0 - bend * bend) * GELU_SCALE * (
                1.0 + 3.0 * GELU_CUBE * square
            )
            d_gu[0, at, across_] = low(d_hidden * up * slope)
            d_gu[1, at, across_] = low(d_hidden * gate * plus)

        if i + 2 < 4:
            load_raw(i + 2)

    copies = {}

    def ring_step(k):
        for direction, ahead in ((0, hops.above), (1, hops.below)):
            near, far = direction * cut, (1 - direction) * cut
            offset = (half - k) * (1 if direction == 0 else -1)
            at = pl.ds(pl.multiple_of(hops.chip_at(offset) * size, size), size)
            term = product_l(x[:, at], hid[...])
            if k == 0:
                first[direction] = low(term[near : near + cut])
                source = first.at[direction]
                target = got.at[direction, 0, pl.ds(near, cut)]
            else:
                copies[(direction, k - 1)].wait_recv()
                came = got.at[direction, k - 1]
                if k == 1:
                    came[near : near + cut, :] = low(
                        term[near : near + cut] + to_float(came[near : near + cut, :])
                    )
                    came[far : far + cut, :] = low(term[far : far + cut])
                else:
                    came[...] = low(term + to_float(came[...]))
                source = came
                if k < half - 2:
                    target = got.at[direction, k]
                else:
                    target = held_up if direction == 0 else held_down
            copies[(direction, k)] = begin(
                remote(source, target, ring_send, ring_recv, (direction, k), ahead)
            )

    core_copies, side_copies = [], []

    def block_out(j, loading):
        loading.wait()
        out = product_t(d_gu[0], gu_v[j % 2, 0]) + product_t(d_gu[1], gu_v[j % 2, 1])
        pairs[j] = out[: 2 * own]
        core_sent[j] = low(out[2 * own :])
        copy = remote(
            core_sent.at[j], core_got.at[j], core_sems.at[0], core_sems.at[1], (j,), hops.partner
        )
        core_copies.append(begin(copy))

    def core_sum(j):
        core_copies[j].wait_recv()
        both = pairs[j] + to_float(core_got[j])
        side_sent[j] = low(both[own:])
        copy = remote(
            side_sent.at[j], side_got.at[j], side_sems.at[0], side_sems.at[1], (j,), hops.across
        )
        side_copies.append(begin(copy))
        result[:, j * size : (j + 1) * size] = both[:own]

    load_x.wait()
    load_dn.wait()
    hidden_part(0)
    from_near.wait_recv()
    hidden_part(1)
    from_far.wait_recv()
    passed = begin(remote(x.at[part(1)], x.at[part(3)], x_send, x_recv, (2,), hops.partner))
    hidden_part(2)
    passed.wait_recv()
    load_hid.wait()
    ring_step(0)
    gu_loads = {0: load_gu(0), 1: load_gu(1)}
    hidden_part(3)
    load_rows.wait()
    for group in range(2):
        wide = product_l(rows_v[...], d_gu[group])
        for direction in range(2):
            wide_first[direction, :, group * ff : (group + 1) * ff] = low(
                wide[direction * cut : (direction + 1) * cut]
            )
    wide_copies = [
        begin(
            remote(
                wide_first.at[direction],
                target,
                wide_sems.at[0],
                wide_sems.at[1],
                (direction,),
                ahead,
            )
        )
        for direction, target, ahead in (
            (0, wide_up, hops.above),
            (1, wide_down, hops.below),
        )
    ]
    begin(pltpu.make_async_copy(x, x_out, stores.at[0]), saved)
    begin(pltpu.make_async_copy(d_gu, d_gu_out, stores.at[1]), saved)
    steps = [half - 1 - (half - 1 - k) for k in range(1, half - 1)]
    for j in range(chips):
        block_out(j, gu_loads[j])
        if j + 2 < chips:
            gu_loads[j + 2] = load_gu(j + 2)
        if j > 0:
            core_sum(j - 1)
        if j % 3 == 2 and steps:
            ring_step(steps.pop(0))
    core_sum(chips - 1)
    for k in steps:
        ring_step(k)
    for j, copy in enumerate(side_copies):
        copy.wait_recv()
        at = slice(j * size, (j + 1) * size)
        result[:, at] = result[:, at] + to_float(side_got[j])
    for direction in range(2):
        copies[(direction, half - 2)].wait_recv()
        wide_copies[direction].wait_recv()
    for copy in started:
        copy.wait_send()
    for copy in saved:
        copy.wait()


def backward(d_own, hidden, raw, dn_full, gu_full, rows_in):
    chips = lax.axis_size("dp") // 2
    half = chips // 2
    own, width = d_own.shape
    m, ff = hidden.shape
    size = width // chips
    dma = pltpu.SemaphoreType.DMA
    vmem = pl.BlockSpec(memory_space=pltpu.VMEM)
    return pl.pallas_call(
        backward_kernel,
        out_shape=[
            jax.ShapeDtypeStruct((m, width), BF16),
            jax.ShapeDtypeStruct((2, m, ff), BF16),
            jax.ShapeDtypeStruct((size, ff), BF16),
            jax.ShapeDtypeStruct((size, ff), BF16),
            jax.ShapeDtypeStruct((size // 2, 2 * ff), BF16),
            jax.ShapeDtypeStruct((size // 2, 2 * ff), BF16),
            jax.ShapeDtypeStruct((own, width), F32),
        ],
        in_specs=[ANY] * 6,
        out_specs=[ANY] * 6 + [vmem],
        scratch_shapes=[
            pltpu.VMEM((m, width), BF16),
            pltpu.VMEM((width, ff), BF16),
            pltpu.VMEM((m, ff), BF16),
            pltpu.VMEM((2, m, ff), BF16),
            pltpu.VMEM((2, 2, own, ff), BF16),
            pltpu.VMEM((2, 2, size, ff), BF16),
            pltpu.VMEM((2, size // 2, ff), BF16),
            pltpu.VMEM((2, half - 2, size, ff), BF16),
            pltpu.VMEM((chips, 2 * own, size), F32),
            pltpu.VMEM((chips, 2 * own, size), BF16),
            pltpu.VMEM((chips, 2 * own, size), BF16),
            pltpu.VMEM((chips, own, size), BF16),
            pltpu.VMEM((chips, own, size), BF16),
            pltpu.VMEM((m, size), BF16),
            pltpu.VMEM((2, size // 2, 2 * ff), BF16),
            dma((3,)),
            dma((3,)),
            dma((2, half - 1)),
            dma((2, half - 1)),
            dma((2, chips)),
            dma((2, chips)),
            dma((2, 2)),
            dma((8 + chips,)),
            dma((2,)),
        ],
        compiler_params=pltpu.CompilerParams(
            collective_id=4, has_side_effects=True, vmem_limit_bytes=60 * 2**20
        ),
        cost_estimate=pl.CostEstimate(
            flops=6 * m * width * ff, bytes_accessed=0, transcendentals=0
        ),
        name="backward",
    )(d_own, hidden, raw, dn_full, gu_full, rows_in)


def prepare_back_kernel(q_cols, kv_cols, spots, raw, d_q, d_kv, after, before, cos, sin, gains, *refs):
    out, gain_grads = refs
    tall = raw.shape[0]
    turn = HD // 2
    cosines, sines = cos[...], sin[...]

    @pl.when(pl.program_id(0) == 0)
    def _():
        gain_grads[...] = jnp.zeros_like(gain_grads)

    early = spots[1 + pl.program_id(0)] < spots[0]
    more = to_float(after[...]) + jnp.where(early, to_float(before[...]), 0.0)

    def back(values, d, gain):
        scale = lax.rsqrt(jnp.mean(values * values, axis=-1, keepdims=True) + EPS)
        d_gain = d if gain is None else d * gain
        inner = jnp.mean(values * d_gain, axis=-1, keepdims=True)
        return scale * d_gain - values * (scale * scale * scale * inner), values * scale * d

    def unturn(d):
        front, rear = d[:, :turn], d[:, turn:]
        return jnp.concatenate(
            [front * cosines + rear * sines, rear * cosines - front * sines], axis=1
        )

    for start in range(0, q_cols + 2 * kv_cols, HD):
        at = slice(start, start + HD)
        values = raw[:, at]
        if start < q_cols:
            d, which = unturn(d_q[:, at]), 0
        else:
            here = slice(start - q_cols, start - q_cols + HD)
            d = d_kv[:, here] + more[:, here]
            which = 1
            if start < q_cols + kv_cols:
                d = unturn(d)
        if start < q_cols + kv_cols:
            d_values, for_gain = back(values, d, gains[which : which + 1, :])
            gain_grads[which : which + 1, :] = gain_grads[which : which + 1, :] + jnp.sum(
                for_gain, axis=0, keepdims=True
            )
        else:
            d_values, _ = back(values, d, None)
        out[:, at] = low(d_values)


def prepare_back(raw, d_q, d_kv, after, before, cos, sin, gains, side, own, tile=128):
    tall, cols = raw.shape
    kv_cols = d_kv.shape[1] // 2
    q_cols = cols - 2 * kv_cols
    tiles = tall // tile
    near = before.shape[0] // tile
    natural = lax.rem(jnp.arange(tiles) + side * (own // tile), tiles)
    spots = jnp.concatenate([jnp.full((1,), near), natural]).astype(jnp.int32)

    def straight(width):
        return pl.BlockSpec((tile, width), lambda t, s: (t, 0))

    def ordered(width):
        return pl.BlockSpec((tile, width), lambda t, s: (s[1 + t], 0))

    return grid_call(
        functools.partial(prepare_back_kernel, q_cols, kv_cols),
        spots,
        (tiles,),
        (raw, d_q, d_kv, after, before, cos, sin, gains),
        [
            straight(cols),
            straight(q_cols),
            ordered(2 * kv_cols),
            ordered(2 * kv_cols),
            pl.BlockSpec((tile, 2 * kv_cols), lambda t, s: (jnp.minimum(s[1 + t], near - 1), 0)),
            straight(HD // 2),
            straight(HD // 2),
            once(gains.shape),
        ],
        [jax.ShapeDtypeStruct((tall, cols), BF16), jax.ShapeDtypeStruct((8, HD), F32)],
        [straight(cols), once((8, HD))],
        [],
        10 * raw.size,
        "prepare_back",
    )


class Gather:
    def __init__(self, ring, block):
        self.ring = ring
        self.rows = block.shape[0]
        self.held = [block, block]
        self.parts = [(0, 0, block)]
        self.step_count = 0

    def step(self):
        ring, half = self.ring, self.ring.chips // 2
        self.step_count += 1
        k = self.step_count
        going_up, going_down = self.held
        if k < half:
            self.held = [ring.up(going_up), ring.down(going_down)]
            self.parts += [(-k, 0, self.held[0]), (k, 0, self.held[1])]
        else:
            cut = self.rows // 2
            self.held = [ring.up(going_up[:cut]), ring.down(going_down[cut:])]
            self.parts += [(half, 0, self.held[0]), (half, cut, self.held[1])]

    def pieces(self):
        spots = [self.ring.chip_at(o) * self.rows + row for o, row, _ in self.parts]
        return jnp.stack(spots).astype(jnp.int32), [part for _, _, part in self.parts]


class BlockReduce:
    def __init__(self, ring, x, d, size):
        self.ring, self.x, self.d, self.size = ring, x, d, size
        self.step_count = 0
        self.held = []

    def offsets(self):
        half = self.ring.chips // 2
        k = self.step_count + 1
        return (half,) if k == 1 else (half + 1 - k, k - 1 - half)

    def blocks(self, offsets, gots=()):
        chips = [self.ring.chip_at(o) for o in offsets]
        return block_grads(self.x, self.d, chips, self.size, gots)

    def terms(self):
        return self.blocks(self.offsets())

    def last_term(self):
        return self.blocks((0,))[0]

    def step(self, terms=None, *beside):
        ring, half = self.ring, self.ring.chips // 2
        self.step_count += 1
        k = self.step_count
        cut = self.size // 2
        if k == 1:
            (term,) = self.blocks((half,))
            up, down = term[:cut], term[cut:]
        elif terms is None:
            up, down = self.blocks((half + 1 - k, k - 1 - half), self.held)
        else:
            up = low(to_float(terms[0]) + to_float(self.held[0]))
            down = low(to_float(terms[1]) + to_float(self.held[1]))
        up, down, beside = tie(up, down, beside)
        self.held = [ring.up(up), ring.down(down)]
        return beside


def region(body):
    shapes = jax.eval_shape(body)
    yes = lax.optimization_barrier(jnp.array(True))
    return lax.cond(
        yes,
        body,
        lambda: jax.tree.map(lambda v: jnp.zeros(v.shape, v.dtype), shapes),
    )


def meet(rings, *values):
    held, values = tie([r.held for r in rings], values)
    for r, h in zip(rings, held):
        r.held = h
    return values if len(values) != 1 else values[0]


def local(
    tokens,
    layer_input,
    block_ids,
    block_table,
    w_query,
    w_key,
    w_value,
    w_output,
    w_left,
    w_right,
    w_gate,
    w_up,
    w_down,
    w_layer_gate,
    w_layer_proj,
    query_gain,
    key_gain,
    gain_input,
    gain_attn_out,
    gain_laurel,
    gain_ffw_in,
    gain_ffw_out,
    gain_layer_out,
    out_grad,
):
    ring = Ring()
    side = lax.axis_index("tensor")
    core = ring.core
    rows = w_query.shape[0]
    own = tokens.shape[0]
    width = tokens.shape[1]
    q_cols = w_query.shape[1]
    kv_cols = w_key.shape[1]
    rank = w_left.shape[1]
    small = w_layer_gate.shape[1]
    ff_cols = w_gate.shape[1] // 2
    chips = ring.chips

    def gain_block(query_part, key_part, parts):
        count = query_part.shape[0]
        columns = parts + [
            jnp.pad(query_part, (0, rows - count)),
            jnp.pad(key_part, (0, rows - count)),
        ]
        block = jnp.stack(columns, axis=1)
        return jnp.pad(block, ((0, 0), (0, 128 - block.shape[1])))

    gains = gain_block(
        query_gain,
        key_gain,
        [gain_input, gain_attn_out, gain_laurel, gain_ffw_in, gain_ffw_out, gain_layer_out],
    )
    half = chips // 2
    (qkv_full, output_t, small_full), (*ff_own, other_tokens) = first_gather(
        [
            jnp.concatenate([w_query, w_key, w_value], axis=1),
            w_output.T,
            jnp.concatenate([w_left, w_right.T, w_layer_gate, w_layer_proj.T, gains], axis=1),
        ],
        w_gate,
        w_up,
        w_down.T,
        tokens,
    )
    left_full = small_full[:, :rank]
    right_t = small_full[:, rank : 2 * rank]
    lgate_full = small_full[:, 2 * rank : 2 * rank + small]
    lproj_t = small_full[:, 2 * rank + small : 2 * rank + 2 * small]
    gains_full = small_full[:, 2 * rank + 2 * small :]

    gain_columns = to_float(gains_full[:, :8])
    (
        input_scale,
        attn_scale,
        laurel_scale,
        ffw_in_scale,
        ffw_out_scale,
        layer_scale,
    ) = (gain_columns[:, i] for i in range(6))
    head_part = query_gain.shape[0]

    def head_gain(column):
        return column.reshape(ring.devices, rows)[:, :head_part].reshape(HD)

    query_scale = head_gain(gain_columns[:, 6])
    key_scale = head_gain(gain_columns[:, 7])

    piece_len = 2 * own
    seq_total = block_ids.shape[1]
    per_seq = seq_total // piece_len
    dp_index = lax.axis_index("dp")
    row_index = dp_index // per_seq
    slot = lax.rem(dp_index, per_seq)
    first = slot * piece_len
    has_before = slot > 0
    has_after = slot < per_seq - 1
    natural = jnp.arange(piece_len, dtype=jnp.int32)
    here = first + lax.rem(natural + side * own, piece_len)
    cosines, sines = rope_tables(here, HD)
    reach_after = min(256, piece_len)
    forward_pairs = [(i, i + 1) for i in range(ring.devices - 1)]
    backward_pairs = [(i + 1, i) for i in range(ring.devices - 1)]

    def in_order(values):
        return jnp.where(
            side == 0, values, jnp.concatenate([values[own:], values[:own]], axis=0)
        )

    ids_row = lax.dynamic_index_in_dim(block_ids, row_index, 0, keepdims=False)
    table_row = lax.dynamic_index_in_dim(block_table, row_index, 0, keepdims=False)
    own_ids = lax.dynamic_slice_in_dim(ids_row, first, piece_len, 0)
    before_ids = lax.dynamic_slice_in_dim(ids_row, jnp.maximum(first - piece_len, 0), piece_len, 0)
    before_ids = jnp.where(has_before, before_ids, -2)
    after_ids = lax.dynamic_slice_in_dim(
        ids_row, jnp.minimum(first + piece_len, seq_total - reach_after), reach_after, 0
    )
    after_ids = jnp.where(has_after, after_ids, -2)
    key_ids = jnp.concatenate([before_ids, own_ids, after_ids], axis=0)
    query_ids = in_order(own_ids)
    block_count = block_table.shape[-1]
    number_rows = jnp.arange(block_count, dtype=jnp.int32)
    sees_last = jnp.sum(
        jnp.where(number_rows[None, :] == number_rows[:, None] - 1, table_row, 0), axis=1
    )
    query_sees = jnp.sum(
        jnp.where(query_ids[:, None] == number_rows[None, :], sees_last[None, :], 0), axis=1
    )
    previous_ids = jnp.where(query_sees == 1, query_ids - 1, query_ids)

    def prepare(qkv_in, query_gains, key_gains):
        query_in = qkv_in[:, :q_cols]
        key_in = qkv_in[:, q_cols : q_cols + kv_cols]
        value_in = qkv_in[:, q_cols + kv_cols :]
        query_out = rotate(
            norm_gain(query_in.reshape(piece_len, -1, HD), query_gains), cosines, sines
        )
        key_out = rotate(norm_gain(key_in.reshape(piece_len, -1, HD), key_gains), cosines, sines)
        return (query_out, key_out, norm_plain(value_in.reshape(piece_len, -1, HD)))

    heads_local = q_cols // HD
    kv_local = kv_cols // HD
    group = heads_local // kv_local

    def scores_for(query_low, keys_all):
        allowed = (query_ids[:, None] == key_ids[None, :]) | (
            previous_ids[:, None] == key_ids[None, :]
        )
        scores = jnp.einsum("qkgd,ckd->kgqc", query_low, keys_all, preferred_element_type=F32)
        return jnp.where(allowed[None, None], scores, NEGATIVE)

    def sum_sides(partial, beside=None):
        got = across(low(partial[own:]))
        if beside is None:
            return partial[:own] + to_float(got)
        got, beside = tie(got, beside())
        return partial[:own] + to_float(got), beside

    def both_sides(values, beside=None):
        got = across(values)
        if beside is None:
            return jnp.concatenate([values, got], axis=0)
        got, beside = tie(got, beside())
        return jnp.concatenate([values, got], axis=0), beside

    def four_ways(values):
        pair = both_sides(values)
        return jnp.concatenate([pair, ring.swap(pair)], axis=0)

    def sum_four(partial, beside=None):
        pair = partial[: 2 * own] + to_float(ring.swap(low(partial[2 * own :])))
        return sum_sides(pair, beside)

    def attend():
        normed_low = low(norm_gain(to_float(tokens), input_scale))
        seq_rows = jnp.concatenate(
            [normed_low, low(norm_gain(to_float(other_tokens), input_scale))], axis=0
        )
        qkv_raw = product(seq_rows, qkv_full)
        query_rot, key_rot, value_nrm = prepare(qkv_raw, query_scale, key_scale)
        query_low = low(query_rot).reshape(piece_len, kv_local, group, HD)
        kv_own = in_order(jnp.concatenate([low(key_rot), low(value_nrm)], axis=1))
        kv_before = lax.ppermute(kv_own, "dp", forward_pairs)
        kv_after = lax.ppermute(kv_own[:reach_after], "dp", backward_pairs)
        kv_all = jnp.concatenate([kv_before, kv_own, kv_after], axis=0)
        scores = scores_for(query_low, kv_all[:, :kv_local])
        highest = jnp.max(scores, axis=-1, keepdims=True)
        weights_exp = jnp.exp(scores - highest)
        totals = jnp.sum(weights_exp, axis=-1, keepdims=True)
        probs_low = low(weights_exp / totals)
        attended = jnp.einsum(
            "kgqc,ckd->qkgd", probs_low, kv_all[:, kv_local:], preferred_element_type=F32
        )
        log_totals = highest + jnp.log(totals)
        heads_low = low(attended.reshape(piece_len, heads_local * HD))
        return seq_rows, qkv_raw, query_low, kv_all, log_totals, heads_low

    gu = Gather(ring, ff_own[0])
    dn = Gather(ring, ff_own[1])
    gu.step()
    seq_rows, qkv_raw, query_low, kv_all, log_totals, heads_low = region(attend)
    heads_low = meet([gu], heads_low)
    gu.step()

    def join(heads_low):
        attn_out = sum_sides(product_t(heads_low, output_t))
        normed = norm_gain(to_float(tokens), input_scale)
        left_low = low(product(low(normed), left_full))
        right_out = product_t(left_low, right_t)
        laurel_normed = norm_gain(right_out, laurel_scale)
        attn_normed = norm_gain(attn_out, attn_scale)
        mixed = (to_float(tokens) + attn_normed + (normed + laurel_normed)) * ROOT_HALF
        return attn_out, left_low, right_out, mixed, low(norm_gain(mixed, ffw_in_scale))

    attn_out, left_low, right_out, mixed, ffw_low = region(lambda: join(heads_low))
    ffw_low = meet([gu], ffw_low)
    fused = (2 * rows) % 256 == 0
    if fused:
        parts = [part for _, _, part in gu.parts]
        ffw_rows, gu_weights, _, dn_whole, raw, hidden_low, ffw_out = forward(
            ffw_low, parts, ff_own[1], 2
        )
        dn_spots, dn_parts = jnp.zeros((1,), jnp.int32), [dn_whole]
    else:
        gu.step()
        ffw_rows = region(lambda: four_ways(ffw_low))
        ffw_rows = meet([gu], ffw_rows)
        for _ in range(half - 4):
            gu.step()
            ffw_rows = meet([gu], ffw_rows)
        gu.step()
        ffw_rows = meet([gu], ffw_rows)

        gu_spots, gu_parts = gu.pieces()
        dn.step()
        raw, hidden_low, gu_weights = region(lambda: gate_up(ffw_rows, gu_spots, gu_parts))
        raw, hidden_low = meet([dn], raw, hidden_low)
        for _ in range(half - 1):
            dn.step()
            raw, hidden_low = meet([dn], raw, hidden_low)
        dn_spots, dn_parts = dn.pieces()
        ffw_out = sum_four(columns_out(hidden_low[None], dn_spots, dn_parts, width))
    ffw_out_normed, ffw_out_back = jax.vjp(norm_gain, ffw_out, ffw_out_scale)
    block_mid = mixed + ffw_out_normed
    mid_low = low(block_mid)
    layer_pre = product(mid_low, lgate_full)

    def layer_gate_fn(pre_values, per_layer):
        return gelu_tanh(pre_values) * per_layer

    gated, gated_back = jax.vjp(layer_gate_fn, layer_pre, to_float(layer_input))
    gated_low = low(gated)
    layer_proj = product_t(gated_low, lproj_t)
    proj_normed, proj_back = jax.vjp(norm_gain, layer_proj, layer_scale)
    result = block_mid + proj_normed

    grad_out = to_float(out_grad)
    d_proj, d_layer_scale = proj_back(grad_out)
    d_proj_low = low(d_proj)
    d_gated = product(d_proj_low, lproj_t)
    d_pre, grad_layer_input = gated_back(d_gated)
    d_pre_low = low(d_pre)
    d_mid = grad_out + product_t(d_pre_low, lgate_full)
    d_ffw_out, d_ffw_out_scale = ffw_out_back(d_mid)
    if fused:
        d_ffw_rows, d_gate_up, *held, d_ffw_normed = backward(
            low(d_ffw_out), hidden_low, raw, dn_whole, gu_weights, ffw_rows
        )
        rd = BlockReduce(ring, d_ffw_rows, hidden_low[None], 2 * rows)
        rd.held, rd.step_count = held[:2], half - 1
        rg = BlockReduce(ring, ffw_rows, d_gate_up, 2 * rows)
        rg.held, rg.step_count = held[2:], 1
    else:
        d_ffw_rows = four_ways(low(d_ffw_out))
        rd = BlockReduce(ring, d_ffw_rows, hidden_low[None], 2 * rows)
        for _ in range(half - 1):
            rd.step()
            meet([rd])
        d_gate_up = hidden_back(d_ffw_rows, raw, dn_spots, dn_parts)
        d_ffw_normed = sum_four(
            product_t(d_gate_up[0], gu_weights[0]) + product_t(d_gate_up[1], gu_weights[1])
        )
        rg = BlockReduce(ring, ffw_rows, d_gate_up, 2 * rows)
        for _ in range(half - 3):
            rg.step()
            meet([rg])
    rd.step()
    rg.step()

    def back_34():
        _, back = jax.vjp(norm_gain, mixed, ffw_in_scale)
        d_mixed_extra, d_ffw_in_scale = back(d_ffw_normed)
        d_branch = (d_mid + d_mixed_extra) * ROOT_HALF
        _, back = jax.vjp(norm_gain, attn_out, attn_scale)
        d_attn, d_attn_scale = back(d_branch)
        d_attn_rows, terms = both_sides(low(d_attn), rg.terms)
        d_heads = low(product(d_attn_rows, output_t)).reshape(piece_len, kv_local, group, HD)
        keys_all, values_all = kv_all[:, :kv_local], kv_all[:, kv_local:]
        probs = jnp.exp(scores_for(query_low, keys_all) - log_totals)
        probs_low = low(probs)
        d_values_all = jnp.einsum(
            "kgqc,qkgd->ckd", probs_low, d_heads, preferred_element_type=F32
        )
        d_probs = jnp.einsum("qkgd,ckd->kgqc", d_heads, values_all, preferred_element_type=F32)
        deltas = jnp.sum(probs * d_probs, axis=-1, keepdims=True)
        d_scores = low(probs * (d_probs - deltas))
        d_keys_all = jnp.einsum("kgqc,qkgd->ckd", d_scores, query_low, preferred_element_type=F32)
        d_query_rot = jnp.einsum("kgqc,ckd->qkgd", d_scores, keys_all, preferred_element_type=F32)
        kv_shape = (kv_all.shape[0], kv_cols)
        d_kv_all = jnp.concatenate(
            [d_keys_all.reshape(kv_shape), d_values_all.reshape(kv_shape)], axis=1
        )
        to_before = low(d_kv_all[:piece_len])
        to_after = low(d_kv_all[2 * piece_len :])
        d_kv_own = d_kv_all[piece_len : 2 * piece_len]
        moving = (to_before, to_after)
        kept = (d_ffw_in_scale, d_attn_scale, d_branch, d_attn_rows, d_kv_own)
        return terms, moving, kept, d_query_rot.reshape(piece_len, q_cols)

    terms, moving, kept, d_query_rot = meet([rd, rg], *region(back_34))
    d_ffw_in_scale, d_attn_scale, d_branch, d_attn_rows, d_kv_own = kept
    from_after = lax.ppermute(moving[0], "dp", backward_pairs)
    from_before = lax.ppermute(moving[1], "dp", forward_pairs)
    from_after, from_before = rg.step(terms, from_after, from_before)

    def back_5():
        both_gains = jnp.stack([query_scale, key_scale])
        d_qkv_low, gain_sums = prepare_back(
            qkv_raw,
            d_query_rot,
            d_kv_own,
            from_after,
            from_before,
            cosines,
            sines,
            jnp.pad(both_gains, ((0, 6), (0, 0))),
            side,
            own,
        )
        d_more, ends = sum_sides(
            product_t(d_qkv_low, qkv_full), lambda: (rd.last_term(), rg.last_term())
        )
        return d_more, ends, d_qkv_low, gain_sums[0], gain_sums[1]

    d_more, ends, d_qkv_low, query_scale_grad, key_scale_grad = meet([rg], *region(back_5))
    rg.step()

    def head_gain_back(grads):
        padded = jnp.pad(grads.reshape(ring.devices, head_part), ((0, 0), (0, rows - head_part)))
        return padded.reshape(width)

    def back_6():
        normed, input_norm_back = jax.vjp(norm_gain, to_float(tokens), input_scale)
        _, laurel_back = jax.vjp(norm_gain, right_out, laurel_scale)
        d_right, d_laurel_scale = laurel_back(d_branch)
        d_right_low = low(d_right)
        d_left_low = low(product(d_right_low, right_t))
        d_normed = d_branch + product_t(d_left_low, left_full)
        d_normed = d_normed + d_more
        d_inputs_extra, d_input_scale = input_norm_back(d_normed)
        grad_tokens = d_branch + d_inputs_extra
        gain_grads = jnp.stack(
            [
                d_input_scale,
                d_attn_scale,
                d_laurel_scale,
                d_ffw_in_scale,
                d_ffw_out_scale,
                d_layer_scale,
                head_gain_back(query_scale_grad),
                head_gain_back(key_scale_grad),
            ],
            axis=0,
        )
        gain_grads = jnp.pad(gain_grads, ((0, 120), (0, 0))).T
        pairs = [
            (d_attn_rows, heads_low),
            (seq_rows, d_qkv_low),
            (mid_low, d_pre_low),
            (d_proj_low, gated_low),
            (low(normed), d_left_low),
            (d_right_low, left_low),
        ]
        return grad_tokens, row_grads(pairs, gain_grads, core, chips, rows)

    grad_tokens, (mine, theirs) = meet([rg], *region(back_6))
    down_end, gate_up_end = ends
    total, small_half, out_gate, out_up, out_down_t = last_reduce(
        mine,
        theirs,
        2 * q_cols + 2 * kv_cols,
        [gate_up_end, *rg.held, down_end, *rd.held],
    )
    out_output = total[:, :q_cols].T
    out_qkv = total[:, q_cols:]
    small_other = across(small_half)
    out_small = jnp.where(
        side == 0,
        jnp.concatenate([small_half, small_other], axis=1),
        jnp.concatenate([small_other, small_half], axis=1),
    )
    out_gains = out_small[:, 2 * rank + 2 * small :]
    return (
        low(result),
        grad_tokens,
        grad_layer_input,
        out_qkv[:, :q_cols],
        out_qkv[:, q_cols : q_cols + kv_cols],
        out_qkv[:, q_cols + kv_cols :],
        out_output,
        out_small[:, 2 * small : 2 * small + rank],
        out_small[:, 2 * small + rank : 2 * small + 2 * rank].T,
        out_gate,
        out_up,
        out_down_t.T,
        out_small[:, :small],
        out_small[:, small : 2 * small].T,
        out_gains[:head_part, 6],
        out_gains[:head_part, 7],
        out_gains[:, 0],
        out_gains[:, 1],
        out_gains[:, 2],
        out_gains[:, 3],
        out_gains[:, 4],
        out_gains[:, 5],
    )


def solution(mesh):
    both = P(("dp", "tensor"), None)
    rows_split = P("dp", "tensor")
    cols_split = P("tensor", "dp")
    by_row = P("dp", None)
    by_col = P(None, "dp")
    flat = P("dp")
    return jax.shard_map(
        local,
        mesh=mesh,
        in_specs=(
            (both, both, P(), P(), rows_split, rows_split, rows_split, cols_split)
            + (by_row, by_col, rows_split, rows_split, cols_split, by_row, by_col)
            + (flat,) * 8
            + (both,)
        ),
        out_specs=(
            (both, both, both, rows_split, rows_split, rows_split, cols_split)
            + (by_row, by_col, rows_split, rows_split, cols_split, by_row, by_col)
            + (flat,) * 8
        ),
        check_vma=False,
    )
```

```python
import functools

import jax
import jax.numpy as jnp
from jax import lax
from jax.experimental import pallas as pl
from jax.experimental.pallas import tpu as pltpu
from jax.sharding import PartitionSpec as P

HD = 256
EPS = 1e-06
ROOT_HALF = 0.7071067811865476
NEGATIVE = -1e30
F32 = jnp.float32
BF16 = jnp.bfloat16


def norm_gain(values, gains):
    return values * lax.rsqrt(jnp.mean(values * values, axis=-1, keepdims=True) + EPS) * gains


def norm_plain(values):
    return values * lax.rsqrt(jnp.mean(values * values, axis=-1, keepdims=True) + EPS)


def gelu_tanh(values):
    return jax.nn.gelu(values, approximate=True)


def rope_tables(positions, head_width):
    positions = positions.astype(F32)[:, None]
    frequency = 10000.0 ** (-2.0 * jnp.arange(head_width // 2, dtype=F32) / head_width)
    angles = positions * frequency[None, :]
    return (jnp.cos(angles), jnp.sin(angles))


def rotate(values, cosines, sines):
    half_width = values.shape[-1] // 2
    front_half = values[..., :half_width]
    back_half = values[..., half_width:]
    cos_wide = cosines[:, None, :]
    sin_wide = sines[:, None, :]
    return jnp.concatenate(
        [
            front_half * cos_wide - back_half * sin_wide,
            back_half * cos_wide + front_half * sin_wide,
        ],
        axis=-1,
    )


def to_float(values):
    return values.astype(F32)


def low(values):
    return values.astype(BF16)


def product(left_in, right_in):
    return jnp.dot(left_in, right_in, preferred_element_type=F32)


def product_t(left_in, right_in):
    return lax.dot_general(left_in, right_in, (((1,), (1,)), ((), ())), preferred_element_type=F32)


def product_l(left_in, right_in):
    return lax.dot_general(left_in, right_in, (((0,), (0,)), ((), ())), preferred_element_type=F32)


def tie(*values):
    return lax.optimization_barrier(values)


class Ring:
    def __init__(self):
        self.devices = lax.axis_size("dp")
        self.chips = self.devices // 2
        order = list(range(0, self.chips, 2)) + list(range(self.chips - 1, 0, -2))
        self.cw = [
            (2 * order[p] + c, 2 * order[(p + 1) % self.chips] + c)
            for p in range(self.chips)
            for c in range(2)
        ]
        self.ccw = [(b, a) for a, b in self.cw]
        self.core_pairs = [(d, d ^ 1) for d in range(self.devices)]
        me = lax.axis_index("dp")
        self.core = lax.rem(me, 2)
        self.chip = me // 2
        self.place = jnp.where(
            lax.rem(self.chip, 2) == 0, self.chip // 2, self.chips - 1 - self.chip // 2
        )

    def chip_at(self, offset):
        place = lax.rem(self.place + offset + self.chips, self.chips)
        return jnp.where(place < self.chips // 2, 2 * place, 2 * (self.chips - 1 - place) + 1)

    def up(self, values):
        return lax.ppermute(values, "dp", self.cw)

    def down(self, values):
        return lax.ppermute(values, "dp", self.ccw)

    def swap(self, values):
        return lax.ppermute(values, "dp", self.core_pairs)


def across(values):
    return lax.ppermute(values, "tensor", [(0, 1), (1, 0)])


def remote(source, target, sends, receives, index, device):
    return pltpu.make_async_remote_copy(
        src_ref=source,
        dst_ref=target,
        send_sem=sends.at[index],
        recv_sem=receives.at[index],
        device_id=device,
        device_id_type=pl.DeviceIdType.MESH,
    )


def greet(devices):
    barrier = pltpu.get_barrier_semaphore()
    for device in devices:
        pl.semaphore_signal(
            barrier, inc=1, device_id=device, device_id_type=pl.DeviceIdType.MESH
        )
    pl.semaphore_wait(barrier, len(devices))


def block_rows(ref, start, count):
    return ref.at[pl.ds(pl.multiple_of(start, 16), count)]


class Hops:
    def __init__(self):
        me = lax.axis_index("dp")
        self.chips = lax.axis_size("dp") // 2
        self.core = lax.rem(me, 2)
        self.chip = me // 2
        self.place = jnp.where(
            lax.rem(self.chip, 2) == 0, self.chip // 2, self.chips - 1 - self.chip // 2
        )
        self.partner = {"dp": self.chip * 2 + 1 - self.core}
        self.above = {"dp": self.chip_at(1) * 2 + self.core}
        self.below = {"dp": self.chip_at(-1) * 2 + self.core}
        self.across = {"tensor": 1 - lax.axis_index("tensor")}

    def chip_at(self, offset):
        place = lax.rem(self.place + offset + self.chips, self.chips)
        return jnp.where(place < self.chips // 2, 2 * place, 2 * (self.chips - 1 - place) + 1)


def staged_apart(source_shape, turned, start):
    cols = source_shape[0] if turned else source_shape[1]
    return turned or start % 128 != 0 or cols % 128 != 0, cols


def first_kernel(layout, down_turned, ff_cols, *refs):
    count = len(layout)
    sources, refs = refs[: sum(len(l) for l in layout)], refs[sum(len(l) for l in layout) :]
    (gate, up, down, tokens), refs = refs[:4], refs[4:]
    wholes, refs = refs[:count], refs[count:]
    (gate_own, up_down_own, other_tokens), refs = refs[:3], refs[3:]
    stages, refs = refs[:count], refs[count:]
    (gate_v, up_v, tokens_v, down_v, down_t), refs = refs[:5], refs[5:]
    apart, refs = list(refs[:-8]), refs[-8:]
    in_sems, out_sems, ring_send, ring_recv, pair_send, pair_recv, ff_send, ff_recv = refs
    hops = Hops()
    half = hops.chips // 2
    mine = pl.ds(pl.multiple_of(hops.core * ff_cols, 128), ff_cols)
    theirs = pl.ds(pl.multiple_of((1 - hops.core) * ff_cols, 128), ff_cols)

    number = 0

    def load(source, target):
        nonlocal number
        copy = pltpu.make_async_copy(source, target, in_sems.at[number])
        copy.start()
        number += 1
        return copy

    taken = list(sources)
    fills = []
    for which, flags in enumerate(layout):
        start, steps = 0, []
        for turned in flags:
            source = taken.pop(0)
            own_buffer, cols = staged_apart(source.shape, turned, start)
            if own_buffer:
                buffer = apart.pop(0)
                steps.append((load(source, buffer), buffer, turned, start, cols))
            else:
                target = stages[which].at[:, pl.ds(start, cols)]
                steps.append((load(source, target), None, turned, start, cols))
            start += cols
        fills.append(steps)
    load_down = load(down, down_v)
    bounces = [(load(gate.at[:, mine], gate_v), gate_v), (load(up.at[:, mine], up_v), up_v)]
    load_tokens = load(tokens, tokens_v)
    greet([hops.above, hops.below, hops.partner, hops.across])
    started, stores = [], []

    def place(which, offset, top, size):
        tall = stages[which].shape[0]
        at = (2 * hops.chip_at(offset) + hops.core) * tall + top
        return wholes[which].at[pl.ds(pl.multiple_of(at, 8 if tall <= 16 else 16), size)]

    def store(source, target):
        copy = pltpu.make_async_copy(source, target, out_sems.at[len(stores)])
        copy.start()
        stores.append(copy)

    def to_partner(number, which, offset, top, size, source=None):
        spot = place(which, offset, top, size)
        copy = remote(
            spot if source is None else source,
            spot,
            pair_send,
            pair_recv,
            (number, which),
            hops.partner,
        )
        copy.start()
        started.append(copy)
        pairs.append(copy)

    def onward(direction, k, which, offset, top, size, source=None):
        spot = place(which, offset, top, size)
        copy = remote(
            spot if source is None else source,
            spot,
            ring_send,
            ring_recv,
            (direction, k, which),
            hops.above if direction == 0 else hops.below,
        )
        copy.start()
        started.append(copy)
        arrivals[(direction, k, which)] = copy

    pairs, arrivals = [], {}
    for which, steps in enumerate(fills):
        stage = stages[which]
        for copy, buffer, turned, start, cols in steps:
            copy.wait()
            if buffer is not None:
                stage[:, start : start + cols] = buffer[...].T if turned else buffer[...]
        tall = stage.shape[0]
        for direction in range(2):
            onward(direction, 0, which, 0, 0, tall, stage)
    own = tokens.shape[0]
    theirs_at = other_tokens.at[pl.ds(own, own)]
    ff_copies = [remote(tokens, theirs_at, ff_send, ff_recv, (3,), hops.across)]
    ff_copies[0].start()
    rows = gate.shape[0]
    own_rows = pl.ds(pl.multiple_of(hops.core * rows, 16), rows)
    targets = [
        gate_own.at[own_rows],
        up_down_own.at[own_rows, pl.ds(0, ff_cols)],
        up_down_own.at[own_rows, pl.ds(ff_cols, ff_cols)],
    ]
    load_down.wait()
    if down_turned:
        down_t[...] = down_v[...].T
        down = down_t
    else:
        down = down_v
    for number_, (weight, target) in enumerate(zip((gate, up, down), targets)):
        copy = remote(
            weight.at[:, theirs], target, ff_send, ff_recv, (number_,), hops.partner
        )
        copy.start()
        ff_copies.append(copy)
    for which, stage in enumerate(stages):
        to_partner(0, which, 0, 0, stage.shape[0], stage)
        store(stage, place(which, 0, 0, stage.shape[0]))
    for (copy, buffer), target in zip(bounces, targets):
        copy.wait()
        store(buffer, target)
    store(down.at[:, mine], targets[2])
    load_tokens.wait()
    store(tokens_v, other_tokens.at[pl.ds(0, own)])
    for k in range(1, half + 1):
        for which in range(count):
            tall = stages[which].shape[0]
            cut = tall // 2
            for direction in range(2):
                arrivals[(direction, k - 1, which)].wait_recv()
                offset = -k if direction == 0 else k
                if k < half - 1:
                    onward(direction, k, which, offset, 0, tall)
                elif k == half - 1:
                    onward(direction, k, which, offset, direction * cut, cut)
                if k < half:
                    to_partner(2 * k - 1 + direction, which, offset, 0, tall)
                else:
                    to_partner(2 * k - 1 + direction, which, half, direction * cut, cut)
    for copy in ff_copies + pairs:
        copy.wait_recv()
    for copy in ff_copies + started:
        copy.wait_send()
    for copy in stores:
        copy.wait()


ANY = pl.BlockSpec(memory_space=pl.ANY)


def comm_call(kernel, number, operands, shapes, stages, semaphores, name):
    moved = sum(v.size * 2 for v in shapes)
    return pl.pallas_call(
        kernel,
        out_shape=shapes,
        in_specs=[ANY] * len(operands),
        out_specs=[ANY] * len(shapes),
        scratch_shapes=stages + [pltpu.SemaphoreType.DMA(shape) for shape in semaphores],
        compiler_params=pltpu.CompilerParams(
            collective_id=number, has_side_effects=True, vmem_limit_bytes=60 * 2**20
        ),
        cost_estimate=pl.CostEstimate(flops=0, bytes_accessed=8 * moved, transcendentals=0),
        name=name,
    )(*operands)


def first_gather(blocks, gate, up, down, tokens):
    chips = lax.axis_size("dp") // 2
    half = chips // 2
    down, down_turned = down
    rows = gate.shape[0]
    ff_cols = gate.shape[1] // 2
    count = len(blocks)
    stages, apart = [], []
    for block in blocks:
        start = 0
        for source, turned in block:
            own_buffer, cols = staged_apart(source.shape, turned, start)
            if own_buffer:
                apart.append(pltpu.VMEM(source.shape, source.dtype))
            start += cols
        first, turned = block[0]
        tall = first.shape[1] if turned else first.shape[0]
        stages.append(pltpu.VMEM((tall, start), first.dtype))
    shapes = [
        jax.ShapeDtypeStruct((2 * chips * stage.shape[0], stage.shape[1]), stage.dtype)
        for stage in stages
    ] + [
        jax.ShapeDtypeStruct((2 * rows, ff_cols), gate.dtype),
        jax.ShapeDtypeStruct((2 * rows, 2 * ff_cols), gate.dtype),
        jax.ShapeDtypeStruct((2 * tokens.shape[0], tokens.shape[1]), tokens.dtype),
    ]
    more = [
        pltpu.VMEM((rows, ff_cols), gate.dtype),
        pltpu.VMEM((rows, ff_cols), gate.dtype),
        pltpu.VMEM(tokens.shape, tokens.dtype),
        pltpu.VMEM(down.shape, down.dtype),
        pltpu.VMEM((rows, 2 * ff_cols), down.dtype),
    ]
    sources = [source for block in blocks for source, _ in block]
    semaphores = [
        (len(sources) + 4,),
        (4 + count,),
        (2, half, count),
        (2, half, count),
        (2 * half + 1, count),
        (2 * half + 1, count),
        (4,),
        (4,),
    ]
    layout = tuple(tuple(turned for _, turned in block) for block in blocks)
    out = comm_call(
        functools.partial(first_kernel, layout, down_turned, ff_cols),
        0,
        (*sources, gate, up, down, tokens),
        shapes,
        stages + more + apart,
        semaphores,
        "first_gather",
    )
    return out[:count], out[count:]


GELU_SCALE = 0.7978845608028654
GELU_CUBE = 0.044715
ROW_TILE = 1024


def fill(spots, whole, parts):
    for number, part in enumerate(parts):
        size = part.shape[0]
        whole[pl.ds(pl.multiple_of(spots[number], size), size), :] = part[...]


def gate_up_kernel(count, spots, x, *refs):
    gate_parts, up_parts = refs[:count], refs[count : 2 * count]
    raw, hidden, weights = refs[2 * count :]
    gate_w, up_w = weights.at[0], weights.at[1]
    fill(spots, gate_w, gate_parts)
    fill(spots, up_w, up_parts)

    @pl.loop(0, x.shape[0] // min(ROW_TILE, x.shape[0]))
    def _(i):
        at = pl.ds(pl.multiple_of(i * ROW_TILE, ROW_TILE), ROW_TILE)
        rows = x[at, :]
        gate = product(rows, gate_w[...])
        up = product(rows, up_w[...])
        raw[0, at, :] = low(gate)
        raw[1, at, :] = low(up)
        bend = jnp.tanh(GELU_SCALE * (gate + GELU_CUBE * gate * gate * gate))
        hidden[at, :] = low(0.5 * gate * (1.0 + bend) * up)


def hidden_back_kernel(count, spots, x, raw, *refs):
    parts, (out, whole) = refs[:count], refs[count:]
    fill(spots, whole, parts)

    @pl.loop(0, x.shape[0] // min(ROW_TILE, x.shape[0]))
    def _(i):
        at = pl.ds(pl.multiple_of(i * ROW_TILE, ROW_TILE), ROW_TILE)
        d_hidden = product(x[at, :], whole[...])
        gate = to_float(raw[0, at, :])
        up = to_float(raw[1, at, :])
        square = gate * gate
        bend = jnp.tanh(GELU_SCALE * gate * (1.0 + GELU_CUBE * square))
        plus = 0.5 * (1.0 + bend)
        slope = plus + 0.5 * gate * (1.0 - bend * bend) * GELU_SCALE * (
            1.0 + 3.0 * GELU_CUBE * square
        )
        out[0, at, :] = low(d_hidden * up * slope)
        out[1, at, :] = low(d_hidden * gate * plus)


def columns_kernel(count, spots, h, *refs):
    parts, (out, whole) = refs[:count], refs[count:]
    fill(spots, whole, parts)
    step = pl.program_id(0)
    width = out.shape[1]
    cols = min(512, width)


    @pl.loop(0, width // cols)
    def _(j):
        across_ = pl.ds(pl.multiple_of(j * cols, cols), cols)
        term = product_t(h[0], whole[across_, :])

        @pl.when(step == 0)
        def _():
            out[:, across_] = term

        @pl.when(step > 0)
        def _():
            out[:, across_] = out[:, across_] + term


def block_kernel(count, came, spots, *refs):
    xs, d, refs = refs[:count], refs[count], refs[count + 1 :]
    gots, refs = refs[:came], refs[came:]
    outs, turned = refs[:count], refs[count:]

    @pl.when(pl.program_id(0) == 0)
    def _():
        for x, t in zip(xs, turned):
            t[...] = x[...].T

    for i, (t, out) in enumerate(zip(turned, outs)):
        term = product(t[...], d[0])
        if came == 0:
            out[...] = low(term)
        elif gots[i].shape == out.shape:
            out[...] = low(term + to_float(gots[i][...]))
        else:
            cut = gots[i].shape[0]
            near, far = slice(i * cut, (i + 1) * cut), slice((1 - i) * cut, (2 - i) * cut)
            out[near, :] = low(term[near] + to_float(gots[i][...]))
            out[far, :] = low(term[far])


def grid_call(kernel, spots, grid, operands, in_specs, shapes, out_specs, scratch, flops, name):
    moved = sum(v.size * v.dtype.itemsize for v in (*operands, *jax.tree.leaves(shapes)))
    if flops == 0:
        moved = 0
    return pl.pallas_call(
        kernel,
        grid_spec=pltpu.PrefetchScalarGridSpec(
            num_scalar_prefetch=1,
            grid=grid,
            in_specs=in_specs,
            out_specs=out_specs,
            scratch_shapes=scratch,
        ),
        out_shape=shapes,
        compiler_params=pltpu.CompilerParams(
            dimension_semantics=("arbitrary",) * len(grid), vmem_limit_bytes=56 * 2**20
        ),
        cost_estimate=pl.CostEstimate(flops=flops, bytes_accessed=moved, transcendentals=0),
        name=name,
    )(spots, *operands)


def once(shape):
    return pl.BlockSpec(
        shape, lambda *index: (0,) * len(shape), pipeline_mode=pl.Buffered(buffer_count=1)
    )


def gate_up(x, spots, parts, up_parts, tile=512):
    count, (m, width), ff = len(parts), x.shape, parts[0].shape[1]
    tiles = ff // tile
    part_specs = [pl.BlockSpec((p.shape[0], tile), lambda n, s: (0, n)) for p in parts] * 2
    return grid_call(
        functools.partial(gate_up_kernel, count),
        spots,
        (tiles,),
        (x, *parts, *up_parts),
        [once((m, width))] + part_specs,
        [
            jax.ShapeDtypeStruct((2, m, ff), BF16),
            jax.ShapeDtypeStruct((m, ff), BF16),
            jax.ShapeDtypeStruct((2, width, ff), BF16),
        ],
        [
            pl.BlockSpec((2, m, tile), lambda n, s: (0, 0, n)),
            pl.BlockSpec((m, tile), lambda n, s: (0, n)),
            pl.BlockSpec((2, width, tile), lambda n, s: (0, 0, n)),
        ],
        [],
        4 * m * width * ff,
        "gate_up",
    )


def hidden_back(x, raw, spots, parts, tile=256):
    count, (m, width), ff = len(parts), x.shape, parts[0].shape[1]
    part_specs = [pl.BlockSpec((p.shape[0], tile), lambda n, s: (0, n)) for p in parts]
    return grid_call(
        functools.partial(hidden_back_kernel, count),
        spots,
        (ff // tile,),
        (x, raw, *parts),
        [once((m, width)), pl.BlockSpec((2, m, tile), lambda n, s: (0, 0, n))] + part_specs,
        jax.ShapeDtypeStruct((2, m, ff), BF16),
        pl.BlockSpec((2, m, tile), lambda n, s: (0, 0, n)),
        [pltpu.VMEM((width, tile), BF16)],
        2 * m * width * ff,
        "hidden_back",
    )


def columns_out(h, spots, parts, width, tile=1024):
    count, (groups, m, ff) = len(parts), h.shape
    tile = min(tile, ff)
    tiles = ff // tile
    part_specs = [pl.BlockSpec((p.shape[0], tile), lambda f, s: (0, f)) for p in parts]
    return grid_call(
        functools.partial(columns_kernel, count),
        spots,
        (groups * tiles,),
        (h, *parts),
        [pl.BlockSpec((1, m, tile), lambda f, s: (f // tiles, 0, f % tiles))] + part_specs,
        jax.ShapeDtypeStruct((m, width), F32),
        once((m, width)),
        [pltpu.VMEM((width, tile), BF16)],
        2 * groups * m * width * ff,
        "columns_out",
    )


def block_grads(x, d, chips, size, gots=(), tile=1024):
    (m, _), (groups, _, ff) = x.shape, d.shape
    count = len(chips)
    tile = min(tile, ff)
    tiles = ff // tile
    spots = jnp.stack(chips).astype(jnp.int32)
    if size % 128:
        xs = [lax.dynamic_slice_in_dim(x, chip * size, size, 1) for chip in chips]
        x_specs = [once((m, size))] * count
    else:
        xs = [x] * count
        x_specs = [
            pl.BlockSpec((m, size), functools.partial(lambda i, f, s: (0, s[i]), i))
            for i in range(count)
        ]
    return grid_call(
        functools.partial(block_kernel, count, len(gots)),
        spots,
        (groups * tiles,),
        (*xs, d, *gots),
        x_specs
        + [pl.BlockSpec((1, m, tile), lambda f, s: (f // tiles, 0, f % tiles))]
        + [pl.BlockSpec((v.shape[0], tile), lambda f, s: (0, f)) for v in gots],
        [jax.ShapeDtypeStruct((size, groups * ff), BF16)] * count,
        [pl.BlockSpec((size, tile), lambda f, s: (0, f))] * count,
        [pltpu.VMEM((size, m), BF16)] * count,
        0,
        "block_grads",
    )


def row_kernel(pairs, spots, *refs):
    xs, ds = refs[:pairs], refs[pairs : 2 * pairs]
    last, mine, theirs, both = refs[2 * pairs :]
    rows = mine.shape[0]
    core = spots[0]
    start = 0
    for x, d in zip(xs, ds):
        cols = d.shape[1]
        both[:, start : start + cols] = product_l(x[...], d[...])
        start += cols
    both[:, start:] = last[...]
    mine[...] = both[pl.ds(pl.multiple_of(core * rows, 128), rows), :]
    theirs[...] = low(both[pl.ds(pl.multiple_of((1 - core) * rows, 128), rows), :])


def row_grads(pairs, last, core, chips, rows):
    xs, ds = [x for x, _ in pairs], [d for _, d in pairs]
    cols = sum(d.shape[1] for d in ds) + last.shape[1]
    if rows % 128:

        def own_columns(values, which):
            blocks = values.reshape(values.shape[0], chips, 2, rows)
            return lax.dynamic_index_in_dim(blocks, which, 2, keepdims=False).reshape(
                values.shape[0], chips * rows
            )

        def terms(which):
            return jnp.concatenate(
                [product_l(own_columns(x, which), d) for x, d in pairs]
                + [own_columns(last.T, which).T],
                axis=1,
            )

        return terms(core), low(terms(1 - core))
    block = pl.BlockSpec((rows, cols), lambda j, s: (j, 0))
    return grid_call(
        functools.partial(row_kernel, len(pairs)),
        core.reshape(1).astype(jnp.int32),
        (chips,),
        (*xs, *ds, last),
        [pl.BlockSpec((x.shape[0], 2 * rows), lambda j, s: (0, j)) for x in xs]
        + [once(d.shape) for d in ds]
        + [pl.BlockSpec((2 * rows, last.shape[1]), lambda j, s: (j, 0))],
        [
            jax.ShapeDtypeStruct((chips * rows, cols), F32),
            jax.ShapeDtypeStruct((chips * rows, cols), BF16),
        ],
        [block, block],
        [pltpu.VMEM((2 * rows, cols), F32)],
        sum(4 * d.size * chips * rows for d in ds),
        "row_grads",
    )


def last_kernel(large, *refs):
    mine, theirs, refs = refs[0], refs[1], refs[2:]
    ff_terms, refs = refs[:6], refs[6:]
    (main, little, *ff_outs), refs = refs[:5], refs[5:]
    own, core_got, side_sent, side_got, first, got, refs = *refs[:6], refs[6:]
    ff_held, (ff_sent,), refs = refs[:6], refs[6:7], refs[7:]
    loads, core_send, core_recv, side_send, side_recv, ring_send, ring_recv, ff_send, ff_recv = refs
    hops = Hops()
    side = lax.axis_index("tensor")
    half = hops.chips // 2
    rows = main.shape[0]
    part = little.shape[1] // 2
    ff_cols = ff_sent.shape[2]
    cut = rows // 2
    greet([hops.above, hops.below, hops.partner, hops.across])
    order = [half]
    for k in range(1, half):
        order += [half - k, k - half]
    order.append(0)

    def rows_at(offset, top=0, size=rows):
        return pl.ds(pl.multiple_of(hops.chip_at(offset) * rows + top, 16), size)

    started, arriving = [], []
    for i, offset in enumerate(order):
        at = rows_at(offset)
        copy = remote(
            theirs.at[at], core_got.at[at], core_send, core_recv, (i,), hops.partner
        )
        copy.start()
        load = pltpu.make_async_copy(mine.at[at], own.at[at], loads.at[i])
        load.start()
        started.append(copy)
        arriving.append((copy, load))
    ff_loads = [
        pltpu.make_async_copy(source, target, loads.at[len(order) + i])
        for i, (source, target) in enumerate(zip(ff_terms, ff_held))
    ]
    for load in ff_loads:
        load.start()

    sides = {}
    my_part = pl.ds(pl.multiple_of(large + side * part, 128), part)
    their_part = pl.ds(pl.multiple_of(large + (1 - side) * part, 128), part)

    def ready(i):
        at = rows_at(order[i])
        copy, load = arriving[i]
        load.wait()
        copy.wait_recv()
        own[at, :] = own[at, :] + to_float(core_got[at, :])
        side_sent[at, :] = low(own[at, their_part])
        copy = remote(
            side_sent.at[at], side_got.at[at], side_send, side_recv, (i,), hops.across
        )
        copy.start()
        started.append(copy)
        sides[order[i]] = copy

    pieces = [(0, large // 2), (large // 2, large // 2), (large, part)]
    copies = {}

    def term(which, offset, top, size):
        at = rows_at(offset, top, size)
        start, cols = pieces[which]
        if which < 2:
            return own[at, start : start + cols]
        return own[at, my_part] + to_float(side_got[at, :])

    def send(which, direction, k, source, top, size):
        start, cols = pieces[which]
        copy = remote(
            source,
            got.at[direction, k, pl.ds(top, size), pl.ds(start, cols)],
            ring_send,
            ring_recv,
            (direction, k, which),
            hops.above if direction == 0 else hops.below,
        )
        copy.start()
        started.append(copy)
        copies[(which, direction, k)] = copy

    def step(which, k):
        start, cols = pieces[which]
        for direction in range(2):
            near, far = direction * cut, (1 - direction) * cut
            if k == 0:
                first[direction, :, start : start + cols] = low(term(which, half, near, cut))
                source = first.at[direction, :, pl.ds(start, cols)]
                send(which, direction, 0, source, near, cut)
                continue
            offset = (half - k) * (1 if direction == 0 else -1)
            copies[(which, direction, k - 1)].wait_recv()
            if k == 1:
                held = got[direction, 0, near : near + cut, start : start + cols]
                got[direction, 0, near : near + cut, start : start + cols] = low(
                    term(which, offset, near, cut) + to_float(held)
                )
                got[direction, 0, far : far + cut, start : start + cols] = low(
                    term(which, offset, far, cut)
                )
            else:
                held = got[direction, k - 1, :, start : start + cols]
                got[direction, k - 1, :, start : start + cols] = low(
                    term(which, offset, 0, rows) + to_float(held)
                )
            source = got.at[direction, k - 1, :, pl.ds(start, cols)]
            send(which, direction, k, source, 0, rows)

    def end_feed_forward():
        for load in ff_loads:
            load.wait()
        wide, wide_up, wide_down, narrow, narrow_up, narrow_down = ff_held
        my_rows = pl.ds(pl.multiple_of(hops.core * rows, 16), rows)
        their_rows = pl.ds(pl.multiple_of((1 - hops.core) * rows, 16), rows)
        my_cols = pl.ds(pl.multiple_of(hops.core * ff_cols, 128), ff_cols)
        groups = [
            (wide, wide_up, wide_down, 0),
            (wide, wide_up, wide_down, ff_cols),
            (narrow, narrow_up, narrow_down, 0),
        ]
        for i, (base, up, down, start) in enumerate(groups):
            cols = slice(start, start + ff_cols)

            def total(at):
                return to_float(base[at, cols]) + to_float(up[at, cols]) + to_float(down[at, cols])

            ff_sent[i] = total(their_rows)
            copy = remote(
                ff_sent.at[i], ff_outs[i].at[:, my_cols], ff_send, ff_recv, (i,), hops.partner
            )
            copy.start()
            ff_copies.append(copy)
            ff_outs[i][:, my_cols] = total(my_rows)

    ff_copies = []
    ready(0)
    step(0, 0)
    step(1, 0)
    ready(1)
    ready(2)
    sides[half].wait_recv()
    step(2, 0)
    for k in range(1, half):
        if k > 1:
            sides[half - k].wait_recv()
            sides[k - half].wait_recv()
            step(2, k)
        step(0, k)
        step(1, k)
        if k == 1:
            end_feed_forward()
        for i in range(2 * k + 1, min(2 * k + 3, len(order))):
            ready(i)
        if k == 1:
            sides[half - k].wait_recv()
            sides[k - half].wait_recv()
            step(2, k)
    sides[0].wait_recv()
    for which in (2, 0, 1):
        start, cols = pieces[which]
        for direction in range(2):
            copies[(which, direction, half - 1)].wait_recv()
        total = (
            term(which, 0, 0, rows)
            + to_float(got[0, half - 1, :, start : start + cols])
            + to_float(got[1, half - 1, :, start : start + cols])
        )
        if which < 2:
            main[:, start : start + cols] = total
        else:
            here = pl.ds(pl.multiple_of(side * part, 128), part)
            little[:, here] = total
            little_copy = remote(
                little.at[:, here],
                little.at[:, here],
                side_send,
                side_recv,
                (len(order),),
                hops.across,
            )
            little_copy.start()
            started.append(little_copy)
    for copy in ff_copies + [little_copy]:
        copy.wait_recv()
    for copy in ff_copies + started:
        copy.wait_send()


def last_reduce(mine, theirs, large, ff_terms):
    chips = lax.axis_size("dp") // 2
    half = chips // 2
    tall, cols = mine.shape
    rows = tall // chips
    part = (cols - large) // 2
    ff = ff_terms[3].shape[1]
    vmem = pl.BlockSpec(memory_space=pltpu.VMEM)
    dma = pltpu.SemaphoreType.DMA
    return pl.pallas_call(
        functools.partial(last_kernel, large),
        out_shape=[
            jax.ShapeDtypeStruct((rows, large), F32),
            jax.ShapeDtypeStruct((rows, 2 * part), F32),
        ]
        + [jax.ShapeDtypeStruct((rows, 2 * ff), F32)] * 3,
        in_specs=[ANY] * 8,
        out_specs=[vmem] * 5,
        scratch_shapes=[
            pltpu.VMEM((tall, cols), F32),
            pltpu.VMEM((tall, cols), BF16),
            pltpu.VMEM((tall, part), BF16),
            pltpu.VMEM((tall, part), BF16),
            pltpu.VMEM((2, rows // 2, large + part), BF16),
            pltpu.VMEM((2, half, rows, large + part), BF16),
        ]
        + [pltpu.VMEM(v.shape, v.dtype) for v in ff_terms]
        + [
            pltpu.VMEM((3, rows, ff), F32),
            dma((2 * half + 6,)),
            dma((2 * half,)),
            dma((2 * half,)),
            dma((2 * half + 1,)),
            dma((2 * half + 1,)),
            dma((2, half, 3)),
            dma((2, half, 3)),
            dma((3,)),
            dma((3,)),
        ],
        compiler_params=pltpu.CompilerParams(
            collective_id=2, has_side_effects=True, vmem_limit_bytes=56 * 2**20
        ),
        cost_estimate=pl.CostEstimate(
            flops=0, bytes_accessed=20 * mine.size * 4, transcendentals=0
        ),
        name="last_reduce",
    )(mine, theirs, *ff_terms)


def forward_kernel(hops_done, tile, x_own, *refs):
    counts = [2 * done + 1 for done in hops_done]
    gate_parts, up_down_parts, refs = refs[: counts[0]], refs[counts[0] : sum(counts)], refs[sum(counts) :]
    gu_parts = (gate_parts, up_down_parts)
    size, ff = gate_parts[0].shape
    dn_parts = [ref.at[:, pl.ds(ff, ff)] for ref in up_down_parts]
    hops_done = (*hops_done, hops_done[1])
    (x_out, gu_full, gu_land, dn_full, raw, hidden, result), refs = refs[:7], refs[7:]
    x, dn, hidden_v, pairs, core_sent, core_got, side_sent, side_got, refs = *refs[:8], refs[8:]
    x_send, x_recv, gu_send, gu_recv, dn_send, dn_recv, core_sems, side_sems, loads, stores = refs
    hops = Hops()
    half, chips = hops.chips // 2, hops.chips
    own = x_own.shape[0]
    cut = size // 2
    greet([hops.above, hops.below, hops.partner, hops.across])
    started, saved = [], []

    def begin(copy, where=started):
        copy.start()
        where.append(copy)
        return copy

    def spot(ref, offset, top=0, tall=size):
        return block_rows(ref, hops.chip_at(offset) * size + top, tall)

    def gu_hop(k):
        copies = []
        for direction, ahead in ((0, hops.above), (1, hops.below)):
            offset = (1 - k) * (1 if direction == 0 else -1)
            top, tall = (0, size) if k < half else (direction * cut, cut)
            for group in range(2):
                if k <= hops_done[group]:
                    continue
                target = spot(gu_land.at[group], offset, top, tall)
                if k == hops_done[group] + 1:
                    held = gu_parts[group][2 * k - 3 + direction]
                    source = held.at[pl.ds(pl.multiple_of(top, 16), tall), pl.ds(0, ff)]
                else:
                    source = target
                index = (direction, k - 1, group)
                copies.append(begin(remote(source, target, gu_send, gu_recv, index, ahead)))
        return copies

    def dn_hop(k):
        copies = []
        for direction, ahead in ((0, hops.above), (1, hops.below)):
            offset = (1 - k) * (1 if direction == 0 else -1)
            top, tall = (0, size) if k < half else (direction * cut, cut)
            block = spot(dn, offset, top, tall)
            copies.append(begin(remote(block, block, dn_send, dn_recv, (direction, k - 1), ahead)))
        return copies

    def arrive(copies):
        for copy in copies:
            copy.wait_recv()

    first_hop = min(hops_done[:2]) + 1
    moving = gu_hop(first_hop)
    mine, far = pl.ds(0, own), pl.ds(own, own)
    near, opposite = pl.ds(2 * own, own), pl.ds(3 * own, own)
    load_x = begin(pltpu.make_async_copy(x_own, x.at[mine], loads.at[0]), saved)
    places = [0]
    for k in range(1, hops_done[2] + 1):
        places += [-k, k]
    dn_loads = [
        begin(pltpu.make_async_copy(ref, spot(dn, offset), loads.at[1 + i]), saved)
        for i, (ref, offset) in enumerate(zip(dn_parts, places))
    ]
    loaded = len(saved)
    from_far = begin(remote(x_own, x.at[far], x_send, x_recv, (0,), hops.across))
    from_near = begin(remote(x_own, x.at[near], x_send, x_recv, (1,), hops.partner))
    from_near.wait_recv()
    load_x.wait()
    arrive(moving)
    if first_hop < half:
        moving = gu_hop(first_hop + 1)
    from_far.wait_recv()
    passed = begin(remote(x.at[far], x.at[opposite], x_send, x_recv, (2,), hops.partner))
    passed.wait_recv()
    begin(pltpu.make_async_copy(x, x_out, stores.at[0]), saved)
    for copy in dn_loads:
        copy.wait()
    for k in range(first_hop + 2, half + 1):
        arrive(moving)
        moving = gu_hop(k)
    if first_hop < half:
        arrive(moving)
    moving = dn_hop(hops_done[2] + 1)

    here, landed = [], []
    for done in hops_done[:2]:
        near_by = [0]
        for k in range(1, done + 1):
            near_by += [-k, k]
        here.append(near_by)
        landed.append([o for o in range(-half + 1, half + 1) if o not in near_by])
    tiles = ff // tile

    def body(*tiles_of):
        ins, (raw_tile, hidden_tile, weights) = tiles_of[:-3], tiles_of[-3:]
        step = pl.program_id(0)
        for group in range(2):
            for number, offset in enumerate(here[group] + landed[group]):
                at = pl.ds(pl.multiple_of(hops.chip_at(offset) * size, size), size)
                weights[group, at, :] = ins[group * chips + number][...]
        gate = product(x[...], weights[0])
        up = product(x[...], weights[1])
        raw_tile[0] = low(gate)
        raw_tile[1] = low(up)
        bend = jnp.tanh(GELU_SCALE * (gate + GELU_CUBE * gate * gate * gate))
        value = low(0.5 * gate * (1.0 + bend) * up)
        hidden_tile[...] = value
        hidden_v[:, pl.ds(pl.multiple_of(step * tile, tile), tile)] = value

    def part_spec(row):
        return pl.BlockSpec((size, tile), lambda n: (row, n))

    in_specs, operands = [], []
    for group in range(2):
        for ref in gu_parts[group]:
            in_specs.append(part_spec(0))
            operands.append(ref)
        for offset in landed[group]:
            in_specs.append(part_spec(hops.chip_at(offset)))
            operands.append(gu_land.at[group])
    m, width = x.shape
    pltpu.emit_pipeline(
        body,
        grid=(tiles,),
        in_specs=in_specs,
        out_specs=[
            pl.BlockSpec((2, m, tile), lambda n: (0, 0, n)),
            pl.BlockSpec((m, tile), lambda n: (0, n)),
            pl.BlockSpec((2, width, tile), lambda n: (0, 0, n)),
        ],
    )(*operands, raw, hidden, gu_full)

    order, core_copies, side_copies = [], [], []

    def block_out(offset):
        i = len(order)
        order.append(offset)
        at = pl.ds(pl.multiple_of(hops.chip_at(offset) * size, size), size)
        out = product_t(hidden_v[...], dn[at, :])
        pairs[i] = out[: 2 * own]
        core_sent[i] = low(out[2 * own :])
        copy = remote(
            core_sent.at[i], core_got.at[i], core_sems.at[0], core_sems.at[1], (i,), hops.partner
        )
        core_copies.append(begin(copy))

    def core_sum():
        i = len(side_copies)
        core_copies[i].wait_recv()
        both = pairs[i] + to_float(core_got[i])
        side_sent[i] = low(both[own:])
        copy = remote(
            side_sent.at[i], side_got.at[i], side_sems.at[0], side_sems.at[1], (i,), hops.across
        )
        side_copies.append(begin(copy))
        at = pl.ds(pl.multiple_of(hops.chip_at(order[i]) * size, size), size)
        result[:, at] = both[:own]

    def out_and_sum(offset):
        block_out(offset)
        if len(order) > 1:
            core_sum()

    for k in range(hops_done[2] + 1, half + 1):
        arrive(moving)
        if k < half:
            moving = dn_hop(k + 1)
        if k == hops_done[2] + 1:
            for offset in places:
                out_and_sum(offset)
        if k < half:
            out_and_sum(-k)
            out_and_sum(k)
        else:
            out_and_sum(half)
    begin(pltpu.make_async_copy(dn, dn_full, stores.at[1]), saved)
    core_sum()
    for i, copy in enumerate(side_copies):
        copy.wait_recv()
        at = pl.ds(pl.multiple_of(hops.chip_at(order[i]) * size, size), size)
        result[:, at] = result[:, at] + to_float(side_got[i])
    for copy in started:
        copy.wait_send()
    for copy in saved[loaded:]:
        copy.wait()


def forward(x_own, gate_parts, up_down_parts, tile=512):
    chips = lax.axis_size("dp") // 2
    half = chips // 2
    own, width = x_own.shape
    size, ff = gate_parts[0].shape
    hops_done = [len(parts) // 2 for parts in (gate_parts, up_down_parts)]
    tile = min(tile, ff)
    m = 4 * own
    dma = pltpu.SemaphoreType.DMA
    vmem = pl.BlockSpec(memory_space=pltpu.VMEM)
    return pl.pallas_call(
        functools.partial(forward_kernel, hops_done, tile),
        out_shape=[
            jax.ShapeDtypeStruct((m, width), BF16),
            jax.ShapeDtypeStruct((2, width, ff), BF16),
            jax.ShapeDtypeStruct((2, width, ff), BF16),
            jax.ShapeDtypeStruct((width, ff), BF16),
            jax.ShapeDtypeStruct((2, m, ff), BF16),
            jax.ShapeDtypeStruct((m, ff), BF16),
            jax.ShapeDtypeStruct((own, width), F32),
        ],
        in_specs=[ANY] * (1 + len(gate_parts) + len(up_down_parts)),
        out_specs=[ANY] * 6 + [vmem],
        scratch_shapes=[
            pltpu.VMEM((m, width), BF16),
            pltpu.VMEM((width, ff), BF16),
            pltpu.VMEM((m, ff), BF16),
            pltpu.VMEM((chips, 2 * own, size), F32),
            pltpu.VMEM((chips, 2 * own, size), BF16),
            pltpu.VMEM((chips, 2 * own, size), BF16),
            pltpu.VMEM((chips, own, size), BF16),
            pltpu.VMEM((chips, own, size), BF16),
            dma((3,)),
            dma((3,)),
            dma((2, half, 2)),
            dma((2, half, 2)),
            dma((2, half)),
            dma((2, half)),
            dma((2, chips)),
            dma((2, chips)),
            dma((1 + len(up_down_parts),)),
            dma((2,)),
        ],
        compiler_params=pltpu.CompilerParams(
            collective_id=3, has_side_effects=True, vmem_limit_bytes=60 * 2**20
        ),
        cost_estimate=pl.CostEstimate(
            flops=6 * m * width * ff, bytes_accessed=0, transcendentals=0
        ),
        name="forward",
    )(x_own, *gate_parts, *up_down_parts)


def backward_kernel(d_own, hidden, raw, dn_full, gu_full, rows_in, *refs):
    (x_out, d_gu_out, held_up, held_down, wide_up, wide_down, result), refs = refs[:7], refs[7:]
    x, dn, hid, d_gu, raw_v, gu_v, first, got, refs = *refs[:8], refs[8:]
    pairs, core_sent, core_got, side_sent, side_got, refs = *refs[:5], refs[5:]
    rows_v, wide_first, refs = *refs[:2], refs[2:]
    x_send, x_recv, ring_send, ring_recv, core_sems, side_sems, wide_sems, loads, stores = refs
    hops = Hops()
    half, chips = hops.chips // 2, hops.chips
    own = d_own.shape[0]
    size, ff = held_up.shape
    cut = size // 2
    m = x.shape[0]
    cols = min(512, ff)
    greet([hops.above, hops.below, hops.partner, hops.across])
    started, saved = [], []

    def begin(copy, where=started):
        copy.start()
        where.append(copy)
        return copy

    def load(source, target, number):
        copy = pltpu.make_async_copy(source, target, loads.at[number])
        copy.start()
        return copy

    def part(r):
        return pl.ds(r * own, own)

    from_far = begin(remote(d_own, x.at[part(1)], x_send, x_recv, (0,), hops.across))
    from_near = begin(remote(d_own, x.at[part(2)], x_send, x_recv, (1,), hops.partner))
    load_x = load(d_own, x.at[part(0)], 0)
    load_dn = load(dn_full, dn, 1)
    rows_order = (0, 2, 1, 3)
    raw_loads = {}

    def load_raw(i):
        r = rows_order[i]
        raw_loads[r] = load(raw.at[:, part(r)], raw_v.at[i % 2], 3 + i)

    def load_gu(j):
        return load(gu_full.at[:, pl.ds(j * size, size)], gu_v.at[j % 2], 7 + j)

    load_raw(0)
    load_raw(1)
    load_hid = load(hidden, hid, 2)
    far_block = pl.ds(pl.multiple_of(hops.chip_at(half) * size, size), size)
    load_rows = load(rows_in.at[:, far_block], rows_v, 7 + chips)

    def hidden_part(i):
        r = rows_order[i]
        at = part(r)
        raw_loads[r].wait()

        @pl.loop(0, ff // cols)
        def _(c):
            across_ = pl.ds(pl.multiple_of(c * cols, cols), cols)
            d_hidden = product(x[at, :], dn[:, across_])
            gate = to_float(raw_v[i % 2, 0, :, across_])
            up = to_float(raw_v[i % 2, 1, :, across_])
            square = gate * gate
            bend = jnp.tanh(GELU_SCALE * gate * (1.0 + GELU_CUBE * square))
            plus = 0.5 * (1.0 + bend)
            slope = plus + 0.5 * gate * (1.0 - bend * bend) * GELU_SCALE * (
                1.0 + 3.0 * GELU_CUBE * square
            )
            d_gu[0, at, across_] = low(d_hidden * up * slope)
            d_gu[1, at, across_] = low(d_hidden * gate * plus)

        if i + 2 < 4:
            load_raw(i + 2)

    copies = {}

    def ring_step(k):
        for direction, ahead in ((0, hops.above), (1, hops.below)):
            near, far = direction * cut, (1 - direction) * cut
            offset = (half - k) * (1 if direction == 0 else -1)
            at = pl.ds(pl.multiple_of(hops.chip_at(offset) * size, size), size)
            term = product_l(x[:, at], hid[...])
            if k == 0:
                first[direction] = low(term[near : near + cut])
                source = first.at[direction]
                target = got.at[direction, 0, pl.ds(near, cut)]
            else:
                copies[(direction, k - 1)].wait_recv()
                came = got.at[direction, k - 1]
                if k == 1:
                    came[near : near + cut, :] = low(
                        term[near : near + cut] + to_float(came[near : near + cut, :])
                    )
                    came[far : far + cut, :] = low(term[far : far + cut])
                else:
                    came[...] = low(term + to_float(came[...]))
                source = came
                if k < half - 2:
                    target = got.at[direction, k]
                else:
                    target = held_up if direction == 0 else held_down
            copies[(direction, k)] = begin(
                remote(source, target, ring_send, ring_recv, (direction, k), ahead)
            )

    core_copies, side_copies = [], []

    def block_out(j, loading):
        loading.wait()
        out = product_t(d_gu[0], gu_v[j % 2, 0]) + product_t(d_gu[1], gu_v[j % 2, 1])
        pairs[j] = out[: 2 * own]
        core_sent[j] = low(out[2 * own :])
        copy = remote(
            core_sent.at[j], core_got.at[j], core_sems.at[0], core_sems.at[1], (j,), hops.partner
        )
        core_copies.append(begin(copy))

    def core_sum(j):
        core_copies[j].wait_recv()
        both = pairs[j] + to_float(core_got[j])
        side_sent[j] = low(both[own:])
        copy = remote(
            side_sent.at[j], side_got.at[j], side_sems.at[0], side_sems.at[1], (j,), hops.across
        )
        side_copies.append(begin(copy))
        result[:, j * size : (j + 1) * size] = both[:own]

    load_x.wait()
    load_dn.wait()
    hidden_part(0)
    from_near.wait_recv()
    hidden_part(1)
    from_far.wait_recv()
    passed = begin(remote(x.at[part(1)], x.at[part(3)], x_send, x_recv, (2,), hops.partner))
    hidden_part(2)
    passed.wait_recv()
    load_hid.wait()
    ring_step(0)
    gu_loads = {0: load_gu(0), 1: load_gu(1)}
    hidden_part(3)
    steps = list(range(1, half - 1))
    if steps:
        ring_step(steps.pop(0))
    load_rows.wait()
    for group in range(2):
        wide = product_l(rows_v[...], d_gu[group])
        for direction in range(2):
            wide_first[direction, :, group * ff : (group + 1) * ff] = low(
                wide[direction * cut : (direction + 1) * cut]
            )
    wide_copies = [
        begin(
            remote(
                wide_first.at[direction],
                target,
                wide_sems.at[0],
                wide_sems.at[1],
                (direction,),
                ahead,
            )
        )
        for direction, target, ahead in (
            (0, wide_up, hops.above),
            (1, wide_down, hops.below),
        )
    ]
    begin(pltpu.make_async_copy(x, x_out, stores.at[0]), saved)
    begin(pltpu.make_async_copy(d_gu, d_gu_out, stores.at[1]), saved)
    for j in range(chips):
        block_out(j, gu_loads[j])
        if j + 2 < chips:
            gu_loads[j + 2] = load_gu(j + 2)
        if j > 0:
            core_sum(j - 1)
        if j == 3 and steps:
            ring_step(steps.pop(0))
    core_sum(chips - 1)
    for k in steps:
        ring_step(k)
    for j, copy in enumerate(side_copies):
        copy.wait_recv()
        at = slice(j * size, (j + 1) * size)
        result[:, at] = result[:, at] + to_float(side_got[j])
    for direction in range(2):
        copies[(direction, half - 2)].wait_recv()
        wide_copies[direction].wait_recv()
    for copy in started:
        copy.wait_send()
    for copy in saved:
        copy.wait()


def backward(d_own, hidden, raw, dn_full, gu_full, rows_in):
    chips = lax.axis_size("dp") // 2
    half = chips // 2
    own, width = d_own.shape
    m, ff = hidden.shape
    size = width // chips
    dma = pltpu.SemaphoreType.DMA
    vmem = pl.BlockSpec(memory_space=pltpu.VMEM)
    return pl.pallas_call(
        backward_kernel,
        out_shape=[
            jax.ShapeDtypeStruct((m, width), BF16),
            jax.ShapeDtypeStruct((2, m, ff), BF16),
            jax.ShapeDtypeStruct((size, ff), BF16),
            jax.ShapeDtypeStruct((size, ff), BF16),
            jax.ShapeDtypeStruct((size // 2, 2 * ff), BF16),
            jax.ShapeDtypeStruct((size // 2, 2 * ff), BF16),
            jax.ShapeDtypeStruct((own, width), F32),
        ],
        in_specs=[ANY] * 6,
        out_specs=[ANY] * 6 + [vmem],
        scratch_shapes=[
            pltpu.VMEM((m, width), BF16),
            pltpu.VMEM((width, ff), BF16),
            pltpu.VMEM((m, ff), BF16),
            pltpu.VMEM((2, m, ff), BF16),
            pltpu.VMEM((2, 2, own, ff), BF16),
            pltpu.VMEM((2, 2, size, ff), BF16),
            pltpu.VMEM((2, size // 2, ff), BF16),
            pltpu.VMEM((2, half - 2, size, ff), BF16),
            pltpu.VMEM((chips, 2 * own, size), F32),
            pltpu.VMEM((chips, 2 * own, size), BF16),
            pltpu.VMEM((chips, 2 * own, size), BF16),
            pltpu.VMEM((chips, own, size), BF16),
            pltpu.VMEM((chips, own, size), BF16),
            pltpu.VMEM((m, size), BF16),
            pltpu.VMEM((2, size // 2, 2 * ff), BF16),
            dma((3,)),
            dma((3,)),
            dma((2, half - 1)),
            dma((2, half - 1)),
            dma((2, chips)),
            dma((2, chips)),
            dma((2, 2)),
            dma((8 + chips,)),
            dma((2,)),
        ],
        compiler_params=pltpu.CompilerParams(
            collective_id=4, has_side_effects=True, vmem_limit_bytes=60 * 2**20
        ),
        cost_estimate=pl.CostEstimate(
            flops=6 * m * width * ff, bytes_accessed=0, transcendentals=0
        ),
        name="backward",
    )(d_own, hidden, raw, dn_full, gu_full, rows_in)


def prepare_kernel(q_cols, kv_cols, spots, x, gain, w, cos, sin, gains, rows, raw, query, kv):
    turn = HD // 2
    values = to_float(x[...])
    scale = lax.rsqrt(jnp.mean(values * values, axis=-1, keepdims=True) + EPS)
    rows[...] = low(values * scale * gain[...])
    raw[...] = product(rows[...], w[...])
    cosines, sines = cos[...], sin[...]
    for start in range(0, q_cols + 2 * kv_cols, HD):
        at = slice(start, start + HD)
        head = raw[:, at]
        head = head * lax.rsqrt(jnp.mean(head * head, axis=-1, keepdims=True) + EPS)
        if start < q_cols + kv_cols:
            which = 0 if start < q_cols else 1
            head = head * gains[which : which + 1, :]
            front, rear = head[:, :turn], head[:, turn:]
            head = jnp.concatenate(
                [front * cosines - rear * sines, rear * cosines + front * sines], axis=1
            )
        if start < q_cols:
            query[start // HD] = low(head)
        else:
            kv[:, start - q_cols : start - q_cols + HD] = low(head)


def prepare(x, gain, w, cos, sin, gains, side, q_cols):
    (tall, width), cols = x.shape, w.shape[1]
    tile = tall // 2
    kv_cols = (cols - q_cols) // 2
    natural = lax.rem(jnp.arange(2) + side, 2).astype(jnp.int32)

    def straight(columns):
        return pl.BlockSpec((tile, columns), lambda t, s: (t, 0))

    return grid_call(
        functools.partial(prepare_kernel, q_cols, kv_cols),
        natural,
        (2,),
        (x, gain, w, cos, sin, gains),
        [
            straight(width),
            once(gain.shape),
            once(w.shape),
            straight(HD // 2),
            straight(HD // 2),
            once(gains.shape),
        ],
        [
            jax.ShapeDtypeStruct((tall, width), BF16),
            jax.ShapeDtypeStruct((tall, cols), F32),
            jax.ShapeDtypeStruct((q_cols // HD, tall, HD), BF16),
            jax.ShapeDtypeStruct((tall, 2 * kv_cols), BF16),
        ],
        [
            straight(width),
            straight(cols),
            pl.BlockSpec((q_cols // HD, tile, HD), lambda t, s: (0, t, 0)),
            pl.BlockSpec((tile, 2 * kv_cols), lambda t, s: (s[t], 0)),
        ],
        [],
        2 * tall * width * cols,
        "prepare",
    )


def prepare_back_kernel(q_cols, kv_cols, spots, raw, d_q, d_kv, after, before, cos, sin, gains, *refs):
    out, gain_grads = refs
    tall = raw.shape[0]
    turn = HD // 2
    cosines, sines = cos[...], sin[...]

    @pl.when(pl.program_id(0) == 0)
    def _():
        gain_grads[...] = jnp.zeros_like(gain_grads)

    early = spots[1 + pl.program_id(0)] < spots[0]
    more = to_float(after[...]) + jnp.where(early, to_float(before[...]), 0.0)

    def back(values, d, gain):
        scale = lax.rsqrt(jnp.mean(values * values, axis=-1, keepdims=True) + EPS)
        d_gain = d if gain is None else d * gain
        inner = jnp.mean(values * d_gain, axis=-1, keepdims=True)
        return scale * d_gain - values * (scale * scale * scale * inner), values * scale * d

    def unturn(d):
        front, rear = d[:, :turn], d[:, turn:]
        return jnp.concatenate(
            [front * cosines + rear * sines, rear * cosines - front * sines], axis=1
        )

    for start in range(0, q_cols + 2 * kv_cols, HD):
        at = slice(start, start + HD)
        values = raw[:, at]
        if start < q_cols:
            d, which = unturn(d_q[start // HD]), 0
        else:
            here = slice(start - q_cols, start - q_cols + HD)
            d = d_kv[:, here] + more[:, here]
            which = 1
            if start < q_cols + kv_cols:
                d = unturn(d)
        if start < q_cols + kv_cols:
            d_values, for_gain = back(values, d, gains[which : which + 1, :])
            gain_grads[which : which + 1, :] = gain_grads[which : which + 1, :] + jnp.sum(
                for_gain, axis=0, keepdims=True
            )
        else:
            d_values, _ = back(values, d, None)
        out[:, at] = low(d_values)


def prepare_back(raw, d_q, d_kv, after, before, cos, sin, gains, side, own, tile=128):
    tall, cols = raw.shape
    kv_cols = d_kv.shape[1] // 2
    q_cols = cols - 2 * kv_cols
    tiles = tall // tile
    near = before.shape[0] // tile
    natural = lax.rem(jnp.arange(tiles) + side * (own // tile), tiles)
    spots = jnp.concatenate([jnp.full((1,), near), natural]).astype(jnp.int32)

    def straight(width):
        return pl.BlockSpec((tile, width), lambda t, s: (t, 0))

    def ordered(width):
        return pl.BlockSpec((tile, width), lambda t, s: (s[1 + t], 0))

    return grid_call(
        functools.partial(prepare_back_kernel, q_cols, kv_cols),
        spots,
        (tiles,),
        (raw, d_q, d_kv, after, before, cos, sin, gains),
        [
            straight(cols),
            pl.BlockSpec((q_cols // HD, tile, HD), lambda t, s: (0, t, 0)),
            ordered(2 * kv_cols),
            ordered(2 * kv_cols),
            pl.BlockSpec((tile, 2 * kv_cols), lambda t, s: (jnp.minimum(s[1 + t], near - 1), 0)),
            straight(HD // 2),
            straight(HD // 2),
            once(gains.shape),
        ],
        [jax.ShapeDtypeStruct((tall, cols), BF16), jax.ShapeDtypeStruct((8, HD), F32)],
        [straight(cols), once((8, HD))],
        [],
        10 * raw.size,
        "prepare_back",
    )


class Gather:
    def __init__(self, ring, block):
        self.ring = ring
        self.rows = block.shape[0]
        self.held = [block, block]
        self.parts = [(0, 0, block)]
        self.step_count = 0

    def step(self):
        ring, half = self.ring, self.ring.chips // 2
        self.step_count += 1
        k = self.step_count
        going_up, going_down = self.held
        if k < half:
            self.held = [ring.up(going_up), ring.down(going_down)]
            self.parts += [(-k, 0, self.held[0]), (k, 0, self.held[1])]
        else:
            cut = self.rows // 2
            self.held = [ring.up(going_up[:cut]), ring.down(going_down[cut:])]
            self.parts += [(half, 0, self.held[0]), (half, cut, self.held[1])]

    def pieces(self):
        spots = [self.ring.chip_at(o) * self.rows + row for o, row, _ in self.parts]
        return jnp.stack(spots).astype(jnp.int32), [part for _, _, part in self.parts]


class BlockReduce:
    def __init__(self, ring, x, d, size):
        self.ring, self.x, self.d, self.size = ring, x, d, size
        self.step_count = 0
        self.held = []

    def offsets(self):
        half = self.ring.chips // 2
        k = self.step_count + 1
        return (half,) if k == 1 else (half + 1 - k, k - 1 - half)

    def blocks(self, offsets, gots=()):
        chips = [self.ring.chip_at(o) for o in offsets]
        return block_grads(self.x, self.d, chips, self.size, gots)

    def terms(self):
        return self.blocks(self.offsets())

    def last_term(self):
        return self.blocks((0,))[0]

    def step(self, terms=None, *beside):
        ring, half = self.ring, self.ring.chips // 2
        self.step_count += 1
        k = self.step_count
        cut = self.size // 2
        if k == 1:
            (term,) = self.blocks((half,))
            up, down = term[:cut], term[cut:]
        elif terms is None:
            up, down = self.blocks((half + 1 - k, k - 1 - half), self.held)
        else:
            up = low(to_float(terms[0]) + to_float(self.held[0]))
            down = low(to_float(terms[1]) + to_float(self.held[1]))
        up, down, beside = tie(up, down, beside)
        self.held = [ring.up(up), ring.down(down)]
        return beside


def region(body):
    shapes = jax.eval_shape(body)
    yes = lax.optimization_barrier(jnp.array(True))
    return lax.cond(
        yes,
        body,
        lambda: jax.tree.map(lambda v: jnp.zeros(v.shape, v.dtype), shapes),
    )


def meet(rings, *values):
    held, values = tie([r.held for r in rings], values)
    for r, h in zip(rings, held):
        r.held = h
    return values if len(values) != 1 else values[0]


def local(
    tokens,
    layer_input,
    block_ids,
    block_table,
    w_query,
    w_key,
    w_value,
    w_output,
    w_left,
    w_right,
    w_gate,
    w_up,
    w_down,
    w_layer_gate,
    w_layer_proj,
    query_gain,
    key_gain,
    gain_input,
    gain_attn_out,
    gain_laurel,
    gain_ffw_in,
    gain_ffw_out,
    gain_layer_out,
    out_grad,
):
    ring = Ring()
    side = lax.axis_index("tensor")
    core = ring.core
    rows = w_query.shape[0]
    own = tokens.shape[0]
    width = tokens.shape[1]
    q_cols = w_query.shape[1]
    kv_cols = w_key.shape[1]
    rank = w_left.shape[1]
    small = w_layer_gate.shape[1]
    ff_cols = w_gate.shape[1] // 2
    chips = ring.chips

    gain_list = [
        gain_input,
        gain_attn_out,
        gain_laurel,
        gain_ffw_in,
        gain_ffw_out,
        gain_layer_out,
        query_gain,
        key_gain,
    ]
    gains = jnp.stack([jnp.pad(to_float(v), (0, 128 - v.shape[0])) for v in gain_list])
    gains = jnp.pad(gains, ((0, 8), (0, 0)))
    half = chips // 2
    if rows % 128 == 0:
        blocks = [
            [(w_query, False), (w_key, False), (w_value, False)],
            [(w_output, True)],
            [(w_left, False), (w_right, True), (w_layer_gate, False), (w_layer_proj, True)],
        ]
        down_source = (w_down, True)
    else:
        blocks = [
            [(jnp.concatenate([w_query, w_key, w_value], axis=1), False)],
            [(w_output.T, False)],
            [(jnp.concatenate([w_left, w_right.T, w_layer_gate, w_layer_proj.T], axis=1), False)],
        ]
        down_source = (w_down.T, False)
    (qkv_full, output_t, small_full, gains_full), (*ff_own, both_tokens) = first_gather(
        blocks + [[(gains, False)]], w_gate, w_up, down_source, tokens
    )
    left_full = small_full[:, :rank]
    right_t = small_full[:, rank : 2 * rank]
    lgate_full = small_full[:, 2 * rank : 2 * rank + small]
    lproj_t = small_full[:, 2 * rank + small : 2 * rank + 2 * small]
    gains_full = gains_full.reshape(ring.devices, 16, 128)
    head_part = query_gain.shape[0]
    (
        input_scale,
        attn_scale,
        laurel_scale,
        ffw_in_scale,
        ffw_out_scale,
        layer_scale,
    ) = (gains_full[:, i, :rows].reshape(width) for i in range(6))
    query_scale, key_scale = (gains_full[:, i, :head_part].reshape(HD) for i in (6, 7))

    piece_len = 2 * own
    seq_total = block_ids.shape[1]
    per_seq = seq_total // piece_len
    dp_index = lax.axis_index("dp")
    row_index = dp_index // per_seq
    slot = lax.rem(dp_index, per_seq)
    first = slot * piece_len
    has_before = slot > 0
    has_after = slot < per_seq - 1
    natural = jnp.arange(piece_len, dtype=jnp.int32)
    here = first + lax.rem(natural + side * own, piece_len)
    cosines, sines = rope_tables(here, HD)
    reach_after = min(256, piece_len)
    forward_pairs = [(i, i + 1) for i in range(ring.devices - 1)]
    backward_pairs = [(i + 1, i) for i in range(ring.devices - 1)]

    def in_order(values):
        return jnp.where(
            side == 0, values, jnp.concatenate([values[own:], values[:own]], axis=0)
        )

    ids_row = lax.dynamic_index_in_dim(block_ids, row_index, 0, keepdims=False)
    table_row = lax.dynamic_index_in_dim(block_table, row_index, 0, keepdims=False)
    own_ids = lax.dynamic_slice_in_dim(ids_row, first, piece_len, 0)
    before_ids = lax.dynamic_slice_in_dim(ids_row, jnp.maximum(first - piece_len, 0), piece_len, 0)
    before_ids = jnp.where(has_before, before_ids, -2)
    after_ids = lax.dynamic_slice_in_dim(
        ids_row, jnp.minimum(first + piece_len, seq_total - reach_after), reach_after, 0
    )
    after_ids = jnp.where(has_after, after_ids, -2)
    key_ids = jnp.concatenate([before_ids, own_ids, after_ids], axis=0)
    query_ids = in_order(own_ids)
    block_count = block_table.shape[-1]
    number_rows = jnp.arange(block_count, dtype=jnp.int32)
    sees_last = jnp.sum(
        jnp.where(number_rows[None, :] == number_rows[:, None] - 1, table_row, 0), axis=1
    )
    query_sees = jnp.sum(
        jnp.where(query_ids[:, None] == number_rows[None, :], sees_last[None, :], 0), axis=1
    )
    previous_ids = jnp.where(query_sees == 1, query_ids - 1, query_ids)

    both_gains = jnp.pad(jnp.stack([query_scale, key_scale]), ((0, 6), (0, 0)))

    heads_local = q_cols // HD
    all_rows = heads_local * piece_len

    def scores_for(query_low, keys):
        allowed = (query_ids[:, None] == key_ids[None, :]) | (
            previous_ids[:, None] == key_ids[None, :]
        )
        scores = product_t(query_low, keys).reshape(heads_local, piece_len, -1)
        return jnp.where(allowed[None], scores, NEGATIVE)

    def sum_sides(partial, beside=None):
        got = across(low(partial[own:]))
        if beside is None:
            return partial[:own] + to_float(got)
        got, beside = tie(got, beside())
        return partial[:own] + to_float(got), beside

    def both_sides(values, beside=None):
        got = across(values)
        if beside is None:
            return jnp.concatenate([values, got], axis=0)
        got, beside = tie(got, beside())
        return jnp.concatenate([values, got], axis=0), beside

    def four_ways(values):
        pair = both_sides(values)
        return jnp.concatenate([pair, ring.swap(pair)], axis=0)

    def sum_four(partial, beside=None):
        pair = partial[: 2 * own] + to_float(ring.swap(low(partial[2 * own :])))
        return sum_sides(pair, beside)

    def attend(query_low, kv_all):
        scores = scores_for(query_low, kv_all[:, :HD])
        highest = jnp.max(scores, axis=-1, keepdims=True)
        weights_exp = jnp.exp(scores - highest)
        totals = jnp.sum(weights_exp, axis=-1, keepdims=True)
        probs_low = low(weights_exp / totals).reshape(all_rows, -1)
        attended = low(product(probs_low, kv_all[:, HD:]))
        attended = attended.reshape(heads_local, piece_len, HD).transpose(1, 0, 2)
        return highest + jnp.log(totals), attended.reshape(piece_len, q_cols)

    fused = (2 * rows) % 256 == 0
    gate_ring, more_ring = (Gather(ring, v) for v in ff_own)
    gate_ring.step()
    seq_rows, qkv_raw, query_low, kv_own = region(
        lambda: prepare(
            both_tokens, input_scale[None], qkv_full, cosines, sines, both_gains, side, q_cols
        )
    )
    query_low = query_low.reshape(all_rows, HD)
    kv_own = meet([gate_ring], kv_own)
    kv_before = lax.ppermute(kv_own, "dp", forward_pairs)
    kv_after = lax.ppermute(kv_own[:reach_after], "dp", backward_pairs)
    kv_before, kv_after, more_ring.held, gate_ring.held = tie(
        kv_before, kv_after, more_ring.held, gate_ring.held
    )
    more_ring.step()
    gate_ring.step()
    kv_all = jnp.concatenate([kv_before, kv_own, kv_after], axis=0)
    def join(heads_low):
        attn_out = sum_sides(product_t(heads_low, output_t))
        normed = norm_gain(to_float(tokens), input_scale)
        left_low = low(product(low(normed), left_full))
        right_out = product_t(left_low, right_t)
        laurel_normed = norm_gain(right_out, laurel_scale)
        attn_normed = norm_gain(attn_out, attn_scale)
        mixed = (to_float(tokens) + attn_normed + (normed + laurel_normed)) * ROOT_HALF
        return attn_out, left_low, right_out, mixed, low(norm_gain(mixed, ffw_in_scale))

    def attend_and_join():
        log_totals, heads_low = attend(query_low, kv_all)
        return log_totals, heads_low, *join(heads_low)

    log_totals, heads_low, attn_out, left_low, right_out, mixed, ffw_low = region(attend_and_join)
    ffw_low = meet([gate_ring, more_ring], ffw_low)

    if fused:
        ffw_rows, gu_weights, _, dn_whole, raw, hidden_low, ffw_out = forward(
            ffw_low,
            [part for _, _, part in gate_ring.parts],
            [part for _, _, part in more_ring.parts],
        )
        dn_spots, dn_parts = jnp.zeros((1,), jnp.int32), [dn_whole]
    else:
        ffw_rows = four_ways(ffw_low)
        for weights_ring in (gate_ring, more_ring):
            while weights_ring.step_count < half:
                weights_ring.step()
        gu_spots, gate_parts = gate_ring.pieces()
        dn_spots, more_parts = more_ring.pieces()
        up_parts = [part[:, :ff_cols] for part in more_parts]
        dn_parts = [part[:, ff_cols:] for part in more_parts]
        raw, hidden_low, gu_weights = gate_up(ffw_rows, gu_spots, gate_parts, up_parts)
        ffw_out = sum_four(columns_out(hidden_low[None], dn_spots, dn_parts, width))
    ffw_out_normed, ffw_out_back = jax.vjp(norm_gain, ffw_out, ffw_out_scale)
    block_mid = mixed + ffw_out_normed
    mid_low = low(block_mid)
    layer_pre = product(mid_low, lgate_full)

    def layer_gate_fn(pre_values, per_layer):
        return gelu_tanh(pre_values) * per_layer

    gated, gated_back = jax.vjp(layer_gate_fn, layer_pre, to_float(layer_input))
    gated_low = low(gated)
    layer_proj = product_t(gated_low, lproj_t)
    proj_normed, proj_back = jax.vjp(norm_gain, layer_proj, layer_scale)
    result = block_mid + proj_normed

    grad_out = to_float(out_grad)
    d_proj, d_layer_scale = proj_back(grad_out)
    d_proj_low = low(d_proj)
    d_gated = product(d_proj_low, lproj_t)
    d_pre, grad_layer_input = gated_back(d_gated)
    d_pre_low = low(d_pre)
    d_mid = grad_out + product_t(d_pre_low, lgate_full)
    d_ffw_out, d_ffw_out_scale = ffw_out_back(d_mid)
    if fused:
        d_ffw_rows, d_gate_up, *held, d_ffw_normed = backward(
            low(d_ffw_out), hidden_low, raw, dn_whole, gu_weights, ffw_rows
        )
        rd = BlockReduce(ring, d_ffw_rows, hidden_low[None], 2 * rows)
        rd.held, rd.step_count = held[:2], half - 1
        rg = BlockReduce(ring, ffw_rows, d_gate_up, 2 * rows)
        rg.held, rg.step_count = held[2:], 1
    else:
        d_ffw_rows = four_ways(low(d_ffw_out))
        rd = BlockReduce(ring, d_ffw_rows, hidden_low[None], 2 * rows)
        for _ in range(half - 1):
            rd.step()
            meet([rd])
        d_gate_up = hidden_back(d_ffw_rows, raw, dn_spots, dn_parts)
        d_ffw_normed = sum_four(
            product_t(d_gate_up[0], gu_weights[0]) + product_t(d_gate_up[1], gu_weights[1])
        )
        rg = BlockReduce(ring, ffw_rows, d_gate_up, 2 * rows)
        for _ in range(half - 3):
            rg.step()
            meet([rg])
    rd.step()
    rg.step()

    def back_34():
        _, back = jax.vjp(norm_gain, mixed, ffw_in_scale)
        d_mixed_extra, d_ffw_in_scale = back(d_ffw_normed)
        d_branch = (d_mid + d_mixed_extra) * ROOT_HALF
        _, back = jax.vjp(norm_gain, attn_out, attn_scale)
        d_attn, d_attn_scale = back(d_branch)
        d_attn_rows, terms = both_sides(low(d_attn), rg.terms)
        d_heads = low(product(d_attn_rows, output_t)).reshape(piece_len, heads_local, HD)
        d_heads = d_heads.transpose(1, 0, 2).reshape(all_rows, HD)
        keys, values = kv_all[:, :HD], kv_all[:, HD:]
        probs = jnp.exp(scores_for(query_low, keys) - log_totals)
        d_values = product_l(low(probs).reshape(all_rows, -1), d_heads)
        d_probs = product_t(d_heads, values).reshape(probs.shape)
        deltas = jnp.sum(probs * d_probs, axis=-1, keepdims=True)
        d_scores = low(probs * (d_probs - deltas)).reshape(all_rows, -1)
        d_keys = product_l(d_scores, query_low)
        d_query_rot = product(d_scores, keys).reshape(heads_local, piece_len, HD)
        d_kv_all = jnp.concatenate([d_keys, d_values], axis=1)
        to_before = low(d_kv_all[:piece_len])
        to_after = low(d_kv_all[2 * piece_len :])
        d_kv_own = d_kv_all[piece_len : 2 * piece_len]
        moving = (to_before, to_after)
        kept = (d_ffw_in_scale, d_attn_scale, d_branch, d_attn_rows, d_kv_own)
        return terms, moving, kept, d_query_rot

    terms, moving, kept, d_query_rot = meet([rd, rg], *region(back_34))
    d_ffw_in_scale, d_attn_scale, d_branch, d_attn_rows, d_kv_own = kept
    from_after = lax.ppermute(moving[0], "dp", backward_pairs)
    from_before = lax.ppermute(moving[1], "dp", forward_pairs)
    from_after, from_before = rg.step(terms, from_after, from_before)

    def back_5():
        d_qkv_low, gain_sums = prepare_back(
            qkv_raw,
            d_query_rot,
            d_kv_own,
            from_after,
            from_before,
            cosines,
            sines,
            both_gains,
            side,
            own,
        )
        d_more, ends = sum_sides(
            product_t(d_qkv_low, qkv_full), lambda: (rd.last_term(), rg.last_term())
        )
        return d_more, ends, d_qkv_low, gain_sums[0], gain_sums[1]

    d_more, ends, d_qkv_low, query_scale_grad, key_scale_grad = meet([rg], *region(back_5))
    rg.step()

    def head_gain_back(grads):
        padded = jnp.pad(grads.reshape(ring.devices, head_part), ((0, 0), (0, rows - head_part)))
        return padded.reshape(width)

    def back_6():
        normed, input_norm_back = jax.vjp(norm_gain, to_float(tokens), input_scale)
        _, laurel_back = jax.vjp(norm_gain, right_out, laurel_scale)
        d_right, d_laurel_scale = laurel_back(d_branch)
        d_right_low = low(d_right)
        d_left_low = low(product(d_right_low, right_t))
        d_normed = d_branch + product_t(d_left_low, left_full)
        d_normed = d_normed + d_more
        d_inputs_extra, d_input_scale = input_norm_back(d_normed)
        grad_tokens = d_branch + d_inputs_extra
        gain_grads = jnp.stack(
            [
                d_input_scale,
                d_attn_scale,
                d_laurel_scale,
                d_ffw_in_scale,
                d_ffw_out_scale,
                d_layer_scale,
                head_gain_back(query_scale_grad),
                head_gain_back(key_scale_grad),
            ],
            axis=0,
        )
        gain_grads = jnp.pad(gain_grads, ((0, 120), (0, 0))).T
        pairs = [
            (d_attn_rows, heads_low),
            (seq_rows, d_qkv_low),
            (mid_low, d_pre_low),
            (d_proj_low, gated_low),
            (low(normed), d_left_low),
            (d_right_low, left_low),
        ]
        return grad_tokens, row_grads(pairs, gain_grads, core, chips, rows)

    grad_tokens, (mine, theirs) = meet([rg], *region(back_6))
    down_end, gate_up_end = ends
    total, out_small, out_gate, out_up, out_down_t = last_reduce(
        mine,
        theirs,
        2 * q_cols + 2 * kv_cols,
        [gate_up_end, *rg.held, down_end, *rd.held],
    )
    out_output = total[:, :q_cols].T
    out_qkv = total[:, q_cols:]
    out_gains = out_small[:, 2 * rank + 2 * small :]
    return (
        low(result),
        grad_tokens,
        grad_layer_input,
        out_qkv[:, :q_cols],
        out_qkv[:, q_cols : q_cols + kv_cols],
        out_qkv[:, q_cols + kv_cols :],
        out_output,
        out_small[:, 2 * small : 2 * small + rank],
        out_small[:, 2 * small + rank : 2 * small + 2 * rank].T,
        out_gate,
        out_up,
        out_down_t.T,
        out_small[:, :small],
        out_small[:, small : 2 * small].T,
        out_gains[:head_part, 6],
        out_gains[:head_part, 7],
        out_gains[:, 0],
        out_gains[:, 1],
        out_gains[:, 2],
        out_gains[:, 3],
        out_gains[:, 4],
        out_gains[:, 5],
    )


def solution(mesh):
    both = P(("dp", "tensor"), None)
    rows_split = P("dp", "tensor")
    cols_split = P("tensor", "dp")
    by_row = P("dp", None)
    by_col = P(None, "dp")
    flat = P("dp")
    return jax.shard_map(
        local,
        mesh=mesh,
        in_specs=(
            (both, both, P(), P(), rows_split, rows_split, rows_split, cols_split)
            + (by_row, by_col, rows_split, rows_split, cols_split, by_row, by_col)
            + (flat,) * 8
            + (both,)
        ),
        out_specs=(
            (both, both, both, rows_split, rows_split, rows_split, cols_split)
            + (by_row, by_col, rows_split, rows_split, cols_split, by_row, by_col)
            + (flat,) * 8
        ),
        check_vma=False,
    )
```

```python
import functools

import jax
import jax.numpy as jnp
from jax import lax
from jax.experimental import pallas as pl
from jax.experimental.pallas import tpu as pltpu
from jax.sharding import PartitionSpec as P

HD = 256
EPS = 1e-06
ROOT_HALF = 0.7071067811865476
NEGATIVE = -1e30
F32 = jnp.float32
BF16 = jnp.bfloat16


def norm_gain(values, gains):
    return values * lax.rsqrt(jnp.mean(values * values, axis=-1, keepdims=True) + EPS) * gains


def norm_plain(values):
    return values * lax.rsqrt(jnp.mean(values * values, axis=-1, keepdims=True) + EPS)


def gelu_tanh(values):
    return jax.nn.gelu(values, approximate=True)


def rope_tables(positions, head_width):
    positions = positions.astype(F32)[:, None]
    frequency = 10000.0 ** (-2.0 * jnp.arange(head_width // 2, dtype=F32) / head_width)
    angles = positions * frequency[None, :]
    return (jnp.cos(angles), jnp.sin(angles))


def rotate(values, cosines, sines):
    half_width = values.shape[-1] // 2
    front_half = values[..., :half_width]
    back_half = values[..., half_width:]
    cos_wide = cosines[:, None, :]
    sin_wide = sines[:, None, :]
    return jnp.concatenate(
        [
            front_half * cos_wide - back_half * sin_wide,
            back_half * cos_wide + front_half * sin_wide,
        ],
        axis=-1,
    )


def to_float(values):
    return values.astype(F32)


def low(values):
    return values.astype(BF16)


def product(left_in, right_in):
    return jnp.dot(left_in, right_in, preferred_element_type=F32)


def product_t(left_in, right_in):
    return lax.dot_general(left_in, right_in, (((1,), (1,)), ((), ())), preferred_element_type=F32)


def product_l(left_in, right_in):
    return lax.dot_general(left_in, right_in, (((0,), (0,)), ((), ())), preferred_element_type=F32)


def tie(*values):
    return lax.optimization_barrier(values)


class Ring:
    def __init__(self):
        self.devices = lax.axis_size("dp")
        self.chips = self.devices // 2
        order = list(range(0, self.chips, 2)) + list(range(self.chips - 1, 0, -2))
        self.cw = [
            (2 * order[p] + c, 2 * order[(p + 1) % self.chips] + c)
            for p in range(self.chips)
            for c in range(2)
        ]
        self.ccw = [(b, a) for a, b in self.cw]
        self.core_pairs = [(d, d ^ 1) for d in range(self.devices)]
        me = lax.axis_index("dp")
        self.core = lax.rem(me, 2)
        self.chip = me // 2
        self.place = jnp.where(
            lax.rem(self.chip, 2) == 0, self.chip // 2, self.chips - 1 - self.chip // 2
        )

    def chip_at(self, offset):
        place = lax.rem(self.place + offset + self.chips, self.chips)
        return jnp.where(place < self.chips // 2, 2 * place, 2 * (self.chips - 1 - place) + 1)

    def up(self, values):
        return lax.ppermute(values, "dp", self.cw)

    def down(self, values):
        return lax.ppermute(values, "dp", self.ccw)

    def swap(self, values):
        return lax.ppermute(values, "dp", self.core_pairs)


def across(values):
    return lax.ppermute(values, "tensor", [(0, 1), (1, 0)])


def remote(source, target, sends, receives, index, device):
    return pltpu.make_async_remote_copy(
        src_ref=source,
        dst_ref=target,
        send_sem=sends.at[index],
        recv_sem=receives.at[index],
        device_id=device,
        device_id_type=pl.DeviceIdType.MESH,
    )


def greet(devices):
    barrier = pltpu.get_barrier_semaphore()
    for device in devices:
        pl.semaphore_signal(
            barrier, inc=1, device_id=device, device_id_type=pl.DeviceIdType.MESH
        )
    pl.semaphore_wait(barrier, len(devices))


def block_rows(ref, start, count):
    return ref.at[pl.ds(pl.multiple_of(start, 16), count)]


class Hops:
    def __init__(self):
        me = lax.axis_index("dp")
        self.chips = lax.axis_size("dp") // 2
        self.core = lax.rem(me, 2)
        self.chip = me // 2
        self.place = jnp.where(
            lax.rem(self.chip, 2) == 0, self.chip // 2, self.chips - 1 - self.chip // 2
        )
        self.partner = {"dp": self.chip * 2 + 1 - self.core}
        self.above = {"dp": self.chip_at(1) * 2 + self.core}
        self.below = {"dp": self.chip_at(-1) * 2 + self.core}
        self.across = {"tensor": 1 - lax.axis_index("tensor")}

    def chip_at(self, offset):
        place = lax.rem(self.place + offset + self.chips, self.chips)
        return jnp.where(place < self.chips // 2, 2 * place, 2 * (self.chips - 1 - place) + 1)


def staged_apart(source_shape, turned, start):
    cols = source_shape[0] if turned else source_shape[1]
    return turned or start % 128 != 0 or cols % 128 != 0, cols


def first_kernel(layout, down_turned, ff_cols, *refs):
    count = len(layout)
    sources, refs = refs[: sum(len(l) for l in layout)], refs[sum(len(l) for l in layout) :]
    (gate, up, down, tokens), refs = refs[:4], refs[4:]
    wholes, refs = refs[:count], refs[count:]
    (gate_own, up_down_own, other_tokens), refs = refs[:3], refs[3:]
    stages, refs = refs[:count], refs[count:]
    (gate_v, up_v, tokens_v, down_v, down_t), refs = refs[:5], refs[5:]
    apart, refs = list(refs[:-8]), refs[-8:]
    in_sems, out_sems, ring_send, ring_recv, pair_send, pair_recv, ff_send, ff_recv = refs
    hops = Hops()
    half = hops.chips // 2
    mine = pl.ds(pl.multiple_of(hops.core * ff_cols, 128), ff_cols)
    theirs = pl.ds(pl.multiple_of((1 - hops.core) * ff_cols, 128), ff_cols)

    number = 0

    def load(source, target):
        nonlocal number
        copy = pltpu.make_async_copy(source, target, in_sems.at[number])
        copy.start()
        number += 1
        return copy

    taken = list(sources)
    fills = []
    for which, flags in enumerate(layout):
        start, steps = 0, []
        for turned in flags:
            source = taken.pop(0)
            own_buffer, cols = staged_apart(source.shape, turned, start)
            if own_buffer:
                buffer = apart.pop(0)
                steps.append((load(source, buffer), buffer, turned, start, cols))
            else:
                target = stages[which].at[:, pl.ds(start, cols)]
                steps.append((load(source, target), None, turned, start, cols))
            start += cols
        fills.append(steps)
    load_down = load(down, down_v)
    bounces = [(load(gate.at[:, mine], gate_v), gate_v), (load(up.at[:, mine], up_v), up_v)]
    load_tokens = load(tokens, tokens_v)
    greet([hops.above, hops.below, hops.partner, hops.across])
    started, stores = [], []

    def place(which, offset, top, size):
        tall = stages[which].shape[0]
        at = (2 * hops.chip_at(offset) + hops.core) * tall + top
        return wholes[which].at[pl.ds(pl.multiple_of(at, 8 if tall <= 16 else 16), size)]

    def store(source, target):
        copy = pltpu.make_async_copy(source, target, out_sems.at[len(stores)])
        copy.start()
        stores.append(copy)

    def to_partner(number, which, offset, top, size, source=None):
        spot = place(which, offset, top, size)
        copy = remote(
            spot if source is None else source,
            spot,
            pair_send,
            pair_recv,
            (number, which),
            hops.partner,
        )
        copy.start()
        started.append(copy)
        pairs.append(copy)

    def onward(direction, k, which, offset, top, size, source=None):
        spot = place(which, offset, top, size)
        copy = remote(
            spot if source is None else source,
            spot,
            ring_send,
            ring_recv,
            (direction, k, which),
            hops.above if direction == 0 else hops.below,
        )
        copy.start()
        started.append(copy)
        arrivals[(direction, k, which)] = copy

    pairs, arrivals = [], {}
    for which, steps in enumerate(fills):
        stage = stages[which]
        for copy, buffer, turned, start, cols in steps:
            copy.wait()
            if buffer is not None:
                stage[:, start : start + cols] = buffer[...].T if turned else buffer[...]
        tall = stage.shape[0]
        for direction in range(2):
            onward(direction, 0, which, 0, 0, tall, stage)
    own = tokens.shape[0]
    theirs_at = other_tokens.at[pl.ds(own, own)]
    ff_copies = [remote(tokens, theirs_at, ff_send, ff_recv, (3,), hops.across)]
    ff_copies[0].start()
    rows = gate.shape[0]
    own_rows = pl.ds(pl.multiple_of(hops.core * rows, 16), rows)
    targets = [
        gate_own.at[own_rows],
        up_down_own.at[own_rows, pl.ds(0, ff_cols)],
        up_down_own.at[own_rows, pl.ds(ff_cols, ff_cols)],
    ]
    load_down.wait()
    if down_turned:
        down_t[...] = down_v[...].T
        down = down_t
    else:
        down = down_v
    for number_, (weight, target) in enumerate(zip((gate, up, down), targets)):
        copy = remote(
            weight.at[:, theirs], target, ff_send, ff_recv, (number_,), hops.partner
        )
        copy.start()
        ff_copies.append(copy)
    for which, stage in enumerate(stages):
        to_partner(0, which, 0, 0, stage.shape[0], stage)
        store(stage, place(which, 0, 0, stage.shape[0]))
    for (copy, buffer), target in zip(bounces, targets):
        copy.wait()
        store(buffer, target)
    store(down.at[:, mine], targets[2])
    load_tokens.wait()
    store(tokens_v, other_tokens.at[pl.ds(0, own)])
    for k in range(1, half + 1):
        for which in range(count):
            tall = stages[which].shape[0]
            cut = tall // 2
            for direction in range(2):
                arrivals[(direction, k - 1, which)].wait_recv()
                offset = -k if direction == 0 else k
                if k < half - 1:
                    onward(direction, k, which, offset, 0, tall)
                elif k == half - 1:
                    onward(direction, k, which, offset, direction * cut, cut)
                if k < half:
                    to_partner(2 * k - 1 + direction, which, offset, 0, tall)
                else:
                    to_partner(2 * k - 1 + direction, which, half, direction * cut, cut)
    for copy in ff_copies + pairs:
        copy.wait_recv()
    for copy in ff_copies + started:
        copy.wait_send()
    for copy in stores:
        copy.wait()


ANY = pl.BlockSpec(memory_space=pl.ANY)


def comm_call(kernel, number, operands, shapes, stages, semaphores, name):
    moved = sum(v.size * 2 for v in shapes)
    return pl.pallas_call(
        kernel,
        out_shape=shapes,
        in_specs=[ANY] * len(operands),
        out_specs=[ANY] * len(shapes),
        scratch_shapes=stages + [pltpu.SemaphoreType.DMA(shape) for shape in semaphores],
        compiler_params=pltpu.CompilerParams(
            collective_id=number, has_side_effects=True, vmem_limit_bytes=60 * 2**20
        ),
        cost_estimate=pl.CostEstimate(flops=0, bytes_accessed=8 * moved, transcendentals=0),
        name=name,
    )(*operands)


def first_gather(blocks, gate, up, down, tokens):
    chips = lax.axis_size("dp") // 2
    half = chips // 2
    down, down_turned = down
    rows = gate.shape[0]
    ff_cols = gate.shape[1] // 2
    count = len(blocks)
    stages, apart = [], []
    for block in blocks:
        start = 0
        for source, turned in block:
            own_buffer, cols = staged_apart(source.shape, turned, start)
            if own_buffer:
                apart.append(pltpu.VMEM(source.shape, source.dtype))
            start += cols
        first, turned = block[0]
        tall = first.shape[1] if turned else first.shape[0]
        stages.append(pltpu.VMEM((tall, start), first.dtype))
    shapes = [
        jax.ShapeDtypeStruct((2 * chips * stage.shape[0], stage.shape[1]), stage.dtype)
        for stage in stages
    ] + [
        jax.ShapeDtypeStruct((2 * rows, ff_cols), gate.dtype),
        jax.ShapeDtypeStruct((2 * rows, 2 * ff_cols), gate.dtype),
        jax.ShapeDtypeStruct((2 * tokens.shape[0], tokens.shape[1]), tokens.dtype),
    ]
    more = [
        pltpu.VMEM((rows, ff_cols), gate.dtype),
        pltpu.VMEM((rows, ff_cols), gate.dtype),
        pltpu.VMEM(tokens.shape, tokens.dtype),
        pltpu.VMEM(down.shape, down.dtype),
        pltpu.VMEM((rows, 2 * ff_cols), down.dtype),
    ]
    sources = [source for block in blocks for source, _ in block]
    semaphores = [
        (len(sources) + 4,),
        (4 + count,),
        (2, half, count),
        (2, half, count),
        (2 * half + 1, count),
        (2 * half + 1, count),
        (4,),
        (4,),
    ]
    layout = tuple(tuple(turned for _, turned in block) for block in blocks)
    out = comm_call(
        functools.partial(first_kernel, layout, down_turned, ff_cols),
        0,
        (*sources, gate, up, down, tokens),
        shapes,
        stages + more + apart,
        semaphores,
        "first_gather",
    )
    return out[:count], out[count:]


GELU_SCALE = 0.7978845608028654
GELU_CUBE = 0.044715
ROW_TILE = 1024


def fill(spots, whole, parts):
    for number, part in enumerate(parts):
        size = part.shape[0]
        whole[pl.ds(pl.multiple_of(spots[number], size), size), :] = part[...]


def gate_up_kernel(count, spots, x, *refs):
    gate_parts, up_parts = refs[:count], refs[count : 2 * count]
    raw, hidden, weights = refs[2 * count :]
    gate_w, up_w = weights.at[0], weights.at[1]
    fill(spots, gate_w, gate_parts)
    fill(spots, up_w, up_parts)

    @pl.loop(0, x.shape[0] // min(ROW_TILE, x.shape[0]))
    def _(i):
        at = pl.ds(pl.multiple_of(i * ROW_TILE, ROW_TILE), ROW_TILE)
        rows = x[at, :]
        gate = product(rows, gate_w[...])
        up = product(rows, up_w[...])
        raw[0, at, :] = low(gate)
        raw[1, at, :] = low(up)
        bend = jnp.tanh(GELU_SCALE * (gate + GELU_CUBE * gate * gate * gate))
        hidden[at, :] = low(0.5 * gate * (1.0 + bend) * up)


def hidden_back_kernel(count, spots, x, raw, *refs):
    parts, (out, whole) = refs[:count], refs[count:]
    fill(spots, whole, parts)

    @pl.loop(0, x.shape[0] // min(ROW_TILE, x.shape[0]))
    def _(i):
        at = pl.ds(pl.multiple_of(i * ROW_TILE, ROW_TILE), ROW_TILE)
        d_hidden = product(x[at, :], whole[...])
        gate = to_float(raw[0, at, :])
        up = to_float(raw[1, at, :])
        square = gate * gate
        bend = jnp.tanh(GELU_SCALE * gate * (1.0 + GELU_CUBE * square))
        plus = 0.5 * (1.0 + bend)
        slope = plus + 0.5 * gate * (1.0 - bend * bend) * GELU_SCALE * (
            1.0 + 3.0 * GELU_CUBE * square
        )
        out[0, at, :] = low(d_hidden * up * slope)
        out[1, at, :] = low(d_hidden * gate * plus)


def columns_kernel(count, spots, h, *refs):
    parts, (out, whole) = refs[:count], refs[count:]
    fill(spots, whole, parts)
    step = pl.program_id(0)
    width = out.shape[1]
    cols = min(512, width)


    @pl.loop(0, width // cols)
    def _(j):
        across_ = pl.ds(pl.multiple_of(j * cols, cols), cols)
        term = product_t(h[0], whole[across_, :])

        @pl.when(step == 0)
        def _():
            out[:, across_] = term

        @pl.when(step > 0)
        def _():
            out[:, across_] = out[:, across_] + term


def block_kernel(count, came, spots, *refs):
    xs, d, refs = refs[:count], refs[count], refs[count + 1 :]
    gots, refs = refs[:came], refs[came:]
    outs, turned = refs[:count], refs[count:]

    @pl.when(pl.program_id(0) == 0)
    def _():
        for x, t in zip(xs, turned):
            t[...] = x[...].T

    for i, (t, out) in enumerate(zip(turned, outs)):
        term = product(t[...], d[0])
        if came == 0:
            out[...] = low(term)
        elif gots[i].shape == out.shape:
            out[...] = low(term + to_float(gots[i][...]))
        else:
            cut = gots[i].shape[0]
            near, far = slice(i * cut, (i + 1) * cut), slice((1 - i) * cut, (2 - i) * cut)
            out[near, :] = low(term[near] + to_float(gots[i][...]))
            out[far, :] = low(term[far])


def grid_call(kernel, spots, grid, operands, in_specs, shapes, out_specs, scratch, flops, name):
    moved = sum(v.size * v.dtype.itemsize for v in (*operands, *jax.tree.leaves(shapes)))
    if flops == 0:
        moved = 0
    return pl.pallas_call(
        kernel,
        grid_spec=pltpu.PrefetchScalarGridSpec(
            num_scalar_prefetch=1,
            grid=grid,
            in_specs=in_specs,
            out_specs=out_specs,
            scratch_shapes=scratch,
        ),
        out_shape=shapes,
        compiler_params=pltpu.CompilerParams(
            dimension_semantics=("arbitrary",) * len(grid), vmem_limit_bytes=56 * 2**20
        ),
        cost_estimate=pl.CostEstimate(flops=flops, bytes_accessed=moved, transcendentals=0),
        name=name,
    )(spots, *operands)


def once(shape):
    return pl.BlockSpec(
        shape, lambda *index: (0,) * len(shape), pipeline_mode=pl.Buffered(buffer_count=1)
    )


def gate_up(x, spots, parts, up_parts, tile=512):
    count, (m, width), ff = len(parts), x.shape, parts[0].shape[1]
    tiles = ff // tile
    part_specs = [pl.BlockSpec((p.shape[0], tile), lambda n, s: (0, n)) for p in parts] * 2
    return grid_call(
        functools.partial(gate_up_kernel, count),
        spots,
        (tiles,),
        (x, *parts, *up_parts),
        [once((m, width))] + part_specs,
        [
            jax.ShapeDtypeStruct((2, m, ff), BF16),
            jax.ShapeDtypeStruct((m, ff), BF16),
            jax.ShapeDtypeStruct((2, width, ff), BF16),
        ],
        [
            pl.BlockSpec((2, m, tile), lambda n, s: (0, 0, n)),
            pl.BlockSpec((m, tile), lambda n, s: (0, n)),
            pl.BlockSpec((2, width, tile), lambda n, s: (0, 0, n)),
        ],
        [],
        4 * m * width * ff,
        "gate_up",
    )


def hidden_back(x, raw, spots, parts, tile=256):
    count, (m, width), ff = len(parts), x.shape, parts[0].shape[1]
    part_specs = [pl.BlockSpec((p.shape[0], tile), lambda n, s: (0, n)) for p in parts]
    return grid_call(
        functools.partial(hidden_back_kernel, count),
        spots,
        (ff // tile,),
        (x, raw, *parts),
        [once((m, width)), pl.BlockSpec((2, m, tile), lambda n, s: (0, 0, n))] + part_specs,
        jax.ShapeDtypeStruct((2, m, ff), BF16),
        pl.BlockSpec((2, m, tile), lambda n, s: (0, 0, n)),
        [pltpu.VMEM((width, tile), BF16)],
        2 * m * width * ff,
        "hidden_back",
    )


def columns_out(h, spots, parts, width, tile=1024):
    count, (groups, m, ff) = len(parts), h.shape
    tile = min(tile, ff)
    tiles = ff // tile
    part_specs = [pl.BlockSpec((p.shape[0], tile), lambda f, s: (0, f)) for p in parts]
    return grid_call(
        functools.partial(columns_kernel, count),
        spots,
        (groups * tiles,),
        (h, *parts),
        [pl.BlockSpec((1, m, tile), lambda f, s: (f // tiles, 0, f % tiles))] + part_specs,
        jax.ShapeDtypeStruct((m, width), F32),
        once((m, width)),
        [pltpu.VMEM((width, tile), BF16)],
        2 * groups * m * width * ff,
        "columns_out",
    )


def block_grads(x, d, chips, size, gots=(), tile=2048):
    (m, _), (groups, _, ff) = x.shape, d.shape
    count = len(chips)
    tile = min(tile, ff)
    tiles = ff // tile
    spots = jnp.stack(chips).astype(jnp.int32)
    if size % 128:
        xs = [lax.dynamic_slice_in_dim(x, chip * size, size, 1) for chip in chips]
        x_specs = [once((m, size))] * count
    else:
        xs = [x] * count
        x_specs = [
            pl.BlockSpec((m, size), functools.partial(lambda i, f, s: (0, s[i]), i))
            for i in range(count)
        ]
    return grid_call(
        functools.partial(block_kernel, count, len(gots)),
        spots,
        (groups * tiles,),
        (*xs, d, *gots),
        x_specs
        + [pl.BlockSpec((1, m, tile), lambda f, s: (f // tiles, 0, f % tiles))]
        + [pl.BlockSpec((v.shape[0], tile), lambda f, s: (0, f)) for v in gots],
        [jax.ShapeDtypeStruct((size, groups * ff), BF16)] * count,
        [pl.BlockSpec((size, tile), lambda f, s: (0, f))] * count,
        [pltpu.VMEM((size, m), BF16)] * count,
        0,
        "block_grads",
    )


def add_kernel(count, spots, *refs):
    terms, gots, outs = refs[:count], refs[count : 2 * count], refs[2 * count :]
    for term, got, out in zip(terms, gots, outs):
        out[...] = low(to_float(term[...]) + to_float(got[...]))


def add_blocks(terms, gots, tile=1024):
    tall, wide = terms[0].shape
    tile = min(tile, wide)
    count = len(terms)
    block = pl.BlockSpec((tall, tile), lambda f, s: (0, f))
    return grid_call(
        functools.partial(add_kernel, count),
        jnp.zeros((1,), jnp.int32),
        (wide // tile,),
        (*terms, *gots),
        [block] * (2 * count),
        [jax.ShapeDtypeStruct((tall, wide), BF16)] * count,
        [block] * count,
        [],
        terms[0].size,
        "add_blocks",
    )


def row_kernel(pairs, spots, *refs):
    xs, ds = refs[:pairs], refs[pairs : 2 * pairs]
    last, mine, theirs, both = refs[2 * pairs :]
    rows = mine.shape[0]
    core = spots[0]
    start = 0
    for x, d in zip(xs, ds):
        cols = d.shape[1]
        both[:, start : start + cols] = product_l(x[...], d[...])
        start += cols
    both[:, start:] = last[...]
    mine[...] = both[pl.ds(pl.multiple_of(core * rows, 128), rows), :]
    theirs[...] = low(both[pl.ds(pl.multiple_of((1 - core) * rows, 128), rows), :])


def row_grads(pairs, last, core, chips, rows):
    xs, ds = [x for x, _ in pairs], [d for _, d in pairs]
    cols = sum(d.shape[1] for d in ds) + last.shape[1]
    if rows % 128:

        def own_columns(values, which):
            blocks = values.reshape(values.shape[0], chips, 2, rows)
            return lax.dynamic_index_in_dim(blocks, which, 2, keepdims=False).reshape(
                values.shape[0], chips * rows
            )

        def terms(which):
            return jnp.concatenate(
                [product_l(own_columns(x, which), d) for x, d in pairs]
                + [own_columns(last.T, which).T],
                axis=1,
            )

        return terms(core), low(terms(1 - core))
    block = pl.BlockSpec((rows, cols), lambda j, s: (j, 0))
    return grid_call(
        functools.partial(row_kernel, len(pairs)),
        core.reshape(1).astype(jnp.int32),
        (chips,),
        (*xs, *ds, last),
        [pl.BlockSpec((x.shape[0], 2 * rows), lambda j, s: (0, j)) for x in xs]
        + [once(d.shape) for d in ds]
        + [pl.BlockSpec((2 * rows, last.shape[1]), lambda j, s: (j, 0))],
        [
            jax.ShapeDtypeStruct((chips * rows, cols), F32),
            jax.ShapeDtypeStruct((chips * rows, cols), BF16),
        ],
        [block, block],
        [pltpu.VMEM((2 * rows, cols), F32)],
        sum(4 * d.size * chips * rows for d in ds),
        "row_grads",
    )


def last_kernel(large, *refs):
    mine, theirs, refs = refs[0], refs[1], refs[2:]
    ff_terms, refs = refs[:6], refs[6:]
    (main, little, *ff_outs), refs = refs[:5], refs[5:]
    own, core_got, side_sent, side_got, first, got, refs = *refs[:6], refs[6:]
    ff_held, (ff_sent,), refs = refs[:6], refs[6:7], refs[7:]
    loads, core_send, core_recv, side_send, side_recv, ring_send, ring_recv, ff_send, ff_recv = refs
    hops = Hops()
    side = lax.axis_index("tensor")
    half = hops.chips // 2
    rows = main.shape[0]
    part = little.shape[1] // 2
    ff_cols = ff_sent.shape[2]
    cut = rows // 2
    greet([hops.above, hops.below, hops.partner, hops.across])
    order = [half]
    for k in range(1, half):
        order += [half - k, k - half]
    order.append(0)

    def rows_at(offset, top=0, size=rows):
        return pl.ds(pl.multiple_of(hops.chip_at(offset) * rows + top, 16), size)

    started, arriving = [], []
    for i, offset in enumerate(order):
        at = rows_at(offset)
        copy = remote(
            theirs.at[at], core_got.at[at], core_send, core_recv, (i,), hops.partner
        )
        copy.start()
        load = pltpu.make_async_copy(mine.at[at], own.at[at], loads.at[i])
        load.start()
        started.append(copy)
        arriving.append((copy, load))
    ff_loads = [
        pltpu.make_async_copy(source, target, loads.at[len(order) + i])
        for i, (source, target) in enumerate(zip(ff_terms, ff_held))
    ]
    for load in ff_loads:
        load.start()

    sides = {}
    my_part = pl.ds(pl.multiple_of(large + side * part, 128), part)
    their_part = pl.ds(pl.multiple_of(large + (1 - side) * part, 128), part)

    def ready(i):
        at = rows_at(order[i])
        copy, load = arriving[i]
        load.wait()
        copy.wait_recv()
        own[at, :] = own[at, :] + to_float(core_got[at, :])
        side_sent[at, :] = low(own[at, their_part])
        copy = remote(
            side_sent.at[at], side_got.at[at], side_send, side_recv, (i,), hops.across
        )
        copy.start()
        started.append(copy)
        sides[order[i]] = copy

    pieces = [(0, large // 2), (large // 2, large // 2), (large, part)]
    copies = {}

    def term(which, offset, top, size):
        at = rows_at(offset, top, size)
        start, cols = pieces[which]
        if which < 2:
            return own[at, start : start + cols]
        return own[at, my_part] + to_float(side_got[at, :])

    def send(which, direction, k, source, top, size):
        start, cols = pieces[which]
        copy = remote(
            source,
            got.at[direction, k, pl.ds(top, size), pl.ds(start, cols)],
            ring_send,
            ring_recv,
            (direction, k, which),
            hops.above if direction == 0 else hops.below,
        )
        copy.start()
        started.append(copy)
        copies[(which, direction, k)] = copy

    def step(which, k):
        start, cols = pieces[which]
        for direction in range(2):
            near, far = direction * cut, (1 - direction) * cut
            if k == 0:
                first[direction, :, start : start + cols] = low(term(which, half, near, cut))
                source = first.at[direction, :, pl.ds(start, cols)]
                send(which, direction, 0, source, near, cut)
                continue
            offset = (half - k) * (1 if direction == 0 else -1)
            copies[(which, direction, k - 1)].wait_recv()
            if k == 1:
                held = got[direction, 0, near : near + cut, start : start + cols]
                got[direction, 0, near : near + cut, start : start + cols] = low(
                    term(which, offset, near, cut) + to_float(held)
                )
                got[direction, 0, far : far + cut, start : start + cols] = low(
                    term(which, offset, far, cut)
                )
            else:
                held = got[direction, k - 1, :, start : start + cols]
                got[direction, k - 1, :, start : start + cols] = low(
                    term(which, offset, 0, rows) + to_float(held)
                )
            source = got.at[direction, k - 1, :, pl.ds(start, cols)]
            send(which, direction, k, source, 0, rows)

    def end_feed_forward():
        for load in ff_loads:
            load.wait()
        wide, wide_up, wide_down, narrow, narrow_up, narrow_down = ff_held
        my_rows = pl.ds(pl.multiple_of(hops.core * rows, 16), rows)
        their_rows = pl.ds(pl.multiple_of((1 - hops.core) * rows, 16), rows)
        my_cols = pl.ds(pl.multiple_of(hops.core * ff_cols, 128), ff_cols)
        groups = [
            (wide, wide_up, wide_down, 0),
            (wide, wide_up, wide_down, ff_cols),
            (narrow, narrow_up, narrow_down, 0),
        ]
        for i, (base, up, down, start) in enumerate(groups):
            cols = slice(start, start + ff_cols)

            def total(at):
                return to_float(base[at, cols]) + to_float(up[at, cols]) + to_float(down[at, cols])

            ff_sent[i] = total(their_rows)
            copy = remote(
                ff_sent.at[i], ff_outs[i].at[:, my_cols], ff_send, ff_recv, (i,), hops.partner
            )
            copy.start()
            ff_copies.append(copy)
            ff_outs[i][:, my_cols] = total(my_rows)

    ff_copies = []
    ready(0)
    step(0, 0)
    step(1, 0)
    ready(1)
    ready(2)
    sides[half].wait_recv()
    step(2, 0)
    for k in range(1, half):
        if k > 1:
            sides[half - k].wait_recv()
            sides[k - half].wait_recv()
            step(2, k)
        step(0, k)
        step(1, k)
        if k == 1:
            end_feed_forward()
        for i in range(2 * k + 1, min(2 * k + 3, len(order))):
            ready(i)
        if k == 1:
            sides[half - k].wait_recv()
            sides[k - half].wait_recv()
            step(2, k)
    sides[0].wait_recv()
    for which in (2, 0, 1):
        start, cols = pieces[which]
        for direction in range(2):
            copies[(which, direction, half - 1)].wait_recv()
        total = (
            term(which, 0, 0, rows)
            + to_float(got[0, half - 1, :, start : start + cols])
            + to_float(got[1, half - 1, :, start : start + cols])
        )
        if which < 2:
            main[:, start : start + cols] = total
        else:
            here = pl.ds(pl.multiple_of(side * part, 128), part)
            little[:, here] = total
            little_copy = remote(
                little.at[:, here],
                little.at[:, here],
                side_send,
                side_recv,
                (len(order),),
                hops.across,
            )
            little_copy.start()
            started.append(little_copy)
    for copy in ff_copies + [little_copy]:
        copy.wait_recv()
    for copy in ff_copies + started:
        copy.wait_send()


def last_reduce(mine, theirs, large, ff_terms):
    chips = lax.axis_size("dp") // 2
    half = chips // 2
    tall, cols = mine.shape
    rows = tall // chips
    part = (cols - large) // 2
    ff = ff_terms[3].shape[1]
    vmem = pl.BlockSpec(memory_space=pltpu.VMEM)
    dma = pltpu.SemaphoreType.DMA
    return pl.pallas_call(
        functools.partial(last_kernel, large),
        out_shape=[
            jax.ShapeDtypeStruct((rows, large), F32),
            jax.ShapeDtypeStruct((rows, 2 * part), F32),
        ]
        + [jax.ShapeDtypeStruct((rows, 2 * ff), F32)] * 3,
        in_specs=[ANY] * 8,
        out_specs=[vmem] * 5,
        scratch_shapes=[
            pltpu.VMEM((tall, cols), F32),
            pltpu.VMEM((tall, cols), BF16),
            pltpu.VMEM((tall, part), BF16),
            pltpu.VMEM((tall, part), BF16),
            pltpu.VMEM((2, rows // 2, large + part), BF16),
            pltpu.VMEM((2, half, rows, large + part), BF16),
        ]
        + [pltpu.VMEM(v.shape, v.dtype) for v in ff_terms]
        + [
            pltpu.VMEM((3, rows, ff), F32),
            dma((2 * half + 6,)),
            dma((2 * half,)),
            dma((2 * half,)),
            dma((2 * half + 1,)),
            dma((2 * half + 1,)),
            dma((2, half, 3)),
            dma((2, half, 3)),
            dma((3,)),
            dma((3,)),
        ],
        compiler_params=pltpu.CompilerParams(
            collective_id=2, has_side_effects=True, vmem_limit_bytes=56 * 2**20
        ),
        cost_estimate=pl.CostEstimate(
            flops=0, bytes_accessed=20 * mine.size * 4, transcendentals=0
        ),
        name="last_reduce",
    )(mine, theirs, *ff_terms)


def forward_kernel(hops_done, tile, x_own, *refs):
    counts = [2 * done + 1 for done in hops_done]
    gate_parts, up_down_parts, refs = refs[: counts[0]], refs[counts[0] : sum(counts)], refs[sum(counts) :]
    gu_parts = (gate_parts, up_down_parts)
    size, ff = gate_parts[0].shape
    dn_parts = [ref.at[:, pl.ds(ff, ff)] for ref in up_down_parts]
    hops_done = (*hops_done, hops_done[1])
    (x_out, gu_full, gu_land, dn_full, raw, hidden, result), refs = refs[:7], refs[7:]
    x, dn, hidden_v, pairs, core_sent, core_got, side_sent, side_got, refs = *refs[:8], refs[8:]
    x_send, x_recv, gu_send, gu_recv, dn_send, dn_recv, core_sems, side_sems, loads, stores = refs
    hops = Hops()
    half, chips = hops.chips // 2, hops.chips
    own = x_own.shape[0]
    cut = size // 2
    greet([hops.above, hops.below, hops.partner, hops.across])
    started, saved = [], []

    def begin(copy, where=started):
        copy.start()
        where.append(copy)
        return copy

    def spot(ref, offset, top=0, tall=size):
        return block_rows(ref, hops.chip_at(offset) * size + top, tall)

    def gu_hop(k):
        copies = []
        for direction, ahead in ((0, hops.above), (1, hops.below)):
            offset = (1 - k) * (1 if direction == 0 else -1)
            top, tall = (0, size) if k < half else (direction * cut, cut)
            for group in range(2):
                if k <= hops_done[group]:
                    continue
                target = spot(gu_land.at[group], offset, top, tall)
                if k == hops_done[group] + 1:
                    held = gu_parts[group][2 * k - 3 + direction]
                    source = held.at[pl.ds(pl.multiple_of(top, 16), tall), pl.ds(0, ff)]
                else:
                    source = target
                index = (direction, k - 1, group)
                copies.append(begin(remote(source, target, gu_send, gu_recv, index, ahead)))
        return copies

    def dn_hop(k):
        copies = []
        for direction, ahead in ((0, hops.above), (1, hops.below)):
            offset = (1 - k) * (1 if direction == 0 else -1)
            top, tall = (0, size) if k < half else (direction * cut, cut)
            block = spot(dn, offset, top, tall)
            copies.append(begin(remote(block, block, dn_send, dn_recv, (direction, k - 1), ahead)))
        return copies

    def arrive(copies):
        for copy in copies:
            copy.wait_recv()

    first_hop = min(hops_done[:2]) + 1
    moving = gu_hop(first_hop)
    mine, far = pl.ds(0, own), pl.ds(own, own)
    near, opposite = pl.ds(2 * own, own), pl.ds(3 * own, own)
    load_x = begin(pltpu.make_async_copy(x_own, x.at[mine], loads.at[0]), saved)
    places = [0]
    for k in range(1, hops_done[2] + 1):
        places += [-k, k]
    dn_loads = [
        begin(pltpu.make_async_copy(ref, spot(dn, offset), loads.at[1 + i]), saved)
        for i, (ref, offset) in enumerate(zip(dn_parts, places))
    ]
    loaded = len(saved)
    from_far = begin(remote(x_own, x.at[far], x_send, x_recv, (0,), hops.across))
    from_near = begin(remote(x_own, x.at[near], x_send, x_recv, (1,), hops.partner))
    from_near.wait_recv()
    load_x.wait()
    arrive(moving)
    if first_hop < half:
        moving = gu_hop(first_hop + 1)
    from_far.wait_recv()
    passed = begin(remote(x.at[far], x.at[opposite], x_send, x_recv, (2,), hops.partner))
    passed.wait_recv()
    begin(pltpu.make_async_copy(x, x_out, stores.at[0]), saved)
    for copy in dn_loads:
        copy.wait()
    for k in range(first_hop + 2, half + 1):
        arrive(moving)
        moving = gu_hop(k)
    if first_hop < half:
        arrive(moving)
    moving = dn_hop(hops_done[2] + 1)

    here, landed = [], []
    for done in hops_done[:2]:
        near_by = [0]
        for k in range(1, done + 1):
            near_by += [-k, k]
        here.append(near_by)
        landed.append([o for o in range(-half + 1, half + 1) if o not in near_by])
    tiles = ff // tile

    def body(*tiles_of):
        ins, (raw_tile, hidden_tile, weights) = tiles_of[:-3], tiles_of[-3:]
        step = pl.program_id(0)
        for group in range(2):
            for number, offset in enumerate(here[group] + landed[group]):
                at = pl.ds(pl.multiple_of(hops.chip_at(offset) * size, size), size)
                weights[group, at, :] = ins[group * chips + number][...]
        gate = product(x[...], weights[0])
        up = product(x[...], weights[1])
        raw_tile[0] = low(gate)
        raw_tile[1] = low(up)
        bend = jnp.tanh(GELU_SCALE * (gate + GELU_CUBE * gate * gate * gate))
        value = low(0.5 * gate * (1.0 + bend) * up)
        hidden_tile[...] = value
        hidden_v[:, pl.ds(pl.multiple_of(step * tile, tile), tile)] = value

    def part_spec(row):
        return pl.BlockSpec((size, tile), lambda n: (row, n))

    in_specs, operands = [], []
    for group in range(2):
        for ref in gu_parts[group]:
            in_specs.append(part_spec(0))
            operands.append(ref)
        for offset in landed[group]:
            in_specs.append(part_spec(hops.chip_at(offset)))
            operands.append(gu_land.at[group])
    m, width = x.shape
    pltpu.emit_pipeline(
        body,
        grid=(tiles,),
        in_specs=in_specs,
        out_specs=[
            pl.BlockSpec((2, m, tile), lambda n: (0, 0, n)),
            pl.BlockSpec((m, tile), lambda n: (0, n)),
            pl.BlockSpec((2, width, tile), lambda n: (0, 0, n)),
        ],
    )(*operands, raw, hidden, gu_full)

    order, core_copies, side_copies = [], [], []

    def block_out(offset):
        i = len(order)
        order.append(offset)
        at = pl.ds(pl.multiple_of(hops.chip_at(offset) * size, size), size)
        out = product_t(hidden_v[...], dn[at, :])
        pairs[i] = out[: 2 * own]
        core_sent[i] = low(out[2 * own :])
        copy = remote(
            core_sent.at[i], core_got.at[i], core_sems.at[0], core_sems.at[1], (i,), hops.partner
        )
        core_copies.append(begin(copy))

    def core_sum():
        i = len(side_copies)
        core_copies[i].wait_recv()
        both = pairs[i] + to_float(core_got[i])
        side_sent[i] = low(both[own:])
        copy = remote(
            side_sent.at[i], side_got.at[i], side_sems.at[0], side_sems.at[1], (i,), hops.across
        )
        side_copies.append(begin(copy))
        at = pl.ds(pl.multiple_of(hops.chip_at(order[i]) * size, size), size)
        result[:, at] = both[:own]

    def out_and_sum(offset):
        block_out(offset)
        if len(order) > 1:
            core_sum()

    for k in range(hops_done[2] + 1, half + 1):
        arrive(moving)
        if k < half:
            moving = dn_hop(k + 1)
        if k == hops_done[2] + 1:
            for offset in places:
                out_and_sum(offset)
        if k < half:
            out_and_sum(-k)
            out_and_sum(k)
        else:
            out_and_sum(half)
    begin(pltpu.make_async_copy(dn, dn_full, stores.at[1]), saved)
    core_sum()
    for i, copy in enumerate(side_copies):
        copy.wait_recv()
        at = pl.ds(pl.multiple_of(hops.chip_at(order[i]) * size, size), size)
        result[:, at] = result[:, at] + to_float(side_got[i])
    for copy in started:
        copy.wait_send()
    for copy in saved[loaded:]:
        copy.wait()


def forward(x_own, gate_parts, up_down_parts, tile=512):
    chips = lax.axis_size("dp") // 2
    half = chips // 2
    own, width = x_own.shape
    size, ff = gate_parts[0].shape
    hops_done = [len(parts) // 2 for parts in (gate_parts, up_down_parts)]
    tile = min(tile, ff)
    m = 4 * own
    dma = pltpu.SemaphoreType.DMA
    vmem = pl.BlockSpec(memory_space=pltpu.VMEM)
    return pl.pallas_call(
        functools.partial(forward_kernel, hops_done, tile),
        out_shape=[
            jax.ShapeDtypeStruct((m, width), BF16),
            jax.ShapeDtypeStruct((2, width, ff), BF16),
            jax.ShapeDtypeStruct((2, width, ff), BF16),
            jax.ShapeDtypeStruct((width, ff), BF16),
            jax.ShapeDtypeStruct((2, m, ff), BF16),
            jax.ShapeDtypeStruct((m, ff), BF16),
            jax.ShapeDtypeStruct((own, width), F32),
        ],
        in_specs=[ANY] * (1 + len(gate_parts) + len(up_down_parts)),
        out_specs=[ANY] * 6 + [vmem],
        scratch_shapes=[
            pltpu.VMEM((m, width), BF16),
            pltpu.VMEM((width, ff), BF16),
            pltpu.VMEM((m, ff), BF16),
            pltpu.VMEM((chips, 2 * own, size), F32),
            pltpu.VMEM((chips, 2 * own, size), BF16),
            pltpu.VMEM((chips, 2 * own, size), BF16),
            pltpu.VMEM((chips, own, size), BF16),
            pltpu.VMEM((chips, own, size), BF16),
            dma((3,)),
            dma((3,)),
            dma((2, half, 2)),
            dma((2, half, 2)),
            dma((2, half)),
            dma((2, half)),
            dma((2, chips)),
            dma((2, chips)),
            dma((1 + len(up_down_parts),)),
            dma((2,)),
        ],
        compiler_params=pltpu.CompilerParams(
            collective_id=3, has_side_effects=True, vmem_limit_bytes=60 * 2**20
        ),
        cost_estimate=pl.CostEstimate(
            flops=6 * m * width * ff, bytes_accessed=0, transcendentals=0
        ),
        name="forward",
    )(x_own, *gate_parts, *up_down_parts)


def backward_kernel(d_own, hidden, raw, dn_full, gu_full, rows_in, *refs):
    (x_out, d_gu_out, held_up, held_down, wide_up, wide_down, result), refs = refs[:7], refs[7:]
    x, dn, hid, d_gu, raw_v, gu_v, first, got, refs = *refs[:8], refs[8:]
    pairs, core_sent, core_got, side_sent, side_got, refs = *refs[:5], refs[5:]
    rows_v, wide_first, refs = *refs[:2], refs[2:]
    x_send, x_recv, ring_send, ring_recv, core_sems, side_sems, wide_sems, loads, stores = refs
    hops = Hops()
    half, chips = hops.chips // 2, hops.chips
    own = d_own.shape[0]
    size, ff = held_up.shape
    cut = size // 2
    m = x.shape[0]
    cols = min(512, ff)
    greet([hops.above, hops.below, hops.partner, hops.across])
    started, saved = [], []

    def begin(copy, where=started):
        copy.start()
        where.append(copy)
        return copy

    def load(source, target, number):
        copy = pltpu.make_async_copy(source, target, loads.at[number])
        copy.start()
        return copy

    def part(r):
        return pl.ds(r * own, own)

    from_far = begin(remote(d_own, x.at[part(1)], x_send, x_recv, (0,), hops.across))
    from_near = begin(remote(d_own, x.at[part(2)], x_send, x_recv, (1,), hops.partner))
    load_x = load(d_own, x.at[part(0)], 0)
    load_dn = load(dn_full, dn, 1)
    rows_order = (0, 2, 1, 3)
    raw_loads = {}

    def load_raw(i):
        r = rows_order[i]
        raw_loads[r] = load(raw.at[:, part(r)], raw_v.at[i % 2], 3 + i)

    def load_gu(j):
        return load(gu_full.at[:, pl.ds(j * size, size)], gu_v.at[j % 2], 7 + j)

    load_raw(0)
    load_raw(1)
    load_hid = load(hidden, hid, 2)
    far_block = pl.ds(pl.multiple_of(hops.chip_at(half) * size, size), size)
    load_rows = load(rows_in.at[:, far_block], rows_v, 7 + chips)

    def hidden_part(i):
        r = rows_order[i]
        at = part(r)
        raw_loads[r].wait()

        @pl.loop(0, ff // cols)
        def _(c):
            across_ = pl.ds(pl.multiple_of(c * cols, cols), cols)
            d_hidden = product(x[at, :], dn[:, across_])
            gate = to_float(raw_v[i % 2, 0, :, across_])
            up = to_float(raw_v[i % 2, 1, :, across_])
            square = gate * gate
            bend = jnp.tanh(GELU_SCALE * gate * (1.0 + GELU_CUBE * square))
            plus = 0.5 * (1.0 + bend)
            slope = plus + 0.5 * gate * (1.0 - bend * bend) * GELU_SCALE * (
                1.0 + 3.0 * GELU_CUBE * square
            )
            d_gu[0, at, across_] = low(d_hidden * up * slope)
            d_gu[1, at, across_] = low(d_hidden * gate * plus)

        if i + 2 < 4:
            load_raw(i + 2)

    copies = {}

    def ring_step(k):
        for direction, ahead in ((0, hops.above), (1, hops.below)):
            near, far = direction * cut, (1 - direction) * cut
            offset = (half - k) * (1 if direction == 0 else -1)
            at = pl.ds(pl.multiple_of(hops.chip_at(offset) * size, size), size)
            term = product_l(x[:, at], hid[...])
            if k == 0:
                first[direction] = low(term[near : near + cut])
                source = first.at[direction]
                target = got.at[direction, 0, pl.ds(near, cut)]
            else:
                copies[(direction, k - 1)].wait_recv()
                came = got.at[direction, k - 1]
                if k == 1:
                    came[near : near + cut, :] = low(
                        term[near : near + cut] + to_float(came[near : near + cut, :])
                    )
                    came[far : far + cut, :] = low(term[far : far + cut])
                else:
                    came[...] = low(term + to_float(came[...]))
                source = came
                target = got.at[direction, k]
            copies[(direction, k)] = begin(
                remote(source, target, ring_send, ring_recv, (direction, k), ahead)
            )

    core_copies, side_copies = [], []

    def block_out(j, loading):
        loading.wait()
        out = product_t(d_gu[0], gu_v[j % 2, 0]) + product_t(d_gu[1], gu_v[j % 2, 1])
        pairs[j] = out[: 2 * own]
        core_sent[j] = low(out[2 * own :])
        copy = remote(
            core_sent.at[j], core_got.at[j], core_sems.at[0], core_sems.at[1], (j,), hops.partner
        )
        core_copies.append(begin(copy))

    def core_sum(j):
        core_copies[j].wait_recv()
        both = pairs[j] + to_float(core_got[j])
        side_sent[j] = low(both[own:])
        copy = remote(
            side_sent.at[j], side_got.at[j], side_sems.at[0], side_sems.at[1], (j,), hops.across
        )
        side_copies.append(begin(copy))
        result[:, j * size : (j + 1) * size] = both[:own]

    load_x.wait()
    load_dn.wait()
    hidden_part(0)
    from_near.wait_recv()
    hidden_part(1)
    from_far.wait_recv()
    passed = begin(remote(x.at[part(1)], x.at[part(3)], x_send, x_recv, (2,), hops.partner))
    hidden_part(2)
    passed.wait_recv()
    load_hid.wait()
    ring_step(0)
    gu_loads = {0: load_gu(0), 1: load_gu(1)}
    hidden_part(3)
    steps = list(range(1, half - 1))
    if steps:
        ring_step(steps.pop(0))
    load_rows.wait()
    for group in range(2):
        wide = product_l(rows_v[...], d_gu[group])
        for direction in range(2):
            wide_first[direction, :, group * ff : (group + 1) * ff] = low(
                wide[direction * cut : (direction + 1) * cut]
            )
    wide_copies = [
        begin(
            remote(
                wide_first.at[direction],
                target,
                wide_sems.at[0],
                wide_sems.at[1],
                (direction,),
                ahead,
            )
        )
        for direction, target, ahead in (
            (0, wide_up, hops.above),
            (1, wide_down, hops.below),
        )
    ]
    begin(pltpu.make_async_copy(x, x_out, stores.at[0]), saved)
    begin(pltpu.make_async_copy(d_gu, d_gu_out, stores.at[1]), saved)
    for j in range(chips):
        block_out(j, gu_loads[j])
        if j + 2 < chips:
            gu_loads[j + 2] = load_gu(j + 2)
        if j > 0:
            core_sum(j - 1)
        if j == 3 and steps:
            ring_step(steps.pop(0))
    core_sum(chips - 1)
    for k in steps:
        ring_step(k)
    for j, copy in enumerate(side_copies):
        copy.wait_recv()
        at = slice(j * size, (j + 1) * size)
        result[:, at] = result[:, at] + to_float(side_got[j])
    for direction, target in ((0, held_up), (1, held_down)):
        offset = 1 if direction == 0 else -1
        at = pl.ds(pl.multiple_of(hops.chip_at(offset) * size, size), size)
        term = product_l(x[:, at], hid[...])
        copies[(direction, half - 2)].wait_recv()
        came = got.at[direction, half - 2]
        came[...] = low(term + to_float(came[...]))
        begin(pltpu.make_async_copy(came, target, stores.at[2 + direction]), saved)
        wide_copies[direction].wait_recv()
    for copy in started:
        copy.wait_send()
    for copy in saved:
        copy.wait()


def backward(d_own, hidden, raw, dn_full, gu_full, rows_in):
    chips = lax.axis_size("dp") // 2
    half = chips // 2
    own, width = d_own.shape
    m, ff = hidden.shape
    size = width // chips
    dma = pltpu.SemaphoreType.DMA
    vmem = pl.BlockSpec(memory_space=pltpu.VMEM)
    return pl.pallas_call(
        backward_kernel,
        out_shape=[
            jax.ShapeDtypeStruct((m, width), BF16),
            jax.ShapeDtypeStruct((2, m, ff), BF16),
            jax.ShapeDtypeStruct((size, ff), BF16),
            jax.ShapeDtypeStruct((size, ff), BF16),
            jax.ShapeDtypeStruct((size // 2, 2 * ff), BF16),
            jax.ShapeDtypeStruct((size // 2, 2 * ff), BF16),
            jax.ShapeDtypeStruct((own, width), F32),
        ],
        in_specs=[ANY] * 6,
        out_specs=[ANY] * 6 + [vmem],
        scratch_shapes=[
            pltpu.VMEM((m, width), BF16),
            pltpu.VMEM((width, ff), BF16),
            pltpu.VMEM((m, ff), BF16),
            pltpu.VMEM((2, m, ff), BF16),
            pltpu.VMEM((2, 2, own, ff), BF16),
            pltpu.VMEM((2, 2, size, ff), BF16),
            pltpu.VMEM((2, size // 2, ff), BF16),
            pltpu.VMEM((2, half - 1, size, ff), BF16),
            pltpu.VMEM((chips, 2 * own, size), F32),
            pltpu.VMEM((chips, 2 * own, size), BF16),
            pltpu.VMEM((chips, 2 * own, size), BF16),
            pltpu.VMEM((chips, own, size), BF16),
            pltpu.VMEM((chips, own, size), BF16),
            pltpu.VMEM((m, size), BF16),
            pltpu.VMEM((2, size // 2, 2 * ff), BF16),
            dma((3,)),
            dma((3,)),
            dma((2, half - 1)),
            dma((2, half - 1)),
            dma((2, chips)),
            dma((2, chips)),
            dma((2, 2)),
            dma((8 + chips,)),
            dma((4,)),
        ],
        compiler_params=pltpu.CompilerParams(
            collective_id=4, has_side_effects=True, vmem_limit_bytes=60 * 2**20
        ),
        cost_estimate=pl.CostEstimate(
            flops=6 * m * width * ff, bytes_accessed=0, transcendentals=0
        ),
        name="backward",
    )(d_own, hidden, raw, dn_full, gu_full, rows_in)


def prepare_kernel(q_cols, kv_cols, spots, x, gain, w, cos, sin, gains, rows, raw, query, kv):
    turn = HD // 2
    values = to_float(x[...])
    scale = lax.rsqrt(jnp.mean(values * values, axis=-1, keepdims=True) + EPS)
    rows[...] = low(values * scale * gain[...])
    raw[...] = product(rows[...], w[...])
    cosines, sines = cos[...], sin[...]
    for start in range(0, q_cols + 2 * kv_cols, HD):
        at = slice(start, start + HD)
        head = raw[:, at]
        head = head * lax.rsqrt(jnp.mean(head * head, axis=-1, keepdims=True) + EPS)
        if start < q_cols + kv_cols:
            which = 0 if start < q_cols else 1
            head = head * gains[which : which + 1, :]
            front, rear = head[:, :turn], head[:, turn:]
            head = jnp.concatenate(
                [front * cosines - rear * sines, rear * cosines + front * sines], axis=1
            )
        if start < q_cols:
            query[start // HD] = low(head)
        else:
            kv[:, start - q_cols : start - q_cols + HD] = low(head)


def prepare(x, gain, w, cos, sin, gains, side, q_cols):
    (tall, width), cols = x.shape, w.shape[1]
    tile = tall // 2
    kv_cols = (cols - q_cols) // 2
    natural = lax.rem(jnp.arange(2) + side, 2).astype(jnp.int32)

    def straight(columns):
        return pl.BlockSpec((tile, columns), lambda t, s: (t, 0))

    return grid_call(
        functools.partial(prepare_kernel, q_cols, kv_cols),
        natural,
        (2,),
        (x, gain, w, cos, sin, gains),
        [
            straight(width),
            once(gain.shape),
            once(w.shape),
            straight(HD // 2),
            straight(HD // 2),
            once(gains.shape),
        ],
        [
            jax.ShapeDtypeStruct((tall, width), BF16),
            jax.ShapeDtypeStruct((tall, cols), F32),
            jax.ShapeDtypeStruct((q_cols // HD, tall, HD), BF16),
            jax.ShapeDtypeStruct((tall, 2 * kv_cols), BF16),
        ],
        [
            straight(width),
            straight(cols),
            pl.BlockSpec((q_cols // HD, tile, HD), lambda t, s: (0, t, 0)),
            pl.BlockSpec((tile, 2 * kv_cols), lambda t, s: (s[t], 0)),
        ],
        [],
        2 * tall * width * cols,
        "prepare",
    )


def prepare_back_kernel(q_cols, kv_cols, spots, raw, d_q, d_kv, after, before, cos, sin, gains, *refs):
    out, gain_grads = refs
    tall = raw.shape[0]
    turn = HD // 2
    cosines, sines = cos[...], sin[...]

    @pl.when(pl.program_id(0) == 0)
    def _():
        gain_grads[...] = jnp.zeros_like(gain_grads)

    early = spots[1 + pl.program_id(0)] < spots[0]
    more = to_float(after[...]) + jnp.where(early, to_float(before[...]), 0.0)

    def back(values, d, gain):
        scale = lax.rsqrt(jnp.mean(values * values, axis=-1, keepdims=True) + EPS)
        d_gain = d if gain is None else d * gain
        inner = jnp.mean(values * d_gain, axis=-1, keepdims=True)
        return scale * d_gain - values * (scale * scale * scale * inner), values * scale * d

    def unturn(d):
        front, rear = d[:, :turn], d[:, turn:]
        return jnp.concatenate(
            [front * cosines + rear * sines, rear * cosines - front * sines], axis=1
        )

    for start in range(0, q_cols + 2 * kv_cols, HD):
        at = slice(start, start + HD)
        values = raw[:, at]
        if start < q_cols:
            d, which = unturn(d_q[start // HD]), 0
        else:
            here = slice(start - q_cols, start - q_cols + HD)
            d = d_kv[:, here] + more[:, here]
            which = 1
            if start < q_cols + kv_cols:
                d = unturn(d)
        if start < q_cols + kv_cols:
            d_values, for_gain = back(values, d, gains[which : which + 1, :])
            gain_grads[which : which + 1, :] = gain_grads[which : which + 1, :] + jnp.sum(
                for_gain, axis=0, keepdims=True
            )
        else:
            d_values, _ = back(values, d, None)
        out[:, at] = low(d_values)


def prepare_back(raw, d_q, d_kv, after, before, cos, sin, gains, side, own, tile=128):
    tall, cols = raw.shape
    kv_cols = d_kv.shape[1] // 2
    q_cols = cols - 2 * kv_cols
    tiles = tall // tile
    near = before.shape[0] // tile
    natural = lax.rem(jnp.arange(tiles) + side * (own // tile), tiles)
    spots = jnp.concatenate([jnp.full((1,), near), natural]).astype(jnp.int32)

    def straight(width):
        return pl.BlockSpec((tile, width), lambda t, s: (t, 0))

    def ordered(width):
        return pl.BlockSpec((tile, width), lambda t, s: (s[1 + t], 0))

    return grid_call(
        functools.partial(prepare_back_kernel, q_cols, kv_cols),
        spots,
        (tiles,),
        (raw, d_q, d_kv, after, before, cos, sin, gains),
        [
            straight(cols),
            pl.BlockSpec((q_cols // HD, tile, HD), lambda t, s: (0, t, 0)),
            ordered(2 * kv_cols),
            ordered(2 * kv_cols),
            pl.BlockSpec((tile, 2 * kv_cols), lambda t, s: (jnp.minimum(s[1 + t], near - 1), 0)),
            straight(HD // 2),
            straight(HD // 2),
            once(gains.shape),
        ],
        [jax.ShapeDtypeStruct((tall, cols), BF16), jax.ShapeDtypeStruct((8, HD), F32)],
        [straight(cols), once((8, HD))],
        [],
        10 * raw.size,
        "prepare_back",
    )


class Gather:
    def __init__(self, ring, block):
        self.ring = ring
        self.rows = block.shape[0]
        self.held = [block, block]
        self.parts = [(0, 0, block)]
        self.step_count = 0

    def step(self):
        ring, half = self.ring, self.ring.chips // 2
        self.step_count += 1
        k = self.step_count
        going_up, going_down = self.held
        if k < half:
            self.held = [ring.up(going_up), ring.down(going_down)]
            self.parts += [(-k, 0, self.held[0]), (k, 0, self.held[1])]
        else:
            cut = self.rows // 2
            self.held = [ring.up(going_up[:cut]), ring.down(going_down[cut:])]
            self.parts += [(half, 0, self.held[0]), (half, cut, self.held[1])]

    def pieces(self):
        spots = [self.ring.chip_at(o) * self.rows + row for o, row, _ in self.parts]
        return jnp.stack(spots).astype(jnp.int32), [part for _, _, part in self.parts]


class BlockReduce:
    def __init__(self, ring, x, d, size):
        self.ring, self.x, self.d, self.size = ring, x, d, size
        self.step_count = 0
        self.held = []

    def offsets(self):
        half = self.ring.chips // 2
        k = self.step_count + 1
        return (half,) if k == 1 else (half + 1 - k, k - 1 - half)

    def blocks(self, offsets, gots=()):
        chips = [self.ring.chip_at(o) for o in offsets]
        return block_grads(self.x, self.d, chips, self.size, gots)

    def terms(self):
        return self.blocks(self.offsets())

    def last_term(self):
        return self.blocks((0,))[0]

    def step(self, terms=None, *beside):
        ring, half = self.ring, self.ring.chips // 2
        self.step_count += 1
        k = self.step_count
        cut = self.size // 2
        if k == 1:
            (term,) = self.blocks((half,))
            up, down = term[:cut], term[cut:]
        elif terms is None:
            up, down = self.blocks((half + 1 - k, k - 1 - half), self.held)
        else:
            up, down = add_blocks(terms, self.held)
        up, down, beside = tie(up, down, beside)
        self.held = [ring.up(up), ring.down(down)]
        return beside


def region(body):
    shapes = jax.eval_shape(body)
    yes = lax.optimization_barrier(jnp.array(True))
    return lax.cond(
        yes,
        body,
        lambda: jax.tree.map(lambda v: jnp.zeros(v.shape, v.dtype), shapes),
    )


def meet(rings, *values):
    held, values = tie([r.held for r in rings], values)
    for r, h in zip(rings, held):
        r.held = h
    return values if len(values) != 1 else values[0]


def local(
    tokens,
    layer_input,
    block_ids,
    block_table,
    w_query,
    w_key,
    w_value,
    w_output,
    w_left,
    w_right,
    w_gate,
    w_up,
    w_down,
    w_layer_gate,
    w_layer_proj,
    query_gain,
    key_gain,
    gain_input,
    gain_attn_out,
    gain_laurel,
    gain_ffw_in,
    gain_ffw_out,
    gain_layer_out,
    out_grad,
):
    ring = Ring()
    side = lax.axis_index("tensor")
    core = ring.core
    rows = w_query.shape[0]
    own = tokens.shape[0]
    width = tokens.shape[1]
    q_cols = w_query.shape[1]
    kv_cols = w_key.shape[1]
    rank = w_left.shape[1]
    small = w_layer_gate.shape[1]
    ff_cols = w_gate.shape[1] // 2
    chips = ring.chips

    gain_list = [
        gain_input,
        gain_attn_out,
        gain_laurel,
        gain_ffw_in,
        gain_ffw_out,
        gain_layer_out,
        query_gain,
        key_gain,
    ]
    gains = jnp.stack([jnp.pad(to_float(v), (0, 128 - v.shape[0])) for v in gain_list])
    gains = jnp.pad(gains, ((0, 8), (0, 0)))
    half = chips // 2
    if rows % 128 == 0:
        blocks = [
            [(w_query, False), (w_key, False), (w_value, False)],
            [(w_output, True)],
            [(w_left, False), (w_right, True), (w_layer_gate, False), (w_layer_proj, True)],
        ]
        down_source = (w_down, True)
    else:
        blocks = [
            [(jnp.concatenate([w_query, w_key, w_value], axis=1), False)],
            [(w_output.T, False)],
            [(jnp.concatenate([w_left, w_right.T, w_layer_gate, w_layer_proj.T], axis=1), False)],
        ]
        down_source = (w_down.T, False)
    (qkv_full, output_t, small_full, gains_full), (*ff_own, both_tokens) = first_gather(
        blocks + [[(gains, False)]], w_gate, w_up, down_source, tokens
    )
    left_full = small_full[:, :rank]
    right_t = small_full[:, rank : 2 * rank]
    lgate_full = small_full[:, 2 * rank : 2 * rank + small]
    lproj_t = small_full[:, 2 * rank + small : 2 * rank + 2 * small]
    gains_full = gains_full.reshape(ring.devices, 16, 128)
    head_part = query_gain.shape[0]
    (
        input_scale,
        attn_scale,
        laurel_scale,
        ffw_in_scale,
        ffw_out_scale,
        layer_scale,
    ) = (gains_full[:, i, :rows].reshape(width) for i in range(6))
    query_scale, key_scale = (gains_full[:, i, :head_part].reshape(HD) for i in (6, 7))

    piece_len = 2 * own
    seq_total = block_ids.shape[1]
    per_seq = seq_total // piece_len
    dp_index = lax.axis_index("dp")
    row_index = dp_index // per_seq
    slot = lax.rem(dp_index, per_seq)
    first = slot * piece_len
    has_before = slot > 0
    has_after = slot < per_seq - 1
    natural = jnp.arange(piece_len, dtype=jnp.int32)
    here = first + lax.rem(natural + side * own, piece_len)
    cosines, sines = rope_tables(here, HD)
    reach_after = min(256, piece_len)
    forward_pairs = [(i, i + 1) for i in range(ring.devices - 1)]
    backward_pairs = [(i + 1, i) for i in range(ring.devices - 1)]

    def in_order(values):
        return jnp.where(
            side == 0, values, jnp.concatenate([values[own:], values[:own]], axis=0)
        )

    ids_row = lax.dynamic_index_in_dim(block_ids, row_index, 0, keepdims=False)
    table_row = lax.dynamic_index_in_dim(block_table, row_index, 0, keepdims=False)
    own_ids = lax.dynamic_slice_in_dim(ids_row, first, piece_len, 0)
    before_ids = lax.dynamic_slice_in_dim(ids_row, jnp.maximum(first - piece_len, 0), piece_len, 0)
    before_ids = jnp.where(has_before, before_ids, -2)
    after_ids = lax.dynamic_slice_in_dim(
        ids_row, jnp.minimum(first + piece_len, seq_total - reach_after), reach_after, 0
    )
    after_ids = jnp.where(has_after, after_ids, -2)
    key_ids = jnp.concatenate([before_ids, own_ids, after_ids], axis=0)
    query_ids = in_order(own_ids)
    block_count = block_table.shape[-1]
    number_rows = jnp.arange(block_count, dtype=jnp.int32)
    sees_last = jnp.sum(
        jnp.where(number_rows[None, :] == number_rows[:, None] - 1, table_row, 0), axis=1
    )
    query_sees = jnp.sum(
        jnp.where(query_ids[:, None] == number_rows[None, :], sees_last[None, :], 0), axis=1
    )
    previous_ids = jnp.where(query_sees == 1, query_ids - 1, query_ids)

    both_gains = jnp.pad(jnp.stack([query_scale, key_scale]), ((0, 6), (0, 0)))

    heads_local = q_cols // HD
    all_rows = heads_local * piece_len

    def scores_for(query_low, keys):
        allowed = (query_ids[:, None] == key_ids[None, :]) | (
            previous_ids[:, None] == key_ids[None, :]
        )
        scores = product_t(query_low, keys).reshape(heads_local, piece_len, -1)
        return jnp.where(allowed[None], scores, NEGATIVE)

    def sum_sides(partial, beside=None):
        got = across(low(partial[own:]))
        if beside is None:
            return partial[:own] + to_float(got)
        got, beside = tie(got, beside())
        return partial[:own] + to_float(got), beside

    def both_sides(values, beside=None):
        got = across(values)
        if beside is None:
            return jnp.concatenate([values, got], axis=0)
        got, beside = tie(got, beside())
        return jnp.concatenate([values, got], axis=0), beside

    def four_ways(values):
        pair = both_sides(values)
        return jnp.concatenate([pair, ring.swap(pair)], axis=0)

    def sum_four(partial, beside=None):
        pair = partial[: 2 * own] + to_float(ring.swap(low(partial[2 * own :])))
        return sum_sides(pair, beside)

    def attend(query_low, kv_all):
        scores = scores_for(query_low, kv_all[:, :HD])
        highest = jnp.max(scores, axis=-1, keepdims=True)
        weights_exp = jnp.exp(scores - highest)
        totals = jnp.sum(weights_exp, axis=-1, keepdims=True)
        probs_low = low(weights_exp / totals).reshape(all_rows, -1)
        attended = low(product(probs_low, kv_all[:, HD:]))
        attended = attended.reshape(heads_local, piece_len, HD).transpose(1, 0, 2)
        return highest + jnp.log(totals), attended.reshape(piece_len, q_cols)

    fused = (2 * rows) % 256 == 0
    gate_ring, more_ring = (Gather(ring, v) for v in ff_own)
    gate_ring.step()
    seq_rows, qkv_raw, query_low, kv_own = region(
        lambda: prepare(
            both_tokens, input_scale[None], qkv_full, cosines, sines, both_gains, side, q_cols
        )
    )
    query_low = query_low.reshape(all_rows, HD)
    kv_own, query_ids, previous_ids, key_ids, *small_parts = meet(
        [gate_ring],
        kv_own,
        query_ids,
        previous_ids,
        key_ids,
        left_full,
        right_t,
        lgate_full,
        lproj_t,
    )
    left_full, right_t, lgate_full, lproj_t = small_parts
    kv_before = lax.ppermute(kv_own, "dp", forward_pairs)
    kv_after = lax.ppermute(kv_own[:reach_after], "dp", backward_pairs)
    kv_before, kv_after, more_ring.held, gate_ring.held = tie(
        kv_before, kv_after, more_ring.held, gate_ring.held
    )
    more_ring.step()
    gate_ring.step()
    kv_all = jnp.concatenate([kv_before, kv_own, kv_after], axis=0)
    def join(heads_low):
        attn_out = sum_sides(product_t(heads_low, output_t))
        normed = norm_gain(to_float(tokens), input_scale)
        left_low = low(product(low(normed), left_full))
        right_out = product_t(left_low, right_t)
        laurel_normed = norm_gain(right_out, laurel_scale)
        attn_normed = norm_gain(attn_out, attn_scale)
        mixed = (to_float(tokens) + attn_normed + (normed + laurel_normed)) * ROOT_HALF
        return attn_out, left_low, right_out, mixed, low(norm_gain(mixed, ffw_in_scale))

    def attend_and_join():
        log_totals, heads_low = attend(query_low, kv_all)
        return log_totals, heads_low, *join(heads_low)

    log_totals, heads_low, attn_out, left_low, right_out, mixed, ffw_low = region(attend_and_join)
    ffw_low = meet([gate_ring, more_ring], ffw_low)

    if fused:
        ffw_rows, gu_weights, _, dn_whole, raw, hidden_low, ffw_out = forward(
            ffw_low,
            [part for _, _, part in gate_ring.parts],
            [part for _, _, part in more_ring.parts],
        )
        dn_spots, dn_parts = jnp.zeros((1,), jnp.int32), [dn_whole]
    else:
        ffw_rows = four_ways(ffw_low)
        for weights_ring in (gate_ring, more_ring):
            while weights_ring.step_count < half:
                weights_ring.step()
        gu_spots, gate_parts = gate_ring.pieces()
        dn_spots, more_parts = more_ring.pieces()
        up_parts = [part[:, :ff_cols] for part in more_parts]
        dn_parts = [part[:, ff_cols:] for part in more_parts]
        raw, hidden_low, gu_weights = gate_up(ffw_rows, gu_spots, gate_parts, up_parts)
        ffw_out = sum_four(columns_out(hidden_low[None], dn_spots, dn_parts, width))
    ffw_out_normed, ffw_out_back = jax.vjp(norm_gain, ffw_out, ffw_out_scale)
    block_mid = mixed + ffw_out_normed
    mid_low = low(block_mid)
    layer_pre = product(mid_low, lgate_full)

    def layer_gate_fn(pre_values, per_layer):
        return gelu_tanh(pre_values) * per_layer

    gated, gated_back = jax.vjp(layer_gate_fn, layer_pre, to_float(layer_input))
    gated_low = low(gated)
    layer_proj = product_t(gated_low, lproj_t)
    proj_normed, proj_back = jax.vjp(norm_gain, layer_proj, layer_scale)
    result = block_mid + proj_normed

    grad_out = to_float(out_grad)
    d_proj, d_layer_scale = proj_back(grad_out)
    d_proj_low = low(d_proj)
    d_gated = product(d_proj_low, lproj_t)
    d_pre, grad_layer_input = gated_back(d_gated)
    d_pre_low = low(d_pre)
    d_mid = grad_out + product_t(d_pre_low, lgate_full)
    d_ffw_out, d_ffw_out_scale = ffw_out_back(d_mid)
    if fused:
        d_ffw_rows, d_gate_up, *held, d_ffw_normed = backward(
            low(d_ffw_out), hidden_low, raw, dn_whole, gu_weights, ffw_rows
        )
        rd = BlockReduce(ring, d_ffw_rows, hidden_low[None], 2 * rows)
        rd.held, rd.step_count = [ring.up(held[0]), ring.down(held[1])], half
        rg = BlockReduce(ring, ffw_rows, d_gate_up, 2 * rows)
        rg.held, rg.step_count = held[2:], 1
    else:
        d_ffw_rows = four_ways(low(d_ffw_out))
        rd = BlockReduce(ring, d_ffw_rows, hidden_low[None], 2 * rows)
        for _ in range(half - 1):
            rd.step()
            meet([rd])
        d_gate_up = hidden_back(d_ffw_rows, raw, dn_spots, dn_parts)
        d_ffw_normed = sum_four(
            product_t(d_gate_up[0], gu_weights[0]) + product_t(d_gate_up[1], gu_weights[1])
        )
        rg = BlockReduce(ring, ffw_rows, d_gate_up, 2 * rows)
        for _ in range(half - 3):
            rg.step()
            meet([rg])
        rd.step()
    rg.step()

    def back_34():
        _, back = jax.vjp(norm_gain, mixed, ffw_in_scale)
        d_mixed_extra, d_ffw_in_scale = back(d_ffw_normed)
        d_branch = (d_mid + d_mixed_extra) * ROOT_HALF
        _, back = jax.vjp(norm_gain, attn_out, attn_scale)
        d_attn, d_attn_scale = back(d_branch)
        d_attn_rows, terms = both_sides(low(d_attn), rg.terms)
        d_heads = low(product(d_attn_rows, output_t)).reshape(piece_len, heads_local, HD)
        d_heads = d_heads.transpose(1, 0, 2).reshape(all_rows, HD)
        keys, values = kv_all[:, :HD], kv_all[:, HD:]
        probs = jnp.exp(scores_for(query_low, keys) - log_totals)
        d_values = product_l(low(probs).reshape(all_rows, -1), d_heads)
        d_probs = product_t(d_heads, values).reshape(probs.shape)
        deltas = jnp.sum(probs * d_probs, axis=-1, keepdims=True)
        d_scores = low(probs * (d_probs - deltas)).reshape(all_rows, -1)
        d_keys = product_l(d_scores, query_low)
        d_query_rot = product(d_scores, keys).reshape(heads_local, piece_len, HD)
        d_kv_all = jnp.concatenate([d_keys, d_values], axis=1)
        to_before = low(d_kv_all[:piece_len])
        to_after = low(d_kv_all[2 * piece_len :])
        d_kv_own = d_kv_all[piece_len : 2 * piece_len]
        moving = (to_before, to_after)
        kept = (d_ffw_in_scale, d_attn_scale, d_branch, d_attn_rows, d_kv_own)
        return terms, moving, kept, d_query_rot

    terms, moving, kept, d_query_rot = meet([rd, rg], *region(back_34))
    d_ffw_in_scale, d_attn_scale, d_branch, d_attn_rows, d_kv_own = kept
    from_after = lax.ppermute(moving[0], "dp", backward_pairs)
    from_before = lax.ppermute(moving[1], "dp", forward_pairs)
    from_after, from_before = rg.step(terms, from_after, from_before)

    def back_5():
        d_qkv_low, gain_sums = prepare_back(
            qkv_raw,
            d_query_rot,
            d_kv_own,
            from_after,
            from_before,
            cosines,
            sines,
            both_gains,
            side,
            own,
        )
        d_more, ends = sum_sides(
            product_t(d_qkv_low, qkv_full), lambda: (rd.last_term(), rg.last_term(), rg.terms())
        )
        return d_more, ends, d_qkv_low, gain_sums[0], gain_sums[1]

    d_more, ends, d_qkv_low, query_scale_grad, key_scale_grad = meet([rg], *region(back_5))
    *ends, terms = ends
    rg.step(terms)

    def head_gain_back(grads):
        padded = jnp.pad(grads.reshape(ring.devices, head_part), ((0, 0), (0, rows - head_part)))
        return padded.reshape(width)

    def back_6():
        normed, input_norm_back = jax.vjp(norm_gain, to_float(tokens), input_scale)
        _, laurel_back = jax.vjp(norm_gain, right_out, laurel_scale)
        d_right, d_laurel_scale = laurel_back(d_branch)
        d_right_low = low(d_right)
        d_left_low = low(product(d_right_low, right_t))
        d_normed = d_branch + product_t(d_left_low, left_full)
        d_normed = d_normed + d_more
        d_inputs_extra, d_input_scale = input_norm_back(d_normed)
        grad_tokens = d_branch + d_inputs_extra
        gain_grads = jnp.stack(
            [
                d_input_scale,
                d_attn_scale,
                d_laurel_scale,
                d_ffw_in_scale,
                d_ffw_out_scale,
                d_layer_scale,
                head_gain_back(query_scale_grad),
                head_gain_back(key_scale_grad),
            ],
            axis=0,
        )
        gain_grads = jnp.pad(gain_grads, ((0, 120), (0, 0))).T
        pairs = [
            (d_attn_rows, heads_low),
            (seq_rows, d_qkv_low),
            (mid_low, d_pre_low),
            (d_proj_low, gated_low),
            (low(normed), d_left_low),
            (d_right_low, left_low),
        ]
        return grad_tokens, row_grads(pairs, gain_grads, core, chips, rows)

    grad_tokens, (mine, theirs) = meet([rg], *region(back_6))
    down_end, gate_up_end = ends
    total, out_small, out_gate, out_up, out_down_t = last_reduce(
        mine,
        theirs,
        2 * q_cols + 2 * kv_cols,
        [gate_up_end, *rg.held, down_end, *rd.held],
    )
    out_output = total[:, :q_cols].T
    out_qkv = total[:, q_cols:]
    out_gains = out_small[:, 2 * rank + 2 * small :]
    return (
        low(result),
        grad_tokens,
        grad_layer_input,
        out_qkv[:, :q_cols],
        out_qkv[:, q_cols : q_cols + kv_cols],
        out_qkv[:, q_cols + kv_cols :],
        out_output,
        out_small[:, 2 * small : 2 * small + rank],
        out_small[:, 2 * small + rank : 2 * small + 2 * rank].T,
        out_gate,
        out_up,
        out_down_t.T,
        out_small[:, :small],
        out_small[:, small : 2 * small].T,
        out_gains[:head_part, 6],
        out_gains[:head_part, 7],
        out_gains[:, 0],
        out_gains[:, 1],
        out_gains[:, 2],
        out_gains[:, 3],
        out_gains[:, 4],
        out_gains[:, 5],
    )


def solution(mesh):
    both = P(("dp", "tensor"), None)
    rows_split = P("dp", "tensor")
    cols_split = P("tensor", "dp")
    by_row = P("dp", None)
    by_col = P(None, "dp")
    flat = P("dp")
    return jax.shard_map(
        local,
        mesh=mesh,
        in_specs=(
            (both, both, P(), P(), rows_split, rows_split, rows_split, cols_split)
            + (by_row, by_col, rows_split, rows_split, cols_split, by_row, by_col)
            + (flat,) * 8
            + (both,)
        ),
        out_specs=(
            (both, both, both, rows_split, rows_split, rows_split, cols_split)
            + (by_row, by_col, rows_split, rows_split, cols_split, by_row, by_col)
            + (flat,) * 8
        ),
        check_vma=False,
    )
```

```python
import functools

import jax
import jax.numpy as jnp
from jax import lax
from jax.experimental import pallas as pl
from jax.experimental.pallas import tpu as pltpu
from jax.sharding import PartitionSpec as P

HD = 256
EPS = 1e-06
ROOT_HALF = 0.7071067811865476
NEGATIVE = -1e30
F32 = jnp.float32
BF16 = jnp.bfloat16


def norm_gain(values, gains):
    return values * lax.rsqrt(jnp.mean(values * values, axis=-1, keepdims=True) + EPS) * gains


def norm_plain(values):
    return values * lax.rsqrt(jnp.mean(values * values, axis=-1, keepdims=True) + EPS)


def gelu_tanh(values):
    return jax.nn.gelu(values, approximate=True)


def rope_tables(positions, head_width):
    positions = positions.astype(F32)[:, None]
    frequency = 10000.0 ** (-2.0 * jnp.arange(head_width // 2, dtype=F32) / head_width)
    angles = positions * frequency[None, :]
    return (jnp.cos(angles), jnp.sin(angles))


def rotate(values, cosines, sines):
    half_width = values.shape[-1] // 2
    front_half = values[..., :half_width]
    back_half = values[..., half_width:]
    cos_wide = cosines[:, None, :]
    sin_wide = sines[:, None, :]
    return jnp.concatenate(
        [
            front_half * cos_wide - back_half * sin_wide,
            back_half * cos_wide + front_half * sin_wide,
        ],
        axis=-1,
    )


def to_float(values):
    return values.astype(F32)


def low(values):
    return values.astype(BF16)


def product(left_in, right_in):
    return jnp.dot(left_in, right_in, preferred_element_type=F32)


def product_t(left_in, right_in):
    return lax.dot_general(left_in, right_in, (((1,), (1,)), ((), ())), preferred_element_type=F32)


def product_l(left_in, right_in):
    return lax.dot_general(left_in, right_in, (((0,), (0,)), ((), ())), preferred_element_type=F32)


def tie(*values):
    return lax.optimization_barrier(values)


class Ring:
    def __init__(self):
        self.devices = lax.axis_size("dp")
        self.chips = self.devices // 2
        order = list(range(0, self.chips, 2)) + list(range(self.chips - 1, 0, -2))
        self.cw = [
            (2 * order[p] + c, 2 * order[(p + 1) % self.chips] + c)
            for p in range(self.chips)
            for c in range(2)
        ]
        self.ccw = [(b, a) for a, b in self.cw]
        self.core_pairs = [(d, d ^ 1) for d in range(self.devices)]
        me = lax.axis_index("dp")
        self.core = lax.rem(me, 2)
        self.chip = me // 2
        self.place = jnp.where(
            lax.rem(self.chip, 2) == 0, self.chip // 2, self.chips - 1 - self.chip // 2
        )

    def chip_at(self, offset):
        place = lax.rem(self.place + offset + self.chips, self.chips)
        return jnp.where(place < self.chips // 2, 2 * place, 2 * (self.chips - 1 - place) + 1)

    def up(self, values):
        return lax.ppermute(values, "dp", self.cw)

    def down(self, values):
        return lax.ppermute(values, "dp", self.ccw)

    def swap(self, values):
        return lax.ppermute(values, "dp", self.core_pairs)


def across(values):
    return lax.ppermute(values, "tensor", [(0, 1), (1, 0)])


def remote(source, target, sends, receives, index, device):
    return pltpu.make_async_remote_copy(
        src_ref=source,
        dst_ref=target,
        send_sem=sends.at[index],
        recv_sem=receives.at[index],
        device_id=device,
        device_id_type=pl.DeviceIdType.MESH,
    )


def greet(devices):
    barrier = pltpu.get_barrier_semaphore()
    for device in devices:
        pl.semaphore_signal(
            barrier, inc=1, device_id=device, device_id_type=pl.DeviceIdType.MESH
        )
    pl.semaphore_wait(barrier, len(devices))


def block_rows(ref, start, count):
    return ref.at[pl.ds(pl.multiple_of(start, 16), count)]


class Hops:
    def __init__(self):
        me = lax.axis_index("dp")
        self.chips = lax.axis_size("dp") // 2
        self.core = lax.rem(me, 2)
        self.chip = me // 2
        self.place = jnp.where(
            lax.rem(self.chip, 2) == 0, self.chip // 2, self.chips - 1 - self.chip // 2
        )
        self.partner = {"dp": self.chip * 2 + 1 - self.core}
        self.above = {"dp": self.chip_at(1) * 2 + self.core}
        self.below = {"dp": self.chip_at(-1) * 2 + self.core}
        self.across = {"tensor": 1 - lax.axis_index("tensor")}

    def chip_at(self, offset):
        place = lax.rem(self.place + offset + self.chips, self.chips)
        return jnp.where(place < self.chips // 2, 2 * place, 2 * (self.chips - 1 - place) + 1)


def staged_apart(source_shape, turned, start):
    cols = source_shape[0] if turned else source_shape[1]
    return turned or start % 128 != 0 or cols % 128 != 0, cols


def first_kernel(layout, down_turned, ff_cols, *refs):
    count = len(layout)
    sources, refs = refs[: sum(len(l) for l in layout)], refs[sum(len(l) for l in layout) :]
    (gate, up, down, tokens), refs = refs[:4], refs[4:]
    wholes, refs = refs[:count], refs[count:]
    (gate_own, up_down_own, other_tokens), refs = refs[:3], refs[3:]
    stages, refs = refs[:count], refs[count:]
    (gate_v, up_v, tokens_v, down_v, down_t), refs = refs[:5], refs[5:]
    apart, refs = list(refs[:-8]), refs[-8:]
    in_sems, out_sems, ring_send, ring_recv, pair_send, pair_recv, ff_send, ff_recv = refs
    hops = Hops()
    half = hops.chips // 2
    mine = pl.ds(pl.multiple_of(hops.core * ff_cols, 128), ff_cols)
    theirs = pl.ds(pl.multiple_of((1 - hops.core) * ff_cols, 128), ff_cols)

    number = 0

    def load(source, target):
        nonlocal number
        copy = pltpu.make_async_copy(source, target, in_sems.at[number])
        copy.start()
        number += 1
        return copy

    taken = list(sources)
    fills = []
    for which, flags in enumerate(layout):
        start, steps = 0, []
        for turned in flags:
            source = taken.pop(0)
            own_buffer, cols = staged_apart(source.shape, turned, start)
            if own_buffer:
                buffer = apart.pop(0)
                steps.append((load(source, buffer), buffer, turned, start, cols))
            else:
                target = stages[which].at[:, pl.ds(start, cols)]
                steps.append((load(source, target), None, turned, start, cols))
            start += cols
        fills.append(steps)
    load_down = load(down, down_v)
    bounces = [(load(gate.at[:, mine], gate_v), gate_v), (load(up.at[:, mine], up_v), up_v)]
    load_tokens = load(tokens, tokens_v)
    greet([hops.above, hops.below, hops.partner, hops.across])
    started, stores = [], []

    def place(which, offset, top, size):
        tall = stages[which].shape[0]
        at = (2 * hops.chip_at(offset) + hops.core) * tall + top
        return wholes[which].at[pl.ds(pl.multiple_of(at, 8 if tall <= 16 else 16), size)]

    def store(source, target):
        copy = pltpu.make_async_copy(source, target, out_sems.at[len(stores)])
        copy.start()
        stores.append(copy)

    def to_partner(number, which, offset, top, size, source=None):
        spot = place(which, offset, top, size)
        copy = remote(
            spot if source is None else source,
            spot,
            pair_send,
            pair_recv,
            (number, which),
            hops.partner,
        )
        copy.start()
        started.append(copy)
        pairs.append(copy)

    def onward(direction, k, which, offset, top, size, source=None):
        spot = place(which, offset, top, size)
        copy = remote(
            spot if source is None else source,
            spot,
            ring_send,
            ring_recv,
            (direction, k, which),
            hops.above if direction == 0 else hops.below,
        )
        copy.start()
        started.append(copy)
        arrivals[(direction, k, which)] = copy

    pairs, arrivals = [], {}
    for which, steps in enumerate(fills):
        stage = stages[which]
        for copy, buffer, turned, start, cols in steps:
            copy.wait()
            if buffer is not None:
                stage[:, start : start + cols] = buffer[...].T if turned else buffer[...]
        tall = stage.shape[0]
        for direction in range(2):
            onward(direction, 0, which, 0, 0, tall, stage)
    own = tokens.shape[0]
    theirs_at = other_tokens.at[pl.ds(own, own)]
    ff_copies = [remote(tokens, theirs_at, ff_send, ff_recv, (3,), hops.across)]
    ff_copies[0].start()
    rows = gate.shape[0]
    own_rows = pl.ds(pl.multiple_of(hops.core * rows, 16), rows)
    targets = [
        gate_own.at[own_rows],
        up_down_own.at[own_rows, pl.ds(0, ff_cols)],
        up_down_own.at[own_rows, pl.ds(ff_cols, ff_cols)],
    ]
    load_down.wait()
    if down_turned:
        down_t[...] = down_v[...].T
        down = down_t
    else:
        down = down_v
    for number_, (weight, target) in enumerate(zip((gate, up, down), targets)):
        copy = remote(
            weight.at[:, theirs], target, ff_send, ff_recv, (number_,), hops.partner
        )
        copy.start()
        ff_copies.append(copy)
    for which, stage in enumerate(stages):
        to_partner(0, which, 0, 0, stage.shape[0], stage)
        store(stage, place(which, 0, 0, stage.shape[0]))
    for (copy, buffer), target in zip(bounces, targets):
        copy.wait()
        store(buffer, target)
    store(down.at[:, mine], targets[2])
    load_tokens.wait()
    store(tokens_v, other_tokens.at[pl.ds(0, own)])
    for k in range(1, half + 1):
        for which in range(count):
            tall = stages[which].shape[0]
            cut = tall // 2
            for direction in range(2):
                arrivals[(direction, k - 1, which)].wait_recv()
                offset = -k if direction == 0 else k
                if k < half - 1:
                    onward(direction, k, which, offset, 0, tall)
                elif k == half - 1:
                    onward(direction, k, which, offset, direction * cut, cut)
                if k < half:
                    to_partner(2 * k - 1 + direction, which, offset, 0, tall)
                else:
                    to_partner(2 * k - 1 + direction, which, half, direction * cut, cut)
    for copy in ff_copies + pairs:
        copy.wait_recv()
    for copy in ff_copies + started:
        copy.wait_send()
    for copy in stores:
        copy.wait()


ANY = pl.BlockSpec(memory_space=pl.ANY)


def comm_call(kernel, number, operands, shapes, stages, semaphores, name):
    moved = sum(v.size * 2 for v in shapes)
    return pl.pallas_call(
        kernel,
        out_shape=shapes,
        in_specs=[ANY] * len(operands),
        out_specs=[ANY] * len(shapes),
        scratch_shapes=stages + [pltpu.SemaphoreType.DMA(shape) for shape in semaphores],
        compiler_params=pltpu.CompilerParams(
            collective_id=number, has_side_effects=True, vmem_limit_bytes=60 * 2**20
        ),
        cost_estimate=pl.CostEstimate(flops=0, bytes_accessed=8 * moved, transcendentals=0),
        name=name,
    )(*operands)


def first_gather(blocks, gate, up, down, tokens):
    chips = lax.axis_size("dp") // 2
    half = chips // 2
    down, down_turned = down
    rows = gate.shape[0]
    ff_cols = gate.shape[1] // 2
    count = len(blocks)
    stages, apart = [], []
    for block in blocks:
        start = 0
        for source, turned in block:
            own_buffer, cols = staged_apart(source.shape, turned, start)
            if own_buffer:
                apart.append(pltpu.VMEM(source.shape, source.dtype))
            start += cols
        first, turned = block[0]
        tall = first.shape[1] if turned else first.shape[0]
        stages.append(pltpu.VMEM((tall, start), first.dtype))
    shapes = [
        jax.ShapeDtypeStruct((2 * chips * stage.shape[0], stage.shape[1]), stage.dtype)
        for stage in stages
    ] + [
        jax.ShapeDtypeStruct((2 * rows, ff_cols), gate.dtype),
        jax.ShapeDtypeStruct((2 * rows, 2 * ff_cols), gate.dtype),
        jax.ShapeDtypeStruct((2 * tokens.shape[0], tokens.shape[1]), tokens.dtype),
    ]
    more = [
        pltpu.VMEM((rows, ff_cols), gate.dtype),
        pltpu.VMEM((rows, ff_cols), gate.dtype),
        pltpu.VMEM(tokens.shape, tokens.dtype),
        pltpu.VMEM(down.shape, down.dtype),
        pltpu.VMEM((rows, 2 * ff_cols), down.dtype),
    ]
    sources = [source for block in blocks for source, _ in block]
    semaphores = [
        (len(sources) + 4,),
        (4 + count,),
        (2, half, count),
        (2, half, count),
        (2 * half + 1, count),
        (2 * half + 1, count),
        (4,),
        (4,),
    ]
    layout = tuple(tuple(turned for _, turned in block) for block in blocks)
    out = comm_call(
        functools.partial(first_kernel, layout, down_turned, ff_cols),
        0,
        (*sources, gate, up, down, tokens),
        shapes,
        stages + more + apart,
        semaphores,
        "first_gather",
    )
    return out[:count], out[count:]


GELU_SCALE = 0.7978845608028654
GELU_CUBE = 0.044715
ROW_TILE = 1024


def fill(spots, whole, parts):
    for number, part in enumerate(parts):
        size = part.shape[0]
        whole[pl.ds(pl.multiple_of(spots[number], size), size), :] = part[...]


def gate_up_kernel(count, spots, x, *refs):
    gate_parts, up_parts = refs[:count], refs[count : 2 * count]
    raw, hidden, weights = refs[2 * count :]
    gate_w, up_w = weights.at[0], weights.at[1]
    fill(spots, gate_w, gate_parts)
    fill(spots, up_w, up_parts)

    @pl.loop(0, x.shape[0] // min(ROW_TILE, x.shape[0]))
    def _(i):
        at = pl.ds(pl.multiple_of(i * ROW_TILE, ROW_TILE), ROW_TILE)
        rows = x[at, :]
        gate = product(rows, gate_w[...])
        up = product(rows, up_w[...])
        raw[0, at, :] = low(gate)
        raw[1, at, :] = low(up)
        bend = jnp.tanh(GELU_SCALE * (gate + GELU_CUBE * gate * gate * gate))
        hidden[at, :] = low(0.5 * gate * (1.0 + bend) * up)


def hidden_back_kernel(count, spots, x, raw, *refs):
    parts, (out, whole) = refs[:count], refs[count:]
    fill(spots, whole, parts)

    @pl.loop(0, x.shape[0] // min(ROW_TILE, x.shape[0]))
    def _(i):
        at = pl.ds(pl.multiple_of(i * ROW_TILE, ROW_TILE), ROW_TILE)
        d_hidden = product(x[at, :], whole[...])
        gate = to_float(raw[0, at, :])
        up = to_float(raw[1, at, :])
        square = gate * gate
        bend = jnp.tanh(GELU_SCALE * gate * (1.0 + GELU_CUBE * square))
        plus = 0.5 * (1.0 + bend)
        slope = plus + 0.5 * gate * (1.0 - bend * bend) * GELU_SCALE * (
            1.0 + 3.0 * GELU_CUBE * square
        )
        out[0, at, :] = low(d_hidden * up * slope)
        out[1, at, :] = low(d_hidden * gate * plus)


def columns_kernel(count, spots, h, *refs):
    parts, (out, whole) = refs[:count], refs[count:]
    fill(spots, whole, parts)
    step = pl.program_id(0)
    width = out.shape[1]
    cols = min(512, width)


    @pl.loop(0, width // cols)
    def _(j):
        across_ = pl.ds(pl.multiple_of(j * cols, cols), cols)
        term = product_t(h[0], whole[across_, :])

        @pl.when(step == 0)
        def _():
            out[:, across_] = term

        @pl.when(step > 0)
        def _():
            out[:, across_] = out[:, across_] + term


def block_kernel(count, came, spots, *refs):
    xs, d, refs = refs[:count], refs[count], refs[count + 1 :]
    gots, refs = refs[:came], refs[came:]
    outs, turned = refs[:count], refs[count:]

    @pl.when(pl.program_id(0) == 0)
    def _():
        for x, t in zip(xs, turned):
            t[...] = x[...].T

    for i, (t, out) in enumerate(zip(turned, outs)):
        term = product(t[...], d[0])
        if came == 0:
            out[...] = low(term)
        elif gots[i].shape == out.shape:
            out[...] = low(term + to_float(gots[i][...]))
        else:
            cut = gots[i].shape[0]
            near, far = slice(i * cut, (i + 1) * cut), slice((1 - i) * cut, (2 - i) * cut)
            out[near, :] = low(term[near] + to_float(gots[i][...]))
            out[far, :] = low(term[far])


def grid_call(kernel, spots, grid, operands, in_specs, shapes, out_specs, scratch, flops, name):
    moved = sum(v.size * v.dtype.itemsize for v in (*operands, *jax.tree.leaves(shapes)))
    if flops == 0:
        moved = 0
    return pl.pallas_call(
        kernel,
        grid_spec=pltpu.PrefetchScalarGridSpec(
            num_scalar_prefetch=1,
            grid=grid,
            in_specs=in_specs,
            out_specs=out_specs,
            scratch_shapes=scratch,
        ),
        out_shape=shapes,
        compiler_params=pltpu.CompilerParams(
            dimension_semantics=("arbitrary",) * len(grid), vmem_limit_bytes=56 * 2**20
        ),
        cost_estimate=pl.CostEstimate(flops=flops, bytes_accessed=moved, transcendentals=0),
        name=name,
    )(spots, *operands)


def once(shape):
    return pl.BlockSpec(
        shape, lambda *index: (0,) * len(shape), pipeline_mode=pl.Buffered(buffer_count=1)
    )


def gate_up(x, spots, parts, up_parts, tile=512):
    count, (m, width), ff = len(parts), x.shape, parts[0].shape[1]
    tiles = ff // tile
    part_specs = [pl.BlockSpec((p.shape[0], tile), lambda n, s: (0, n)) for p in parts] * 2
    return grid_call(
        functools.partial(gate_up_kernel, count),
        spots,
        (tiles,),
        (x, *parts, *up_parts),
        [once((m, width))] + part_specs,
        [
            jax.ShapeDtypeStruct((2, m, ff), BF16),
            jax.ShapeDtypeStruct((m, ff), BF16),
            jax.ShapeDtypeStruct((2, width, ff), BF16),
        ],
        [
            pl.BlockSpec((2, m, tile), lambda n, s: (0, 0, n)),
            pl.BlockSpec((m, tile), lambda n, s: (0, n)),
            pl.BlockSpec((2, width, tile), lambda n, s: (0, 0, n)),
        ],
        [],
        4 * m * width * ff,
        "gate_up",
    )


def hidden_back(x, raw, spots, parts, tile=256):
    count, (m, width), ff = len(parts), x.shape, parts[0].shape[1]
    part_specs = [pl.BlockSpec((p.shape[0], tile), lambda n, s: (0, n)) for p in parts]
    return grid_call(
        functools.partial(hidden_back_kernel, count),
        spots,
        (ff // tile,),
        (x, raw, *parts),
        [once((m, width)), pl.BlockSpec((2, m, tile), lambda n, s: (0, 0, n))] + part_specs,
        jax.ShapeDtypeStruct((2, m, ff), BF16),
        pl.BlockSpec((2, m, tile), lambda n, s: (0, 0, n)),
        [pltpu.VMEM((width, tile), BF16)],
        2 * m * width * ff,
        "hidden_back",
    )


def columns_out(h, spots, parts, width, tile=1024):
    count, (groups, m, ff) = len(parts), h.shape
    tile = min(tile, ff)
    tiles = ff // tile
    part_specs = [pl.BlockSpec((p.shape[0], tile), lambda f, s: (0, f)) for p in parts]
    return grid_call(
        functools.partial(columns_kernel, count),
        spots,
        (groups * tiles,),
        (h, *parts),
        [pl.BlockSpec((1, m, tile), lambda f, s: (f // tiles, 0, f % tiles))] + part_specs,
        jax.ShapeDtypeStruct((m, width), F32),
        once((m, width)),
        [pltpu.VMEM((width, tile), BF16)],
        2 * groups * m * width * ff,
        "columns_out",
    )


def block_grads(x, d, chips, size, gots=(), tile=2048):
    (m, _), (groups, _, ff) = x.shape, d.shape
    count = len(chips)
    tile = min(tile, ff)
    tiles = ff // tile
    spots = jnp.stack(chips).astype(jnp.int32)
    if size % 128:
        xs = [lax.dynamic_slice_in_dim(x, chip * size, size, 1) for chip in chips]
        x_specs = [once((m, size))] * count
    else:
        xs = [x] * count
        x_specs = [
            pl.BlockSpec((m, size), functools.partial(lambda i, f, s: (0, s[i]), i))
            for i in range(count)
        ]
    return grid_call(
        functools.partial(block_kernel, count, len(gots)),
        spots,
        (groups * tiles,),
        (*xs, d, *gots),
        x_specs
        + [pl.BlockSpec((1, m, tile), lambda f, s: (f // tiles, 0, f % tiles))]
        + [pl.BlockSpec((v.shape[0], tile), lambda f, s: (0, f)) for v in gots],
        [jax.ShapeDtypeStruct((size, groups * ff), BF16)] * count,
        [pl.BlockSpec((size, tile), lambda f, s: (0, f))] * count,
        [pltpu.VMEM((size, m), BF16)] * count,
        0,
        "block_grads",
    )


def add_kernel(count, spots, *refs):
    terms, gots, outs = refs[:count], refs[count : 2 * count], refs[2 * count :]
    for term, got, out in zip(terms, gots, outs):
        out[...] = low(to_float(term[...]) + to_float(got[...]))


def add_blocks(terms, gots, tile=2048):
    tall, wide = terms[0].shape
    tile = min(tile, wide)
    count = len(terms)
    block = pl.BlockSpec((tall, tile), lambda f, s: (0, f))
    return grid_call(
        functools.partial(add_kernel, count),
        jnp.zeros((1,), jnp.int32),
        (wide // tile,),
        (*terms, *gots),
        [block] * (2 * count),
        [jax.ShapeDtypeStruct((tall, wide), BF16)] * count,
        [block] * count,
        [],
        terms[0].size,
        "add_blocks",
    )


def row_kernel(pairs, spots, *refs):
    xs, ds = refs[:pairs], refs[pairs : 2 * pairs]
    last, mine, theirs, both = refs[2 * pairs :]
    rows = mine.shape[0]
    core = spots[0]
    start = 0
    for x, d in zip(xs, ds):
        cols = d.shape[1]
        both[:, start : start + cols] = product_l(x[...], d[...])
        start += cols
    both[:, start:] = last[...]
    mine[...] = both[pl.ds(pl.multiple_of(core * rows, 128), rows), :]
    theirs[...] = low(both[pl.ds(pl.multiple_of((1 - core) * rows, 128), rows), :])


def row_grads(pairs, last, core, chips, rows):
    xs, ds = [x for x, _ in pairs], [d for _, d in pairs]
    cols = sum(d.shape[1] for d in ds) + last.shape[1]
    if rows % 128:

        def own_columns(values, which):
            blocks = values.reshape(values.shape[0], chips, 2, rows)
            return lax.dynamic_index_in_dim(blocks, which, 2, keepdims=False).reshape(
                values.shape[0], chips * rows
            )

        def terms(which):
            return jnp.concatenate(
                [product_l(own_columns(x, which), d) for x, d in pairs]
                + [own_columns(last.T, which).T],
                axis=1,
            )

        return terms(core), low(terms(1 - core))
    block = pl.BlockSpec((rows, cols), lambda j, s: (j, 0))
    return grid_call(
        functools.partial(row_kernel, len(pairs)),
        core.reshape(1).astype(jnp.int32),
        (chips,),
        (*xs, *ds, last),
        [pl.BlockSpec((x.shape[0], 2 * rows), lambda j, s: (0, j)) for x in xs]
        + [once(d.shape) for d in ds]
        + [pl.BlockSpec((2 * rows, last.shape[1]), lambda j, s: (j, 0))],
        [
            jax.ShapeDtypeStruct((chips * rows, cols), F32),
            jax.ShapeDtypeStruct((chips * rows, cols), BF16),
        ],
        [block, block],
        [pltpu.VMEM((2 * rows, cols), F32)],
        sum(4 * d.size * chips * rows for d in ds),
        "row_grads",
    )


def last_kernel(large, *refs):
    mine, theirs, refs = refs[0], refs[1], refs[2:]
    ff_terms, refs = refs[:6], refs[6:]
    (main, little, *ff_outs), refs = refs[:5], refs[5:]
    own, core_got, side_sent, side_got, first, got, refs = *refs[:6], refs[6:]
    ff_held, (ff_sent,), refs = refs[:6], refs[6:7], refs[7:]
    loads, core_send, core_recv, side_send, side_recv, ring_send, ring_recv, ff_send, ff_recv = refs
    hops = Hops()
    side = lax.axis_index("tensor")
    half = hops.chips // 2
    rows = main.shape[0]
    part = little.shape[1] // 2
    ff_cols = ff_sent.shape[2]
    cut = rows // 2
    greet([hops.above, hops.below, hops.partner, hops.across])
    order = [half]
    for k in range(1, half):
        order += [half - k, k - half]
    order.append(0)

    def rows_at(offset, top=0, size=rows):
        return pl.ds(pl.multiple_of(hops.chip_at(offset) * rows + top, 16), size)

    started, arriving = [], []
    for i, offset in enumerate(order):
        at = rows_at(offset)
        copy = remote(
            theirs.at[at], core_got.at[at], core_send, core_recv, (i,), hops.partner
        )
        copy.start()
        load = pltpu.make_async_copy(mine.at[at], own.at[at], loads.at[i])
        load.start()
        started.append(copy)
        arriving.append((copy, load))
    ff_loads = [
        pltpu.make_async_copy(source, target, loads.at[len(order) + i])
        for i, (source, target) in enumerate(zip(ff_terms, ff_held))
    ]
    for load in ff_loads:
        load.start()

    sides = {}
    my_part = pl.ds(pl.multiple_of(large + side * part, 128), part)
    their_part = pl.ds(pl.multiple_of(large + (1 - side) * part, 128), part)

    def ready(i):
        at = rows_at(order[i])
        copy, load = arriving[i]
        load.wait()
        copy.wait_recv()
        own[at, :] = own[at, :] + to_float(core_got[at, :])
        side_sent[at, :] = low(own[at, their_part])
        copy = remote(
            side_sent.at[at], side_got.at[at], side_send, side_recv, (i,), hops.across
        )
        copy.start()
        started.append(copy)
        sides[order[i]] = copy

    pieces = [(0, large // 2), (large // 2, large // 2), (large, part)]
    copies = {}

    def term(which, offset, top, size):
        at = rows_at(offset, top, size)
        start, cols = pieces[which]
        if which < 2:
            return own[at, start : start + cols]
        return own[at, my_part] + to_float(side_got[at, :])

    def send(which, direction, k, source, top, size):
        start, cols = pieces[which]
        copy = remote(
            source,
            got.at[direction, k, pl.ds(top, size), pl.ds(start, cols)],
            ring_send,
            ring_recv,
            (direction, k, which),
            hops.above if direction == 0 else hops.below,
        )
        copy.start()
        started.append(copy)
        copies[(which, direction, k)] = copy

    def step(which, k):
        start, cols = pieces[which]
        for direction in range(2):
            near, far = direction * cut, (1 - direction) * cut
            if k == 0:
                first[direction, :, start : start + cols] = low(term(which, half, near, cut))
                source = first.at[direction, :, pl.ds(start, cols)]
                send(which, direction, 0, source, near, cut)
                continue
            offset = (half - k) * (1 if direction == 0 else -1)
            copies[(which, direction, k - 1)].wait_recv()
            if k == 1:
                held = got[direction, 0, near : near + cut, start : start + cols]
                got[direction, 0, near : near + cut, start : start + cols] = low(
                    term(which, offset, near, cut) + to_float(held)
                )
                got[direction, 0, far : far + cut, start : start + cols] = low(
                    term(which, offset, far, cut)
                )
            else:
                held = got[direction, k - 1, :, start : start + cols]
                got[direction, k - 1, :, start : start + cols] = low(
                    term(which, offset, 0, rows) + to_float(held)
                )
            source = got.at[direction, k - 1, :, pl.ds(start, cols)]
            send(which, direction, k, source, 0, rows)

    def end_feed_forward():
        for load in ff_loads:
            load.wait()
        wide, wide_up, wide_down, narrow, narrow_up, narrow_down = ff_held
        my_rows = pl.ds(pl.multiple_of(hops.core * rows, 16), rows)
        their_rows = pl.ds(pl.multiple_of((1 - hops.core) * rows, 16), rows)
        my_cols = pl.ds(pl.multiple_of(hops.core * ff_cols, 128), ff_cols)
        groups = [
            (wide, wide_up, wide_down, 0),
            (wide, wide_up, wide_down, ff_cols),
            (narrow, narrow_up, narrow_down, 0),
        ]
        for i, (base, up, down, start) in enumerate(groups):
            cols = slice(start, start + ff_cols)

            def total(at):
                return to_float(base[at, cols]) + to_float(up[at, cols]) + to_float(down[at, cols])

            ff_sent[i] = total(their_rows)
            copy = remote(
                ff_sent.at[i], ff_outs[i].at[:, my_cols], ff_send, ff_recv, (i,), hops.partner
            )
            copy.start()
            ff_copies.append(copy)
            ff_outs[i][:, my_cols] = total(my_rows)

    ff_copies = []
    ready(0)
    step(0, 0)
    step(1, 0)
    ready(1)
    ready(2)
    sides[half].wait_recv()
    step(2, 0)
    for k in range(1, half):
        if k > 1:
            sides[half - k].wait_recv()
            sides[k - half].wait_recv()
            step(2, k)
        step(0, k)
        step(1, k)
        if k == 1:
            end_feed_forward()
        for i in range(2 * k + 1, min(2 * k + 3, len(order))):
            ready(i)
        if k == 1:
            sides[half - k].wait_recv()
            sides[k - half].wait_recv()
            step(2, k)
    sides[0].wait_recv()
    for which in (2, 0, 1):
        start, cols = pieces[which]
        for direction in range(2):
            copies[(which, direction, half - 1)].wait_recv()
        total = (
            term(which, 0, 0, rows)
            + to_float(got[0, half - 1, :, start : start + cols])
            + to_float(got[1, half - 1, :, start : start + cols])
        )
        if which < 2:
            main[:, start : start + cols] = total
        else:
            here = pl.ds(pl.multiple_of(side * part, 128), part)
            little[:, here] = total
            little_copy = remote(
                little.at[:, here],
                little.at[:, here],
                side_send,
                side_recv,
                (len(order),),
                hops.across,
            )
            little_copy.start()
            started.append(little_copy)
    for copy in ff_copies + [little_copy]:
        copy.wait_recv()
    for copy in ff_copies + started:
        copy.wait_send()


def last_reduce(mine, theirs, large, ff_terms):
    chips = lax.axis_size("dp") // 2
    half = chips // 2
    tall, cols = mine.shape
    rows = tall // chips
    part = (cols - large) // 2
    ff = ff_terms[3].shape[1]
    vmem = pl.BlockSpec(memory_space=pltpu.VMEM)
    dma = pltpu.SemaphoreType.DMA
    return pl.pallas_call(
        functools.partial(last_kernel, large),
        out_shape=[
            jax.ShapeDtypeStruct((rows, large), F32),
            jax.ShapeDtypeStruct((rows, 2 * part), F32),
        ]
        + [jax.ShapeDtypeStruct((rows, 2 * ff), F32)] * 3,
        in_specs=[ANY] * 8,
        out_specs=[vmem] * 5,
        scratch_shapes=[
            pltpu.VMEM((tall, cols), F32),
            pltpu.VMEM((tall, cols), BF16),
            pltpu.VMEM((tall, part), BF16),
            pltpu.VMEM((tall, part), BF16),
            pltpu.VMEM((2, rows // 2, large + part), BF16),
            pltpu.VMEM((2, half, rows, large + part), BF16),
        ]
        + [pltpu.VMEM(v.shape, v.dtype) for v in ff_terms]
        + [
            pltpu.VMEM((3, rows, ff), F32),
            dma((2 * half + 6,)),
            dma((2 * half,)),
            dma((2 * half,)),
            dma((2 * half + 1,)),
            dma((2 * half + 1,)),
            dma((2, half, 3)),
            dma((2, half, 3)),
            dma((3,)),
            dma((3,)),
        ],
        compiler_params=pltpu.CompilerParams(
            collective_id=2, has_side_effects=True, vmem_limit_bytes=56 * 2**20
        ),
        cost_estimate=pl.CostEstimate(
            flops=0, bytes_accessed=20 * mine.size * 4, transcendentals=0
        ),
        name="last_reduce",
    )(mine, theirs, *ff_terms)


def forward_kernel(hops_done, tile, x_own, *refs):
    counts = [2 * done + 1 for done in hops_done]
    gate_parts, up_down_parts, refs = refs[: counts[0]], refs[counts[0] : sum(counts)], refs[sum(counts) :]
    gu_parts = (gate_parts, up_down_parts)
    size, ff = gate_parts[0].shape
    dn_parts = [ref.at[:, pl.ds(ff, ff)] for ref in up_down_parts]
    hops_done = (*hops_done, hops_done[1])
    (x_out, gu_full, gu_land, dn_full, raw, hidden, result), refs = refs[:7], refs[7:]
    x, dn, hidden_v, pairs, core_sent, core_got, side_sent, side_got, refs = *refs[:8], refs[8:]
    x_send, x_recv, gu_send, gu_recv, dn_send, dn_recv, core_sems, side_sems, loads, stores = refs
    hops = Hops()
    half, chips = hops.chips // 2, hops.chips
    own = x_own.shape[0]
    cut = size // 2
    greet([hops.above, hops.below, hops.partner, hops.across])
    started, saved = [], []

    def begin(copy, where=started):
        copy.start()
        where.append(copy)
        return copy

    def spot(ref, offset, top=0, tall=size):
        return block_rows(ref, hops.chip_at(offset) * size + top, tall)

    def gu_hop(k):
        copies = []
        for direction, ahead in ((0, hops.above), (1, hops.below)):
            offset = (1 - k) * (1 if direction == 0 else -1)
            top, tall = (0, size) if k < half else (direction * cut, cut)
            for group in range(2):
                if k <= hops_done[group]:
                    continue
                target = spot(gu_land.at[group], offset, top, tall)
                if k == hops_done[group] + 1:
                    held = gu_parts[group][2 * k - 3 + direction]
                    source = held.at[pl.ds(pl.multiple_of(top, 16), tall), pl.ds(0, ff)]
                else:
                    source = target
                index = (direction, k - 1, group)
                copies.append(begin(remote(source, target, gu_send, gu_recv, index, ahead)))
        return copies

    def dn_hop(k):
        copies = []
        for direction, ahead in ((0, hops.above), (1, hops.below)):
            offset = (1 - k) * (1 if direction == 0 else -1)
            top, tall = (0, size) if k < half else (direction * cut, cut)
            block = spot(dn, offset, top, tall)
            copies.append(begin(remote(block, block, dn_send, dn_recv, (direction, k - 1), ahead)))
        return copies

    def arrive(copies):
        for copy in copies:
            copy.wait_recv()

    first_hop = min(hops_done[:2]) + 1
    moving = gu_hop(first_hop)
    mine, far = pl.ds(0, own), pl.ds(own, own)
    near, opposite = pl.ds(2 * own, own), pl.ds(3 * own, own)
    load_x = begin(pltpu.make_async_copy(x_own, x.at[mine], loads.at[0]), saved)
    places = [0]
    for k in range(1, hops_done[2] + 1):
        places += [-k, k]
    dn_loads = [
        begin(pltpu.make_async_copy(ref, spot(dn, offset), loads.at[1 + i]), saved)
        for i, (ref, offset) in enumerate(zip(dn_parts, places))
    ]
    loaded = len(saved)
    from_far = begin(remote(x_own, x.at[far], x_send, x_recv, (0,), hops.across))
    from_near = begin(remote(x_own, x.at[near], x_send, x_recv, (1,), hops.partner))
    from_near.wait_recv()
    load_x.wait()
    arrive(moving)
    if first_hop < half:
        moving = gu_hop(first_hop + 1)
    from_far.wait_recv()
    passed = begin(remote(x.at[far], x.at[opposite], x_send, x_recv, (2,), hops.partner))
    passed.wait_recv()
    begin(pltpu.make_async_copy(x, x_out, stores.at[0]), saved)
    for copy in dn_loads:
        copy.wait()
    for k in range(first_hop + 2, half + 1):
        arrive(moving)
        moving = gu_hop(k)
    if first_hop < half:
        arrive(moving)
    moving = dn_hop(hops_done[2] + 1)

    here, landed = [], []
    for done in hops_done[:2]:
        near_by = [0]
        for k in range(1, done + 1):
            near_by += [-k, k]
        here.append(near_by)
        landed.append([o for o in range(-half + 1, half + 1) if o not in near_by])
    tiles = ff // tile

    def body(*tiles_of):
        ins, (raw_tile, hidden_tile, weights) = tiles_of[:-3], tiles_of[-3:]
        step = pl.program_id(0)
        for group in range(2):
            for number, offset in enumerate(here[group] + landed[group]):
                at = pl.ds(pl.multiple_of(hops.chip_at(offset) * size, size), size)
                weights[group, at, :] = ins[group * chips + number][...]
        gate = product(x[...], weights[0])
        up = product(x[...], weights[1])
        raw_tile[0] = low(gate)
        raw_tile[1] = low(up)
        bend = jnp.tanh(GELU_SCALE * (gate + GELU_CUBE * gate * gate * gate))
        value = low(0.5 * gate * (1.0 + bend) * up)
        hidden_tile[...] = value
        hidden_v[:, pl.ds(pl.multiple_of(step * tile, tile), tile)] = value

    def part_spec(row):
        return pl.BlockSpec((size, tile), lambda n: (row, n))

    in_specs, operands = [], []
    for group in range(2):
        for ref in gu_parts[group]:
            in_specs.append(part_spec(0))
            operands.append(ref)
        for offset in landed[group]:
            in_specs.append(part_spec(hops.chip_at(offset)))
            operands.append(gu_land.at[group])
    m, width = x.shape
    pltpu.emit_pipeline(
        body,
        grid=(tiles,),
        in_specs=in_specs,
        out_specs=[
            pl.BlockSpec((2, m, tile), lambda n: (0, 0, n)),
            pl.BlockSpec((m, tile), lambda n: (0, n)),
            pl.BlockSpec((2, width, tile), lambda n: (0, 0, n)),
        ],
    )(*operands, raw, hidden, gu_full)

    order, core_copies, side_copies = [], [], []

    def block_out(offset):
        i = len(order)
        order.append(offset)
        at = pl.ds(pl.multiple_of(hops.chip_at(offset) * size, size), size)
        out = product_t(hidden_v[...], dn[at, :])
        pairs[i] = out[: 2 * own]
        core_sent[i] = low(out[2 * own :])
        copy = remote(
            core_sent.at[i], core_got.at[i], core_sems.at[0], core_sems.at[1], (i,), hops.partner
        )
        core_copies.append(begin(copy))

    def core_sum():
        i = len(side_copies)
        core_copies[i].wait_recv()
        both = pairs[i] + to_float(core_got[i])
        side_sent[i] = low(both[own:])
        copy = remote(
            side_sent.at[i], side_got.at[i], side_sems.at[0], side_sems.at[1], (i,), hops.across
        )
        side_copies.append(begin(copy))
        at = pl.ds(pl.multiple_of(hops.chip_at(order[i]) * size, size), size)
        result[:, at] = both[:own]

    def out_and_sum(offset):
        block_out(offset)
        if len(order) > 1:
            core_sum()

    for k in range(hops_done[2] + 1, half + 1):
        arrive(moving)
        if k < half:
            moving = dn_hop(k + 1)
        if k == hops_done[2] + 1:
            for offset in places:
                out_and_sum(offset)
        if k < half:
            out_and_sum(-k)
            out_and_sum(k)
        else:
            out_and_sum(half)
    begin(pltpu.make_async_copy(dn, dn_full, stores.at[1]), saved)
    core_sum()
    for i, copy in enumerate(side_copies):
        copy.wait_recv()
        at = pl.ds(pl.multiple_of(hops.chip_at(order[i]) * size, size), size)
        result[:, at] = result[:, at] + to_float(side_got[i])
    for copy in started:
        copy.wait_send()
    for copy in saved[loaded:]:
        copy.wait()


def forward(x_own, gate_parts, up_down_parts, tile=512):
    chips = lax.axis_size("dp") // 2
    half = chips // 2
    own, width = x_own.shape
    size, ff = gate_parts[0].shape
    hops_done = [len(parts) // 2 for parts in (gate_parts, up_down_parts)]
    tile = min(tile, ff)
    m = 4 * own
    dma = pltpu.SemaphoreType.DMA
    vmem = pl.BlockSpec(memory_space=pltpu.VMEM)
    return pl.pallas_call(
        functools.partial(forward_kernel, hops_done, tile),
        out_shape=[
            jax.ShapeDtypeStruct((m, width), BF16),
            jax.ShapeDtypeStruct((2, width, ff), BF16),
            jax.ShapeDtypeStruct((2, width, ff), BF16),
            jax.ShapeDtypeStruct((width, ff), BF16),
            jax.ShapeDtypeStruct((2, m, ff), BF16),
            jax.ShapeDtypeStruct((m, ff), BF16),
            jax.ShapeDtypeStruct((own, width), F32),
        ],
        in_specs=[ANY] * (1 + len(gate_parts) + len(up_down_parts)),
        out_specs=[ANY] * 6 + [vmem],
        scratch_shapes=[
            pltpu.VMEM((m, width), BF16),
            pltpu.VMEM((width, ff), BF16),
            pltpu.VMEM((m, ff), BF16),
            pltpu.VMEM((chips, 2 * own, size), F32),
            pltpu.VMEM((chips, 2 * own, size), BF16),
            pltpu.VMEM((chips, 2 * own, size), BF16),
            pltpu.VMEM((chips, own, size), BF16),
            pltpu.VMEM((chips, own, size), BF16),
            dma((3,)),
            dma((3,)),
            dma((2, half, 2)),
            dma((2, half, 2)),
            dma((2, half)),
            dma((2, half)),
            dma((2, chips)),
            dma((2, chips)),
            dma((1 + len(up_down_parts),)),
            dma((2,)),
        ],
        compiler_params=pltpu.CompilerParams(
            collective_id=3, has_side_effects=True, vmem_limit_bytes=60 * 2**20
        ),
        cost_estimate=pl.CostEstimate(
            flops=6 * m * width * ff, bytes_accessed=0, transcendentals=0
        ),
        name="forward",
    )(x_own, *gate_parts, *up_down_parts)


def backward_kernel(d_own, hidden, raw, dn_full, gu_full, rows_in, *refs):
    (x_out, d_gu_out, held_up, held_down, wide_up, wide_down, result), refs = refs[:7], refs[7:]
    x, dn, hid, d_gu, raw_v, gu_v, first, got, refs = *refs[:8], refs[8:]
    pairs, core_sent, core_got, side_sent, side_got, refs = *refs[:5], refs[5:]
    rows_v, wide_first, refs = *refs[:2], refs[2:]
    x_send, x_recv, ring_send, ring_recv, core_sems, side_sems, wide_sems, loads, stores = refs
    hops = Hops()
    half, chips = hops.chips // 2, hops.chips
    own = d_own.shape[0]
    size, ff = held_up.shape
    cut = size // 2
    m = x.shape[0]
    cols = min(1024, ff)
    greet([hops.above, hops.below, hops.partner, hops.across])
    started, saved = [], []

    def begin(copy, where=started):
        copy.start()
        where.append(copy)
        return copy

    def load(source, target, number):
        copy = pltpu.make_async_copy(source, target, loads.at[number])
        copy.start()
        return copy

    def part(r):
        return pl.ds(r * own, own)

    from_far = begin(remote(d_own, x.at[part(1)], x_send, x_recv, (0,), hops.across))
    from_near = begin(remote(d_own, x.at[part(2)], x_send, x_recv, (1,), hops.partner))
    load_x = load(d_own, x.at[part(0)], 0)
    load_dn = load(dn_full, dn, 1)
    rows_order = (0, 2, 1, 3)
    raw_loads = {}

    def load_raw(i):
        r = rows_order[i]
        raw_loads[r] = load(raw.at[:, part(r)], raw_v.at[i % 2], 3 + i)

    def load_gu(j):
        return load(gu_full.at[:, pl.ds(j * size, size)], gu_v.at[j % 2], 7 + j)

    load_raw(0)
    load_raw(1)
    load_hid = load(hidden, hid, 2)
    far_block = pl.ds(pl.multiple_of(hops.chip_at(half) * size, size), size)
    load_rows = load(rows_in.at[:, far_block], rows_v, 7 + chips)

    def hidden_part(i):
        r = rows_order[i]
        at = part(r)
        raw_loads[r].wait()

        @pl.loop(0, ff // cols)
        def _(c):
            across_ = pl.ds(pl.multiple_of(c * cols, cols), cols)
            d_hidden = product(x[at, :], dn[:, across_])
            gate = to_float(raw_v[i % 2, 0, :, across_])
            up = to_float(raw_v[i % 2, 1, :, across_])
            square = gate * gate
            bend = jnp.tanh(GELU_SCALE * gate * (1.0 + GELU_CUBE * square))
            plus = 0.5 * (1.0 + bend)
            slope = plus + 0.5 * gate * (1.0 - bend * bend) * GELU_SCALE * (
                1.0 + 3.0 * GELU_CUBE * square
            )
            d_gu[0, at, across_] = low(d_hidden * up * slope)
            d_gu[1, at, across_] = low(d_hidden * gate * plus)

        if i + 2 < 4:
            load_raw(i + 2)

    copies = {}

    def ring_step(k):
        for direction, ahead in ((0, hops.above), (1, hops.below)):
            near, far = direction * cut, (1 - direction) * cut
            offset = (half - k) * (1 if direction == 0 else -1)
            at = pl.ds(pl.multiple_of(hops.chip_at(offset) * size, size), size)
            term = product_l(x[:, at], hid[...])
            if k == 0:
                first[direction] = low(term[near : near + cut])
                source = first.at[direction]
                target = got.at[direction, 0, pl.ds(near, cut)]
            else:
                copies[(direction, k - 1)].wait_recv()
                came = got.at[direction, k - 1]
                if k == 1:
                    came[near : near + cut, :] = low(
                        term[near : near + cut] + to_float(came[near : near + cut, :])
                    )
                    came[far : far + cut, :] = low(term[far : far + cut])
                else:
                    came[...] = low(term + to_float(came[...]))
                source = came
                target = got.at[direction, k]
            copies[(direction, k)] = begin(
                remote(source, target, ring_send, ring_recv, (direction, k), ahead)
            )

    core_copies, side_copies = [], []

    def block_out(j, loading):
        loading.wait()
        out = product_t(d_gu[0], gu_v[j % 2, 0]) + product_t(d_gu[1], gu_v[j % 2, 1])
        pairs[j] = out[: 2 * own]
        core_sent[j] = low(out[2 * own :])
        copy = remote(
            core_sent.at[j], core_got.at[j], core_sems.at[0], core_sems.at[1], (j,), hops.partner
        )
        core_copies.append(begin(copy))

    def core_sum(j):
        core_copies[j].wait_recv()
        both = pairs[j] + to_float(core_got[j])
        side_sent[j] = low(both[own:])
        copy = remote(
            side_sent.at[j], side_got.at[j], side_sems.at[0], side_sems.at[1], (j,), hops.across
        )
        side_copies.append(begin(copy))
        result[:, j * size : (j + 1) * size] = both[:own]

    load_x.wait()
    load_dn.wait()
    hidden_part(0)
    from_near.wait_recv()
    hidden_part(1)
    from_far.wait_recv()
    passed = begin(remote(x.at[part(1)], x.at[part(3)], x_send, x_recv, (2,), hops.partner))
    hidden_part(2)
    passed.wait_recv()
    load_hid.wait()
    ring_step(0)
    gu_loads = {0: load_gu(0), 1: load_gu(1)}
    hidden_part(3)
    steps = list(range(1, half - 1))
    if steps:
        ring_step(steps.pop(0))
    load_rows.wait()
    for group in range(2):
        wide = product_l(rows_v[...], d_gu[group])
        for direction in range(2):
            wide_first[direction, :, group * ff : (group + 1) * ff] = low(
                wide[direction * cut : (direction + 1) * cut]
            )
    wide_copies = [
        begin(
            remote(
                wide_first.at[direction],
                target,
                wide_sems.at[0],
                wide_sems.at[1],
                (direction,),
                ahead,
            )
        )
        for direction, target, ahead in (
            (0, wide_up, hops.above),
            (1, wide_down, hops.below),
        )
    ]
    begin(pltpu.make_async_copy(x, x_out, stores.at[0]), saved)
    begin(pltpu.make_async_copy(d_gu, d_gu_out, stores.at[1]), saved)
    for j in range(chips):
        block_out(j, gu_loads[j])
        if j + 2 < chips:
            gu_loads[j + 2] = load_gu(j + 2)
        if j > 0:
            core_sum(j - 1)
        if j == 3 and steps:
            ring_step(steps.pop(0))
    core_sum(chips - 1)
    for k in steps:
        ring_step(k)
    for j, copy in enumerate(side_copies):
        copy.wait_recv()
        at = slice(j * size, (j + 1) * size)
        result[:, at] = result[:, at] + to_float(side_got[j])
    for direction, target in ((0, held_up), (1, held_down)):
        offset = 1 if direction == 0 else -1
        at = pl.ds(pl.multiple_of(hops.chip_at(offset) * size, size), size)
        term = product_l(x[:, at], hid[...])
        copies[(direction, half - 2)].wait_recv()
        came = got.at[direction, half - 2]
        came[...] = low(term + to_float(came[...]))
        begin(pltpu.make_async_copy(came, target, stores.at[2 + direction]), saved)
        wide_copies[direction].wait_recv()
    for copy in started:
        copy.wait_send()
    for copy in saved:
        copy.wait()


def backward(d_own, hidden, raw, dn_full, gu_full, rows_in):
    chips = lax.axis_size("dp") // 2
    half = chips // 2
    own, width = d_own.shape
    m, ff = hidden.shape
    size = width // chips
    dma = pltpu.SemaphoreType.DMA
    vmem = pl.BlockSpec(memory_space=pltpu.VMEM)
    return pl.pallas_call(
        backward_kernel,
        out_shape=[
            jax.ShapeDtypeStruct((m, width), BF16),
            jax.ShapeDtypeStruct((2, m, ff), BF16),
            jax.ShapeDtypeStruct((size, ff), BF16),
            jax.ShapeDtypeStruct((size, ff), BF16),
            jax.ShapeDtypeStruct((size // 2, 2 * ff), BF16),
            jax.ShapeDtypeStruct((size // 2, 2 * ff), BF16),
            jax.ShapeDtypeStruct((own, width), F32),
        ],
        in_specs=[ANY] * 6,
        out_specs=[ANY] * 6 + [vmem],
        scratch_shapes=[
            pltpu.VMEM((m, width), BF16),
            pltpu.VMEM((width, ff), BF16),
            pltpu.VMEM((m, ff), BF16),
            pltpu.VMEM((2, m, ff), BF16),
            pltpu.VMEM((2, 2, own, ff), BF16),
            pltpu.VMEM((2, 2, size, ff), BF16),
            pltpu.VMEM((2, size // 2, ff), BF16),
            pltpu.VMEM((2, half - 1, size, ff), BF16),
            pltpu.VMEM((chips, 2 * own, size), F32),
            pltpu.VMEM((chips, 2 * own, size), BF16),
            pltpu.VMEM((chips, 2 * own, size), BF16),
            pltpu.VMEM((chips, own, size), BF16),
            pltpu.VMEM((chips, own, size), BF16),
            pltpu.VMEM((m, size), BF16),
            pltpu.VMEM((2, size // 2, 2 * ff), BF16),
            dma((3,)),
            dma((3,)),
            dma((2, half - 1)),
            dma((2, half - 1)),
            dma((2, chips)),
            dma((2, chips)),
            dma((2, 2)),
            dma((8 + chips,)),
            dma((4,)),
        ],
        compiler_params=pltpu.CompilerParams(
            collective_id=4, has_side_effects=True, vmem_limit_bytes=60 * 2**20
        ),
        cost_estimate=pl.CostEstimate(
            flops=6 * m * width * ff, bytes_accessed=0, transcendentals=0
        ),
        name="backward",
    )(d_own, hidden, raw, dn_full, gu_full, rows_in)


def prepare_kernel(q_cols, kv_cols, spots, x, gain, w, cos, sin, gains, rows, raw, query, kv):
    turn = HD // 2
    values = to_float(x[...])
    scale = lax.rsqrt(jnp.mean(values * values, axis=-1, keepdims=True) + EPS)
    rows[...] = low(values * scale * gain[...])
    raw[...] = product(rows[...], w[...])
    cosines, sines = cos[...], sin[...]
    for start in range(0, q_cols + 2 * kv_cols, HD):
        at = slice(start, start + HD)
        head = raw[:, at]
        head = head * lax.rsqrt(jnp.mean(head * head, axis=-1, keepdims=True) + EPS)
        if start < q_cols + kv_cols:
            which = 0 if start < q_cols else 1
            head = head * gains[which : which + 1, :]
            front, rear = head[:, :turn], head[:, turn:]
            head = jnp.concatenate(
                [front * cosines - rear * sines, rear * cosines + front * sines], axis=1
            )
        if start < q_cols:
            query[start // HD] = low(head)
        else:
            kv[:, start - q_cols : start - q_cols + HD] = low(head)


def prepare(x, gain, w, cos, sin, gains, side, q_cols):
    (tall, width), cols = x.shape, w.shape[1]
    tile = tall // 2
    kv_cols = (cols - q_cols) // 2
    natural = lax.rem(jnp.arange(2) + side, 2).astype(jnp.int32)

    def straight(columns):
        return pl.BlockSpec((tile, columns), lambda t, s: (t, 0))

    return grid_call(
        functools.partial(prepare_kernel, q_cols, kv_cols),
        natural,
        (2,),
        (x, gain, w, cos, sin, gains),
        [
            straight(width),
            once(gain.shape),
            once(w.shape),
            straight(HD // 2),
            straight(HD // 2),
            once(gains.shape),
        ],
        [
            jax.ShapeDtypeStruct((tall, width), BF16),
            jax.ShapeDtypeStruct((tall, cols), F32),
            jax.ShapeDtypeStruct((q_cols // HD, tall, HD), BF16),
            jax.ShapeDtypeStruct((tall, 2 * kv_cols), BF16),
        ],
        [
            straight(width),
            straight(cols),
            pl.BlockSpec((q_cols // HD, tile, HD), lambda t, s: (0, t, 0)),
            pl.BlockSpec((tile, 2 * kv_cols), lambda t, s: (s[t], 0)),
        ],
        [],
        2 * tall * width * cols,
        "prepare",
    )


def prepare_back_kernel(q_cols, kv_cols, spots, raw, d_q, d_kv, after, before, cos, sin, gains, *refs):
    out, gain_grads = refs
    tall = raw.shape[0]
    turn = HD // 2
    cosines, sines = cos[...], sin[...]

    @pl.when(pl.program_id(0) == 0)
    def _():
        gain_grads[...] = jnp.zeros_like(gain_grads)

    early = spots[1 + pl.program_id(0)] < spots[0]
    more = to_float(after[...]) + jnp.where(early, to_float(before[...]), 0.0)

    def back(values, d, gain):
        scale = lax.rsqrt(jnp.mean(values * values, axis=-1, keepdims=True) + EPS)
        d_gain = d if gain is None else d * gain
        inner = jnp.mean(values * d_gain, axis=-1, keepdims=True)
        return scale * d_gain - values * (scale * scale * scale * inner), values * scale * d

    def unturn(d):
        front, rear = d[:, :turn], d[:, turn:]
        return jnp.concatenate(
            [front * cosines + rear * sines, rear * cosines - front * sines], axis=1
        )

    for start in range(0, q_cols + 2 * kv_cols, HD):
        at = slice(start, start + HD)
        values = raw[:, at]
        if start < q_cols:
            d, which = unturn(d_q[start // HD]), 0
        else:
            here = slice(start - q_cols, start - q_cols + HD)
            d = d_kv[:, here] + more[:, here]
            which = 1
            if start < q_cols + kv_cols:
                d = unturn(d)
        if start < q_cols + kv_cols:
            d_values, for_gain = back(values, d, gains[which : which + 1, :])
            gain_grads[which : which + 1, :] = gain_grads[which : which + 1, :] + jnp.sum(
                for_gain, axis=0, keepdims=True
            )
        else:
            d_values, _ = back(values, d, None)
        out[:, at] = low(d_values)


def prepare_back(raw, d_q, d_kv, after, before, cos, sin, gains, side, own, tile=128):
    tall, cols = raw.shape
    kv_cols = d_kv.shape[1] // 2
    q_cols = cols - 2 * kv_cols
    tiles = tall // tile
    near = before.shape[0] // tile
    natural = lax.rem(jnp.arange(tiles) + side * (own // tile), tiles)
    spots = jnp.concatenate([jnp.full((1,), near), natural]).astype(jnp.int32)

    def straight(width):
        return pl.BlockSpec((tile, width), lambda t, s: (t, 0))

    def ordered(width):
        return pl.BlockSpec((tile, width), lambda t, s: (s[1 + t], 0))

    return grid_call(
        functools.partial(prepare_back_kernel, q_cols, kv_cols),
        spots,
        (tiles,),
        (raw, d_q, d_kv, after, before, cos, sin, gains),
        [
            straight(cols),
            pl.BlockSpec((q_cols // HD, tile, HD), lambda t, s: (0, t, 0)),
            ordered(2 * kv_cols),
            ordered(2 * kv_cols),
            pl.BlockSpec((tile, 2 * kv_cols), lambda t, s: (jnp.minimum(s[1 + t], near - 1), 0)),
            straight(HD // 2),
            straight(HD // 2),
            once(gains.shape),
        ],
        [jax.ShapeDtypeStruct((tall, cols), BF16), jax.ShapeDtypeStruct((8, HD), F32)],
        [straight(cols), once((8, HD))],
        [],
        10 * raw.size,
        "prepare_back",
    )


class Gather:
    def __init__(self, ring, block):
        self.ring = ring
        self.rows = block.shape[0]
        self.held = [block, block]
        self.parts = [(0, 0, block)]
        self.step_count = 0

    def step(self):
        ring, half = self.ring, self.ring.chips // 2
        self.step_count += 1
        k = self.step_count
        going_up, going_down = self.held
        if k < half:
            self.held = [ring.up(going_up), ring.down(going_down)]
            self.parts += [(-k, 0, self.held[0]), (k, 0, self.held[1])]
        else:
            cut = self.rows // 2
            self.held = [ring.up(going_up[:cut]), ring.down(going_down[cut:])]
            self.parts += [(half, 0, self.held[0]), (half, cut, self.held[1])]

    def pieces(self):
        spots = [self.ring.chip_at(o) * self.rows + row for o, row, _ in self.parts]
        return jnp.stack(spots).astype(jnp.int32), [part for _, _, part in self.parts]


class BlockReduce:
    def __init__(self, ring, x, d, size):
        self.ring, self.x, self.d, self.size = ring, x, d, size
        self.step_count = 0
        self.held = []

    def offsets(self):
        half = self.ring.chips // 2
        k = self.step_count + 1
        return (half,) if k == 1 else (half + 1 - k, k - 1 - half)

    def blocks(self, offsets, gots=()):
        chips = [self.ring.chip_at(o) for o in offsets]
        return block_grads(self.x, self.d, chips, self.size, gots)

    def terms(self):
        return self.blocks(self.offsets())

    def last_term(self):
        return self.blocks((0,))[0]

    def step(self, terms=None, *beside):
        ring, half = self.ring, self.ring.chips // 2
        self.step_count += 1
        k = self.step_count
        cut = self.size // 2
        if k == 1:
            (term,) = self.blocks((half,))
            up, down = term[:cut], term[cut:]
        elif terms is None:
            up, down = self.blocks((half + 1 - k, k - 1 - half), self.held)
        else:
            up, down = add_blocks(terms, self.held)
        up, down, beside = tie(up, down, beside)
        self.held = [ring.up(up), ring.down(down)]
        return beside


def region(body):
    shapes = jax.eval_shape(body)
    yes = lax.optimization_barrier(jnp.array(True))
    return lax.cond(
        yes,
        body,
        lambda: jax.tree.map(lambda v: jnp.zeros(v.shape, v.dtype), shapes),
    )


def meet(rings, *values):
    held, values = tie([r.held for r in rings], values)
    for r, h in zip(rings, held):
        r.held = h
    return values if len(values) != 1 else values[0]


def local(
    tokens,
    layer_input,
    block_ids,
    block_table,
    w_query,
    w_key,
    w_value,
    w_output,
    w_left,
    w_right,
    w_gate,
    w_up,
    w_down,
    w_layer_gate,
    w_layer_proj,
    query_gain,
    key_gain,
    gain_input,
    gain_attn_out,
    gain_laurel,
    gain_ffw_in,
    gain_ffw_out,
    gain_layer_out,
    out_grad,
):
    ring = Ring()
    side = lax.axis_index("tensor")
    core = ring.core
    rows = w_query.shape[0]
    own = tokens.shape[0]
    width = tokens.shape[1]
    q_cols = w_query.shape[1]
    kv_cols = w_key.shape[1]
    rank = w_left.shape[1]
    small = w_layer_gate.shape[1]
    ff_cols = w_gate.shape[1] // 2
    chips = ring.chips

    gain_list = [
        gain_input,
        gain_attn_out,
        gain_laurel,
        gain_ffw_in,
        gain_ffw_out,
        gain_layer_out,
        query_gain,
        key_gain,
    ]
    gains = jnp.stack([jnp.pad(to_float(v), (0, 128 - v.shape[0])) for v in gain_list])
    gains = jnp.pad(gains, ((0, 8), (0, 0)))
    half = chips // 2
    if rows % 128 == 0:
        blocks = [
            [(w_query, False), (w_key, False), (w_value, False)],
            [(w_output, True)],
            [(w_left, False), (w_right, True), (w_layer_gate, False), (w_layer_proj, True)],
        ]
        down_source = (w_down, True)
    else:
        blocks = [
            [(jnp.concatenate([w_query, w_key, w_value], axis=1), False)],
            [(w_output.T, False)],
            [(jnp.concatenate([w_left, w_right.T, w_layer_gate, w_layer_proj.T], axis=1), False)],
        ]
        down_source = (w_down.T, False)
    (qkv_full, output_t, small_full, gains_full), (*ff_own, both_tokens) = first_gather(
        blocks + [[(gains, False)]], w_gate, w_up, down_source, tokens
    )
    left_full = small_full[:, :rank]
    right_t = small_full[:, rank : 2 * rank]
    lgate_full = small_full[:, 2 * rank : 2 * rank + small]
    lproj_t = small_full[:, 2 * rank + small : 2 * rank + 2 * small]
    gains_full = gains_full.reshape(ring.devices, 16, 128)
    head_part = query_gain.shape[0]
    (
        input_scale,
        attn_scale,
        laurel_scale,
        ffw_in_scale,
        ffw_out_scale,
        layer_scale,
    ) = (gains_full[:, i, :rows].reshape(width) for i in range(6))
    query_scale, key_scale = (gains_full[:, i, :head_part].reshape(HD) for i in (6, 7))

    piece_len = 2 * own
    seq_total = block_ids.shape[1]
    per_seq = seq_total // piece_len
    dp_index = lax.axis_index("dp")
    row_index = dp_index // per_seq
    slot = lax.rem(dp_index, per_seq)
    first = slot * piece_len
    has_before = slot > 0
    has_after = slot < per_seq - 1
    natural = jnp.arange(piece_len, dtype=jnp.int32)
    here = first + lax.rem(natural + side * own, piece_len)
    cosines, sines = rope_tables(here, HD)
    reach_after = min(256, piece_len)
    forward_pairs = [(i, i + 1) for i in range(ring.devices - 1)]
    backward_pairs = [(i + 1, i) for i in range(ring.devices - 1)]

    def in_order(values):
        return jnp.where(
            side == 0, values, jnp.concatenate([values[own:], values[:own]], axis=0)
        )

    ids_row = lax.dynamic_index_in_dim(block_ids, row_index, 0, keepdims=False)
    table_row = lax.dynamic_index_in_dim(block_table, row_index, 0, keepdims=False)
    own_ids = lax.dynamic_slice_in_dim(ids_row, first, piece_len, 0)
    before_ids = lax.dynamic_slice_in_dim(ids_row, jnp.maximum(first - piece_len, 0), piece_len, 0)
    before_ids = jnp.where(has_before, before_ids, -2)
    after_ids = lax.dynamic_slice_in_dim(
        ids_row, jnp.minimum(first + piece_len, seq_total - reach_after), reach_after, 0
    )
    after_ids = jnp.where(has_after, after_ids, -2)
    key_ids = jnp.concatenate([before_ids, own_ids, after_ids], axis=0)
    query_ids = in_order(own_ids)
    block_count = block_table.shape[-1]
    number_rows = jnp.arange(block_count, dtype=jnp.int32)
    sees_last = jnp.sum(
        jnp.where(number_rows[None, :] == number_rows[:, None] - 1, table_row, 0), axis=1
    )
    query_sees = jnp.sum(
        jnp.where(query_ids[:, None] == number_rows[None, :], sees_last[None, :], 0), axis=1
    )
    previous_ids = jnp.where(query_sees == 1, query_ids - 1, query_ids)

    both_gains = jnp.pad(jnp.stack([query_scale, key_scale]), ((0, 6), (0, 0)))

    heads_local = q_cols // HD
    all_rows = heads_local * piece_len

    def scores_for(query_low, keys):
        allowed = (query_ids[:, None] == key_ids[None, :]) | (
            previous_ids[:, None] == key_ids[None, :]
        )
        scores = product_t(query_low, keys).reshape(heads_local, piece_len, -1)
        return jnp.where(allowed[None], scores, NEGATIVE)

    def sum_sides(partial, beside=None):
        got = across(low(partial[own:]))
        if beside is None:
            return partial[:own] + to_float(got)
        got, beside = tie(got, beside())
        return partial[:own] + to_float(got), beside

    def both_sides(values, beside=None):
        got = across(values)
        if beside is None:
            return jnp.concatenate([values, got], axis=0)
        got, beside = tie(got, beside())
        return jnp.concatenate([values, got], axis=0), beside

    def four_ways(values):
        pair = both_sides(values)
        return jnp.concatenate([pair, ring.swap(pair)], axis=0)

    def sum_four(partial, beside=None):
        pair = partial[: 2 * own] + to_float(ring.swap(low(partial[2 * own :])))
        return sum_sides(pair, beside)

    def attend(query_low, kv_all):
        scores = scores_for(query_low, kv_all[:, :HD])
        highest = jnp.max(scores, axis=-1, keepdims=True)
        weights_exp = jnp.exp(scores - highest)
        totals = jnp.sum(weights_exp, axis=-1, keepdims=True)
        probs_low = low(weights_exp / totals).reshape(all_rows, -1)
        attended = low(product(probs_low, kv_all[:, HD:]))
        attended = attended.reshape(heads_local, piece_len, HD).transpose(1, 0, 2)
        return highest + jnp.log(totals), attended.reshape(piece_len, q_cols)

    fused = (2 * rows) % 256 == 0
    gate_ring, more_ring = (Gather(ring, v) for v in ff_own)
    gate_ring.step()
    seq_rows, qkv_raw, query_low, kv_own = region(
        lambda: prepare(
            both_tokens, input_scale[None], qkv_full, cosines, sines, both_gains, side, q_cols
        )
    )
    query_low = query_low.reshape(all_rows, HD)
    kv_own, query_ids, previous_ids, key_ids, *small_parts = meet(
        [gate_ring],
        kv_own,
        query_ids,
        previous_ids,
        key_ids,
        left_full,
        right_t,
        lgate_full,
        lproj_t,
    )
    left_full, right_t, lgate_full, lproj_t = small_parts
    kv_before = lax.ppermute(kv_own, "dp", forward_pairs)
    kv_after = lax.ppermute(kv_own[:reach_after], "dp", backward_pairs)
    kv_before, kv_after, more_ring.held, gate_ring.held = tie(
        kv_before, kv_after, more_ring.held, gate_ring.held
    )
    more_ring.step()
    gate_ring.step()
    kv_all = jnp.concatenate([kv_before, kv_own, kv_after], axis=0)
    def join(heads_low):
        attn_out = sum_sides(product_t(heads_low, output_t))
        normed = norm_gain(to_float(tokens), input_scale)
        left_low = low(product(low(normed), left_full))
        right_out = product_t(left_low, right_t)
        laurel_normed = norm_gain(right_out, laurel_scale)
        attn_normed = norm_gain(attn_out, attn_scale)
        mixed = (to_float(tokens) + attn_normed + (normed + laurel_normed)) * ROOT_HALF
        return attn_out, left_low, right_out, mixed, low(norm_gain(mixed, ffw_in_scale))

    def attend_and_join():
        log_totals, heads_low = attend(query_low, kv_all)
        return log_totals, heads_low, *join(heads_low)

    log_totals, heads_low, attn_out, left_low, right_out, mixed, ffw_low = region(attend_and_join)
    ffw_low = meet([gate_ring, more_ring], ffw_low)

    if fused:
        ffw_rows, gu_weights, _, dn_whole, raw, hidden_low, ffw_out = forward(
            ffw_low,
            [part for _, _, part in gate_ring.parts],
            [part for _, _, part in more_ring.parts],
        )
        dn_spots, dn_parts = jnp.zeros((1,), jnp.int32), [dn_whole]
    else:
        ffw_rows = four_ways(ffw_low)
        for weights_ring in (gate_ring, more_ring):
            while weights_ring.step_count < half:
                weights_ring.step()
        gu_spots, gate_parts = gate_ring.pieces()
        dn_spots, more_parts = more_ring.pieces()
        up_parts = [part[:, :ff_cols] for part in more_parts]
        dn_parts = [part[:, ff_cols:] for part in more_parts]
        raw, hidden_low, gu_weights = gate_up(ffw_rows, gu_spots, gate_parts, up_parts)
        ffw_out = sum_four(columns_out(hidden_low[None], dn_spots, dn_parts, width))
    ffw_out_normed, ffw_out_back = jax.vjp(norm_gain, ffw_out, ffw_out_scale)
    block_mid = mixed + ffw_out_normed
    mid_low = low(block_mid)
    layer_pre = product(mid_low, lgate_full)

    def layer_gate_fn(pre_values, per_layer):
        return gelu_tanh(pre_values) * per_layer

    gated, gated_back = jax.vjp(layer_gate_fn, layer_pre, to_float(layer_input))
    gated_low = low(gated)
    layer_proj = product_t(gated_low, lproj_t)
    proj_normed, proj_back = jax.vjp(norm_gain, layer_proj, layer_scale)
    result = block_mid + proj_normed

    grad_out = to_float(out_grad)
    d_proj, d_layer_scale = proj_back(grad_out)
    d_proj_low = low(d_proj)
    d_gated = product(d_proj_low, lproj_t)
    d_pre, grad_layer_input = gated_back(d_gated)
    d_pre_low = low(d_pre)
    d_mid = grad_out + product_t(d_pre_low, lgate_full)
    d_ffw_out, d_ffw_out_scale = ffw_out_back(d_mid)
    if fused:
        d_ffw_rows, d_gate_up, *held, d_ffw_normed = backward(
            low(d_ffw_out), hidden_low, raw, dn_whole, gu_weights, ffw_rows
        )
        rd = BlockReduce(ring, d_ffw_rows, hidden_low[None], 2 * rows)
        rd.held, rd.step_count = [ring.up(held[0]), ring.down(held[1])], half
        rg = BlockReduce(ring, ffw_rows, d_gate_up, 2 * rows)
        rg.held, rg.step_count = held[2:], 1
    else:
        d_ffw_rows = four_ways(low(d_ffw_out))
        rd = BlockReduce(ring, d_ffw_rows, hidden_low[None], 2 * rows)
        for _ in range(half - 1):
            rd.step()
            meet([rd])
        d_gate_up = hidden_back(d_ffw_rows, raw, dn_spots, dn_parts)
        d_ffw_normed = sum_four(
            product_t(d_gate_up[0], gu_weights[0]) + product_t(d_gate_up[1], gu_weights[1])
        )
        rg = BlockReduce(ring, ffw_rows, d_gate_up, 2 * rows)
        for _ in range(half - 3):
            rg.step()
            meet([rg])
        rd.step()
    rg.step()

    def back_34():
        _, back = jax.vjp(norm_gain, mixed, ffw_in_scale)
        d_mixed_extra, d_ffw_in_scale = back(d_ffw_normed)
        d_branch = (d_mid + d_mixed_extra) * ROOT_HALF
        _, back = jax.vjp(norm_gain, attn_out, attn_scale)
        d_attn, d_attn_scale = back(d_branch)
        d_attn_rows, terms = both_sides(low(d_attn), rg.terms)
        d_heads = low(product(d_attn_rows, output_t)).reshape(piece_len, heads_local, HD)
        d_heads = d_heads.transpose(1, 0, 2).reshape(all_rows, HD)
        keys, values = kv_all[:, :HD], kv_all[:, HD:]
        probs = jnp.exp(scores_for(query_low, keys) - log_totals)
        d_values = product_l(low(probs).reshape(all_rows, -1), d_heads)
        d_probs = product_t(d_heads, values).reshape(probs.shape)
        deltas = jnp.sum(probs * d_probs, axis=-1, keepdims=True)
        d_scores = low(probs * (d_probs - deltas)).reshape(all_rows, -1)
        d_keys = product_l(d_scores, query_low)
        d_query_rot = product(d_scores, keys).reshape(heads_local, piece_len, HD)
        d_kv_all = jnp.concatenate([d_keys, d_values], axis=1)
        to_before = low(d_kv_all[:piece_len])
        to_after = low(d_kv_all[2 * piece_len :])
        d_kv_own = d_kv_all[piece_len : 2 * piece_len]
        moving = (to_before, to_after)
        kept = (d_ffw_in_scale, d_attn_scale, d_branch, d_attn_rows, d_kv_own)
        return terms, moving, kept, d_query_rot

    terms, moving, kept, d_query_rot = meet([rd, rg], *region(back_34))
    d_ffw_in_scale, d_attn_scale, d_branch, d_attn_rows, d_kv_own = kept
    from_after = lax.ppermute(moving[0], "dp", backward_pairs)
    from_before = lax.ppermute(moving[1], "dp", forward_pairs)
    from_after, from_before = rg.step(terms, from_after, from_before)

    def back_5():
        d_qkv_low, gain_sums = prepare_back(
            qkv_raw,
            d_query_rot,
            d_kv_own,
            from_after,
            from_before,
            cosines,
            sines,
            both_gains,
            side,
            own,
        )
        d_more, ends = sum_sides(
            product_t(d_qkv_low, qkv_full), lambda: (rd.last_term(), rg.last_term(), rg.terms())
        )
        return d_more, ends, d_qkv_low, gain_sums[0], gain_sums[1]

    d_more, ends, d_qkv_low, query_scale_grad, key_scale_grad = meet([rg], *region(back_5))
    *ends, terms = ends
    rg.step(terms)

    def head_gain_back(grads):
        padded = jnp.pad(grads.reshape(ring.devices, head_part), ((0, 0), (0, rows - head_part)))
        return padded.reshape(width)

    def back_6():
        normed, input_norm_back = jax.vjp(norm_gain, to_float(tokens), input_scale)
        _, laurel_back = jax.vjp(norm_gain, right_out, laurel_scale)
        d_right, d_laurel_scale = laurel_back(d_branch)
        d_right_low = low(d_right)
        d_left_low = low(product(d_right_low, right_t))
        d_normed = d_branch + product_t(d_left_low, left_full)
        d_normed = d_normed + d_more
        d_inputs_extra, d_input_scale = input_norm_back(d_normed)
        grad_tokens = d_branch + d_inputs_extra
        gain_grads = jnp.stack(
            [
                d_input_scale,
                d_attn_scale,
                d_laurel_scale,
                d_ffw_in_scale,
                d_ffw_out_scale,
                d_layer_scale,
                head_gain_back(query_scale_grad),
                head_gain_back(key_scale_grad),
            ],
            axis=0,
        )
        gain_grads = jnp.pad(gain_grads, ((0, 120), (0, 0))).T
        pairs = [
            (d_attn_rows, heads_low),
            (seq_rows, d_qkv_low),
            (mid_low, d_pre_low),
            (d_proj_low, gated_low),
            (low(normed), d_left_low),
            (d_right_low, left_low),
        ]
        return grad_tokens, row_grads(pairs, gain_grads, core, chips, rows)

    grad_tokens, (mine, theirs) = meet([rg], *region(back_6))
    down_end, gate_up_end = ends
    total, out_small, out_gate, out_up, out_down_t = last_reduce(
        mine,
        theirs,
        2 * q_cols + 2 * kv_cols,
        [gate_up_end, *rg.held, down_end, *rd.held],
    )
    out_output = total[:, :q_cols].T
    out_qkv = total[:, q_cols:]
    out_gains = out_small[:, 2 * rank + 2 * small :]
    return (
        low(result),
        grad_tokens,
        grad_layer_input,
        out_qkv[:, :q_cols],
        out_qkv[:, q_cols : q_cols + kv_cols],
        out_qkv[:, q_cols + kv_cols :],
        out_output,
        out_small[:, 2 * small : 2 * small + rank],
        out_small[:, 2 * small + rank : 2 * small + 2 * rank].T,
        out_gate,
        out_up,
        out_down_t.T,
        out_small[:, :small],
        out_small[:, small : 2 * small].T,
        out_gains[:head_part, 6],
        out_gains[:head_part, 7],
        out_gains[:, 0],
        out_gains[:, 1],
        out_gains[:, 2],
        out_gains[:, 3],
        out_gains[:, 4],
        out_gains[:, 5],
    )


def solution(mesh):
    both = P(("dp", "tensor"), None)
    rows_split = P("dp", "tensor")
    cols_split = P("tensor", "dp")
    by_row = P("dp", None)
    by_col = P(None, "dp")
    flat = P("dp")
    return jax.shard_map(
        local,
        mesh=mesh,
        in_specs=(
            (both, both, P(), P(), rows_split, rows_split, rows_split, cols_split)
            + (by_row, by_col, rows_split, rows_split, cols_split, by_row, by_col)
            + (flat,) * 8
            + (both,)
        ),
        out_specs=(
            (both, both, both, rows_split, rows_split, rows_split, cols_split)
            + (by_row, by_col, rows_split, rows_split, cols_split, by_row, by_col)
            + (flat,) * 8
        ),
        check_vma=False,
    )
```
